32 devices in a mesh: ctx: 8 (over y, x, core), wsh: 4 (over z).
Axes of the slice: x: 2, y: 2, z: 4, core: 2. Of those that a mesh axis runs over, the one named last changes fastest.
Arguments:
- states: bfloat16 [4, 2048, 2, 768], P('wsh', 'ctx'), may hold values from -6 to 6
- block_slot: int32 [4, 32], P('wsh'), may hold values from 0 to 31, as said below
- cont_lengths: int32 [4, 4], P('wsh'), may hold values from 1 to 384, 1024 in all within a row
- valid_mask: int32 [4, 2048], P('wsh', 'ctx'), may hold values from 0 to 1
- teacher: bfloat16 [4, 2048, 2, 768], P('wsh', 'ctx'), may hold values from -6 to 6
- out_grad: bfloat16 [4, 2048, 2, 768], P('wsh', 'ctx'), may hold values from -6 to 6
- predict: float32 [2, 2], replicated, may hold values from 0.2 to 1
- correct: float32 [2], replicated, may hold values from 0.5 to 1.5
- norm_attn: bfloat16 [768], P('wsh'), may hold values from 0.5 to 1.5
- w_query: bfloat16 [768, 768], P('wsh'), may hold values from -0.0546875 to 0.0546875
- w_key: bfloat16 [768, 768], P('wsh'), may hold values from -0.21875 to 0.21875
- w_value: bfloat16 [768, 768], P('wsh'), may hold values from -0.21875 to 0.21875
- w_out: bfloat16 [768, 768], P('wsh'), may hold values from -1.75 to 1.75
- norm_ffn: bfloat16 [768], P('wsh'), may hold values from 0.5 to 1.5
- w_gate: bfloat16 [768, 3072], P('wsh'), may hold values from -0.21875 to 0.21875
- w_up: bfloat16 [768, 3072], P('wsh'), may hold values from -0.21875 to 0.21875
- w_down: bfloat16 [3072, 768], P('wsh'), may hold values from -0.109375 to 0.109375
Outputs:
- new_states: bfloat16 [4, 2048, 2, 768], P('wsh', 'ctx')
- states_grad: bfloat16 [4, 2048, 2, 768], P('wsh', 'ctx')
- predict_grad: float32 [2, 2], replicated
- correct_grad: float32 [2], replicated
- norm_attn_grad: float32 [768], P('wsh')
- w_query_grad: float32 [768, 768], P('wsh')
- w_key_grad: float32 [768, 768], P('wsh')
- w_value_grad: float32 [768, 768], P('wsh')
- w_out_grad: float32 [768, 768], P('wsh')
- norm_ffn_grad: float32 [768], P('wsh')
- w_gate_grad: float32 [768, 3072], P('wsh')
- w_up_grad: float32 [768, 3072], P('wsh')
- w_down_grad: float32 [3072, 768], P('wsh')
The draws below stay inside these ranges and needn't reach their ends.
Inputs may be any that keep to these rules, and one draw needn't show every extreme that they name: `block_slot`: each row is a permutation of 0 to 31 in which slots 2 i and 2 i + 1 hold a block b and the block 31 - b. `cont_lengths`: each row sums to 1024, and its longest continuation has exactly 384 tokens.
All inputs are finite; a program needn't handle non-finite values.
Results may differ from the reference program's by a relative error of at most 0.022.
Values may be sent and summed in bfloat16 or wider, within the bound.
A program may use at most 192 MiB of HBM per device.

```python
import math
import jax
import jax.numpy as jnp
import numpy as np
from jax import lax

D = 768
HEADS = 12
HD = 64
FF = 3072
KB = 2
PROMPT = 1024
NCONT = 4
CONT_TOTAL = 1024
CONT_MOST = 384
BLK = 64
GROUP_LEN = 2048
NBLK = 32
BATCH = 4
TOKENS = 8192


def draw_block_slot(key, part):
    order_key, flip_key = jax.random.split(key)
    pair_count = NBLK // 2
    orders = jax.vmap(lambda single: jax.random.permutation(single, pair_count))(jax.random.split(order_key, BATCH))
    flip_bits = jax.random.randint(flip_key, (BATCH, pair_count), 0, 2)
    first_block = jnp.where(flip_bits == 1, NBLK - 1 - orders, orders)
    second = NBLK - 1 - first_block
    return jnp.stack([first_block, second], axis=-1).reshape(BATCH, NBLK).astype(jnp.int32)


def draw_valid_mask(key, part):
    slot_index = jnp.arange(GROUP_LEN, dtype=jnp.int32)
    raw_draws = jax.random.randint(key, (BATCH, GROUP_LEN), 0, 5 * GROUP_LEN)
    return (raw_draws < GROUP_LEN + 3 * slot_index[None, :]).astype(jnp.int32)


def levels(rng, dims, cuts, smallest, largest):
    factor_of, own = 1.0, jax.random.fold_in(rng, 6)
    for position, blocks in cuts:
        heights = jnp.exp(jax.random.uniform(jax.random.fold_in(own, position), (blocks,), jnp.float32, smallest / len(cuts), largest / len(cuts)))
        factor_of = factor_of * jnp.repeat(heights, dims[position] // blocks).reshape([-1 if axis == position else 1 for axis in range(len(dims))])
    return factor_of


def length_profile(amount, total, limit, slope):
    loads = [(1 << 20) // math.isqrt(standing ** slope) + 1 for standing in range(2, amount + 1)]
    spare, given = total - limit - (amount - 1), [1] * (amount - 1)
    while spare > 0:
        movable = [i for i in range(amount - 1) if given[i] < limit]
        pool, left = sum([loads[i] for i in movable]), spare
        for i in movable:
            more = min(limit - given[i], max(1, left * loads[i] // pool), spare)
            given[i] = given[i] + more
            spare = spare - more
    return np.array([limit] + given)


def uneven_parts(stream_key, number_of, total, bound, lean):
    if number_of == 2:
        one = jax.random.randint(stream_key, (), max(1, total - bound), min(bound, total - 1) + 1)
        return jnp.stack([one, total - one])
    lengths = jnp.asarray(length_profile(number_of, total, bound, lean), jnp.int32)
    pairs = (number_of - 1) // 2
    giver, receiver = lengths[1:1 + 2 * pairs:2], lengths[2:2 + 2 * pairs:2]
    slack = jnp.minimum(giver - 1, bound - receiver)
    moved = jax.random.randint(jax.random.fold_in(stream_key, 1), (pairs,), 0, 1 << 20) % (slack + 1)
    lengths = lengths.at[1:1 + 2 * pairs:2].set(giver - moved).at[2:2 + 2 * pairs:2].set(receiver + moved)
    return lengths[jax.random.permutation(jax.random.fold_in(stream_key, 2), number_of)]


def normal_values(key, dims, spread, limit, pieces=(), held_as=jnp.bfloat16):
    values = spread * jax.random.normal(key, dims, jnp.float32)
    if pieces:
        values = values * levels(key, dims, pieces, -0.22, 0.18)
    return jnp.clip(values, -limit, limit).astype(held_as)


def setup_inputs(seed: int = 0) -> dict:
    splits = jax.random.split(jax.random.key(seed), 18)
    states = normal_values(splits[0], (BATCH, GROUP_LEN, KB, D), 1.0, 6.0, ((0, 4), (1, 8)))
    block_slot = draw_block_slot(jax.random.fold_in(splits[17], 71), 0)
    cont_lengths = jax.vmap(lambda own: uneven_parts(own, NCONT, CONT_TOTAL, CONT_MOST, 1))(jax.random.split(splits[2], BATCH)).reshape((BATCH, NCONT)).astype(jnp.int32)
    valid_mask = draw_valid_mask(jax.random.fold_in(splits[17], 71), 0)
    teacher = normal_values(splits[4], (BATCH, GROUP_LEN, KB, D), 1.0, 6.0, ((0, 4), (1, 8)))
    out_grad = normal_values(splits[5], (BATCH, GROUP_LEN, KB, D), 1.0, 6.0, ((0, 4), (1, 8)))
    predict = jnp.clip(jax.random.uniform(splits[6], (KB, KB), jnp.float32, 0.2, 1.0), 0.2, 1.0)
    correct = jnp.clip(jax.random.uniform(splits[7], (KB,), jnp.float32, 0.5, 1.5), 0.5, 1.5)
    norm_attn = jnp.clip(1.0 + 0.1 * jax.random.normal(splits[8], (D,), jnp.float32), 0.5, 1.5).astype(jnp.bfloat16)
    w_query = normal_values(splits[9], (D, D), (16 * D) ** -0.5, 0.0546875, ((0, 4),))
    w_key = normal_values(splits[10], (D, D), D ** -0.5, 0.21875, ((0, 4),))
    w_value = normal_values(splits[11], (D, D), D ** -0.5, 0.21875, ((0, 4),))
    w_out = normal_values(splits[12], (D, D), (D // 64) ** -0.5, 1.75, ((0, 4),))
    norm_ffn = jnp.clip(1.0 + 0.1 * jax.random.normal(splits[13], (D,), jnp.float32), 0.5, 1.5).astype(jnp.bfloat16)
    w_gate = normal_values(splits[14], (D, FF), D ** -0.5, 0.21875, ((0, 4),))
    w_up = normal_values(splits[15], (D, FF), D ** -0.5, 0.21875, ((0, 4),))
    w_down = normal_values(splits[16], (FF, D), FF ** -0.5, 0.109375, ((0, 4),))
    return {"states": states, "block_slot": block_slot, "cont_lengths": cont_lengths, "valid_mask": valid_mask, "teacher": teacher, "out_grad": out_grad, "predict": predict, "correct": correct, "norm_attn": norm_attn, "w_query": w_query, "w_key": w_key, "w_value": w_value, "w_out": w_out, "norm_ffn": norm_ffn, "w_gate": w_gate, "w_up": w_up, "w_down": w_down}


@jax.custom_vjp
def low(v):
    return lax.optimization_barrier(v.astype(jnp.bfloat16)).astype(jnp.float32)

@jax.custom_vjp
def low_back(v):
    return v

def low_keep(v):
    return (low(v), None)

def low_pass(kept, grad):
    return (grad,)

def back_keep(v):
    return (v, None)

def back_low(kept, grad):
    return (low(grad),)
low.defvjp(low_keep, low_pass)
low_back.defvjp(back_keep, back_low)
EPSILON = 1e-06
NEGATIVE = -1e+30
HIGHEST = lax.Precision.HIGHEST

def product(left_side, right_side):
    return jnp.dot(left_side, right_side, precision=HIGHEST, preferred_element_type=jnp.float32)

def rms_norm(tensor, gain_vec):
    return tensor * lax.rsqrt(lax.optimization_barrier(jnp.mean(tensor * tensor, axis=-1, keepdims=True)) + EPSILON) * gain_vec

def places_of(slots_row, lengths_row):
    offsets = jnp.arange(BLK, dtype=jnp.int32)
    places = (slots_row[:, None] * BLK + offsets[None, :]).reshape(GROUP_LEN)
    starts = PROMPT + jnp.cumsum(lengths_row) - lengths_row
    segments = lax.optimization_barrier(jnp.sum((places[:, None] >= starts[None, :]).astype(jnp.int32), axis=1)).astype(jnp.int32)
    return (places, segments)

def group_objective(params, group_states, group_grad, group_teacher, group_valid, slots_row, lengths_row, loss_ratio):
    gain_one, query_w, key_w, value_w, out_w, gain_two, gate_w, up_w, down_w, predict, correct = params
    mixed_states = jnp.einsum('ij,tjd->tid', predict, group_states, precision=HIGHEST)
    active = mixed_states[:, 0]
    normed = low(rms_norm(active, gain_one))
    queries = low(low_back(product(normed, query_w))).reshape(GROUP_LEN, HEADS, HD)
    key_rows = low(low_back(product(normed, key_w))).reshape(GROUP_LEN, HEADS, HD)
    values = low(low_back(product(normed, value_w))).reshape(GROUP_LEN, HEADS, HD)
    places, segments = places_of(slots_row, lengths_row)
    block_rows = min(512, GROUP_LEN)

    def attend(block_inputs):
        block_queries, block_places, block_segments = block_inputs
        scores = low_back(jnp.einsum('qhd,khd->hqk', block_queries, key_rows, precision=HIGHEST))
        allowed = (places[None, :] <= block_places[:, None]) & ((segments[None, :] == 0) | (segments[None, :] == block_segments[:, None]))
        masked = jnp.where(allowed[None], scores, NEGATIVE)
        row_top = lax.optimization_barrier(jnp.max(masked, axis=-1, keepdims=True))
        exponent = jnp.where(allowed[None], jnp.exp(masked - row_top), 0.0)
        probability = low(exponent / lax.optimization_barrier(jnp.sum(exponent, axis=-1, keepdims=True)))
        return jnp.einsum('hqk,khd->qhd', probability, values, precision=HIGHEST)
    blocks = (queries.reshape(GROUP_LEN // block_rows, block_rows, HEADS, HD), places.reshape(-1, block_rows), segments.reshape(-1, block_rows))
    attended = lax.map(jax.checkpoint(attend), blocks).reshape(GROUP_LEN, D)
    attended = low(low_back(attended))
    hidden = active + low_back(product(attended, out_w))
    normed_two = low(rms_norm(hidden, gain_two))
    gate_proj = low_back(product(normed_two, gate_w))
    up_proj = low_back(product(normed_two, up_w))
    inner_act = low(jax.nn.gelu(gate_proj, approximate=True) * up_proj)
    result = hidden + low_back(product(inner_act, down_w))
    out_states = mixed_states + correct[None, :, None] * (result - active)[:, None, :]
    mismatch = out_states - group_teacher
    objective = jnp.sum(out_states * group_grad) + 0.5 * loss_ratio * jnp.sum(group_valid[:, None, None] * mismatch * mismatch)
    return (objective, out_states)

def reference(states, block_slot, cont_lengths, valid_mask, teacher, out_grad, predict, correct, norm_attn, w_query, w_key, w_value, w_out, norm_ffn, w_gate, w_up, w_down):
    params = tuple((weight.astype(jnp.float32) for weight in (norm_attn, w_query, w_key, w_value, w_out, norm_ffn, w_gate, w_up, w_down, predict, correct)))
    inputs = states.astype(jnp.float32)
    valid_float = valid_mask.astype(jnp.float32)
    loss_ratio = TOKENS / jnp.sum(valid_float)
    group_fn = jax.checkpoint(group_objective)

    def whole_objective(param_set, input_states):

        def scan_step(running, group_item):
            group_states, group_grad, group_teacher, group_valid, slots_row, lengths_row = group_item
            objective, out_states = group_fn(param_set, group_states, group_grad.astype(jnp.float32), group_teacher.astype(jnp.float32), group_valid, slots_row, lengths_row, loss_ratio)
            return (running + objective, out_states)
        return lax.scan(scan_step, jnp.zeros((), jnp.float32), (input_states, out_grad, teacher, valid_float, block_slot, cont_lengths))
    objective, pullback, out_full = jax.vjp(whole_objective, params, inputs, has_aux=True)
    new_states = out_full.astype(jnp.bfloat16)
    param_grads, states_grad = pullback(jnp.ones((), jnp.float32))
    norm_attn_grad, w_query_grad, w_key_grad, w_value_grad, w_out_grad, norm_ffn_grad, w_gate_grad, w_up_grad, w_down_grad, predict_grad, correct_grad = param_grads
    return (new_states, states_grad.astype(jnp.bfloat16), predict_grad, correct_grad, norm_attn_grad, w_query_grad, w_key_grad, w_value_grad, w_out_grad, norm_ffn_grad, w_gate_grad, w_up_grad, w_down_grad)
```

```python
import functools
import math

import jax
import jax.numpy as jnp
from jax import lax
from jax.experimental import pallas as pl
from jax.experimental.pallas import tpu as pltpu
from jax.sharding import PartitionSpec as P

HEADS = 12
HD = 64
PROMPT = 1024
BLK = 64


EPSILON = 1e-06
NEGATIVE = -1e30
HIGHEST = lax.Precision.HIGHEST


def rms_forward(tensor, gain_vec):
    factor = lax.rsqrt(jnp.mean(tensor * tensor, axis=-1, keepdims=True) + EPSILON)
    return (tensor * factor * gain_vec, factor)


def rms_backward(tensor, factor, gain_vec, upstream):
    weighted = upstream * gain_vec
    gain_grad = jnp.sum(upstream * tensor * factor, axis=0)
    middle = jnp.mean(weighted * tensor, axis=-1, keepdims=True)
    return (factor * weighted - tensor * factor * factor * factor * middle, gain_grad)


def segment_starts(cont_lengths):
    count = cont_lengths.shape[1]
    index = jnp.arange(count, dtype=jnp.int32)
    before = index[:, None] < index[None, :]
    return PROMPT + jnp.sum(jnp.where(before[None], cont_lengths[:, :, None], 0), axis=1)


def token_places(block_slot, cont_lengths):
    groups, blocks = block_slot.shape
    offsets = jnp.arange(BLK, dtype=jnp.int32)
    places = (block_slot[:, :, None] * BLK + offsets[None, None, :]).reshape(groups, blocks * BLK)
    starts = segment_starts(cont_lengths)
    segments = jnp.sum((places[:, :, None] >= starts[:, None, :]).astype(jnp.int32), axis=2)
    return (places, segments)


def visible(query_place, query_segment, key_place, key_segment):
    earlier = key_place[:, None, :] <= query_place[:, :, None]
    shared = (key_segment[:, None, :] == 0) | (key_segment[:, None, :] == query_segment[:, :, None])
    return earlier & shared


def split_heads(tensor):
    return tensor.reshape(tensor.shape[0], tensor.shape[1], HEADS, HD)


def forward_block(running, query_part, key_part, value_part, allowed):

    def forward_compute(current):
        maximum, denominator, accumulated = current
        scores = jnp.einsum(
            "gqhd,gkhd->ghqk",
            split_heads(query_part),
            split_heads(key_part),
            preferred_element_type=jnp.float32,
        )
        masked = jnp.where(allowed[:, None], scores, NEGATIVE)
        new_max = jnp.maximum(maximum, jnp.max(masked, axis=-1))
        exponent = jnp.where(allowed[:, None], jnp.exp(masked - new_max[..., None]), 0.0)
        factor = jnp.exp(maximum - new_max)
        rescale = jnp.swapaxes(factor, 1, 2)[..., None]
        update = jnp.einsum(
            "ghqk,gkhd->gqhd",
            exponent.astype(jnp.bfloat16),
            split_heads(value_part),
            preferred_element_type=jnp.float32,
        )
        merged = (split_heads(accumulated) * rescale + update).reshape(accumulated.shape)
        return (new_max, denominator * factor + jnp.sum(exponent, axis=-1), merged)

    return lax.cond(jnp.any(allowed), forward_compute, lambda current: current, running)


def backward_block(
    query_part, grad_part, key_part, value_part, allowed, maximum, denominator, delta_sum
):
    scores = jnp.einsum(
        "gqhd,gkhd->ghqk",
        split_heads(query_part),
        split_heads(key_part),
        preferred_element_type=jnp.float32,
    )
    exponent = jnp.where(allowed[:, None], jnp.exp(scores - maximum[..., None]), 0.0)
    probability = exponent / denominator[..., None]
    prob_grad = jnp.einsum(
        "gqhd,gkhd->ghqk",
        split_heads(grad_part),
        split_heads(value_part),
        preferred_element_type=jnp.float32,
    )
    score_grad = (probability * (prob_grad - delta_sum[..., None])).astype(jnp.bfloat16)
    return (probability.astype(jnp.bfloat16), score_grad)


def general_shards(
    states,
    block_slot,
    cont_lengths,
    valid_mask,
    teacher,
    out_grad,
    predict,
    correct,
    norm_attn,
    w_query,
    w_key,
    w_value,
    w_out,
    norm_ffn,
    w_gate,
    w_up,
    w_down,
):
    groups, local_len = valid_mask.shape
    model_width = states.shape[3]
    row_count = groups * local_len
    group_len = block_slot.shape[1] * BLK
    gain_one, query_w, key_w, value_w, out_w, gain_two, gate_w, up_w, down_w = (
        lax.all_gather(norm_attn, "wsh", axis=0, tiled=True),
        lax.all_gather(w_query, "wsh", axis=0, tiled=True),
        lax.all_gather(w_key, "wsh", axis=0, tiled=True),
        lax.all_gather(w_value, "wsh", axis=0, tiled=True),
        lax.all_gather(w_out, "wsh", axis=0, tiled=True),
        lax.all_gather(norm_ffn, "wsh", axis=0, tiled=True),
        lax.all_gather(w_gate, "wsh", axis=0, tiled=True),
        lax.all_gather(w_up, "wsh", axis=0, tiled=True),
        lax.all_gather(w_down, "wsh", axis=0, tiled=True),
    )
    valid_float = valid_mask.astype(jnp.float32)
    valid_total = lax.psum(jnp.sum(valid_float), ("ctx", "wsh"))
    places, segments = token_places(block_slot, cont_lengths)
    offset = lax.axis_index("ctx") * local_len
    own_place = lax.dynamic_slice_in_dim(places, offset, local_len, 1)
    own_segment = lax.dynamic_slice_in_dim(segments, offset, local_len, 1)
    inputs = states.astype(jnp.float32)
    mixed_states = jnp.einsum("ij,gtjd->gtid", predict, inputs, precision=HIGHEST)
    active = mixed_states[:, :, 0].reshape(row_count, model_width)
    gain_first = gain_one.astype(jnp.float32)
    normed, factor_one = rms_forward(active, gain_first)
    normed_low = normed.astype(jnp.bfloat16)
    queries = (
        jnp.dot(normed_low, query_w, preferred_element_type=jnp.float32)
        .astype(jnp.bfloat16)
        .reshape(groups, local_len, model_width)
    )
    key_rows = (
        jnp.dot(normed_low, key_w, preferred_element_type=jnp.float32)
        .astype(jnp.bfloat16)
        .reshape(groups, local_len, model_width)
    )
    values = (
        jnp.dot(normed_low, value_w, preferred_element_type=jnp.float32)
        .astype(jnp.bfloat16)
        .reshape(groups, local_len, model_width)
    )
    initial = (
        jnp.full((groups, HEADS, local_len), NEGATIVE, jnp.float32),
        jnp.zeros((groups, HEADS, local_len), jnp.float32),
        jnp.zeros((groups, local_len, model_width), jnp.float32),
    )
    piece_keys = lax.all_gather(key_rows, "ctx", axis=1, tiled=True)
    piece_values = lax.all_gather(values, "ctx", axis=1, tiled=True)
    piece_len = piece_keys.shape[1]
    block_size = math.gcd(piece_len, local_len)

    def fold_one_block(current, block_index):
        begin = block_index * block_size
        key_part = lax.dynamic_slice_in_dim(piece_keys, begin, block_size, 1)
        value_part = lax.dynamic_slice_in_dim(piece_values, begin, block_size, 1)
        key_place = lax.dynamic_slice_in_dim(places, begin, block_size, 1)
        key_segment = lax.dynamic_slice_in_dim(segments, begin, block_size, 1)
        allowed = visible(own_place, own_segment, key_place, key_segment)
        return (forward_block(current, queries, key_part, value_part, allowed), None)

    finished, unused = lax.scan(
        fold_one_block, initial, jnp.arange(piece_len // block_size, dtype=jnp.int32)
    )
    maximum, denominator, accumulated = finished
    attended = (split_heads(accumulated) / jnp.swapaxes(denominator, 1, 2)[..., None]).reshape(
        row_count, model_width
    )
    attended_low = attended.astype(jnp.bfloat16)
    hidden = active + jnp.dot(attended_low, out_w, preferred_element_type=jnp.float32)
    gain_second = gain_two.astype(jnp.float32)
    normed_two, factor_two = rms_forward(hidden, gain_second)
    normed_two_low = normed_two.astype(jnp.bfloat16)
    gate_proj = jnp.dot(normed_two_low, gate_w, preferred_element_type=jnp.float32)
    up_proj = jnp.dot(normed_two_low, up_w, preferred_element_type=jnp.float32)
    inner_act, inner_pull = jax.vjp(
        lambda gate_in, up_in: jax.nn.gelu(gate_in, approximate=True) * up_in, gate_proj, up_proj
    )
    inner_low = inner_act.astype(jnp.bfloat16)
    result = hidden + jnp.dot(inner_low, down_w, preferred_element_type=jnp.float32)
    difference = (result - active).reshape(groups, local_len, 1, model_width)
    out_states = mixed_states + correct[None, None, :, None] * difference
    new_states = out_states.astype(jnp.bfloat16)
    loss_ratio = lax.axis_size("wsh") * groups * group_len / valid_total
    upstream = out_grad.astype(jnp.float32) + loss_ratio * valid_float[:, :, None, None] * (
        out_states - teacher.astype(jnp.float32)
    )
    correct_local = jnp.sum(upstream * difference, axis=(0, 1, 3))
    result_grad = jnp.einsum("i,gtid->gtd", correct, upstream, precision=HIGHEST).reshape(
        row_count, model_width
    )
    result_low = result_grad.astype(jnp.bfloat16)
    down_grad = jnp.einsum("rf,rd->fd", inner_low, result_low, preferred_element_type=jnp.float32)
    inner_grad = jnp.einsum("rd,fd->rf", result_low, down_w, preferred_element_type=jnp.float32)
    gate_grad, up_grad = inner_pull(inner_grad)
    gate_low = gate_grad.astype(jnp.bfloat16)
    up_low = up_grad.astype(jnp.bfloat16)
    gate_w_grad = jnp.einsum(
        "rd,rf->df", normed_two_low, gate_low, preferred_element_type=jnp.float32
    )
    up_w_grad = jnp.einsum("rd,rf->df", normed_two_low, up_low, preferred_element_type=jnp.float32)
    normed_two_grad = jnp.einsum(
        "rf,df->rd", gate_low, gate_w, preferred_element_type=jnp.float32
    ) + jnp.einsum("rf,df->rd", up_low, up_w, preferred_element_type=jnp.float32)
    hidden_norm_grad, gain_two_grad = rms_backward(hidden, factor_two, gain_second, normed_two_grad)
    hidden_grad = result_grad + hidden_norm_grad
    hidden_low = hidden_grad.astype(jnp.bfloat16)
    out_w_grad = jnp.einsum(
        "rc,rd->cd", attended_low, hidden_low, preferred_element_type=jnp.float32
    )
    attended_grad = jnp.einsum(
        "rd,cd->rc", hidden_low, out_w, preferred_element_type=jnp.float32
    ).astype(jnp.bfloat16)
    delta_sum = jnp.swapaxes(
        jnp.sum(
            split_heads(
                (attended_grad.astype(jnp.float32) * attended).reshape(
                    groups, local_len, model_width
                )
            ),
            axis=-1,
        ),
        1,
        2,
    )
    grad_local = attended_grad.reshape(groups, local_len, model_width)
    zero_grad = jnp.zeros((groups, local_len, model_width), jnp.float32)
    all_keys, all_values = (
        lax.all_gather(key_rows, "ctx", axis=1, tiled=True),
        lax.all_gather(values, "ctx", axis=1, tiled=True),
    )

    def query_step(current, block_index):
        begin = block_index * local_len
        key_part = lax.dynamic_slice_in_dim(all_keys, begin, local_len, 1)
        value_part = lax.dynamic_slice_in_dim(all_values, begin, local_len, 1)
        key_place = lax.dynamic_slice_in_dim(places, begin, local_len, 1)
        key_segment = lax.dynamic_slice_in_dim(segments, begin, local_len, 1)
        allowed = visible(own_place, own_segment, key_place, key_segment)

        def query_compute(query_sum):
            prob_low, score_grad = backward_block(
                queries, grad_local, key_part, value_part, allowed, maximum, denominator, delta_sum
            )
            return query_sum + jnp.einsum(
                "ghqk,gkhd->gqhd",
                score_grad,
                split_heads(key_part),
                preferred_element_type=jnp.float32,
            ).reshape(groups, local_len, model_width)

        return (
            lax.cond(jnp.any(allowed), query_compute, lambda query_sum: query_sum, current),
            None,
        )

    finished, unused = lax.scan(
        query_step, zero_grad, jnp.arange(group_len // local_len, dtype=jnp.int32)
    )
    term_rows = local_len * lax.axis_size("ctx")
    key_block_size = math.gcd(term_rows, local_len)

    def key_one_block(block_index):
        begin = block_index * key_block_size
        key_part = lax.dynamic_slice_in_dim(all_keys, begin, key_block_size, 1)
        value_part = lax.dynamic_slice_in_dim(all_values, begin, key_block_size, 1)
        key_place = lax.dynamic_slice_in_dim(places, begin, key_block_size, 1)
        key_segment = lax.dynamic_slice_in_dim(segments, begin, key_block_size, 1)
        allowed = visible(own_place, own_segment, key_place, key_segment)

        def one_compute(unused_arg):
            prob_low, score_grad = backward_block(
                queries, grad_local, key_part, value_part, allowed, maximum, denominator, delta_sum
            )
            key_add = jnp.einsum(
                "ghqk,gqhd->kghd",
                score_grad,
                split_heads(queries),
                preferred_element_type=jnp.float32,
            ).reshape(key_block_size, groups, model_width)
            value_add = jnp.einsum(
                "ghqk,gqhd->kghd",
                prob_low,
                split_heads(grad_local),
                preferred_element_type=jnp.float32,
            ).reshape(key_block_size, groups, model_width)
            return jnp.stack([key_add, value_add], axis=1)

        return lax.cond(
            jnp.any(allowed),
            one_compute,
            lambda unused_arg: jnp.zeros((key_block_size, 2, groups, model_width), jnp.float32),
            0,
        )

    summed = lax.psum_scatter(
        lax.map(key_one_block, jnp.arange(term_rows // key_block_size, dtype=jnp.int32))
        .reshape(term_rows, 2, groups, model_width)
        .astype(jnp.bfloat16),
        "ctx",
        scatter_dimension=0,
        tiled=True,
    ).astype(jnp.float32)
    key_grad = jnp.swapaxes(summed[:, 0], 0, 1)
    value_grad = jnp.swapaxes(summed[:, 1], 0, 1)
    query_low = finished.reshape(row_count, model_width).astype(jnp.bfloat16)
    key_low = key_grad.reshape(row_count, model_width).astype(jnp.bfloat16)
    value_low = value_grad.reshape(row_count, model_width).astype(jnp.bfloat16)
    query_w_grad = jnp.einsum(
        "rc,rd->cd", normed_low, query_low, preferred_element_type=jnp.float32
    )
    key_w_grad = jnp.einsum("rc,rd->cd", normed_low, key_low, preferred_element_type=jnp.float32)
    value_w_grad = jnp.einsum(
        "rc,rd->cd", normed_low, value_low, preferred_element_type=jnp.float32
    )
    normed_grad = (
        jnp.einsum("rd,cd->rc", query_low, query_w, preferred_element_type=jnp.float32)
        + jnp.einsum("rd,cd->rc", key_low, key_w, preferred_element_type=jnp.float32)
        + jnp.einsum("rd,cd->rc", value_low, value_w, preferred_element_type=jnp.float32)
    )
    active_norm_grad, gain_one_grad = rms_backward(active, factor_one, gain_first, normed_grad)
    active_grad = (hidden_grad + active_norm_grad - result_grad).reshape(
        groups, local_len, 1, model_width
    )
    mixed_grad = jnp.concatenate([upstream[:, :, :1] + active_grad, upstream[:, :, 1:]], axis=2)
    predict_local = jnp.einsum("gtid,gtjd->ij", mixed_grad, inputs, precision=HIGHEST)
    states_grad = jnp.einsum("ij,gtid->gtjd", predict, mixed_grad, precision=HIGHEST).astype(
        jnp.bfloat16
    )
    predict_grad, correct_grad = lax.psum((predict_local, correct_local), ("ctx", "wsh"))
    (
        gain_one_rows,
        query_rows,
        key_grad_rows,
        value_rows,
        out_rows,
        gain_two_rows,
        gate_rows,
        up_rows,
        down_rows,
    ) = (
        lax.psum_scatter(
            gain_one_grad.astype(jnp.bfloat16), "wsh", scatter_dimension=0, tiled=True
        ).astype(jnp.float32),
        lax.psum_scatter(
            query_w_grad.astype(jnp.bfloat16), "wsh", scatter_dimension=0, tiled=True
        ).astype(jnp.float32),
        lax.psum_scatter(
            key_w_grad.astype(jnp.bfloat16), "wsh", scatter_dimension=0, tiled=True
        ).astype(jnp.float32),
        lax.psum_scatter(
            value_w_grad.astype(jnp.bfloat16), "wsh", scatter_dimension=0, tiled=True
        ).astype(jnp.float32),
        lax.psum_scatter(
            out_w_grad.astype(jnp.bfloat16), "wsh", scatter_dimension=0, tiled=True
        ).astype(jnp.float32),
        lax.psum_scatter(
            gain_two_grad.astype(jnp.bfloat16), "wsh", scatter_dimension=0, tiled=True
        ).astype(jnp.float32),
        lax.psum_scatter(
            gate_w_grad.astype(jnp.bfloat16), "wsh", scatter_dimension=0, tiled=True
        ).astype(jnp.float32),
        lax.psum_scatter(
            up_w_grad.astype(jnp.bfloat16), "wsh", scatter_dimension=0, tiled=True
        ).astype(jnp.float32),
        lax.psum_scatter(
            down_grad.astype(jnp.bfloat16), "wsh", scatter_dimension=0, tiled=True
        ).astype(jnp.float32),
    )
    totals = (
        lax.psum(gain_one_rows.astype(jnp.bfloat16), "ctx").astype(jnp.float32),
        lax.psum(query_rows.astype(jnp.bfloat16), "ctx").astype(jnp.float32),
        lax.psum(key_grad_rows.astype(jnp.bfloat16), "ctx").astype(jnp.float32),
        lax.psum(value_rows.astype(jnp.bfloat16), "ctx").astype(jnp.float32),
        lax.psum(out_rows.astype(jnp.bfloat16), "ctx").astype(jnp.float32),
        lax.psum(gain_two_rows.astype(jnp.bfloat16), "ctx").astype(jnp.float32),
        lax.psum(gate_rows.astype(jnp.bfloat16), "ctx").astype(jnp.float32),
        lax.psum(up_rows.astype(jnp.bfloat16), "ctx").astype(jnp.float32),
        lax.psum(down_rows.astype(jnp.bfloat16), "ctx").astype(jnp.float32),
    )
    return (new_states, states_grad, predict_grad, correct_grad) + tuple(totals)


MESH = pl.DeviceIdType.MESH
F32 = jnp.float32
BF16 = jnp.bfloat16
CHIPS = 4
VMEM_LIMIT = 60 * 2**20


def place_on_mesh():
    ctx = lax.axis_index("ctx")
    depth = lax.axis_index("wsh")
    chip = ctx // 2
    core = ctx % 2
    chip_x = chip + 1 - 2 * (chip % 2)
    chip_y = chip + 2 - 4 * (chip // 2)
    return depth, chip, core, chip_x, chip_y, 3 - chip


def signal_and_wait(devices):
    barrier = pltpu.get_barrier_semaphore()
    for device in devices:
        pl.semaphore_signal(barrier, inc=1, device_id=device, device_id_type=MESH)
    pl.semaphore_wait(barrier, len(devices))


def remote(src, dst, send, recv, index, device):
    return pltpu.make_async_remote_copy(
        src_ref=src,
        dst_ref=dst,
        send_sem=send.at[index],
        recv_sem=recv.at[index],
        device_id=device,
        device_id_type=MESH,
    )


def comm_params(collective_id):
    return pltpu.CompilerParams(
        collective_id=collective_id, has_side_effects=True, vmem_limit_bytes=VMEM_LIMIT
    )


ANY = pl.BlockSpec(memory_space=pl.ANY)
VM = pl.BlockSpec(memory_space=pltpu.VMEM)
SM = pl.BlockSpec(memory_space=pltpu.SMEM)


def ring_sends(own, out, slot_of, chip, core, depth, chip_x, chip_y, send, recv):
    half = own.shape[0] // 2
    top, low = pl.ds(0, half), pl.ds(half, half)
    dev_x, dev_y = (2 * chip_x + core, depth), (2 * chip_y + core, depth)
    here = slot_of(chip)
    return [
        remote(own.at[top], out.at[here, top], send, recv, 0, dev_x),
        remote(own.at[low], out.at[here, low], send, recv, 1, dev_y),
        remote(own.at[low], out.at[here, low], send, recv, 2, dev_x),
        remote(own.at[top], out.at[here, top], send, recv, 3, dev_y),
        remote(out.at[slot_of(chip_x), top], out.at[slot_of(chip_x), top], send, recv, 4, dev_y),
        remote(out.at[slot_of(chip_y), low], out.at[slot_of(chip_y), low], send, recv, 5, dev_x),
    ]


def gather_plane(block, collective_id):
    def kernel(x_ref, out_ref, send, recv, local):
        depth, chip, core, chip_x, chip_y, _ = place_on_mesh()
        signal_and_wait([(2 * chip_x + core, depth), (2 * chip_y + core, depth)])
        copies = ring_sends(
            x_ref, out_ref, lambda c: c, chip, core, depth, chip_x, chip_y, send, recv
        )
        for copy in copies[:4]:
            copy.start()
        mine = pltpu.make_async_copy(x_ref, out_ref.at[chip], local)
        mine.start()
        copies[0].wait_recv()
        copies[4].start()
        copies[1].wait_recv()
        copies[5].start()
        for copy in copies[2:]:
            copy.wait_recv()
        for copy in copies:
            copy.wait_send()
        mine.wait()

    return pl.pallas_call(
        kernel,
        out_shape=jax.ShapeDtypeStruct((CHIPS,) + block.shape, block.dtype),
        in_specs=[ANY],
        out_specs=ANY,
        scratch_shapes=[
            pltpu.SemaphoreType.DMA((6,)),
            pltpu.SemaphoreType.DMA((6,)),
            pltpu.SemaphoreType.DMA,
        ],
        compiler_params=comm_params(collective_id),
        name="gather_plane",
    )(block)


def scatter_plane(parts, collective_id):
    _, rows, width = parts.shape
    half = rows // 2

    def kernel(x_ref, out_ref, near, diagonal, staged, send, recv):
        depth, chip, core, chip_x, chip_y, chip_d = place_on_mesh()
        dev_x, dev_y = (2 * chip_x + core, depth), (2 * chip_y + core, depth)
        signal_and_wait([dev_x, dev_y])
        top, low = pl.ds(0, half), pl.ds(half, half)
        first = [
            remote(x_ref.at[chip_d, top], diagonal.at[0], send, recv, 0, dev_x),
            remote(x_ref.at[chip_d, low], diagonal.at[1], send, recv, 1, dev_y),
            remote(x_ref.at[chip_x, top], near.at[0, top], send, recv, 2, dev_x),
            remote(x_ref.at[chip_y, low], near.at[1, low], send, recv, 3, dev_y),
        ]
        for copy in first:
            copy.start()
        second = [
            remote(staged.at[0], near.at[1, top], send, recv, 4, dev_y),
            remote(staged.at[1], near.at[0, low], send, recv, 5, dev_x),
        ]
        first[0].wait_recv()
        staged[0] = (x_ref[chip_y, top].astype(F32) + diagonal[0].astype(F32)).astype(BF16)
        second[0].start()
        first[1].wait_recv()
        staged[1] = (x_ref[chip_x, low].astype(F32) + diagonal[1].astype(F32)).astype(BF16)
        second[1].start()
        for copy in first[2:] + second:
            copy.wait_recv()
        out_ref[...] = (
            x_ref[chip].astype(F32) + near[0].astype(F32) + near[1].astype(F32)
        )
        for copy in first + second:
            copy.wait_send()

    return pl.pallas_call(
        kernel,
        out_shape=jax.ShapeDtypeStruct((rows, width), F32),
        in_specs=[VM],
        out_specs=VM,
        scratch_shapes=[
            pltpu.VMEM((2, rows, width), BF16),
            pltpu.VMEM((2, half, width), BF16),
            pltpu.VMEM((2, half, width), BF16),
            pltpu.SemaphoreType.DMA((6,)),
            pltpu.SemaphoreType.DMA((6,)),
        ],
        compiler_params=comm_params(collective_id),
        name="scatter_plane",
    )(parts)


def share_cores(arrays, collective_id):
    count = len(arrays)

    def kernel(*refs):
        ins, outs, (send, recv, local) = refs[:count], refs[count : 2 * count], refs[2 * count :]
        depth, chip, core, _, _, _ = place_on_mesh()
        other = (2 * chip + 1 - core, depth)
        signal_and_wait([other])
        copies = [
            remote(ins[i], outs[i].at[core], send, recv, i, other) for i in range(count)
        ]
        mine = [
            pltpu.make_async_copy(ins[i], outs[i].at[core], local.at[i]) for i in range(count)
        ]
        for copy in copies + mine:
            copy.start()
        for copy in copies + mine:
            copy.wait()

    return pl.pallas_call(
        kernel,
        out_shape=[jax.ShapeDtypeStruct((2,) + a.shape, a.dtype) for a in arrays],
        in_specs=[ANY] * count,
        out_specs=[ANY] * count,
        scratch_shapes=[pltpu.SemaphoreType.DMA((count,))] * 3,
        compiler_params=comm_params(collective_id),
        name="share_cores",
    )(*arrays)


def swap_cores(arrays, collective_id):
    count = len(arrays)

    def kernel(*refs):
        ins, outs, (send, recv) = refs[:count], refs[count : 2 * count], refs[2 * count :]
        depth, chip, core, _, _, _ = place_on_mesh()
        other = (2 * chip + 1 - core, depth)
        signal_and_wait([other])
        copies = [
            remote(ins[i].at[:, 1 - core], outs[i], send, recv, i, other) for i in range(count)
        ]
        for copy in copies:
            copy.start()
        for copy in copies:
            copy.wait()

    return pl.pallas_call(
        kernel,
        out_shape=[jax.ShapeDtypeStruct(a.shape[:1] + a.shape[2:], a.dtype) for a in arrays],
        in_specs=[ANY] * count,
        out_specs=[ANY] * count,
        scratch_shapes=[pltpu.SemaphoreType.DMA((count,))] * 2,
        compiler_params=comm_params(collective_id),
        name="swap_cores",
    )(*arrays)


def gather_inputs(block, weights, collective_id):
    depths = lax.axis_size("wsh")

    def kernel(x_ref, w_ref, out_ref, wall_ref, send, recv, wsend, wrecv, ssend, srecv, local):
        depth, chip, core, chip_x, chip_y, chip_d = place_on_mesh()
        other = (2 * chip + 1 - core, depth)
        across = [
            (2 * chip + core, lax.rem(depth + step, depths)) for step in range(1, depths)
        ]
        signal_and_wait(
            [(2 * chip_x + core, depth), (2 * chip_y + core, depth), other] + across
        )

        def slot(chip_index):
            return 2 * chip_index + core

        copies = ring_sends(
            x_ref, out_ref, slot, chip, core, depth, chip_x, chip_y, send, recv
        )
        for copy in copies[:4]:
            copy.start()
        w_copies = [
            remote(w_ref, wall_ref.at[:, depth, core], wsend, wrecv, i, device)
            for i, device in enumerate(across)
        ]
        for copy in w_copies:
            copy.start()
        mine = [
            pltpu.make_async_copy(x_ref, out_ref.at[slot(chip)], local.at[0]),
            pltpu.make_async_copy(w_ref, wall_ref.at[:, depth, core], local.at[1]),
        ]
        for copy in mine:
            copy.start()

        def pass_on(index, slot_index):
            ref = out_ref.at[slot_index]
            return remote(ref, ref, ssend, srecv, index, other)

        def pass_weights(index, depth_index):
            ref = wall_ref.at[:, depth_index, core]
            return remote(ref, ref, ssend, srecv, index, other)

        shared = [
            remote(x_ref, out_ref.at[slot(chip)], ssend, srecv, 0, other),
            pass_on(1, slot(chip_x)),
            pass_on(2, slot(chip_y)),
            pass_on(3, slot(chip_d)),
            remote(w_ref, wall_ref.at[:, depth, core], ssend, srecv, 4, other),
        ] + [
            pass_weights(5 + i, lax.rem(depth + depths - 1 - i, depths))
            for i in range(depths - 1)
        ]
        shared[0].start()
        shared[4].start()
        copies[0].wait_recv()
        copies[4].start()
        copies[1].wait_recv()
        copies[5].start()
        for i in range(depths - 1):
            w_copies[i].wait_recv()
            shared[5 + i].start()
        copies[2].wait_recv()
        shared[1].start()
        copies[3].wait_recv()
        shared[2].start()
        copies[4].wait_recv()
        copies[5].wait_recv()
        shared[3].start()
        for copy in shared:
            copy.wait()
        for copy in copies + w_copies:
            copy.wait_send()
        for copy in mine:
            copy.wait()

    shape = (lax.axis_size("ctx"),) + block.shape
    parts, rows, columns = weights.shape
    return pl.pallas_call(
        kernel,
        out_shape=[
            jax.ShapeDtypeStruct(shape, block.dtype),
            jax.ShapeDtypeStruct((parts, depths, 2, rows, columns), weights.dtype),
        ],
        in_specs=[ANY, ANY],
        out_specs=[ANY, ANY],
        scratch_shapes=[
            pltpu.SemaphoreType.DMA((6,)),
            pltpu.SemaphoreType.DMA((6,)),
            pltpu.SemaphoreType.DMA((depths - 1,)),
            pltpu.SemaphoreType.DMA((depths - 1,)),
            pltpu.SemaphoreType.DMA((depths + 4,)),
            pltpu.SemaphoreType.DMA((depths + 4,)),
            pltpu.SemaphoreType.DMA((2,)),
        ],
        compiler_params=comm_params(collective_id),
        name="gather_inputs",
    )(block, weights)


NT = (((1,), (1,)), ((), ()))
TILE = 256
LOCAL_HEADS = HEADS // CHIPS
CHIP_COLS = LOCAL_HEADS * HD


def head_mask(rows, head):
    lane = lax.broadcasted_iota(jnp.int32, (rows, CHIP_COLS), 1)
    return (lane >= head * HD) & (lane < (head + 1) * HD)


def aligned(index, size):
    return pl.ds(pl.multiple_of(index * size, size), size)


def attention_forward(all_rows, weights, slots, q_slots, q_local, low, high):
    tokens, width = all_rows.shape
    tiles = low.shape[0]
    queries = tiles * TILE
    blocks = tokens // BLK

    def kernel(
        slots_ref, q_slots_ref, q_local_ref, x_ref, w_ref, low_ref, high_ref,
        att_ref, oT_ref, q_ref, k_ref, v_ref, lse_ref, xs, xq, vT, s_ref, p_ref,
    ):
        def gather_block(b, _):
            xs[aligned(b, BLK), :] = x_ref[aligned(slots_ref[b], BLK), :]
            return 0

        lax.fori_loop(0, blocks, gather_block, 0)

        def gather_query(b, _):
            xq[aligned(b, BLK), :] = x_ref[aligned(q_slots_ref[b], BLK), :]
            return 0

        lax.fori_loop(0, queries // BLK, gather_query, 0)

        def project_keys(i, _):
            rows = aligned(i, TILE)
            x = xs[rows, :]
            k_ref[rows, :] = jnp.dot(x, w_ref[1], preferred_element_type=F32).astype(BF16)
            v = jnp.dot(x, w_ref[2], preferred_element_type=F32).astype(BF16)
            v_ref[rows, :] = v
            vT[:, rows] = v.T
            return 0

        lax.fori_loop(0, tokens // TILE, project_keys, 0)

        def project_queries(i, _):
            rows = aligned(i, TILE)
            q_ref[rows, :] = jnp.dot(xq[rows, :], w_ref[0], preferred_element_type=F32).astype(BF16)
            return 0

        lax.fori_loop(0, tiles, project_queries, 0)

        for kind in range(2):
            key_tiles = (PROMPT if kind == 0 else tokens) // TILE
            first_masked = 0 if kind == 0 else PROMPT // TILE

            def one_tile(step, _):
                tile = kind * (tiles // 2) + step
                q = q_ref[aligned(tile, TILE), :]
                q_low = low_ref[pl.ds(tile, 1)][0]
                q_high = high_ref[pl.ds(tile, 1)][0]
                for head in range(LOCAL_HEADS):
                    q_head = jnp.where(head_mask(TILE, head), q, jnp.zeros_like(q))
                    top = jnp.full((1, TILE), NEGATIVE, F32)
                    for k_tile in range(key_tiles):
                        rows = pl.ds(k_tile * TILE, TILE)
                        s = lax.dot_general(k_ref[rows, :], q_head, NT, preferred_element_type=F32)
                        if k_tile >= first_masked:
                            place = lax.broadcasted_iota(jnp.int32, (TILE, TILE), 0) + k_tile * TILE
                            seen = (place >= q_low) & (place <= q_high)
                            s = jnp.where(seen, s, NEGATIVE)
                        s_ref[rows, :] = s
                        top = jnp.maximum(top, jnp.max(s, axis=0, keepdims=True))
                    total = jnp.zeros((1, TILE), F32)
                    for k_tile in range(key_tiles):
                        rows = pl.ds(k_tile * TILE, TILE)
                        p = jnp.exp(s_ref[rows, :] - top)
                        total = total + jnp.sum(p, axis=0, keepdims=True)
                        p_ref[rows, :] = p.astype(BF16)
                    keys = key_tiles * TILE
                    out = jnp.dot(
                        vT[head * HD : (head + 1) * HD, :keys],
                        p_ref[:keys, :],
                        preferred_element_type=F32,
                    )
                    oT_ref[tile, head * HD : (head + 1) * HD, :] = out / total
                    lse_ref[tile, head] = top + jnp.log(total)
                att = oT_ref[tile].T.astype(BF16)
                for b in range(TILE // BLK):
                    where = q_local_ref[tile * (TILE // BLK) + b]
                    att_ref[aligned(where, BLK), :] = att[b * BLK : (b + 1) * BLK]
                return 0

            lax.fori_loop(0, tiles // 2, one_tile, 0)

    return pl.pallas_call(
        kernel,
        out_shape=[
            jax.ShapeDtypeStruct((queries, CHIP_COLS), BF16),
            jax.ShapeDtypeStruct((tiles, CHIP_COLS, TILE), F32),
            jax.ShapeDtypeStruct((queries, CHIP_COLS), BF16),
            jax.ShapeDtypeStruct((tokens, CHIP_COLS), BF16),
            jax.ShapeDtypeStruct((tokens, CHIP_COLS), BF16),
            jax.ShapeDtypeStruct((tiles, LOCAL_HEADS, 1, TILE), F32),
        ],
        in_specs=[SM, SM, SM, VM, VM, VM, VM],
        out_specs=[VM] * 6,
        scratch_shapes=[
            pltpu.VMEM((tokens, width), BF16),
            pltpu.VMEM((queries, width), BF16),
            pltpu.VMEM((CHIP_COLS, tokens), BF16),
            pltpu.VMEM((tokens, TILE), F32),
            pltpu.VMEM((tokens, TILE), BF16),
        ],
        compiler_params=pltpu.CompilerParams(vmem_limit_bytes=VMEM_LIMIT),
        name="attention_forward",
    )(slots, q_slots, q_local, all_rows, weights, low, high)


def attention_backward(hidden_rows, w_out, saved, slots, q_local, low, high):
    oT, q, k, v, lse = saved
    queries, width = hidden_rows.shape
    tokens = k.shape[0]
    tiles = low.shape[0]
    blocks = tokens // BLK
    wide = LOCAL_HEADS * TILE

    def kernel(
        slots_ref, q_local_ref, h_ref, w_ref, oT_ref, q_ref, k_ref, v_ref, lse_ref, low_ref, high_ref,
        dq_ref, dk_ref, dv_ref, hq, kT, doT, dqT, q_stack, do_stack, p_buf, ds_buf, dk_acc, dv_acc,
    ):
        def gather_query(b, _):
            hq[aligned(b, BLK), :] = h_ref[aligned(q_local_ref[b], BLK), :]
            return 0

        lax.fori_loop(0, queries // BLK, gather_query, 0)

        def transpose_keys(i, _):
            rows = aligned(i, TILE)
            kT[:, rows] = k_ref[rows, :].T
            return 0

        lax.fori_loop(0, tokens // TILE, transpose_keys, 0)

        for kind in (1, 0):
            key_tiles = (PROMPT if kind == 0 else tokens) // TILE
            first_masked = 0 if kind == 0 else PROMPT // TILE

            def one_tile(step, _):
                tile = kind * (tiles // 2) + step
                q_tile = q_ref[aligned(tile, TILE), :]
                q_low = low_ref[pl.ds(tile, 1)][0]
                q_high = high_ref[pl.ds(tile, 1)][0]
                wide_do = lax.dot_general(
                    w_ref[...], hq[aligned(tile, TILE), :], NT, preferred_element_type=F32
                )
                do_tile = wide_do.T.astype(BF16)
                doT[...] = wide_do.astype(BF16).astype(F32) * oT_ref[tile]
                for head in range(LOCAL_HEADS):
                    lanes = pl.ds(head * TILE, TILE)
                    heads = pl.ds(head * HD, HD)
                    mask = head_mask(TILE, head)
                    q_head = jnp.where(mask, q_tile, jnp.zeros_like(q_tile))
                    do_head = jnp.where(mask, do_tile, jnp.zeros_like(do_tile))
                    q_stack[lanes, :] = q_head
                    do_stack[lanes, :] = do_head
                    delta = jnp.sum(doT[heads, :], axis=0, keepdims=True)
                    norm = lse_ref[tile, head]
                    for k_tile in range(key_tiles):
                        rows = pl.ds(k_tile * TILE, TILE)
                        s = lax.dot_general(k_ref[rows, :], q_head, NT, preferred_element_type=F32)
                        dp = lax.dot_general(v_ref[rows, :], do_head, NT, preferred_element_type=F32)
                        p = jnp.exp(s - norm)
                        if k_tile >= first_masked:
                            place = lax.broadcasted_iota(jnp.int32, (TILE, TILE), 0) + k_tile * TILE
                            seen = (place >= q_low) & (place <= q_high)
                            p = jnp.where(seen, p, 0.0)
                        p_buf[rows, lanes] = p.astype(BF16)
                        ds_buf[rows, lanes] = (p * (dp - delta)).astype(BF16)
                    keys = key_tiles * TILE
                    dqT[heads, :] = jnp.dot(
                        kT[heads, :keys], ds_buf[:keys, lanes], preferred_element_type=F32
                    )
                for k_tile in range(key_tiles):
                    rows = pl.ds(k_tile * TILE, TILE)
                    dv = jnp.dot(p_buf[rows, :], do_stack[...], preferred_element_type=F32)
                    dk = jnp.dot(ds_buf[rows, :], q_stack[...], preferred_element_type=F32)
                    if kind == 1:
                        fresh = step == 0
                        dv = dv + jnp.where(fresh, 0.0, dv_acc[rows, :])
                        dk = dk + jnp.where(fresh, 0.0, dk_acc[rows, :])
                    else:
                        dv = dv + dv_acc[rows, :]
                        dk = dk + dk_acc[rows, :]
                    dv_acc[rows, :] = dv
                    dk_acc[rows, :] = dk
                dq = dqT[...].T.astype(BF16)
                for b in range(TILE // BLK):
                    where = q_local_ref[tile * (TILE // BLK) + b]
                    dq_ref[aligned(where, BLK), :] = dq[b * BLK : (b + 1) * BLK]
                return 0

            lax.fori_loop(0, tiles // 2, one_tile, 0)

        def give_block(b, _):
            where = aligned(slots_ref[b], BLK)
            dk_ref[where, :] = dk_acc[aligned(b, BLK), :].astype(BF16)
            dv_ref[where, :] = dv_acc[aligned(b, BLK), :].astype(BF16)
            return 0

        lax.fori_loop(0, blocks, give_block, 0)

    return pl.pallas_call(
        kernel,
        out_shape=[
            jax.ShapeDtypeStruct((queries, CHIP_COLS), BF16),
            jax.ShapeDtypeStruct((tokens, CHIP_COLS), BF16),
            jax.ShapeDtypeStruct((tokens, CHIP_COLS), BF16),
        ],
        in_specs=[SM, SM] + [VM] * 9,
        out_specs=[VM] * 3,
        scratch_shapes=[
            pltpu.VMEM((queries, width), BF16),
            pltpu.VMEM((CHIP_COLS, tokens), BF16),
            pltpu.VMEM((CHIP_COLS, TILE), F32),
            pltpu.VMEM((CHIP_COLS, TILE), F32),
            pltpu.VMEM((wide, CHIP_COLS), BF16),
            pltpu.VMEM((wide, CHIP_COLS), BF16),
            pltpu.VMEM((tokens, wide), BF16),
            pltpu.VMEM((tokens, wide), BF16),
            pltpu.VMEM((tokens, CHIP_COLS), F32),
            pltpu.VMEM((tokens, CHIP_COLS), F32),
        ],
        compiler_params=pltpu.CompilerParams(vmem_limit_bytes=VMEM_LIMIT),
        name="attention_backward",
    )(slots, q_local, hidden_rows, w_out, oT, q, k, v, lse, low, high)


def query_tables(slots_row, lengths_row, core):
    blocks = slots_row.shape[0]
    index = jnp.arange(blocks, dtype=jnp.int32)
    slot_of = jnp.sum(
        jnp.where(slots_row[None, :] == index[:, None], index[None, :], 0), axis=1, dtype=jnp.int32
    )
    per_device = blocks // (2 * CHIPS)
    own = slots_row.reshape(CHIPS, 2, per_device)
    own = lax.dynamic_index_in_dim(own, core, 1, keepdims=False).reshape(-1, 2)
    pairs = own.shape[0]
    swapped = (own[:, 0] >= PROMPT // BLK).astype(jnp.int32)
    pair = jnp.arange(pairs, dtype=jnp.int32)
    local = jnp.concatenate([2 * pair + swapped, 2 * pair + 1 - swapped])
    block = jnp.concatenate([jnp.min(own, axis=1), jnp.max(own, axis=1)])
    owner = local // per_device
    slot = owner * (2 * per_device) + core * per_device + local % per_device
    high = (block[:, None] * BLK + jnp.arange(BLK, dtype=jnp.int32)[None, :]).reshape(-1)
    starts = segment_starts(lengths_row[None])[0]
    low = jnp.max(jnp.where(starts[None, :] <= high[:, None], starts[None, :], 0), axis=1)
    shape = (2 * pairs * BLK // TILE, 1, TILE)
    return slot_of, slot, local, low.reshape(shape), high.reshape(shape)


def plane_shards(
    states, block_slot, cont_lengths, valid_mask, teacher, out_grad, predict, correct,
    norm_attn, w_query, w_key, w_value, w_out, norm_ffn, w_gate, w_up, w_down,
):
    depths = lax.axis_size("wsh")
    ctx = lax.axis_index("ctx")
    chip, core = ctx // 2, ctx % 2
    _, rows, _, width = states.shape
    shard = w_query.shape[0]
    half = shard // 2
    hidden_cols = w_gate.shape[1] // CHIPS
    group_len = block_slot.shape[1] * BLK

    def columns(weight):
        return lax.dynamic_slice_in_dim(weight, chip * CHIP_COLS, CHIP_COLS, 1)

    def core_half(weight):
        return lax.dynamic_slice_in_dim(weight, core * half, half, 0)

    qkv_piece = jnp.stack([columns(core_half(w)) for w in (w_query, w_key, w_value)])
    ff_split = hidden_cols // depths

    def ff_columns(weight):
        piece = core_half(weight).reshape(half, depths, CHIPS, ff_split)
        return lax.dynamic_index_in_dim(piece, chip, 2, keepdims=False).reshape(half, hidden_cols)

    down_rows = lax.dynamic_slice_in_dim(w_down, chip * ff_split + core * (ff_split // 2), ff_split // 2, 0)
    gain_one = lax.all_gather(norm_attn, "wsh", axis=0, tiled=True).astype(F32)
    gain_two = lax.all_gather(norm_ffn, "wsh", axis=0, tiled=True).astype(F32)
    out_w = lax.all_gather(w_out, "wsh", axis=0, tiled=True)
    out_w = lax.dynamic_slice_in_dim(out_w, chip * CHIP_COLS, CHIP_COLS, 0)
    ff_piece = lax.all_gather(
        jnp.stack([ff_columns(w_gate), ff_columns(w_up), down_rows]), "wsh", axis=0, tiled=False
    )
    valid_float = valid_mask.astype(F32)
    valid_total = lax.psum(jnp.sum(valid_float), ("ctx", "wsh"))

    slots, q_slots, q_local, low, high = query_tables(block_slot[0], cont_lengths[0], core)

    inputs = states[0].astype(F32)
    mixed = jnp.stack(
        [predict[i, 0] * inputs[:, 0] + predict[i, 1] * inputs[:, 1] for i in range(2)], axis=1
    )
    active = mixed[:, 0]
    normed, factor_one = rms_forward(active, gain_one)
    all_rows, qkv = gather_inputs(normed.astype(BF16), qkv_piece, 1)
    all_rows = all_rows.reshape(-1, width)
    qkv = qkv.reshape(3, width, CHIP_COLS)
    attended, *saved = attention_forward(all_rows, qkv, slots, q_slots, q_local, low, high)
    part = jnp.dot(attended, out_w, preferred_element_type=F32).astype(BF16)
    hidden = active + scatter_plane(part.reshape(CHIPS, rows, width), 2)
    normed_two, factor_two = rms_forward(hidden, gain_two)

    [ff] = share_cores([ff_piece], 3)
    gate_w, up_w, down_w = (
        jnp.swapaxes(ff[:, :, i], 0, 1).reshape(-1, ff.shape[-1]) for i in range(3)
    )
    two_rows = gather_plane(normed_two.astype(BF16), 4).reshape(-1, width)
    gate = jnp.dot(two_rows, gate_w, preferred_element_type=F32)
    up = jnp.dot(two_rows, up_w, preferred_element_type=F32)
    inner, inner_pull = jax.vjp(
        lambda gate_in, up_in: jax.nn.gelu(gate_in, approximate=True) * up_in, gate, up
    )
    inner = inner.astype(BF16)
    part = jnp.dot(inner, down_w, preferred_element_type=F32).astype(BF16)
    result = hidden + scatter_plane(part.reshape(CHIPS, rows, width), 5)

    difference = (result - active)[:, None]
    out_states = mixed + correct[None, :, None] * difference
    ratio = depths * group_len / valid_total
    upstream = out_grad[0].astype(F32) + ratio * valid_float[0][:, None, None] * (
        out_states - teacher[0].astype(F32)
    )
    correct_local = jnp.sum(upstream * difference, axis=(0, 2))
    result_grad = correct[0] * upstream[:, 0] + correct[1] * upstream[:, 1]

    grad_rows = gather_plane(result_grad.astype(BF16), 6).reshape(-1, width)
    inner_grad = lax.dot_general(grad_rows, down_w, NT, preferred_element_type=F32)
    gate_grad, up_grad = inner_pull(inner_grad)
    gate_grad, up_grad = gate_grad.astype(BF16), up_grad.astype(BF16)
    part = lax.dot_general(gate_grad, gate_w, NT, preferred_element_type=F32) + lax.dot_general(
        up_grad, up_w, NT, preferred_element_type=F32
    )
    normed_two_grad = scatter_plane(part.astype(BF16).reshape(CHIPS, rows, width), 7)

    def outer(left, right):
        return lax.dot_general(
            left, right, (((0,), (0,)), ((), ())), preferred_element_type=F32
        ).astype(BF16)

    gate_w_grad = outer(two_rows, gate_grad)
    up_w_grad = outer(two_rows, up_grad)
    down_w_grad = outer(inner, grad_rows)
    ff_grads = [g.reshape(depths, 2, half, hidden_cols) for g in (gate_w_grad, up_w_grad, down_w_grad)]
    ff_swapped = swap_cores(ff_grads, 8)

    def own_half(grad):
        return lax.dynamic_index_in_dim(grad, core, 1, keepdims=False)

    ff_sum = jnp.stack(
        [own_half(g).astype(F32) + s.astype(F32) for g, s in zip(ff_grads, ff_swapped)], axis=1
    ).astype(BF16)
    ff_sum = lax.psum_scatter(ff_sum, "wsh", scatter_dimension=0, tiled=False)
    ff_all = lax.all_gather(ff_sum, "ctx", axis=0, tiled=False)

    hidden_norm_grad, gain_two_grad = rms_backward(hidden, factor_two, gain_two, normed_two_grad)
    hidden_grad = result_grad + hidden_norm_grad
    hidden_rows = gather_plane(hidden_grad.astype(BF16), 9).reshape(-1, width)
    out_w_part = outer(attended, hidden_rows)
    dq, dk, dv = attention_backward(hidden_rows, out_w, saved, slots, q_local, low, high)
    by_core = [g.reshape(CHIPS, 2, rows, CHIP_COLS) for g in (dk, dv)]
    swapped = swap_cores(by_core, 10)
    dk, dv = (
        (own_half(g).astype(F32) + s.astype(F32)).astype(BF16).reshape(-1, CHIP_COLS)
        for g, s in zip(by_core, swapped)
    )
    part = (
        lax.dot_general(dq, qkv[0], NT, preferred_element_type=F32)
        + lax.dot_general(dk, qkv[1], NT, preferred_element_type=F32)
        + lax.dot_general(dv, qkv[2], NT, preferred_element_type=F32)
    )
    normed_grad = scatter_plane(part.astype(BF16).reshape(CHIPS, rows, width), 11)
    own_rows = lax.dynamic_index_in_dim(
        all_rows.reshape(CHIPS, 2, rows, width), core, 1, keepdims=False
    ).reshape(-1, width)
    qkv_grads = [outer(own_rows, g).reshape(depths, 2, half, CHIP_COLS) for g in (dq, dk, dv)]
    qkv_swapped = swap_cores(qkv_grads, 12)
    qkv_sum = jnp.stack(
        [own_half(g).astype(F32) + s.astype(F32) for g, s in zip(qkv_grads, qkv_swapped)], axis=1
    ).astype(BF16)
    qkv_sum = lax.psum_scatter(qkv_sum, "wsh", scatter_dimension=0, tiled=False)
    qkv_all = lax.all_gather(qkv_sum, "ctx", axis=0, tiled=False)

    spread = jnp.where(
        jnp.arange(CHIPS, dtype=jnp.int32)[:, None, None] == chip, out_w_part[None], jnp.zeros((), BF16)
    )
    out_w_grad = lax.psum(
        lax.psum_scatter(spread, "wsh", scatter_dimension=0, tiled=False), "ctx"
    ).astype(F32)

    active_norm_grad, gain_one_grad = rms_backward(active, factor_one, gain_one, normed_grad)
    active_grad = hidden_grad + active_norm_grad - result_grad
    mixed_grad = jnp.stack([upstream[:, 0] + active_grad, upstream[:, 1]], axis=1)
    predict_local = jnp.stack(
        [jnp.stack([jnp.sum(mixed_grad[:, i] * inputs[:, j]) for j in range(2)]) for i in range(2)]
    )
    states_grad = jnp.stack(
        [predict[0, j] * mixed_grad[:, 0] + predict[1, j] * mixed_grad[:, 1] for j in range(2)], axis=1
    ).astype(BF16)
    predict_grad, correct_grad, gain_one_grad, gain_two_grad = lax.psum(
        (predict_local, correct_local, gain_one_grad, gain_two_grad), ("ctx", "wsh")
    )
    offset = lax.axis_index("wsh") * shard

    def own_gain(grad):
        return lax.dynamic_slice_in_dim(grad, offset, shard, 0)

    def wide_rows(pieces, split):
        pieces = pieces.reshape(CHIPS, 2, half, split, -1)
        return jnp.transpose(pieces, (1, 2, 3, 0, 4)).reshape(shard, -1).astype(F32)

    query_grad, key_grad, value_grad = (wide_rows(qkv_all[:, i], 1) for i in range(3))
    gate_out, up_out = (wide_rows(ff_all[:, i], depths) for i in range(2))
    down_out = ff_all[:, 2].reshape(-1, width).astype(F32)
    return (
        out_states.astype(BF16)[None],
        states_grad[None],
        predict_grad,
        correct_grad,
        own_gain(gain_one_grad),
        query_grad,
        key_grad,
        value_grad,
        out_w_grad,
        own_gain(gain_two_grad),
        gate_out,
        up_out,
        down_out,
    )


def fits_plane(mesh, states, block_slot, w_query, w_gate):
    ctx, depths = mesh.shape["ctx"], mesh.shape["wsh"]
    return (
        ctx == 2 * CHIPS
        and states.shape[0] == depths
        and block_slot.shape[1] * BLK == 2 * PROMPT
        and states.shape[1] == 2 * PROMPT
        and w_query.shape[0] % (32 * depths) == 0
        and w_gate.shape[1] % (32 * CHIPS * depths) == 0
    )


def solution(mesh):
    in_specs = (
        P("wsh", "ctx", None, None),
        P("wsh", None),
        P("wsh", None),
        P("wsh", "ctx"),
        P("wsh", "ctx", None, None),
        P("wsh", "ctx", None, None),
        P(),
        P(),
        P("wsh"),
        P("wsh", None),
        P("wsh", None),
        P("wsh", None),
        P("wsh", None),
        P("wsh"),
        P("wsh", None),
        P("wsh", None),
        P("wsh", None),
    )
    out_specs = (
        P("wsh", "ctx", None, None),
        P("wsh", "ctx", None, None),
        P(),
        P(),
        P("wsh"),
        P("wsh", None),
        P("wsh", None),
        P("wsh", None),
        P("wsh", None),
        P("wsh"),
        P("wsh", None),
        P("wsh", None),
        P("wsh", None),
    )

    def step(*args):
        plane = fits_plane(mesh, args[0], args[1], args[9], args[14])
        body = plane_shards if plane else general_shards
        return jax.shard_map(
            body, mesh=mesh, in_specs=in_specs, out_specs=out_specs, check_vma=False
        )(*args)

    return step
```

```python
import functools
import math

import jax
import jax.numpy as jnp
from jax import lax
from jax.experimental import pallas as pl
from jax.experimental.pallas import tpu as pltpu
from jax.sharding import PartitionSpec as P

HEADS = 12
HD = 64
PROMPT = 1024
BLK = 64


EPSILON = 1e-06
NEGATIVE = -1e30
HIGHEST = lax.Precision.HIGHEST


def rms_forward(tensor, gain_vec):
    factor = lax.rsqrt(jnp.mean(tensor * tensor, axis=-1, keepdims=True) + EPSILON)
    return (tensor * factor * gain_vec, factor)


def rms_backward(tensor, factor, gain_vec, upstream):
    weighted = upstream * gain_vec
    gain_grad = jnp.sum(upstream * tensor * factor, axis=0)
    middle = jnp.mean(weighted * tensor, axis=-1, keepdims=True)
    return (factor * weighted - tensor * factor * factor * factor * middle, gain_grad)


def segment_starts(cont_lengths):
    count = cont_lengths.shape[1]
    index = jnp.arange(count, dtype=jnp.int32)
    before = index[:, None] < index[None, :]
    return PROMPT + jnp.sum(jnp.where(before[None], cont_lengths[:, :, None], 0), axis=1)


def token_places(block_slot, cont_lengths):
    groups, blocks = block_slot.shape
    offsets = jnp.arange(BLK, dtype=jnp.int32)
    places = (block_slot[:, :, None] * BLK + offsets[None, None, :]).reshape(groups, blocks * BLK)
    starts = segment_starts(cont_lengths)
    segments = jnp.sum((places[:, :, None] >= starts[:, None, :]).astype(jnp.int32), axis=2)
    return (places, segments)


def visible(query_place, query_segment, key_place, key_segment):
    earlier = key_place[:, None, :] <= query_place[:, :, None]
    shared = (key_segment[:, None, :] == 0) | (key_segment[:, None, :] == query_segment[:, :, None])
    return earlier & shared


def split_heads(tensor):
    return tensor.reshape(tensor.shape[0], tensor.shape[1], HEADS, HD)


def forward_block(running, query_part, key_part, value_part, allowed):

    def forward_compute(current):
        maximum, denominator, accumulated = current
        scores = jnp.einsum(
            "gqhd,gkhd->ghqk",
            split_heads(query_part),
            split_heads(key_part),
            preferred_element_type=jnp.float32,
        )
        masked = jnp.where(allowed[:, None], scores, NEGATIVE)
        new_max = jnp.maximum(maximum, jnp.max(masked, axis=-1))
        exponent = jnp.where(allowed[:, None], jnp.exp(masked - new_max[..., None]), 0.0)
        factor = jnp.exp(maximum - new_max)
        rescale = jnp.swapaxes(factor, 1, 2)[..., None]
        update = jnp.einsum(
            "ghqk,gkhd->gqhd",
            exponent.astype(jnp.bfloat16),
            split_heads(value_part),
            preferred_element_type=jnp.float32,
        )
        merged = (split_heads(accumulated) * rescale + update).reshape(accumulated.shape)
        return (new_max, denominator * factor + jnp.sum(exponent, axis=-1), merged)

    return lax.cond(jnp.any(allowed), forward_compute, lambda current: current, running)


def backward_block(
    query_part, grad_part, key_part, value_part, allowed, maximum, denominator, delta_sum
):
    scores = jnp.einsum(
        "gqhd,gkhd->ghqk",
        split_heads(query_part),
        split_heads(key_part),
        preferred_element_type=jnp.float32,
    )
    exponent = jnp.where(allowed[:, None], jnp.exp(scores - maximum[..., None]), 0.0)
    probability = exponent / denominator[..., None]
    prob_grad = jnp.einsum(
        "gqhd,gkhd->ghqk",
        split_heads(grad_part),
        split_heads(value_part),
        preferred_element_type=jnp.float32,
    )
    score_grad = (probability * (prob_grad - delta_sum[..., None])).astype(jnp.bfloat16)
    return (probability.astype(jnp.bfloat16), score_grad)


def general_shards(
    states,
    block_slot,
    cont_lengths,
    valid_mask,
    teacher,
    out_grad,
    predict,
    correct,
    norm_attn,
    w_query,
    w_key,
    w_value,
    w_out,
    norm_ffn,
    w_gate,
    w_up,
    w_down,
):
    groups, local_len = valid_mask.shape
    model_width = states.shape[3]
    row_count = groups * local_len
    group_len = block_slot.shape[1] * BLK
    gain_one, query_w, key_w, value_w, out_w, gain_two, gate_w, up_w, down_w = (
        lax.all_gather(norm_attn, "wsh", axis=0, tiled=True),
        lax.all_gather(w_query, "wsh", axis=0, tiled=True),
        lax.all_gather(w_key, "wsh", axis=0, tiled=True),
        lax.all_gather(w_value, "wsh", axis=0, tiled=True),
        lax.all_gather(w_out, "wsh", axis=0, tiled=True),
        lax.all_gather(norm_ffn, "wsh", axis=0, tiled=True),
        lax.all_gather(w_gate, "wsh", axis=0, tiled=True),
        lax.all_gather(w_up, "wsh", axis=0, tiled=True),
        lax.all_gather(w_down, "wsh", axis=0, tiled=True),
    )
    valid_float = valid_mask.astype(jnp.float32)
    valid_total = lax.psum(jnp.sum(valid_float), ("ctx", "wsh"))
    places, segments = token_places(block_slot, cont_lengths)
    offset = lax.axis_index("ctx") * local_len
    own_place = lax.dynamic_slice_in_dim(places, offset, local_len, 1)
    own_segment = lax.dynamic_slice_in_dim(segments, offset, local_len, 1)
    inputs = states.astype(jnp.float32)
    mixed_states = jnp.einsum("ij,gtjd->gtid", predict, inputs, precision=HIGHEST)
    active = mixed_states[:, :, 0].reshape(row_count, model_width)
    gain_first = gain_one.astype(jnp.float32)
    normed, factor_one = rms_forward(active, gain_first)
    normed_low = normed.astype(jnp.bfloat16)
    queries = (
        jnp.dot(normed_low, query_w, preferred_element_type=jnp.float32)
        .astype(jnp.bfloat16)
        .reshape(groups, local_len, model_width)
    )
    key_rows = (
        jnp.dot(normed_low, key_w, preferred_element_type=jnp.float32)
        .astype(jnp.bfloat16)
        .reshape(groups, local_len, model_width)
    )
    values = (
        jnp.dot(normed_low, value_w, preferred_element_type=jnp.float32)
        .astype(jnp.bfloat16)
        .reshape(groups, local_len, model_width)
    )
    initial = (
        jnp.full((groups, HEADS, local_len), NEGATIVE, jnp.float32),
        jnp.zeros((groups, HEADS, local_len), jnp.float32),
        jnp.zeros((groups, local_len, model_width), jnp.float32),
    )
    piece_keys = lax.all_gather(key_rows, "ctx", axis=1, tiled=True)
    piece_values = lax.all_gather(values, "ctx", axis=1, tiled=True)
    piece_len = piece_keys.shape[1]
    block_size = math.gcd(piece_len, local_len)

    def fold_one_block(current, block_index):
        begin = block_index * block_size
        key_part = lax.dynamic_slice_in_dim(piece_keys, begin, block_size, 1)
        value_part = lax.dynamic_slice_in_dim(piece_values, begin, block_size, 1)
        key_place = lax.dynamic_slice_in_dim(places, begin, block_size, 1)
        key_segment = lax.dynamic_slice_in_dim(segments, begin, block_size, 1)
        allowed = visible(own_place, own_segment, key_place, key_segment)
        return (forward_block(current, queries, key_part, value_part, allowed), None)

    finished, unused = lax.scan(
        fold_one_block, initial, jnp.arange(piece_len // block_size, dtype=jnp.int32)
    )
    maximum, denominator, accumulated = finished
    attended = (split_heads(accumulated) / jnp.swapaxes(denominator, 1, 2)[..., None]).reshape(
        row_count, model_width
    )
    attended_low = attended.astype(jnp.bfloat16)
    hidden = active + jnp.dot(attended_low, out_w, preferred_element_type=jnp.float32)
    gain_second = gain_two.astype(jnp.float32)
    normed_two, factor_two = rms_forward(hidden, gain_second)
    normed_two_low = normed_two.astype(jnp.bfloat16)
    gate_proj = jnp.dot(normed_two_low, gate_w, preferred_element_type=jnp.float32)
    up_proj = jnp.dot(normed_two_low, up_w, preferred_element_type=jnp.float32)
    inner_act, inner_pull = jax.vjp(
        lambda gate_in, up_in: jax.nn.gelu(gate_in, approximate=True) * up_in, gate_proj, up_proj
    )
    inner_low = inner_act.astype(jnp.bfloat16)
    result = hidden + jnp.dot(inner_low, down_w, preferred_element_type=jnp.float32)
    difference = (result - active).reshape(groups, local_len, 1, model_width)
    out_states = mixed_states + correct[None, None, :, None] * difference
    new_states = out_states.astype(jnp.bfloat16)
    loss_ratio = lax.axis_size("wsh") * groups * group_len / valid_total
    upstream = out_grad.astype(jnp.float32) + loss_ratio * valid_float[:, :, None, None] * (
        out_states - teacher.astype(jnp.float32)
    )
    correct_local = jnp.sum(upstream * difference, axis=(0, 1, 3))
    result_grad = jnp.einsum("i,gtid->gtd", correct, upstream, precision=HIGHEST).reshape(
        row_count, model_width
    )
    result_low = result_grad.astype(jnp.bfloat16)
    down_grad = jnp.einsum("rf,rd->fd", inner_low, result_low, preferred_element_type=jnp.float32)
    inner_grad = jnp.einsum("rd,fd->rf", result_low, down_w, preferred_element_type=jnp.float32)
    gate_grad, up_grad = inner_pull(inner_grad)
    gate_low = gate_grad.astype(jnp.bfloat16)
    up_low = up_grad.astype(jnp.bfloat16)
    gate_w_grad = jnp.einsum(
        "rd,rf->df", normed_two_low, gate_low, preferred_element_type=jnp.float32
    )
    up_w_grad = jnp.einsum("rd,rf->df", normed_two_low, up_low, preferred_element_type=jnp.float32)
    normed_two_grad = jnp.einsum(
        "rf,df->rd", gate_low, gate_w, preferred_element_type=jnp.float32
    ) + jnp.einsum("rf,df->rd", up_low, up_w, preferred_element_type=jnp.float32)
    hidden_norm_grad, gain_two_grad = rms_backward(hidden, factor_two, gain_second, normed_two_grad)
    hidden_grad = result_grad + hidden_norm_grad
    hidden_low = hidden_grad.astype(jnp.bfloat16)
    out_w_grad = jnp.einsum(
        "rc,rd->cd", attended_low, hidden_low, preferred_element_type=jnp.float32
    )
    attended_grad = jnp.einsum(
        "rd,cd->rc", hidden_low, out_w, preferred_element_type=jnp.float32
    ).astype(jnp.bfloat16)
    delta_sum = jnp.swapaxes(
        jnp.sum(
            split_heads(
                (attended_grad.astype(jnp.float32) * attended).reshape(
                    groups, local_len, model_width
                )
            ),
            axis=-1,
        ),
        1,
        2,
    )
    grad_local = attended_grad.reshape(groups, local_len, model_width)
    zero_grad = jnp.zeros((groups, local_len, model_width), jnp.float32)
    all_keys, all_values = (
        lax.all_gather(key_rows, "ctx", axis=1, tiled=True),
        lax.all_gather(values, "ctx", axis=1, tiled=True),
    )

    def query_step(current, block_index):
        begin = block_index * local_len
        key_part = lax.dynamic_slice_in_dim(all_keys, begin, local_len, 1)
        value_part = lax.dynamic_slice_in_dim(all_values, begin, local_len, 1)
        key_place = lax.dynamic_slice_in_dim(places, begin, local_len, 1)
        key_segment = lax.dynamic_slice_in_dim(segments, begin, local_len, 1)
        allowed = visible(own_place, own_segment, key_place, key_segment)

        def query_compute(query_sum):
            prob_low, score_grad = backward_block(
                queries, grad_local, key_part, value_part, allowed, maximum, denominator, delta_sum
            )
            return query_sum + jnp.einsum(
                "ghqk,gkhd->gqhd",
                score_grad,
                split_heads(key_part),
                preferred_element_type=jnp.float32,
            ).reshape(groups, local_len, model_width)

        return (
            lax.cond(jnp.any(allowed), query_compute, lambda query_sum: query_sum, current),
            None,
        )

    finished, unused = lax.scan(
        query_step, zero_grad, jnp.arange(group_len // local_len, dtype=jnp.int32)
    )
    term_rows = local_len * lax.axis_size("ctx")
    key_block_size = math.gcd(term_rows, local_len)

    def key_one_block(block_index):
        begin = block_index * key_block_size
        key_part = lax.dynamic_slice_in_dim(all_keys, begin, key_block_size, 1)
        value_part = lax.dynamic_slice_in_dim(all_values, begin, key_block_size, 1)
        key_place = lax.dynamic_slice_in_dim(places, begin, key_block_size, 1)
        key_segment = lax.dynamic_slice_in_dim(segments, begin, key_block_size, 1)
        allowed = visible(own_place, own_segment, key_place, key_segment)

        def one_compute(unused_arg):
            prob_low, score_grad = backward_block(
                queries, grad_local, key_part, value_part, allowed, maximum, denominator, delta_sum
            )
            key_add = jnp.einsum(
                "ghqk,gqhd->kghd",
                score_grad,
                split_heads(queries),
                preferred_element_type=jnp.float32,
            ).reshape(key_block_size, groups, model_width)
            value_add = jnp.einsum(
                "ghqk,gqhd->kghd",
                prob_low,
                split_heads(grad_local),
                preferred_element_type=jnp.float32,
            ).reshape(key_block_size, groups, model_width)
            return jnp.stack([key_add, value_add], axis=1)

        return lax.cond(
            jnp.any(allowed),
            one_compute,
            lambda unused_arg: jnp.zeros((key_block_size, 2, groups, model_width), jnp.float32),
            0,
        )

    summed = lax.psum_scatter(
        lax.map(key_one_block, jnp.arange(term_rows // key_block_size, dtype=jnp.int32))
        .reshape(term_rows, 2, groups, model_width)
        .astype(jnp.bfloat16),
        "ctx",
        scatter_dimension=0,
        tiled=True,
    ).astype(jnp.float32)
    key_grad = jnp.swapaxes(summed[:, 0], 0, 1)
    value_grad = jnp.swapaxes(summed[:, 1], 0, 1)
    query_low = finished.reshape(row_count, model_width).astype(jnp.bfloat16)
    key_low = key_grad.reshape(row_count, model_width).astype(jnp.bfloat16)
    value_low = value_grad.reshape(row_count, model_width).astype(jnp.bfloat16)
    query_w_grad = jnp.einsum(
        "rc,rd->cd", normed_low, query_low, preferred_element_type=jnp.float32
    )
    key_w_grad = jnp.einsum("rc,rd->cd", normed_low, key_low, preferred_element_type=jnp.float32)
    value_w_grad = jnp.einsum(
        "rc,rd->cd", normed_low, value_low, preferred_element_type=jnp.float32
    )
    normed_grad = (
        jnp.einsum("rd,cd->rc", query_low, query_w, preferred_element_type=jnp.float32)
        + jnp.einsum("rd,cd->rc", key_low, key_w, preferred_element_type=jnp.float32)
        + jnp.einsum("rd,cd->rc", value_low, value_w, preferred_element_type=jnp.float32)
    )
    active_norm_grad, gain_one_grad = rms_backward(active, factor_one, gain_first, normed_grad)
    active_grad = (hidden_grad + active_norm_grad - result_grad).reshape(
        groups, local_len, 1, model_width
    )
    mixed_grad = jnp.concatenate([upstream[:, :, :1] + active_grad, upstream[:, :, 1:]], axis=2)
    predict_local = jnp.einsum("gtid,gtjd->ij", mixed_grad, inputs, precision=HIGHEST)
    states_grad = jnp.einsum("ij,gtid->gtjd", predict, mixed_grad, precision=HIGHEST).astype(
        jnp.bfloat16
    )
    predict_grad, correct_grad = lax.psum((predict_local, correct_local), ("ctx", "wsh"))
    (
        gain_one_rows,
        query_rows,
        key_grad_rows,
        value_rows,
        out_rows,
        gain_two_rows,
        gate_rows,
        up_rows,
        down_rows,
    ) = (
        lax.psum_scatter(
            gain_one_grad.astype(jnp.bfloat16), "wsh", scatter_dimension=0, tiled=True
        ).astype(jnp.float32),
        lax.psum_scatter(
            query_w_grad.astype(jnp.bfloat16), "wsh", scatter_dimension=0, tiled=True
        ).astype(jnp.float32),
        lax.psum_scatter(
            key_w_grad.astype(jnp.bfloat16), "wsh", scatter_dimension=0, tiled=True
        ).astype(jnp.float32),
        lax.psum_scatter(
            value_w_grad.astype(jnp.bfloat16), "wsh", scatter_dimension=0, tiled=True
        ).astype(jnp.float32),
        lax.psum_scatter(
            out_w_grad.astype(jnp.bfloat16), "wsh", scatter_dimension=0, tiled=True
        ).astype(jnp.float32),
        lax.psum_scatter(
            gain_two_grad.astype(jnp.bfloat16), "wsh", scatter_dimension=0, tiled=True
        ).astype(jnp.float32),
        lax.psum_scatter(
            gate_w_grad.astype(jnp.bfloat16), "wsh", scatter_dimension=0, tiled=True
        ).astype(jnp.float32),
        lax.psum_scatter(
            up_w_grad.astype(jnp.bfloat16), "wsh", scatter_dimension=0, tiled=True
        ).astype(jnp.float32),
        lax.psum_scatter(
            down_grad.astype(jnp.bfloat16), "wsh", scatter_dimension=0, tiled=True
        ).astype(jnp.float32),
    )
    totals = (
        lax.psum(gain_one_rows.astype(jnp.bfloat16), "ctx").astype(jnp.float32),
        lax.psum(query_rows.astype(jnp.bfloat16), "ctx").astype(jnp.float32),
        lax.psum(key_grad_rows.astype(jnp.bfloat16), "ctx").astype(jnp.float32),
        lax.psum(value_rows.astype(jnp.bfloat16), "ctx").astype(jnp.float32),
        lax.psum(out_rows.astype(jnp.bfloat16), "ctx").astype(jnp.float32),
        lax.psum(gain_two_rows.astype(jnp.bfloat16), "ctx").astype(jnp.float32),
        lax.psum(gate_rows.astype(jnp.bfloat16), "ctx").astype(jnp.float32),
        lax.psum(up_rows.astype(jnp.bfloat16), "ctx").astype(jnp.float32),
        lax.psum(down_rows.astype(jnp.bfloat16), "ctx").astype(jnp.float32),
    )
    return (new_states, states_grad, predict_grad, correct_grad) + tuple(totals)


MESH = pl.DeviceIdType.MESH
F32 = jnp.float32
BF16 = jnp.bfloat16
CHIPS = 4
VMEM_LIMIT = 60 * 2**20


def place_on_mesh():
    ctx = lax.axis_index("ctx")
    depth = lax.axis_index("wsh")
    chip = ctx // 2
    core = ctx % 2
    chip_x = chip + 1 - 2 * (chip % 2)
    chip_y = chip + 2 - 4 * (chip // 2)
    return depth, chip, core, chip_x, chip_y, 3 - chip


def signal_and_wait(devices):
    barrier = pltpu.get_barrier_semaphore()
    for device in devices:
        pl.semaphore_signal(barrier, inc=1, device_id=device, device_id_type=MESH)
    pl.semaphore_wait(barrier, len(devices))


def remote(src, dst, send, recv, index, device):
    return pltpu.make_async_remote_copy(
        src_ref=src,
        dst_ref=dst,
        send_sem=send.at[index],
        recv_sem=recv.at[index],
        device_id=device,
        device_id_type=MESH,
    )


def comm_params(collective_id):
    return pltpu.CompilerParams(
        collective_id=collective_id, has_side_effects=True, vmem_limit_bytes=VMEM_LIMIT
    )


ANY = pl.BlockSpec(memory_space=pl.ANY)
VM = pl.BlockSpec(memory_space=pltpu.VMEM)
SM = pl.BlockSpec(memory_space=pltpu.SMEM)


def ring_sends(own, out, slot_of, chip, core, depth, chip_x, chip_y, send, recv):
    half = own.shape[0] // 2
    top, low = pl.ds(0, half), pl.ds(half, half)
    dev_x, dev_y = (2 * chip_x + core, depth), (2 * chip_y + core, depth)
    here = slot_of(chip)
    return [
        remote(own.at[top], out.at[here, top], send, recv, 0, dev_x),
        remote(own.at[low], out.at[here, low], send, recv, 1, dev_y),
        remote(own.at[low], out.at[here, low], send, recv, 2, dev_x),
        remote(own.at[top], out.at[here, top], send, recv, 3, dev_y),
        remote(out.at[slot_of(chip_x), top], out.at[slot_of(chip_x), top], send, recv, 4, dev_y),
        remote(out.at[slot_of(chip_y), low], out.at[slot_of(chip_y), low], send, recv, 5, dev_x),
    ]


def gather_plane(block, collective_id):
    def kernel(x_ref, out_ref, send, recv, local):
        depth, chip, core, chip_x, chip_y, _ = place_on_mesh()
        signal_and_wait([(2 * chip_x + core, depth), (2 * chip_y + core, depth)])
        copies = ring_sends(
            x_ref, out_ref, lambda c: c, chip, core, depth, chip_x, chip_y, send, recv
        )
        for copy in copies[:4]:
            copy.start()
        mine = pltpu.make_async_copy(x_ref, out_ref.at[chip], local)
        mine.start()
        copies[0].wait_recv()
        copies[4].start()
        copies[1].wait_recv()
        copies[5].start()
        for copy in copies[2:]:
            copy.wait_recv()
        for copy in copies:
            copy.wait_send()
        mine.wait()

    return pl.pallas_call(
        kernel,
        out_shape=jax.ShapeDtypeStruct((CHIPS,) + block.shape, block.dtype),
        in_specs=[ANY],
        out_specs=ANY,
        scratch_shapes=[
            pltpu.SemaphoreType.DMA((6,)),
            pltpu.SemaphoreType.DMA((6,)),
            pltpu.SemaphoreType.DMA,
        ],
        compiler_params=comm_params(collective_id),
        name="gather_plane",
    )(block)


def scatter_plane(parts, collective_id):
    _, rows, width = parts.shape
    half = rows // 2

    def kernel(x_ref, out_ref, near, diagonal, staged, send, recv):
        depth, chip, core, chip_x, chip_y, chip_d = place_on_mesh()
        dev_x, dev_y = (2 * chip_x + core, depth), (2 * chip_y + core, depth)
        signal_and_wait([dev_x, dev_y])
        top, low = pl.ds(0, half), pl.ds(half, half)
        first = [
            remote(x_ref.at[chip_d, top], diagonal.at[0], send, recv, 0, dev_x),
            remote(x_ref.at[chip_d, low], diagonal.at[1], send, recv, 1, dev_y),
            remote(x_ref.at[chip_x, top], near.at[0, top], send, recv, 2, dev_x),
            remote(x_ref.at[chip_y, low], near.at[1, low], send, recv, 3, dev_y),
        ]
        for copy in first:
            copy.start()
        second = [
            remote(staged.at[0], near.at[1, top], send, recv, 4, dev_y),
            remote(staged.at[1], near.at[0, low], send, recv, 5, dev_x),
        ]
        first[0].wait_recv()
        staged[0] = (x_ref[chip_y, top].astype(F32) + diagonal[0].astype(F32)).astype(BF16)
        second[0].start()
        first[1].wait_recv()
        staged[1] = (x_ref[chip_x, low].astype(F32) + diagonal[1].astype(F32)).astype(BF16)
        second[1].start()
        for copy in first[2:] + second:
            copy.wait_recv()
        out_ref[...] = (
            x_ref[chip].astype(F32) + near[0].astype(F32) + near[1].astype(F32)
        )
        for copy in first + second:
            copy.wait_send()

    return pl.pallas_call(
        kernel,
        out_shape=jax.ShapeDtypeStruct((rows, width), F32),
        in_specs=[VM],
        out_specs=VM,
        scratch_shapes=[
            pltpu.VMEM((2, rows, width), BF16),
            pltpu.VMEM((2, half, width), BF16),
            pltpu.VMEM((2, half, width), BF16),
            pltpu.SemaphoreType.DMA((6,)),
            pltpu.SemaphoreType.DMA((6,)),
        ],
        compiler_params=comm_params(collective_id),
        name="scatter_plane",
    )(parts)


def swap_cores(arrays, collective_id):
    count = len(arrays)

    def kernel(*refs):
        ins, outs, (send, recv) = refs[:count], refs[count : 2 * count], refs[2 * count :]
        depth, chip, core, _, _, _ = place_on_mesh()
        other = (2 * chip + 1 - core, depth)
        signal_and_wait([other])
        copies = [
            remote(ins[i].at[:, 1 - core], outs[i], send, recv, i, other) for i in range(count)
        ]
        for copy in copies:
            copy.start()
        for copy in copies:
            copy.wait()

    return pl.pallas_call(
        kernel,
        out_shape=[jax.ShapeDtypeStruct(a.shape[:1] + a.shape[2:], a.dtype) for a in arrays],
        in_specs=[ANY] * count,
        out_specs=[ANY] * count,
        scratch_shapes=[pltpu.SemaphoreType.DMA((count,))] * 2,
        compiler_params=comm_params(collective_id),
        name="swap_cores",
    )(*arrays)


def line_relay(ref, chip, depth, depths, send, recv, send_base):
    _, _, core, _, _, _ = place_on_mesh()
    up = remote(ref, ref, send, recv, send_base, (2 * chip + core, lax.rem(depth + 1, depths)))
    down = remote(
        ref, ref, send, recv, send_base + 1, (2 * chip + core, lax.rem(depth + depths - 1, depths))
    )
    goes_up = (depth >= chip) & (depth < depths - 1)
    goes_down = (depth <= chip) & (depth > 0)

    def start():
        @pl.when(goes_up)
        def _():
            up.start()

        @pl.when(goes_down)
        def _():
            down.start()

    def receive():
        @pl.when(depth > chip)
        def _():
            up.wait_recv()

        @pl.when(depth < chip)
        def _():
            down.wait_recv()

    def finish():
        @pl.when(goes_up)
        def _():
            up.wait_send()

        @pl.when(goes_down)
        def _():
            down.wait_send()

    return start, receive, finish


def gather_inputs(pre, small, weights, out_half, collective_id):
    depths = lax.axis_size("wsh")

    def kernel(
        pre_ref, small_ref, w_ref, o_ref, out_ref, wall_ref, oall_ref, sum_ref,
        own, arrived, count, counted,
        send, recv, wsend, wrecv, ssend, srecv, bsend, brecv, csend, crecv, osend, orecv, local,
    ):
        depth, chip, core, chip_x, chip_y, chip_d = place_on_mesh()
        dev_x, dev_y = (2 * chip_x + core, depth), (2 * chip_y + core, depth)
        other = (2 * chip + 1 - core, depth)
        across = [
            (2 * chip + core, lax.rem(depth + step, depths)) for step in range(1, depths)
        ]
        signal_and_wait([dev_x, dev_y, other] + across)

        def slot(chip_index):
            return 2 * chip_index + core

        small_copies = [
            remote(small_ref, arrived.at[i], bsend, brecv, i, device)
            for i, device in enumerate(across)
        ]
        for copy in small_copies:
            copy.start()
        w_copies = [
            remote(w_ref, wall_ref.at[:, depth, core], wsend, wrecv, i, device)
            for i, device in enumerate(across)
        ]
        for copy in w_copies:
            copy.start()
        mine = pltpu.make_async_copy(w_ref, wall_ref.at[:, depth, core], local.at[1])
        mine.start()

        def pass_on(index, slot_index):
            ref = out_ref.at[slot_index]
            return remote(ref, ref, ssend, srecv, index, other)

        def pass_weights(index, depth_index):
            ref = wall_ref.at[:, depth_index, core]
            return remote(ref, ref, ssend, srecv, index, other)

        shared = [
            remote(own, out_ref.at[slot(chip)], ssend, srecv, 0, other),
            pass_on(1, slot(chip_x)),
            pass_on(2, slot(chip_y)),
            pass_on(3, slot(chip_d)),
            remote(w_ref, wall_ref.at[:, depth, core], ssend, srecv, 4, other),
        ] + [
            pass_weights(5 + i, lax.rem(depth + depths - 1 - i, depths))
            for i in range(depths - 1)
        ]
        shared[4].start()

        @pl.when(depth == chip)
        def _():
            fill = pltpu.make_async_copy(o_ref, oall_ref.at[core], local.at[2])
            fill.start()
            fill.wait()

        relay_start, relay_receive, relay_finish = line_relay(
            oall_ref.at[core], chip, depth, depths, osend, orecv, 0
        )

        @pl.when(depth == chip)
        def _():
            relay_start()

        for copy in small_copies:
            copy.wait_recv()
        total = small_ref[...]
        for i in range(depths - 1):
            total = total + arrived[i]
        own[...] = (pre_ref[...] * total[0:1, :]).astype(BF16)
        copies = ring_sends(
            own, out_ref, slot, chip, core, depth, chip_x, chip_y, send, recv
        )
        for copy in copies[:4]:
            copy.start()
        shared[0].start()
        mine_rows = pltpu.make_async_copy(own, out_ref.at[slot(chip)], local.at[0])
        mine_rows.start()
        sum_ref[...] = total

        def count_stage(index, device):
            return remote(count.at[index], counted.at[index], csend, crecv, index, device)

        stages = [count_stage(0, dev_x), count_stage(1, dev_y), count_stage(2, other)]
        running = jnp.broadcast_to(total[2:3, 0:128], (8, 128))
        count[0] = running
        stages[0].start()
        copies[0].wait_recv()
        copies[4].start()
        copies[1].wait_recv()
        copies[5].start()
        stages[0].wait_recv()
        running = running + counted[0]
        count[1] = running
        stages[1].start()

        @pl.when(depth != chip)
        def _():
            relay_receive()
            relay_start()

        pass_out = remote(oall_ref.at[core], oall_ref.at[core], osend, orecv, 2, other)
        pass_out.start()
        stages[1].wait_recv()
        running = running + counted[1]
        count[2] = running
        stages[2].start()
        for i in range(depths - 1):
            w_copies[i].wait_recv()
            shared[5 + i].start()
        copies[2].wait_recv()
        shared[1].start()
        copies[3].wait_recv()
        shared[2].start()
        stages[2].wait_recv()
        sum_ref[2:3, 0:128] = (running + counted[2])[0:1]
        copies[4].wait_recv()
        copies[5].wait_recv()
        shared[3].start()
        for copy in shared + [pass_out]:
            copy.wait()
        for copy in copies + w_copies + small_copies + stages:
            copy.wait_send()
        relay_finish()
        mine.wait()
        mine_rows.wait()

    rows, width = pre.shape
    parts, half, columns = weights.shape
    dma = pltpu.SemaphoreType.DMA
    return pl.pallas_call(
        kernel,
        out_shape=[
            jax.ShapeDtypeStruct((lax.axis_size("ctx"), rows, width), BF16),
            jax.ShapeDtypeStruct((parts, depths, 2, half, columns), weights.dtype),
            jax.ShapeDtypeStruct((2,) + out_half.shape, out_half.dtype),
            jax.ShapeDtypeStruct(small.shape, F32),
        ],
        in_specs=[VM, VM, ANY, ANY],
        out_specs=[ANY, ANY, ANY, VM],
        scratch_shapes=[
            pltpu.VMEM((rows, width), BF16),
            pltpu.VMEM((depths - 1,) + small.shape, F32),
            pltpu.VMEM((3, 8, 128), F32),
            pltpu.VMEM((3, 8, 128), F32),
            dma((6,)),
            dma((6,)),
            dma((depths - 1,)),
            dma((depths - 1,)),
            dma((depths + 4,)),
            dma((depths + 4,)),
            dma((depths - 1,)),
            dma((depths - 1,)),
            dma((3,)),
            dma((3,)),
            dma((3,)),
            dma((3,)),
            dma((3,)),
        ],
        compiler_params=comm_params(collective_id),
        name="gather_inputs",
    )(pre, small, weights, out_half)


def share_weights(piece, collective_id):
    depths, parts, half, columns = piece.shape

    def kernel(x_ref, out_ref, send, recv, local):
        depth, chip, core, _, _, _ = place_on_mesh()
        other = (2 * chip + 1 - core, depth)
        signal_and_wait([other])
        copies = []
        for i in range(parts):
            dst = out_ref.at[i, :, core]
            copies.append(remote(x_ref.at[:, i], dst, send, recv, i, other))
            copies.append(pltpu.make_async_copy(x_ref.at[:, i], dst, local.at[i]))
        for copy in copies:
            copy.start()
        for copy in copies:
            copy.wait()

    return pl.pallas_call(
        kernel,
        out_shape=jax.ShapeDtypeStruct((parts, depths, 2, half, columns), piece.dtype),
        in_specs=[ANY],
        out_specs=ANY,
        scratch_shapes=[pltpu.SemaphoreType.DMA((parts,))] * 3,
        compiler_params=comm_params(collective_id),
        name="share_weights",
    )(piece)


def scatter_and_reduce(parts, qkv, out, collective_id):
    _, rows, width = parts.shape
    half = rows // 2
    depths = qkv.shape[0]

    def kernel(
        x_ref, q_ref, o_ref, out_ref, qsum_ref, osum_ref,
        near, diagonal, staged, q_other, q_mine, q_far, o_other, o_mine, o_far,
        send, recv, ssend, srecv, zsend, zrecv, osend, orecv,
    ):
        depth, chip, core, chip_x, chip_y, chip_d = place_on_mesh()
        dev_x, dev_y = (2 * chip_x + core, depth), (2 * chip_y + core, depth)
        other = (2 * chip + 1 - core, depth)
        across = [
            (2 * chip + core, lax.rem(depth + step, depths)) for step in range(1, depths)
        ]
        signal_and_wait([dev_x, dev_y, other] + across)
        top, low = pl.ds(0, half), pl.ds(half, half)
        first = [
            remote(x_ref.at[chip_d, top], diagonal.at[0], send, recv, 0, dev_x),
            remote(x_ref.at[chip_d, low], diagonal.at[1], send, recv, 1, dev_y),
            remote(x_ref.at[chip_x, top], near.at[0, top], send, recv, 2, dev_x),
            remote(x_ref.at[chip_y, low], near.at[1, low], send, recv, 3, dev_y),
        ]
        swaps = [
            remote(q_ref.at[:, 1 - core], q_other, ssend, srecv, 0, other),
            remote(o_ref.at[1 - core], o_other, ssend, srecv, 1, other),
        ]
        for copy in first + swaps:
            copy.start()
        swaps[0].wait_recv()
        for i in range(depths):
            q_mine[i] = (q_ref[i, core].astype(F32) + q_other[i].astype(F32)).astype(BF16)
        q_copies = [
            remote(q_mine.at[lax.rem(depth + i + 1, depths)], q_far.at[i], zsend, zrecv, i, device)
            for i, device in enumerate(across)
        ]
        for copy in q_copies:
            copy.start()
        swaps[1].wait_recv()
        o_mine[...] = (o_ref[core].astype(F32) + o_other[...].astype(F32)).astype(BF16)
        distance = lax.rem(chip + depths - depth, depths)
        o_copies = [
            remote(o_mine, o_far.at[i], osend, orecv, i, device) for i, device in enumerate(across)
        ]
        for i in range(depths - 1):

            @pl.when(distance == i + 1)
            def _(i=i):
                o_copies[i].start()

        second = [
            remote(staged.at[0], near.at[1, top], send, recv, 4, dev_y),
            remote(staged.at[1], near.at[0, low], send, recv, 5, dev_x),
        ]
        first[0].wait_recv()
        staged[0] = (x_ref[chip_y, top].astype(F32) + diagonal[0].astype(F32)).astype(BF16)
        second[0].start()
        first[1].wait_recv()
        staged[1] = (x_ref[chip_x, low].astype(F32) + diagonal[1].astype(F32)).astype(BF16)
        second[1].start()
        for copy in q_copies:
            copy.wait_recv()
        total = q_mine[depth].astype(F32)
        for i in range(depths - 1):
            total = total + q_far[i].astype(F32)
        qsum_ref[...] = total.astype(BF16)
        osum_ref[...] = jnp.zeros_like(osum_ref)

        @pl.when(distance == 0)
        def _():
            for copy in o_copies:
                copy.wait_recv()
            total = o_mine[...].astype(F32)
            for i in range(depths - 1):
                total = total + o_far[i].astype(F32)
            osum_ref[...] = total.astype(BF16)

        for copy in first[2:] + second:
            copy.wait_recv()
        out_ref[...] = (
            x_ref[chip].astype(F32) + near[0].astype(F32) + near[1].astype(F32)
        )
        for copy in first + second + swaps + q_copies:
            copy.wait_send()
        for i in range(depths - 1):

            @pl.when(distance == i + 1)
            def _(i=i):
                o_copies[i].wait_send()

    q_block, o_block = qkv.shape[2:], out.shape[1:]
    dma = pltpu.SemaphoreType.DMA
    return pl.pallas_call(
        kernel,
        out_shape=[
            jax.ShapeDtypeStruct((rows, width), F32),
            jax.ShapeDtypeStruct(q_block, BF16),
            jax.ShapeDtypeStruct(o_block, BF16),
        ],
        in_specs=[VM] * 3,
        out_specs=[VM] * 3,
        scratch_shapes=[
            pltpu.VMEM((2, rows, width), BF16),
            pltpu.VMEM((2, half, width), BF16),
            pltpu.VMEM((2, half, width), BF16),
            pltpu.VMEM((depths,) + q_block, BF16),
            pltpu.VMEM((depths,) + q_block, BF16),
            pltpu.VMEM((depths - 1,) + q_block, BF16),
            pltpu.VMEM(o_block, BF16),
            pltpu.VMEM(o_block, BF16),
            pltpu.VMEM((depths - 1,) + o_block, BF16),
            dma((6,)),
            dma((6,)),
            dma((2,)),
            dma((2,)),
            dma((depths - 1,)),
            dma((depths - 1,)),
            dma((depths - 1,)),
            dma((depths - 1,)),
        ],
        compiler_params=comm_params(collective_id),
        name="scatter_and_reduce",
    )(parts, qkv, out)


def finish_gradients(ff, qkv, out, small, collective_id):
    depths = lax.axis_size("wsh")
    half, width = out.shape
    columns = ff.shape[1]
    chip_columns = qkv.shape[1]
    split = columns // depths

    def kernel(
        f_ref, q_ref, o_ref, s_ref,
        dq_ref, dk_ref, dv_ref, do_ref, dg_ref, du_ref, dd_ref, small_ref,
        f_all, q_all, o_all, arrived, count, counted,
        fsend, frecv, qsend, qrecv, osend, orecv, ssend, srecv, bsend, brecv, csend, crecv,
    ):
        depth, chip, core, chip_x, chip_y, chip_d = place_on_mesh()
        dev_x, dev_y = (2 * chip_x + core, depth), (2 * chip_y + core, depth)
        other = (2 * chip + 1 - core, depth)
        across = [
            (2 * chip + core, lax.rem(depth + step, depths)) for step in range(1, depths)
        ]
        signal_and_wait([dev_x, dev_y, other] + across)

        def slot(chip_index):
            return 2 * chip_index + core

        f_copies = ring_sends(
            f_ref, f_all, slot, chip, core, depth, chip_x, chip_y, fsend, frecv
        )
        q_copies = ring_sends(
            q_ref, q_all, slot, chip, core, depth, chip_x, chip_y, qsend, qrecv
        )
        small_copies = [
            remote(s_ref, arrived.at[i], bsend, brecv, i, device) for i, device in enumerate(across)
        ]
        for copy in small_copies + q_copies[:2] + f_copies[:2]:
            copy.start()
        quarter = half // 2
        o_top, o_low = o_all.at[core, pl.ds(0, quarter)], o_all.at[core, pl.ds(quarter, quarter)]
        o_source_top, o_source_low = o_ref.at[pl.ds(0, quarter)], o_ref.at[pl.ds(quarter, quarter)]
        o_copies = [
            remote(o_source_top, o_top, osend, orecv, 0, dev_x),
            remote(o_source_low, o_low, osend, orecv, 1, dev_y),
            remote(o_source_low, o_low, osend, orecv, 2, dev_x),
            remote(o_source_top, o_top, osend, orecv, 3, dev_y),
            remote(o_top, o_top, osend, orecv, 4, dev_y),
            remote(o_low, o_low, osend, orecv, 5, dev_x),
        ]
        source, from_x, from_y = chip == depth, chip_x == depth, chip_y == depth

        @pl.when(source)
        def _():
            for copy in o_copies[:4]:
                copy.start()
            o_all[core] = o_ref[...]

        for copy in q_copies[2:4] + f_copies[2:4]:
            copy.start()
        f_all[slot(chip)] = f_ref[...]
        q_all[slot(chip)] = q_ref[...]

        def shared(index, ref):
            return remote(ref, ref, ssend, srecv, index, other)

        f_shared = [shared(i, f_all.at[slot(c)]) for i, c in enumerate((chip, chip_x, chip_y, chip_d))]
        q_shared = [shared(4 + i, q_all.at[slot(c)]) for i, c in enumerate((chip, chip_x, chip_y, chip_d))]
        o_shared = shared(8, o_all.at[core])
        f_shared[0].start()
        q_shared[0].start()
        for copies in (q_copies, f_copies):
            copies[0].wait_recv()
            copies[4].start()
            copies[1].wait_recv()
            copies[5].start()
        for copy in small_copies:
            copy.wait_recv()
        total = s_ref[...]
        for i in range(depths - 1):
            total = total + arrived[i]
        count[0] = total
        stages = [
            remote(count.at[i], counted.at[i], csend, crecv, i, device)
            for i, device in enumerate((dev_x, dev_y, other))
        ]
        stages[0].start()

        @pl.when(from_x)
        def _():
            o_copies[0].wait_recv()
            o_copies[4].start()
            o_copies[2].wait_recv()

        @pl.when(from_y)
        def _():
            o_copies[1].wait_recv()
            o_copies[5].start()
            o_copies[3].wait_recv()

        @pl.when(chip_d == depth)
        def _():
            o_copies[4].wait_recv()
            o_copies[5].wait_recv()

        o_shared.start()
        for i in range(3):
            stages[i].wait_recv()
            total = total + counted[i]
            if i < 2:
                count[i + 1] = total
                stages[i + 1].start()
        small_ref[...] = total
        for copies, passed in ((q_copies, q_shared), (f_copies, f_shared)):
            copies[2].wait_recv()
            passed[1].start()
            copies[3].wait_recv()
            passed[2].start()
            copies[4].wait_recv()
            copies[5].wait_recv()
            passed[3].start()
        for copy in q_shared + [o_shared] + f_shared:
            copy.wait()
        for copy in f_copies + q_copies + small_copies + stages:
            copy.wait_send()

        @pl.when(source)
        def _():
            for copy in o_copies[:4]:
                copy.wait_send()

        @pl.when(from_x)
        def _():
            o_copies[4].wait_send()

        @pl.when(from_y)
        def _():
            o_copies[5].wait_send()

        for c in range(2):
            rows = slice(c * half, (c + 1) * half)
            do_ref[rows, :] = o_all[c].astype(F32)
            for i, ref in enumerate((dq_ref, dk_ref, dv_ref)):
                ref[rows, :] = jnp.concatenate(
                    [q_all[2 * p + c, i * half : (i + 1) * half, :].astype(F32) for p in range(CHIPS)],
                    axis=1,
                )
            for i, ref in enumerate((dg_ref, du_ref)):
                for z in range(depths):
                    ref[rows, z * CHIPS * split : (z + 1) * CHIPS * split] = jnp.concatenate(
                        [
                            f_all[
                                2 * p + c, i * half : (i + 1) * half, z * split : (z + 1) * split
                            ].astype(F32)
                            for p in range(CHIPS)
                        ],
                        axis=1,
                    )
            for p in range(CHIPS):
                at = (2 * p + c) * half
                dd_ref[at : at + half, :] = f_all[2 * p + c, 2 * half :, :].astype(F32)

    dma = pltpu.SemaphoreType.DMA
    shard = 2 * half
    ctx = lax.axis_size("ctx")
    square = jax.ShapeDtypeStruct((shard, width), F32)
    return pl.pallas_call(
        kernel,
        out_shape=[
            square,
            square,
            square,
            square,
            jax.ShapeDtypeStruct((shard, columns * CHIPS), F32),
            jax.ShapeDtypeStruct((shard, columns * CHIPS), F32),
            jax.ShapeDtypeStruct((ctx * half, width), F32),
            jax.ShapeDtypeStruct(small.shape, F32),
        ],
        in_specs=[VM] * 4,
        out_specs=[VM] * 8,
        scratch_shapes=[
            pltpu.VMEM((ctx,) + ff.shape, BF16),
            pltpu.VMEM((ctx,) + qkv.shape, BF16),
            pltpu.VMEM((2,) + out.shape, BF16),
            pltpu.VMEM((depths - 1,) + small.shape, F32),
            pltpu.VMEM((3,) + small.shape, F32),
            pltpu.VMEM((3,) + small.shape, F32),
            dma((6,)),
            dma((6,)),
            dma((6,)),
            dma((6,)),
            dma((6,)),
            dma((6,)),
            dma((9,)),
            dma((9,)),
            dma((depths - 1,)),
            dma((depths - 1,)),
            dma((3,)),
            dma((3,)),
        ],
        compiler_params=comm_params(collective_id),
        name="finish_gradients",
    )(ff, qkv, out, small)


NT = (((1,), (1,)), ((), ()))
TILE = 256
LOCAL_HEADS = HEADS // CHIPS
CHIP_COLS = LOCAL_HEADS * HD


def head_mask(rows, head):
    lane = lax.broadcasted_iota(jnp.int32, (rows, CHIP_COLS), 1)
    return (lane >= head * HD) & (lane < (head + 1) * HD)


def aligned(index, size):
    return pl.ds(pl.multiple_of(index * size, size), size)


def pair_blocks(slots_ref, pair, per_device):
    core = lax.axis_index("ctx") % 2
    pairs = per_device // 2
    slot = (pair // pairs) * (2 * per_device) + core * per_device + 2 * (pair % pairs)
    one, two = slots_ref[slot], slots_ref[slot + 1]
    second = (one >= PROMPT // BLK).astype(jnp.int32)
    return slot, second, jnp.minimum(one, two), jnp.maximum(one, two)


def tile_tables(kind, step, slots_ref, lengths_ref, per_device):
    lane = lax.broadcasted_iota(jnp.int32, (1, TILE), 1)
    high = jnp.zeros((1, TILE), jnp.int32)
    local = []
    per_tile = TILE // BLK
    for i in range(per_tile):
        pair = step * per_tile + i
        _, second, prompt, cont = pair_blocks(slots_ref, pair, per_device)
        block = prompt if kind == 0 else cont
        local.append(2 * pair + (second if kind == 0 else 1 - second))
        high = jnp.where(lane >= i * BLK, (block - i) * BLK + lane, high)
    low = jnp.zeros((1, TILE), jnp.int32)
    if kind == 1:
        start = PROMPT
        for i in range(lengths_ref.shape[0]):
            low = jnp.where(high >= start, start, low)
            start = start + lengths_ref[i]
    return local, low, high


def attention_forward(all_rows, weights, slots, lengths):
    tokens, width = all_rows.shape
    queries = tokens // 2
    tiles = queries // TILE
    blocks = tokens // BLK
    per_device = blocks // (2 * CHIPS)

    def kernel(
        slots_ref, lengths_ref, x_ref, w_ref,
        att_ref, oT_ref, q_ref, k_ref, v_ref, lse_ref, slot_of, xs, xq, vT, s_ref, p_ref,
    ):
        def place_slot(s, _):
            slot_of[slots_ref[s]] = s
            return 0

        lax.fori_loop(0, blocks, place_slot, 0)
        def gather_block(b, _):
            xs[aligned(b, BLK), :] = x_ref[aligned(slot_of[b], BLK), :]
            return 0

        lax.fori_loop(0, blocks, gather_block, 0)

        def gather_query(pair, _):
            slot, second, _, _ = pair_blocks(slots_ref, pair, per_device)
            xq[aligned(pair, BLK), :] = x_ref[aligned(slot + second, BLK), :]
            xq[aligned(pair + queries // (2 * BLK), BLK), :] = x_ref[
                aligned(slot + 1 - second, BLK), :
            ]
            return 0

        lax.fori_loop(0, queries // (2 * BLK), gather_query, 0)

        def project_keys(i, _):
            rows = aligned(i, TILE)
            x = xs[rows, :]
            k_ref[rows, :] = jnp.dot(x, w_ref[1], preferred_element_type=F32).astype(BF16)
            v = jnp.dot(x, w_ref[2], preferred_element_type=F32).astype(BF16)
            v_ref[rows, :] = v
            vT[:, rows] = v.T
            return 0

        lax.fori_loop(0, tokens // TILE, project_keys, 0)

        def project_queries(i, _):
            rows = aligned(i, TILE)
            q_ref[rows, :] = jnp.dot(xq[rows, :], w_ref[0], preferred_element_type=F32).astype(BF16)
            return 0

        lax.fori_loop(0, tiles, project_queries, 0)

        for kind in range(2):
            key_tiles = (PROMPT if kind == 0 else tokens) // TILE
            first_masked = 0 if kind == 0 else PROMPT // TILE

            def one_tile(step, _):
                tile = kind * (tiles // 2) + step
                q = q_ref[aligned(tile, TILE), :]
                local, q_low, q_high = tile_tables(kind, step, slots_ref, lengths_ref, per_device)
                for head in range(LOCAL_HEADS):
                    q_head = jnp.where(head_mask(TILE, head), q, jnp.zeros_like(q))
                    top = jnp.full((1, TILE), NEGATIVE, F32)
                    for k_tile in range(key_tiles):
                        rows = pl.ds(k_tile * TILE, TILE)
                        s = lax.dot_general(k_ref[rows, :], q_head, NT, preferred_element_type=F32)
                        if k_tile >= first_masked:
                            place = lax.broadcasted_iota(jnp.int32, (TILE, TILE), 0) + k_tile * TILE
                            seen = (place >= q_low) & (place <= q_high)
                            s = jnp.where(seen, s, NEGATIVE)
                        s_ref[rows, :] = s
                        top = jnp.maximum(top, jnp.max(s, axis=0, keepdims=True))
                    total = jnp.zeros((1, TILE), F32)
                    for k_tile in range(key_tiles):
                        rows = pl.ds(k_tile * TILE, TILE)
                        p = jnp.exp(s_ref[rows, :] - top)
                        total = total + jnp.sum(p, axis=0, keepdims=True)
                        p_ref[rows, :] = p.astype(BF16)
                    keys = key_tiles * TILE
                    out = jnp.dot(
                        vT[head * HD : (head + 1) * HD, :keys],
                        p_ref[:keys, :],
                        preferred_element_type=F32,
                    )
                    oT_ref[tile, head * HD : (head + 1) * HD, :] = out / total
                    lse_ref[tile, head] = top + jnp.log(total)
                att = oT_ref[tile].T.astype(BF16)
                for b in range(TILE // BLK):
                    att_ref[aligned(local[b], BLK), :] = att[b * BLK : (b + 1) * BLK]
                return 0

            lax.fori_loop(0, tiles // 2, one_tile, 0)

    return pl.pallas_call(
        kernel,
        out_shape=[
            jax.ShapeDtypeStruct((queries, CHIP_COLS), BF16),
            jax.ShapeDtypeStruct((tiles, CHIP_COLS, TILE), F32),
            jax.ShapeDtypeStruct((queries, CHIP_COLS), BF16),
            jax.ShapeDtypeStruct((tokens, CHIP_COLS), BF16),
            jax.ShapeDtypeStruct((tokens, CHIP_COLS), BF16),
            jax.ShapeDtypeStruct((tiles, LOCAL_HEADS, 1, TILE), F32),
        ],
        in_specs=[SM, SM, VM, VM],
        out_specs=[VM] * 6,
        scratch_shapes=[
            pltpu.SMEM((blocks,), jnp.int32),
            pltpu.VMEM((tokens, width), BF16),
            pltpu.VMEM((queries, width), BF16),
            pltpu.VMEM((CHIP_COLS, tokens), BF16),
            pltpu.VMEM((tokens, TILE), F32),
            pltpu.VMEM((tokens, TILE), BF16),
        ],
        compiler_params=pltpu.CompilerParams(vmem_limit_bytes=VMEM_LIMIT),
        name="attention_forward",
    )(slots, lengths, all_rows, weights)


def attention_backward(hidden_rows, w_out, saved, slots, lengths):
    oT, q, k, v, lse = saved
    queries, width = hidden_rows.shape
    tokens = k.shape[0]
    tiles = queries // TILE
    blocks = tokens // BLK
    per_device = blocks // (2 * CHIPS)
    wide = LOCAL_HEADS * TILE

    def kernel(
        slots_ref, lengths_ref, h_ref, w_ref, oT_ref, q_ref, k_ref, v_ref, lse_ref,
        dq_ref, dk_ref, dv_ref, hq, kT, doT, dqT, q_stack, do_stack, p_buf, ds_buf, dk_acc, dv_acc,
    ):
        def gather_query(pair, _):
            _, second, _, _ = pair_blocks(slots_ref, pair, per_device)
            hq[aligned(pair, BLK), :] = h_ref[aligned(2 * pair + second, BLK), :]
            hq[aligned(pair + queries // (2 * BLK), BLK), :] = h_ref[
                aligned(2 * pair + 1 - second, BLK), :
            ]
            return 0

        lax.fori_loop(0, queries // (2 * BLK), gather_query, 0)

        def transpose_keys(i, _):
            rows = aligned(i, TILE)
            kT[:, rows] = k_ref[rows, :].T
            return 0

        lax.fori_loop(0, tokens // TILE, transpose_keys, 0)

        for kind in (1, 0):
            key_tiles = (PROMPT if kind == 0 else tokens) // TILE
            first_masked = 0 if kind == 0 else PROMPT // TILE

            def one_tile(step, _):
                tile = kind * (tiles // 2) + step
                q_tile = q_ref[aligned(tile, TILE), :]
                local, q_low, q_high = tile_tables(kind, step, slots_ref, lengths_ref, per_device)
                wide_do = lax.dot_general(
                    w_ref[...], hq[aligned(tile, TILE), :], NT, preferred_element_type=F32
                )
                do_tile = wide_do.T.astype(BF16)
                doT[...] = wide_do.astype(BF16).astype(F32) * oT_ref[tile]
                for head in range(LOCAL_HEADS):
                    lanes = pl.ds(head * TILE, TILE)
                    heads = pl.ds(head * HD, HD)
                    mask = head_mask(TILE, head)
                    q_head = jnp.where(mask, q_tile, jnp.zeros_like(q_tile))
                    do_head = jnp.where(mask, do_tile, jnp.zeros_like(do_tile))
                    q_stack[lanes, :] = q_head
                    do_stack[lanes, :] = do_head
                    delta = jnp.sum(doT[heads, :], axis=0, keepdims=True)
                    norm = lse_ref[tile, head]
                    for k_tile in range(key_tiles):
                        rows = pl.ds(k_tile * TILE, TILE)
                        s = lax.dot_general(k_ref[rows, :], q_head, NT, preferred_element_type=F32)
                        dp = lax.dot_general(v_ref[rows, :], do_head, NT, preferred_element_type=F32)
                        p = jnp.exp(s - norm)
                        if k_tile >= first_masked:
                            place = lax.broadcasted_iota(jnp.int32, (TILE, TILE), 0) + k_tile * TILE
                            seen = (place >= q_low) & (place <= q_high)
                            p = jnp.where(seen, p, 0.0)
                        p_buf[rows, lanes] = p.astype(BF16)
                        ds_buf[rows, lanes] = (p * (dp - delta)).astype(BF16)
                    keys = key_tiles * TILE
                    dqT[heads, :] = jnp.dot(
                        kT[heads, :keys], ds_buf[:keys, lanes], preferred_element_type=F32
                    )
                for k_tile in range(key_tiles):
                    rows = pl.ds(k_tile * TILE, TILE)
                    dv = jnp.dot(p_buf[rows, :], do_stack[...], preferred_element_type=F32)
                    dk = jnp.dot(ds_buf[rows, :], q_stack[...], preferred_element_type=F32)
                    if kind == 1:
                        fresh = step == 0
                        dv = dv + jnp.where(fresh, 0.0, dv_acc[rows, :])
                        dk = dk + jnp.where(fresh, 0.0, dk_acc[rows, :])
                    else:
                        dv = dv + dv_acc[rows, :]
                        dk = dk + dk_acc[rows, :]
                    dv_acc[rows, :] = dv
                    dk_acc[rows, :] = dk
                dq = dqT[...].T.astype(BF16)
                for b in range(TILE // BLK):
                    dq_ref[aligned(local[b], BLK), :] = dq[b * BLK : (b + 1) * BLK]
                return 0

            lax.fori_loop(0, tiles // 2, one_tile, 0)

        def give_block(slot, _):
            block = aligned(slots_ref[slot], BLK)
            dk_ref[aligned(slot, BLK), :] = dk_acc[block, :].astype(BF16)
            dv_ref[aligned(slot, BLK), :] = dv_acc[block, :].astype(BF16)
            return 0

        lax.fori_loop(0, blocks, give_block, 0)

    return pl.pallas_call(
        kernel,
        out_shape=[
            jax.ShapeDtypeStruct((queries, CHIP_COLS), BF16),
            jax.ShapeDtypeStruct((tokens, CHIP_COLS), BF16),
            jax.ShapeDtypeStruct((tokens, CHIP_COLS), BF16),
        ],
        in_specs=[SM, SM] + [VM] * 7,
        out_specs=[VM] * 3,
        scratch_shapes=[
            pltpu.VMEM((queries, width), BF16),
            pltpu.VMEM((CHIP_COLS, tokens), BF16),
            pltpu.VMEM((CHIP_COLS, TILE), F32),
            pltpu.VMEM((CHIP_COLS, TILE), F32),
            pltpu.VMEM((wide, CHIP_COLS), BF16),
            pltpu.VMEM((wide, CHIP_COLS), BF16),
            pltpu.VMEM((tokens, wide), BF16),
            pltpu.VMEM((tokens, wide), BF16),
            pltpu.VMEM((tokens, CHIP_COLS), F32),
            pltpu.VMEM((tokens, CHIP_COLS), F32),
        ],
        compiler_params=pltpu.CompilerParams(vmem_limit_bytes=VMEM_LIMIT),
        name="attention_backward",
    )(slots, lengths, hidden_rows, w_out, oT, q, k, v, lse)


def plane_shards(
    states, block_slot, cont_lengths, valid_mask, teacher, out_grad, predict, correct,
    norm_attn, w_query, w_key, w_value, w_out, norm_ffn, w_gate, w_up, w_down,
):
    depths = lax.axis_size("wsh")
    ctx, depth = lax.axis_index("ctx"), lax.axis_index("wsh")
    chip, core = ctx // 2, ctx % 2
    _, rows, _, width = states.shape
    shard = w_query.shape[0]
    half = shard // 2
    hidden_cols = w_gate.shape[1] // CHIPS
    group_len = block_slot.shape[1] * BLK
    slots, lengths = block_slot[0], cont_lengths[0]

    def columns(weight):
        return lax.dynamic_slice(weight, (core * half, chip * CHIP_COLS), (half, CHIP_COLS))

    qkv_piece = jnp.stack([columns(w) for w in (w_query, w_key, w_value)])
    out_half = lax.dynamic_slice_in_dim(w_out, core * half, half, 0)
    ff_split = hidden_cols // depths

    def ff_columns(weight):
        piece = lax.dynamic_slice_in_dim(weight, core * half, half, 0)
        piece = piece.reshape(half, depths, CHIPS, ff_split)
        return lax.dynamic_index_in_dim(piece, chip, 2, keepdims=False).reshape(half, hidden_cols)

    down_rows = lax.dynamic_slice_in_dim(w_down, chip * ff_split + core * (ff_split // 2), ff_split // 2, 0)
    ff_piece = lax.all_gather(
        jnp.concatenate([ff_columns(w_gate), ff_columns(w_up), down_rows], axis=0),
        "wsh", axis=0, tiled=True,
    ).reshape(depths, 3, half, hidden_cols)
    valid_float = valid_mask.astype(F32)
    count = jnp.sum(valid_float)

    def own_columns(gain):
        return lax.dynamic_update_slice_in_dim(jnp.zeros((width,), F32), gain.astype(F32), depth * shard, 0)

    small = jnp.concatenate(
        [
            own_columns(norm_attn)[None],
            own_columns(norm_ffn)[None],
            jnp.full((1, width), count, F32),
            jnp.zeros((5, width), F32),
        ]
    )

    inputs = states[0].astype(F32)
    mixed = [predict[i, 0] * inputs[:, 0] + predict[i, 1] * inputs[:, 1] for i in range(2)]
    active = mixed[0]
    factor_one = lax.rsqrt(jnp.mean(active * active, axis=-1, keepdims=True) + EPSILON)
    all_rows, qkv, out_w, small = gather_inputs(active * factor_one, small, qkv_piece, out_half, 1)
    gain_one, gain_two, valid_total = small[0], small[1], small[2, 0]
    all_rows = all_rows.reshape(-1, width)
    qkv = qkv.reshape(3, width, CHIP_COLS)
    out_w = out_w.reshape(CHIP_COLS, width)
    attended, *saved = attention_forward(all_rows, qkv, slots, lengths)
    part = jnp.dot(attended, out_w, preferred_element_type=F32).astype(BF16)
    hidden = active + scatter_plane(part.reshape(CHIPS, rows, width), 2)
    normed_two, factor_two = rms_forward(hidden, gain_two)

    gate_w, up_w, down_w = share_weights(ff_piece, 3).reshape(3, -1, hidden_cols)
    two_rows = gather_plane(normed_two.astype(BF16), 4).reshape(-1, width)
    gate = jnp.dot(two_rows, gate_w, preferred_element_type=F32)
    up = jnp.dot(two_rows, up_w, preferred_element_type=F32)
    inner, inner_pull = jax.vjp(
        lambda gate_in, up_in: jax.nn.gelu(gate_in, approximate=True) * up_in, gate, up
    )
    inner = inner.astype(BF16)
    part = jnp.dot(inner, down_w, preferred_element_type=F32).astype(BF16)
    result = hidden + scatter_plane(part.reshape(CHIPS, rows, width), 5)

    difference = result - active
    weight = (depths * group_len / valid_total) * valid_float[0][:, None]
    outs = [mixed[i] + correct[i] * difference for i in range(2)]
    upstream = [
        out_grad[0, :, i].astype(F32) + weight * (outs[i] - teacher[0, :, i].astype(F32)) for i in range(2)
    ]
    correct_local = [jnp.sum(upstream[i] * difference) for i in range(2)]
    result_grad = correct[0] * upstream[0] + correct[1] * upstream[1]

    grad_rows = gather_plane(result_grad.astype(BF16), 6).reshape(-1, width)
    inner_grad = lax.dot_general(grad_rows, down_w, NT, preferred_element_type=F32)
    gate_grad, up_grad = inner_pull(inner_grad)
    gate_grad, up_grad = gate_grad.astype(BF16), up_grad.astype(BF16)
    part = lax.dot_general(gate_grad, gate_w, NT, preferred_element_type=F32) + lax.dot_general(
        up_grad, up_w, NT, preferred_element_type=F32
    )
    normed_two_grad = scatter_plane(part.astype(BF16).reshape(CHIPS, rows, width), 7)

    def outer(left, right):
        return lax.dot_general(
            left, right, (((0,), (0,)), ((), ())), preferred_element_type=F32
        ).astype(BF16)

    gate_w_grad = outer(two_rows, gate_grad)
    up_w_grad = outer(two_rows, up_grad)
    down_w_grad = outer(inner, grad_rows)
    ff_grads = [g.reshape(depths, 2, half, hidden_cols) for g in (gate_w_grad, up_w_grad, down_w_grad)]
    ff_swapped = swap_cores(ff_grads, 8)

    def own_half(grad):
        return lax.dynamic_index_in_dim(grad, core, 1, keepdims=False)

    ff_sum = jnp.concatenate(
        [own_half(g).astype(F32) + s.astype(F32) for g, s in zip(ff_grads, ff_swapped)], axis=1
    ).astype(BF16)
    ff_sum = lax.psum_scatter(
        ff_sum.reshape(depths * 3 * half, hidden_cols), "wsh", scatter_dimension=0, tiled=True
    )

    hidden_norm_grad, gain_two_grad = rms_backward(hidden, factor_two, gain_two, normed_two_grad)
    hidden_grad = result_grad + hidden_norm_grad
    hidden_rows = gather_plane(hidden_grad.astype(BF16), 9).reshape(-1, width)
    out_w_part = outer(attended, hidden_rows)
    dq, dk, dv = attention_backward(hidden_rows, out_w, saved, slots, lengths)
    by_core = [g.reshape(CHIPS, 2, rows, CHIP_COLS) for g in (dk, dv)]
    swapped = swap_cores(by_core, 10)
    dk, dv = (
        (own_half(g).astype(F32) + s.astype(F32)).astype(BF16).reshape(-1, CHIP_COLS)
        for g, s in zip(by_core, swapped)
    )
    part = (
        lax.dot_general(dq, qkv[0], NT, preferred_element_type=F32)
        + lax.dot_general(dk, qkv[1], NT, preferred_element_type=F32)
        + lax.dot_general(dv, qkv[2], NT, preferred_element_type=F32)
    )
    own_rows = lax.dynamic_index_in_dim(
        all_rows.reshape(CHIPS, 2, rows, width), core, 1, keepdims=False
    ).reshape(-1, width)
    qkv_grads = jnp.concatenate(
        [outer(own_rows, g).reshape(depths, 2, half, CHIP_COLS) for g in (dq, dk, dv)], axis=2
    )
    normed_grad, qkv_sum, out_sum = scatter_and_reduce(
        part.astype(BF16).reshape(CHIPS, rows, width), qkv_grads, out_w_part.reshape(2, half, width), 11
    )

    active_norm_grad, gain_one_grad = rms_backward(active, factor_one, gain_one, normed_grad)
    active_grad = hidden_grad + active_norm_grad - result_grad
    mixed_grad = [upstream[0] + active_grad, upstream[1]]
    predict_local = [jnp.sum(mixed_grad[i] * inputs[:, j]) for i in range(2) for j in range(2)]
    states_grad = jnp.stack(
        [predict[0, j] * mixed_grad[0] + predict[1, j] * mixed_grad[1] for j in range(2)], axis=1
    ).astype(BF16)
    scalars = jnp.stack(predict_local + correct_local)
    small = jnp.concatenate(
        [
            gain_one_grad[None],
            gain_two_grad[None],
            jnp.pad(scalars, (0, width - scalars.shape[0]))[None],
            jnp.zeros((5, width), F32),
        ]
    )
    query_grad, key_grad, value_grad, out_w_grad, gate_out, up_out, down_out, small = finish_gradients(
        ff_sum, qkv_sum, out_sum, small, 12
    )

    def own_gain(grad):
        return lax.dynamic_slice_in_dim(grad, depth * shard, shard, 0)

    return (
        jnp.stack(outs, axis=1).astype(BF16)[None],
        states_grad[None],
        small[2, 0:4].reshape(2, 2),
        small[2, 4:6],
        own_gain(small[0]),
        query_grad,
        key_grad,
        value_grad,
        out_w_grad,
        own_gain(small[1]),
        gate_out,
        up_out,
        down_out,
    )


def fits_plane(mesh, states, block_slot, w_query, w_gate):
    ctx, depths = mesh.shape["ctx"], mesh.shape["wsh"]
    return (
        ctx == 2 * CHIPS
        and depths == CHIPS
        and states.shape[0] == depths
        and block_slot.shape[1] * BLK == 2 * PROMPT
        and states.shape[1] == 2 * PROMPT
        and w_query.shape[0] % (32 * depths) == 0
        and w_gate.shape[1] % (32 * CHIPS * depths) == 0
    )


def solution(mesh):
    in_specs = (
        P("wsh", "ctx", None, None),
        P("wsh", None),
        P("wsh", None),
        P("wsh", "ctx"),
        P("wsh", "ctx", None, None),
        P("wsh", "ctx", None, None),
        P(),
        P(),
        P("wsh"),
        P("wsh", None),
        P("wsh", None),
        P("wsh", None),
        P("wsh", None),
        P("wsh"),
        P("wsh", None),
        P("wsh", None),
        P("wsh", None),
    )
    out_specs = (
        P("wsh", "ctx", None, None),
        P("wsh", "ctx", None, None),
        P(),
        P(),
        P("wsh"),
        P("wsh", None),
        P("wsh", None),
        P("wsh", None),
        P("wsh", None),
        P("wsh"),
        P("wsh", None),
        P("wsh", None),
        P("wsh", None),
    )

    def step(*args):
        plane = fits_plane(mesh, args[0], args[1], args[9], args[14])
        body = plane_shards if plane else general_shards
        return jax.shard_map(
            body, mesh=mesh, in_specs=in_specs, out_specs=out_specs, check_vma=False
        )(*args)

    return step
```

```python
import functools
import math

import jax
import jax.numpy as jnp
from jax import lax
from jax.experimental import pallas as pl
from jax.experimental.pallas import tpu as pltpu
from jax.sharding import PartitionSpec as P

HEADS = 12
HD = 64
PROMPT = 1024
BLK = 64


EPSILON = 1e-06
NEGATIVE = -1e30
HIGHEST = lax.Precision.HIGHEST


def rms_forward(tensor, gain_vec):
    factor = lax.rsqrt(jnp.mean(tensor * tensor, axis=-1, keepdims=True) + EPSILON)
    return (tensor * factor * gain_vec, factor)


def rms_backward(tensor, factor, gain_vec, upstream):
    weighted = upstream * gain_vec
    gain_grad = jnp.sum(upstream * tensor * factor, axis=0)
    middle = jnp.mean(weighted * tensor, axis=-1, keepdims=True)
    return (factor * weighted - tensor * factor * factor * factor * middle, gain_grad)


def segment_starts(cont_lengths):
    count = cont_lengths.shape[1]
    index = jnp.arange(count, dtype=jnp.int32)
    before = index[:, None] < index[None, :]
    return PROMPT + jnp.sum(jnp.where(before[None], cont_lengths[:, :, None], 0), axis=1)


def token_places(block_slot, cont_lengths):
    groups, blocks = block_slot.shape
    offsets = jnp.arange(BLK, dtype=jnp.int32)
    places = (block_slot[:, :, None] * BLK + offsets[None, None, :]).reshape(groups, blocks * BLK)
    starts = segment_starts(cont_lengths)
    segments = jnp.sum((places[:, :, None] >= starts[:, None, :]).astype(jnp.int32), axis=2)
    return (places, segments)


def visible(query_place, query_segment, key_place, key_segment):
    earlier = key_place[:, None, :] <= query_place[:, :, None]
    shared = (key_segment[:, None, :] == 0) | (key_segment[:, None, :] == query_segment[:, :, None])
    return earlier & shared


def split_heads(tensor):
    return tensor.reshape(tensor.shape[0], tensor.shape[1], HEADS, HD)


def forward_block(running, query_part, key_part, value_part, allowed):

    def forward_compute(current):
        maximum, denominator, accumulated = current
        scores = jnp.einsum(
            "gqhd,gkhd->ghqk",
            split_heads(query_part),
            split_heads(key_part),
            preferred_element_type=jnp.float32,
        )
        masked = jnp.where(allowed[:, None], scores, NEGATIVE)
        new_max = jnp.maximum(maximum, jnp.max(masked, axis=-1))
        exponent = jnp.where(allowed[:, None], jnp.exp(masked - new_max[..., None]), 0.0)
        factor = jnp.exp(maximum - new_max)
        rescale = jnp.swapaxes(factor, 1, 2)[..., None]
        update = jnp.einsum(
            "ghqk,gkhd->gqhd",
            exponent.astype(jnp.bfloat16),
            split_heads(value_part),
            preferred_element_type=jnp.float32,
        )
        merged = (split_heads(accumulated) * rescale + update).reshape(accumulated.shape)
        return (new_max, denominator * factor + jnp.sum(exponent, axis=-1), merged)

    return lax.cond(jnp.any(allowed), forward_compute, lambda current: current, running)


def backward_block(
    query_part, grad_part, key_part, value_part, allowed, maximum, denominator, delta_sum
):
    scores = jnp.einsum(
        "gqhd,gkhd->ghqk",
        split_heads(query_part),
        split_heads(key_part),
        preferred_element_type=jnp.float32,
    )
    exponent = jnp.where(allowed[:, None], jnp.exp(scores - maximum[..., None]), 0.0)
    probability = exponent / denominator[..., None]
    prob_grad = jnp.einsum(
        "gqhd,gkhd->ghqk",
        split_heads(grad_part),
        split_heads(value_part),
        preferred_element_type=jnp.float32,
    )
    score_grad = (probability * (prob_grad - delta_sum[..., None])).astype(jnp.bfloat16)
    return (probability.astype(jnp.bfloat16), score_grad)


def general_shards(
    states,
    block_slot,
    cont_lengths,
    valid_mask,
    teacher,
    out_grad,
    predict,
    correct,
    norm_attn,
    w_query,
    w_key,
    w_value,
    w_out,
    norm_ffn,
    w_gate,
    w_up,
    w_down,
):
    groups, local_len = valid_mask.shape
    model_width = states.shape[3]
    row_count = groups * local_len
    group_len = block_slot.shape[1] * BLK
    gain_one, query_w, key_w, value_w, out_w, gain_two, gate_w, up_w, down_w = (
        lax.all_gather(norm_attn, "wsh", axis=0, tiled=True),
        lax.all_gather(w_query, "wsh", axis=0, tiled=True),
        lax.all_gather(w_key, "wsh", axis=0, tiled=True),
        lax.all_gather(w_value, "wsh", axis=0, tiled=True),
        lax.all_gather(w_out, "wsh", axis=0, tiled=True),
        lax.all_gather(norm_ffn, "wsh", axis=0, tiled=True),
        lax.all_gather(w_gate, "wsh", axis=0, tiled=True),
        lax.all_gather(w_up, "wsh", axis=0, tiled=True),
        lax.all_gather(w_down, "wsh", axis=0, tiled=True),
    )
    valid_float = valid_mask.astype(jnp.float32)
    valid_total = lax.psum(jnp.sum(valid_float), ("ctx", "wsh"))
    places, segments = token_places(block_slot, cont_lengths)
    offset = lax.axis_index("ctx") * local_len
    own_place = lax.dynamic_slice_in_dim(places, offset, local_len, 1)
    own_segment = lax.dynamic_slice_in_dim(segments, offset, local_len, 1)
    inputs = states.astype(jnp.float32)
    mixed_states = jnp.einsum("ij,gtjd->gtid", predict, inputs, precision=HIGHEST)
    active = mixed_states[:, :, 0].reshape(row_count, model_width)
    gain_first = gain_one.astype(jnp.float32)
    normed, factor_one = rms_forward(active, gain_first)
    normed_low = normed.astype(jnp.bfloat16)
    queries = (
        jnp.dot(normed_low, query_w, preferred_element_type=jnp.float32)
        .astype(jnp.bfloat16)
        .reshape(groups, local_len, model_width)
    )
    key_rows = (
        jnp.dot(normed_low, key_w, preferred_element_type=jnp.float32)
        .astype(jnp.bfloat16)
        .reshape(groups, local_len, model_width)
    )
    values = (
        jnp.dot(normed_low, value_w, preferred_element_type=jnp.float32)
        .astype(jnp.bfloat16)
        .reshape(groups, local_len, model_width)
    )
    initial = (
        jnp.full((groups, HEADS, local_len), NEGATIVE, jnp.float32),
        jnp.zeros((groups, HEADS, local_len), jnp.float32),
        jnp.zeros((groups, local_len, model_width), jnp.float32),
    )
    piece_keys = lax.all_gather(key_rows, "ctx", axis=1, tiled=True)
    piece_values = lax.all_gather(values, "ctx", axis=1, tiled=True)
    piece_len = piece_keys.shape[1]
    block_size = math.gcd(piece_len, local_len)

    def fold_one_block(current, block_index):
        begin = block_index * block_size
        key_part = lax.dynamic_slice_in_dim(piece_keys, begin, block_size, 1)
        value_part = lax.dynamic_slice_in_dim(piece_values, begin, block_size, 1)
        key_place = lax.dynamic_slice_in_dim(places, begin, block_size, 1)
        key_segment = lax.dynamic_slice_in_dim(segments, begin, block_size, 1)
        allowed = visible(own_place, own_segment, key_place, key_segment)
        return (forward_block(current, queries, key_part, value_part, allowed), None)

    finished, unused = lax.scan(
        fold_one_block, initial, jnp.arange(piece_len // block_size, dtype=jnp.int32)
    )
    maximum, denominator, accumulated = finished
    attended = (split_heads(accumulated) / jnp.swapaxes(denominator, 1, 2)[..., None]).reshape(
        row_count, model_width
    )
    attended_low = attended.astype(jnp.bfloat16)
    hidden = active + jnp.dot(attended_low, out_w, preferred_element_type=jnp.float32)
    gain_second = gain_two.astype(jnp.float32)
    normed_two, factor_two = rms_forward(hidden, gain_second)
    normed_two_low = normed_two.astype(jnp.bfloat16)
    gate_proj = jnp.dot(normed_two_low, gate_w, preferred_element_type=jnp.float32)
    up_proj = jnp.dot(normed_two_low, up_w, preferred_element_type=jnp.float32)
    inner_act, inner_pull = jax.vjp(
        lambda gate_in, up_in: jax.nn.gelu(gate_in, approximate=True) * up_in, gate_proj, up_proj
    )
    inner_low = inner_act.astype(jnp.bfloat16)
    result = hidden + jnp.dot(inner_low, down_w, preferred_element_type=jnp.float32)
    difference = (result - active).reshape(groups, local_len, 1, model_width)
    out_states = mixed_states + correct[None, None, :, None] * difference
    new_states = out_states.astype(jnp.bfloat16)
    loss_ratio = lax.axis_size("wsh") * groups * group_len / valid_total
    upstream = out_grad.astype(jnp.float32) + loss_ratio * valid_float[:, :, None, None] * (
        out_states - teacher.astype(jnp.float32)
    )
    correct_local = jnp.sum(upstream * difference, axis=(0, 1, 3))
    result_grad = jnp.einsum("i,gtid->gtd", correct, upstream, precision=HIGHEST).reshape(
        row_count, model_width
    )
    result_low = result_grad.astype(jnp.bfloat16)
    down_grad = jnp.einsum("rf,rd->fd", inner_low, result_low, preferred_element_type=jnp.float32)
    inner_grad = jnp.einsum("rd,fd->rf", result_low, down_w, preferred_element_type=jnp.float32)
    gate_grad, up_grad = inner_pull(inner_grad)
    gate_low = gate_grad.astype(jnp.bfloat16)
    up_low = up_grad.astype(jnp.bfloat16)
    gate_w_grad = jnp.einsum(
        "rd,rf->df", normed_two_low, gate_low, preferred_element_type=jnp.float32
    )
    up_w_grad = jnp.einsum("rd,rf->df", normed_two_low, up_low, preferred_element_type=jnp.float32)
    normed_two_grad = jnp.einsum(
        "rf,df->rd", gate_low, gate_w, preferred_element_type=jnp.float32
    ) + jnp.einsum("rf,df->rd", up_low, up_w, preferred_element_type=jnp.float32)
    hidden_norm_grad, gain_two_grad = rms_backward(hidden, factor_two, gain_second, normed_two_grad)
    hidden_grad = result_grad + hidden_norm_grad
    hidden_low = hidden_grad.astype(jnp.bfloat16)
    out_w_grad = jnp.einsum(
        "rc,rd->cd", attended_low, hidden_low, preferred_element_type=jnp.float32
    )
    attended_grad = jnp.einsum(
        "rd,cd->rc", hidden_low, out_w, preferred_element_type=jnp.float32
    ).astype(jnp.bfloat16)
    delta_sum = jnp.swapaxes(
        jnp.sum(
            split_heads(
                (attended_grad.astype(jnp.float32) * attended).reshape(
                    groups, local_len, model_width
                )
            ),
            axis=-1,
        ),
        1,
        2,
    )
    grad_local = attended_grad.reshape(groups, local_len, model_width)
    zero_grad = jnp.zeros((groups, local_len, model_width), jnp.float32)
    all_keys, all_values = (
        lax.all_gather(key_rows, "ctx", axis=1, tiled=True),
        lax.all_gather(values, "ctx", axis=1, tiled=True),
    )

    def query_step(current, block_index):
        begin = block_index * local_len
        key_part = lax.dynamic_slice_in_dim(all_keys, begin, local_len, 1)
        value_part = lax.dynamic_slice_in_dim(all_values, begin, local_len, 1)
        key_place = lax.dynamic_slice_in_dim(places, begin, local_len, 1)
        key_segment = lax.dynamic_slice_in_dim(segments, begin, local_len, 1)
        allowed = visible(own_place, own_segment, key_place, key_segment)

        def query_compute(query_sum):
            prob_low, score_grad = backward_block(
                queries, grad_local, key_part, value_part, allowed, maximum, denominator, delta_sum
            )
            return query_sum + jnp.einsum(
                "ghqk,gkhd->gqhd",
                score_grad,
                split_heads(key_part),
                preferred_element_type=jnp.float32,
            ).reshape(groups, local_len, model_width)

        return (
            lax.cond(jnp.any(allowed), query_compute, lambda query_sum: query_sum, current),
            None,
        )

    finished, unused = lax.scan(
        query_step, zero_grad, jnp.arange(group_len // local_len, dtype=jnp.int32)
    )
    term_rows = local_len * lax.axis_size("ctx")
    key_block_size = math.gcd(term_rows, local_len)

    def key_one_block(block_index):
        begin = block_index * key_block_size
        key_part = lax.dynamic_slice_in_dim(all_keys, begin, key_block_size, 1)
        value_part = lax.dynamic_slice_in_dim(all_values, begin, key_block_size, 1)
        key_place = lax.dynamic_slice_in_dim(places, begin, key_block_size, 1)
        key_segment = lax.dynamic_slice_in_dim(segments, begin, key_block_size, 1)
        allowed = visible(own_place, own_segment, key_place, key_segment)

        def one_compute(unused_arg):
            prob_low, score_grad = backward_block(
                queries, grad_local, key_part, value_part, allowed, maximum, denominator, delta_sum
            )
            key_add = jnp.einsum(
                "ghqk,gqhd->kghd",
                score_grad,
                split_heads(queries),
                preferred_element_type=jnp.float32,
            ).reshape(key_block_size, groups, model_width)
            value_add = jnp.einsum(
                "ghqk,gqhd->kghd",
                prob_low,
                split_heads(grad_local),
                preferred_element_type=jnp.float32,
            ).reshape(key_block_size, groups, model_width)
            return jnp.stack([key_add, value_add], axis=1)

        return lax.cond(
            jnp.any(allowed),
            one_compute,
            lambda unused_arg: jnp.zeros((key_block_size, 2, groups, model_width), jnp.float32),
            0,
        )

    summed = lax.psum_scatter(
        lax.map(key_one_block, jnp.arange(term_rows // key_block_size, dtype=jnp.int32))
        .reshape(term_rows, 2, groups, model_width)
        .astype(jnp.bfloat16),
        "ctx",
        scatter_dimension=0,
        tiled=True,
    ).astype(jnp.float32)
    key_grad = jnp.swapaxes(summed[:, 0], 0, 1)
    value_grad = jnp.swapaxes(summed[:, 1], 0, 1)
    query_low = finished.reshape(row_count, model_width).astype(jnp.bfloat16)
    key_low = key_grad.reshape(row_count, model_width).astype(jnp.bfloat16)
    value_low = value_grad.reshape(row_count, model_width).astype(jnp.bfloat16)
    query_w_grad = jnp.einsum(
        "rc,rd->cd", normed_low, query_low, preferred_element_type=jnp.float32
    )
    key_w_grad = jnp.einsum("rc,rd->cd", normed_low, key_low, preferred_element_type=jnp.float32)
    value_w_grad = jnp.einsum(
        "rc,rd->cd", normed_low, value_low, preferred_element_type=jnp.float32
    )
    normed_grad = (
        jnp.einsum("rd,cd->rc", query_low, query_w, preferred_element_type=jnp.float32)
        + jnp.einsum("rd,cd->rc", key_low, key_w, preferred_element_type=jnp.float32)
        + jnp.einsum("rd,cd->rc", value_low, value_w, preferred_element_type=jnp.float32)
    )
    active_norm_grad, gain_one_grad = rms_backward(active, factor_one, gain_first, normed_grad)
    active_grad = (hidden_grad + active_norm_grad - result_grad).reshape(
        groups, local_len, 1, model_width
    )
    mixed_grad = jnp.concatenate([upstream[:, :, :1] + active_grad, upstream[:, :, 1:]], axis=2)
    predict_local = jnp.einsum("gtid,gtjd->ij", mixed_grad, inputs, precision=HIGHEST)
    states_grad = jnp.einsum("ij,gtid->gtjd", predict, mixed_grad, precision=HIGHEST).astype(
        jnp.bfloat16
    )
    predict_grad, correct_grad = lax.psum((predict_local, correct_local), ("ctx", "wsh"))
    (
        gain_one_rows,
        query_rows,
        key_grad_rows,
        value_rows,
        out_rows,
        gain_two_rows,
        gate_rows,
        up_rows,
        down_rows,
    ) = (
        lax.psum_scatter(
            gain_one_grad.astype(jnp.bfloat16), "wsh", scatter_dimension=0, tiled=True
        ).astype(jnp.float32),
        lax.psum_scatter(
            query_w_grad.astype(jnp.bfloat16), "wsh", scatter_dimension=0, tiled=True
        ).astype(jnp.float32),
        lax.psum_scatter(
            key_w_grad.astype(jnp.bfloat16), "wsh", scatter_dimension=0, tiled=True
        ).astype(jnp.float32),
        lax.psum_scatter(
            value_w_grad.astype(jnp.bfloat16), "wsh", scatter_dimension=0, tiled=True
        ).astype(jnp.float32),
        lax.psum_scatter(
            out_w_grad.astype(jnp.bfloat16), "wsh", scatter_dimension=0, tiled=True
        ).astype(jnp.float32),
        lax.psum_scatter(
            gain_two_grad.astype(jnp.bfloat16), "wsh", scatter_dimension=0, tiled=True
        ).astype(jnp.float32),
        lax.psum_scatter(
            gate_w_grad.astype(jnp.bfloat16), "wsh", scatter_dimension=0, tiled=True
        ).astype(jnp.float32),
        lax.psum_scatter(
            up_w_grad.astype(jnp.bfloat16), "wsh", scatter_dimension=0, tiled=True
        ).astype(jnp.float32),
        lax.psum_scatter(
            down_grad.astype(jnp.bfloat16), "wsh", scatter_dimension=0, tiled=True
        ).astype(jnp.float32),
    )
    totals = (
        lax.psum(gain_one_rows.astype(jnp.bfloat16), "ctx").astype(jnp.float32),
        lax.psum(query_rows.astype(jnp.bfloat16), "ctx").astype(jnp.float32),
        lax.psum(key_grad_rows.astype(jnp.bfloat16), "ctx").astype(jnp.float32),
        lax.psum(value_rows.astype(jnp.bfloat16), "ctx").astype(jnp.float32),
        lax.psum(out_rows.astype(jnp.bfloat16), "ctx").astype(jnp.float32),
        lax.psum(gain_two_rows.astype(jnp.bfloat16), "ctx").astype(jnp.float32),
        lax.psum(gate_rows.astype(jnp.bfloat16), "ctx").astype(jnp.float32),
        lax.psum(up_rows.astype(jnp.bfloat16), "ctx").astype(jnp.float32),
        lax.psum(down_rows.astype(jnp.bfloat16), "ctx").astype(jnp.float32),
    )
    return (new_states, states_grad, predict_grad, correct_grad) + tuple(totals)


MESH = pl.DeviceIdType.MESH
F32 = jnp.float32
BF16 = jnp.bfloat16
CHIPS = 4
VMEM_LIMIT = 60 * 2**20


def place_on_mesh():
    ctx = lax.axis_index("ctx")
    depth = lax.axis_index("wsh")
    chip = ctx // 2
    core = ctx % 2
    chip_x = chip + 1 - 2 * (chip % 2)
    chip_y = chip + 2 - 4 * (chip // 2)
    return depth, chip, core, chip_x, chip_y, 3 - chip


def signal_and_wait(devices):
    barrier = pltpu.get_barrier_semaphore()
    for device in devices:
        pl.semaphore_signal(barrier, inc=1, device_id=device, device_id_type=MESH)
    pl.semaphore_wait(barrier, len(devices))


def remote(src, dst, send, recv, index, device):
    return pltpu.make_async_remote_copy(
        src_ref=src,
        dst_ref=dst,
        send_sem=send.at[index],
        recv_sem=recv.at[index],
        device_id=device,
        device_id_type=MESH,
    )


def comm_params(collective_id):
    return pltpu.CompilerParams(
        collective_id=collective_id, has_side_effects=True, vmem_limit_bytes=VMEM_LIMIT
    )


ANY = pl.BlockSpec(memory_space=pl.ANY)
VM = pl.BlockSpec(memory_space=pltpu.VMEM)
SM = pl.BlockSpec(memory_space=pltpu.SMEM)


def ring_sends(own, out, slot_of, chip, core, depth, chip_x, chip_y, send, recv):
    half = own.shape[0] // 2
    top, low = pl.ds(0, half), pl.ds(half, half)
    dev_x, dev_y = (2 * chip_x + core, depth), (2 * chip_y + core, depth)
    here = slot_of(chip)
    return [
        remote(own.at[top], out.at[here, top], send, recv, 0, dev_x),
        remote(own.at[low], out.at[here, low], send, recv, 1, dev_y),
        remote(own.at[low], out.at[here, low], send, recv, 2, dev_x),
        remote(own.at[top], out.at[here, top], send, recv, 3, dev_y),
        remote(out.at[slot_of(chip_x), top], out.at[slot_of(chip_x), top], send, recv, 4, dev_y),
        remote(out.at[slot_of(chip_y), low], out.at[slot_of(chip_y), low], send, recv, 5, dev_x),
    ]


def swap_cores(arrays, collective_id):
    count = len(arrays)

    def kernel(*refs):
        ins, outs, (send, recv) = refs[:count], refs[count : 2 * count], refs[2 * count :]
        depth, chip, core, _, _, _ = place_on_mesh()
        other = (2 * chip + 1 - core, depth)
        signal_and_wait([other])
        copies = [
            remote(ins[i].at[:, 1 - core], outs[i], send, recv, i, other) for i in range(count)
        ]
        for copy in copies:
            copy.start()
        for copy in copies:
            copy.wait()

    return pl.pallas_call(
        kernel,
        out_shape=[jax.ShapeDtypeStruct(a.shape[:1] + a.shape[2:], a.dtype) for a in arrays],
        in_specs=[ANY] * count,
        out_specs=[ANY] * count,
        scratch_shapes=[pltpu.SemaphoreType.DMA((count,))] * 2,
        compiler_params=comm_params(collective_id),
        name="swap_cores",
    )(*arrays)


def line_relay(ref, chip, depth, depths, send, recv, send_base):
    _, _, core, _, _, _ = place_on_mesh()
    up = remote(ref, ref, send, recv, send_base, (2 * chip + core, lax.rem(depth + 1, depths)))
    down = remote(
        ref, ref, send, recv, send_base + 1, (2 * chip + core, lax.rem(depth + depths - 1, depths))
    )
    goes_up = (depth >= chip) & (depth < depths - 1)
    goes_down = (depth <= chip) & (depth > 0)

    def start():
        @pl.when(goes_up)
        def _():
            up.start()

        @pl.when(goes_down)
        def _():
            down.start()

    def receive():
        @pl.when(depth > chip)
        def _():
            up.wait_recv()

        @pl.when(depth < chip)
        def _():
            down.wait_recv()

    def finish():
        @pl.when(goes_up)
        def _():
            up.wait_send()

        @pl.when(goes_down)
        def _():
            down.wait_send()

    return start, receive, finish


def gather_inputs(pre, small, weights, out_half, collective_id):
    depths = lax.axis_size("wsh")

    def kernel(
        pre_ref, small_ref, w_ref, o_ref, out_ref, wall_ref, oall_ref, sum_ref,
        own, arrived, count, counted,
        send, recv, wsend, wrecv, ssend, srecv, bsend, brecv, csend, crecv, osend, orecv, local,
    ):
        depth, chip, core, chip_x, chip_y, chip_d = place_on_mesh()
        dev_x, dev_y = (2 * chip_x + core, depth), (2 * chip_y + core, depth)
        other = (2 * chip + 1 - core, depth)
        across = [
            (2 * chip + core, lax.rem(depth + step, depths)) for step in range(1, depths)
        ]
        signal_and_wait([dev_x, dev_y, other] + across)

        def slot(chip_index):
            return 2 * chip_index + core

        small_copies = [
            remote(small_ref, arrived.at[i], bsend, brecv, i, device)
            for i, device in enumerate(across)
        ]
        for copy in small_copies:
            copy.start()
        w_copies = [
            remote(w_ref, wall_ref.at[:, depth, core], wsend, wrecv, i, device)
            for i, device in enumerate(across)
        ]
        for copy in w_copies:
            copy.start()
        wall_ref[:, depth, core] = w_ref[...]

        def pass_on(index, slot_index):
            ref = out_ref.at[slot_index]
            return remote(ref, ref, ssend, srecv, index, other)

        def pass_weights(index, depth_index):
            ref = wall_ref.at[:, depth_index, core]
            return remote(ref, ref, ssend, srecv, index, other)

        shared = [
            remote(own, out_ref.at[slot(chip)], ssend, srecv, 0, other),
            pass_on(1, slot(chip_x)),
            pass_on(2, slot(chip_y)),
            pass_on(3, slot(chip_d)),
            remote(w_ref, wall_ref.at[:, depth, core], ssend, srecv, 4, other),
        ] + [
            pass_weights(5 + i, lax.rem(depth + depths - 1 - i, depths))
            for i in range(depths - 1)
        ]
        shared[4].start()

        @pl.when(depth == chip)
        def _():
            oall_ref[core] = o_ref[...]

        relay_start, relay_receive, relay_finish = line_relay(
            oall_ref.at[core], chip, depth, depths, osend, orecv, 0
        )

        @pl.when(depth == chip)
        def _():
            relay_start()

        for copy in small_copies:
            copy.wait_recv()
        total = small_ref[...]
        for i in range(depths - 1):
            total = total + arrived[i]
        own[...] = (pre_ref[...] * total[0:1, :]).astype(BF16)
        copies = ring_sends(
            own, out_ref, slot, chip, core, depth, chip_x, chip_y, send, recv
        )
        for copy in copies[:4]:
            copy.start()
        shared[0].start()
        mine_rows = pltpu.make_async_copy(own, out_ref.at[slot(chip)], local)
        mine_rows.start()
        sum_ref[...] = total

        def count_stage(index, device):
            return remote(count.at[index], counted.at[index], csend, crecv, index, device)

        stages = [count_stage(0, dev_x), count_stage(1, dev_y), count_stage(2, other)]
        running = jnp.broadcast_to(total[2:3, 0:128], (8, 128))
        count[0] = running
        stages[0].start()
        copies[0].wait_recv()
        copies[4].start()
        copies[1].wait_recv()
        copies[5].start()
        stages[0].wait_recv()
        running = running + counted[0]
        count[1] = running
        stages[1].start()

        @pl.when(depth != chip)
        def _():
            relay_receive()
            relay_start()

        pass_out = remote(oall_ref.at[core], oall_ref.at[core], osend, orecv, 2, other)
        pass_out.start()
        stages[1].wait_recv()
        running = running + counted[1]
        count[2] = running
        stages[2].start()
        for i in range(depths - 1):
            w_copies[i].wait_recv()
            shared[5 + i].start()
        copies[2].wait_recv()
        shared[1].start()
        copies[3].wait_recv()
        shared[2].start()
        stages[2].wait_recv()
        sum_ref[2:3, 0:128] = (running + counted[2])[0:1]
        copies[4].wait_recv()
        copies[5].wait_recv()
        shared[3].start()
        for copy in shared + [pass_out]:
            copy.wait()
        for copy in copies + w_copies + small_copies + stages:
            copy.wait_send()
        relay_finish()
        mine_rows.wait()

    rows, width = pre.shape
    parts, half, columns = weights.shape
    dma = pltpu.SemaphoreType.DMA
    return pl.pallas_call(
        kernel,
        out_shape=[
            jax.ShapeDtypeStruct((lax.axis_size("ctx"), rows, width), BF16),
            jax.ShapeDtypeStruct((parts, depths, 2, half, columns), weights.dtype),
            jax.ShapeDtypeStruct((2,) + out_half.shape, out_half.dtype),
            jax.ShapeDtypeStruct(small.shape, F32),
        ],
        in_specs=[VM] * 4,
        out_specs=[ANY, VM, VM, VM],
        scratch_shapes=[
            pltpu.VMEM((rows, width), BF16),
            pltpu.VMEM((depths - 1,) + small.shape, F32),
            pltpu.VMEM((3, 8, 128), F32),
            pltpu.VMEM((3, 8, 128), F32),
            dma((6,)),
            dma((6,)),
            dma((depths - 1,)),
            dma((depths - 1,)),
            dma((depths + 4,)),
            dma((depths + 4,)),
            dma((depths - 1,)),
            dma((depths - 1,)),
            dma((3,)),
            dma((3,)),
            dma((3,)),
            dma((3,)),
            dma,
        ],
        compiler_params=comm_params(collective_id),
        name="gather_inputs",
    )(pre, small, weights, out_half)


def scatter_and_reduce(parts, qkv, out, collective_id):
    _, rows, width = parts.shape
    half = rows // 2
    depths = qkv.shape[0]

    def kernel(
        x_ref, q_ref, o_ref, out_ref, qsum_ref, osum_ref,
        near, diagonal, staged, q_other, q_mine, q_far, o_other, o_mine, o_far,
        send, recv, ssend, srecv, zsend, zrecv, osend, orecv,
    ):
        depth, chip, core, chip_x, chip_y, chip_d = place_on_mesh()
        dev_x, dev_y = (2 * chip_x + core, depth), (2 * chip_y + core, depth)
        other = (2 * chip + 1 - core, depth)
        across = [
            (2 * chip + core, lax.rem(depth + step, depths)) for step in range(1, depths)
        ]
        signal_and_wait([dev_x, dev_y, other] + across)
        top, low = pl.ds(0, half), pl.ds(half, half)
        first = [
            remote(x_ref.at[chip_d, top], diagonal.at[0], send, recv, 0, dev_x),
            remote(x_ref.at[chip_d, low], diagonal.at[1], send, recv, 1, dev_y),
            remote(x_ref.at[chip_x, top], near.at[0, top], send, recv, 2, dev_x),
            remote(x_ref.at[chip_y, low], near.at[1, low], send, recv, 3, dev_y),
        ]
        swaps = [
            remote(q_ref.at[:, 1 - core], q_other, ssend, srecv, 0, other),
            remote(o_ref.at[1 - core], o_other, ssend, srecv, 1, other),
        ]
        for copy in first + swaps:
            copy.start()
        swaps[0].wait_recv()
        for i in range(depths):
            q_mine[i] = (q_ref[i, core].astype(F32) + q_other[i].astype(F32)).astype(BF16)
        q_copies = [
            remote(q_mine.at[lax.rem(depth + i + 1, depths)], q_far.at[i], zsend, zrecv, i, device)
            for i, device in enumerate(across)
        ]
        for copy in q_copies:
            copy.start()
        swaps[1].wait_recv()
        o_mine[...] = (o_ref[core].astype(F32) + o_other[...].astype(F32)).astype(BF16)
        distance = lax.rem(chip + depths - depth, depths)
        o_copies = [
            remote(o_mine, o_far.at[i], osend, orecv, i, device) for i, device in enumerate(across)
        ]
        for i in range(depths - 1):

            @pl.when(distance == i + 1)
            def _(i=i):
                o_copies[i].start()

        second = [
            remote(staged.at[0], near.at[1, top], send, recv, 4, dev_y),
            remote(staged.at[1], near.at[0, low], send, recv, 5, dev_x),
        ]
        first[0].wait_recv()
        staged[0] = (x_ref[chip_y, top].astype(F32) + diagonal[0].astype(F32)).astype(BF16)
        second[0].start()
        first[1].wait_recv()
        staged[1] = (x_ref[chip_x, low].astype(F32) + diagonal[1].astype(F32)).astype(BF16)
        second[1].start()
        for copy in q_copies:
            copy.wait_recv()
        total = q_mine[depth].astype(F32)
        for i in range(depths - 1):
            total = total + q_far[i].astype(F32)
        qsum_ref[...] = total.astype(BF16)
        osum_ref[...] = jnp.zeros_like(osum_ref)

        @pl.when(distance == 0)
        def _():
            for copy in o_copies:
                copy.wait_recv()
            total = o_mine[...].astype(F32)
            for i in range(depths - 1):
                total = total + o_far[i].astype(F32)
            osum_ref[...] = total.astype(BF16)

        for copy in first[2:] + second:
            copy.wait_recv()
        out_ref[...] = (
            x_ref[chip].astype(F32) + near[0].astype(F32) + near[1].astype(F32)
        )
        for copy in first + second + swaps + q_copies:
            copy.wait_send()
        for i in range(depths - 1):

            @pl.when(distance == i + 1)
            def _(i=i):
                o_copies[i].wait_send()

    q_block, o_block = qkv.shape[2:], out.shape[1:]
    dma = pltpu.SemaphoreType.DMA
    return pl.pallas_call(
        kernel,
        out_shape=[
            jax.ShapeDtypeStruct((rows, width), F32),
            jax.ShapeDtypeStruct(q_block, BF16),
            jax.ShapeDtypeStruct(o_block, BF16),
        ],
        in_specs=[VM] * 3,
        out_specs=[VM] * 3,
        scratch_shapes=[
            pltpu.VMEM((2, rows, width), BF16),
            pltpu.VMEM((2, half, width), BF16),
            pltpu.VMEM((2, half, width), BF16),
            pltpu.VMEM((depths,) + q_block, BF16),
            pltpu.VMEM((depths,) + q_block, BF16),
            pltpu.VMEM((depths - 1,) + q_block, BF16),
            pltpu.VMEM(o_block, BF16),
            pltpu.VMEM(o_block, BF16),
            pltpu.VMEM((depths - 1,) + o_block, BF16),
            dma((6,)),
            dma((6,)),
            dma((2,)),
            dma((2,)),
            dma((depths - 1,)),
            dma((depths - 1,)),
            dma((depths - 1,)),
            dma((depths - 1,)),
        ],
        compiler_params=comm_params(collective_id),
        name="scatter_and_reduce",
    )(parts, qkv, out)


def finish_gradients(ff, qkv, out, small, collective_id):
    depths = lax.axis_size("wsh")
    half, width = out.shape
    columns = ff.shape[1]
    chip_columns = qkv.shape[1]
    split = columns // depths

    def kernel(
        f_ref, q_ref, o_ref, s_ref,
        dq_ref, dk_ref, dv_ref, do_ref, dg_ref, du_ref, dd_ref, small_ref,
        f_all, q_all, o_all, arrived, count, counted,
        fsend, frecv, qsend, qrecv, osend, orecv, ssend, srecv, bsend, brecv, csend, crecv,
    ):
        depth, chip, core, chip_x, chip_y, chip_d = place_on_mesh()
        dev_x, dev_y = (2 * chip_x + core, depth), (2 * chip_y + core, depth)
        other = (2 * chip + 1 - core, depth)
        across = [
            (2 * chip + core, lax.rem(depth + step, depths)) for step in range(1, depths)
        ]
        signal_and_wait([dev_x, dev_y, other] + across)

        def slot(chip_index):
            return 2 * chip_index + core

        f_copies = ring_sends(
            f_ref, f_all, slot, chip, core, depth, chip_x, chip_y, fsend, frecv
        )
        q_copies = ring_sends(
            q_ref, q_all, slot, chip, core, depth, chip_x, chip_y, qsend, qrecv
        )
        small_copies = [
            remote(s_ref, arrived.at[i], bsend, brecv, i, device) for i, device in enumerate(across)
        ]
        for copy in small_copies + q_copies[:2] + f_copies[:2]:
            copy.start()
        quarter = half // 2
        o_top, o_low = o_all.at[core, pl.ds(0, quarter)], o_all.at[core, pl.ds(quarter, quarter)]
        o_source_top, o_source_low = o_ref.at[pl.ds(0, quarter)], o_ref.at[pl.ds(quarter, quarter)]
        o_copies = [
            remote(o_source_top, o_top, osend, orecv, 0, dev_x),
            remote(o_source_low, o_low, osend, orecv, 1, dev_y),
            remote(o_source_low, o_low, osend, orecv, 2, dev_x),
            remote(o_source_top, o_top, osend, orecv, 3, dev_y),
            remote(o_top, o_top, osend, orecv, 4, dev_y),
            remote(o_low, o_low, osend, orecv, 5, dev_x),
        ]
        source, from_x, from_y = chip == depth, chip_x == depth, chip_y == depth

        @pl.when(source)
        def _():
            for copy in o_copies[:4]:
                copy.start()
            o_all[core] = o_ref[...]

        for copy in q_copies[2:4] + f_copies[2:4]:
            copy.start()
        f_all[slot(chip)] = f_ref[...]
        q_all[slot(chip)] = q_ref[...]

        def shared(index, ref):
            return remote(ref, ref, ssend, srecv, index, other)

        f_shared = [shared(i, f_all.at[slot(c)]) for i, c in enumerate((chip, chip_x, chip_y, chip_d))]
        q_shared = [shared(4 + i, q_all.at[slot(c)]) for i, c in enumerate((chip, chip_x, chip_y, chip_d))]
        o_shared = shared(8, o_all.at[core])
        f_shared[0].start()
        q_shared[0].start()
        for copies in (q_copies, f_copies):
            copies[0].wait_recv()
            copies[4].start()
            copies[1].wait_recv()
            copies[5].start()
        for copy in small_copies:
            copy.wait_recv()
        total = s_ref[...]
        for i in range(depths - 1):
            total = total + arrived[i]
        count[0] = total
        stages = [
            remote(count.at[i], counted.at[i], csend, crecv, i, device)
            for i, device in enumerate((dev_x, dev_y, other))
        ]
        stages[0].start()

        @pl.when(from_x)
        def _():
            o_copies[0].wait_recv()
            o_copies[4].start()
            o_copies[2].wait_recv()

        @pl.when(from_y)
        def _():
            o_copies[1].wait_recv()
            o_copies[5].start()
            o_copies[3].wait_recv()

        @pl.when(chip_d == depth)
        def _():
            o_copies[4].wait_recv()
            o_copies[5].wait_recv()

        o_shared.start()
        for i in range(3):
            stages[i].wait_recv()
            total = total + counted[i]
            if i < 2:
                count[i + 1] = total
                stages[i + 1].start()
        small_ref[...] = total
        for copies, passed in ((q_copies, q_shared), (f_copies, f_shared)):
            copies[2].wait_recv()
            passed[1].start()
            copies[3].wait_recv()
            passed[2].start()
            copies[4].wait_recv()
            copies[5].wait_recv()
            passed[3].start()
        for copy in q_shared + [o_shared] + f_shared:
            copy.wait()
        for copy in f_copies + q_copies + small_copies + stages:
            copy.wait_send()

        @pl.when(source)
        def _():
            for copy in o_copies[:4]:
                copy.wait_send()

        @pl.when(from_x)
        def _():
            o_copies[4].wait_send()

        @pl.when(from_y)
        def _():
            o_copies[5].wait_send()

        for c in range(2):
            rows = slice(c * half, (c + 1) * half)
            do_ref[rows, :] = o_all[c].astype(F32)
            for i, ref in enumerate((dq_ref, dk_ref, dv_ref)):
                ref[rows, :] = jnp.concatenate(
                    [q_all[2 * p + c, i * half : (i + 1) * half, :].astype(F32) for p in range(CHIPS)],
                    axis=1,
                )
            for i, ref in enumerate((dg_ref, du_ref)):
                for z in range(depths):
                    ref[rows, z * CHIPS * split : (z + 1) * CHIPS * split] = jnp.concatenate(
                        [
                            f_all[
                                2 * p + c, i * half : (i + 1) * half, z * split : (z + 1) * split
                            ].astype(F32)
                            for p in range(CHIPS)
                        ],
                        axis=1,
                    )
            for p in range(CHIPS):
                at = (2 * p + c) * half
                dd_ref[at : at + half, :] = f_all[2 * p + c, 2 * half :, :].astype(F32)

    dma = pltpu.SemaphoreType.DMA
    shard = 2 * half
    ctx = lax.axis_size("ctx")
    square = jax.ShapeDtypeStruct((shard, width), F32)
    return pl.pallas_call(
        kernel,
        out_shape=[
            square,
            square,
            square,
            square,
            jax.ShapeDtypeStruct((shard, columns * CHIPS), F32),
            jax.ShapeDtypeStruct((shard, columns * CHIPS), F32),
            jax.ShapeDtypeStruct((ctx * half, width), F32),
            jax.ShapeDtypeStruct(small.shape, F32),
        ],
        in_specs=[VM] * 4,
        out_specs=[VM] * 8,
        scratch_shapes=[
            pltpu.VMEM((ctx,) + ff.shape, BF16),
            pltpu.VMEM((ctx,) + qkv.shape, BF16),
            pltpu.VMEM((2,) + out.shape, BF16),
            pltpu.VMEM((depths - 1,) + small.shape, F32),
            pltpu.VMEM((3,) + small.shape, F32),
            pltpu.VMEM((3,) + small.shape, F32),
            dma((6,)),
            dma((6,)),
            dma((6,)),
            dma((6,)),
            dma((6,)),
            dma((6,)),
            dma((9,)),
            dma((9,)),
            dma((depths - 1,)),
            dma((depths - 1,)),
            dma((3,)),
            dma((3,)),
        ],
        compiler_params=comm_params(collective_id),
        name="finish_gradients",
    )(ff, qkv, out, small)


NT = (((1,), (1,)), ((), ()))
TILE = 256
LOCAL_HEADS = HEADS // CHIPS
CHIP_COLS = LOCAL_HEADS * HD


def head_mask(rows, head):
    lane = lax.broadcasted_iota(jnp.int32, (rows, CHIP_COLS), 1)
    return (lane >= head * HD) & (lane < (head + 1) * HD)


def aligned(index, size):
    return pl.ds(pl.multiple_of(index * size, size), size)


def pair_blocks(slots_ref, pair, per_device):
    core = lax.axis_index("ctx") % 2
    pairs = per_device // 2
    slot = (pair // pairs) * (2 * per_device) + core * per_device + 2 * (pair % pairs)
    one, two = slots_ref[slot], slots_ref[slot + 1]
    second = (one >= PROMPT // BLK).astype(jnp.int32)
    return slot, second, jnp.minimum(one, two), jnp.maximum(one, two)


def tile_tables(kind, step, slots_ref, lengths_ref, per_device):
    lane = lax.broadcasted_iota(jnp.int32, (1, TILE), 1)
    high = jnp.zeros((1, TILE), jnp.int32)
    local = []
    per_tile = TILE // BLK
    for i in range(per_tile):
        pair = step * per_tile + i
        _, second, prompt, cont = pair_blocks(slots_ref, pair, per_device)
        block = prompt if kind == 0 else cont
        local.append(2 * pair + (second if kind == 0 else 1 - second))
        high = jnp.where(lane >= i * BLK, (block - i) * BLK + lane, high)
    low = jnp.zeros((1, TILE), jnp.int32)
    if kind == 1:
        start = PROMPT
        for i in range(lengths_ref.shape[0]):
            low = jnp.where(high >= start, start, low)
            start = start + lengths_ref[i]
    return local, low, high


def attention_forward(all_rows, weights, slots, lengths):
    tokens, width = all_rows.shape
    queries = tokens // 2
    tiles = queries // TILE
    blocks = tokens // BLK
    per_device = blocks // (2 * CHIPS)

    def kernel(
        slots_ref, lengths_ref, x_ref, w_ref,
        att_ref, oT_ref, q_ref, k_ref, v_ref, lse_ref, slot_of, xs, xq, vT, s_ref, p_ref,
    ):
        def place_slot(s, _):
            slot_of[slots_ref[s]] = s
            return 0

        lax.fori_loop(0, blocks, place_slot, 0)
        def gather_block(b, _):
            xs[aligned(b, BLK), :] = x_ref[aligned(slot_of[b], BLK), :]
            return 0

        lax.fori_loop(0, blocks, gather_block, 0)

        def gather_query(pair, _):
            slot, second, _, _ = pair_blocks(slots_ref, pair, per_device)
            xq[aligned(pair, BLK), :] = x_ref[aligned(slot + second, BLK), :]
            xq[aligned(pair + queries // (2 * BLK), BLK), :] = x_ref[
                aligned(slot + 1 - second, BLK), :
            ]
            return 0

        lax.fori_loop(0, queries // (2 * BLK), gather_query, 0)

        def project_keys(i, _):
            rows = aligned(i, TILE)
            x = xs[rows, :]
            k_ref[rows, :] = jnp.dot(x, w_ref[1], preferred_element_type=F32).astype(BF16)
            v = jnp.dot(x, w_ref[2], preferred_element_type=F32).astype(BF16)
            v_ref[rows, :] = v
            vT[:, rows] = v.T
            return 0

        lax.fori_loop(0, tokens // TILE, project_keys, 0)

        def project_queries(i, _):
            rows = aligned(i, TILE)
            q_ref[rows, :] = jnp.dot(xq[rows, :], w_ref[0], preferred_element_type=F32).astype(BF16)
            return 0

        lax.fori_loop(0, tiles, project_queries, 0)

        for kind in range(2):
            key_tiles = (PROMPT if kind == 0 else tokens) // TILE
            first_masked = 0 if kind == 0 else PROMPT // TILE

            def one_tile(step, _):
                tile = kind * (tiles // 2) + step
                q = q_ref[aligned(tile, TILE), :]
                local, q_low, q_high = tile_tables(kind, step, slots_ref, lengths_ref, per_device)
                for head in range(LOCAL_HEADS):
                    q_head = jnp.where(head_mask(TILE, head), q, jnp.zeros_like(q))
                    top = jnp.full((1, TILE), NEGATIVE, F32)
                    for k_tile in range(key_tiles):
                        rows = pl.ds(k_tile * TILE, TILE)
                        s = lax.dot_general(k_ref[rows, :], q_head, NT, preferred_element_type=F32)
                        if k_tile >= first_masked:
                            place = lax.broadcasted_iota(jnp.int32, (TILE, TILE), 0) + k_tile * TILE
                            seen = (place >= q_low) & (place <= q_high)
                            s = jnp.where(seen, s, NEGATIVE)
                        s_ref[rows, :] = s
                        top = jnp.maximum(top, jnp.max(s, axis=0, keepdims=True))
                    total = jnp.zeros((1, TILE), F32)
                    for k_tile in range(key_tiles):
                        rows = pl.ds(k_tile * TILE, TILE)
                        p = jnp.exp(s_ref[rows, :] - top)
                        total = total + jnp.sum(p, axis=0, keepdims=True)
                        p_ref[rows, :] = p.astype(BF16)
                    keys = key_tiles * TILE
                    out = jnp.dot(
                        vT[head * HD : (head + 1) * HD, :keys],
                        p_ref[:keys, :],
                        preferred_element_type=F32,
                    )
                    oT_ref[tile, head * HD : (head + 1) * HD, :] = out / total
                    lse_ref[tile, head] = top + jnp.log(total)
                att = oT_ref[tile].T.astype(BF16)
                for b in range(TILE // BLK):
                    att_ref[aligned(local[b], BLK), :] = att[b * BLK : (b + 1) * BLK]
                return 0

            lax.fori_loop(0, tiles // 2, one_tile, 0)

    return pl.pallas_call(
        kernel,
        out_shape=[
            jax.ShapeDtypeStruct((queries, CHIP_COLS), BF16),
            jax.ShapeDtypeStruct((tiles, CHIP_COLS, TILE), F32),
            jax.ShapeDtypeStruct((queries, CHIP_COLS), BF16),
            jax.ShapeDtypeStruct((tokens, CHIP_COLS), BF16),
            jax.ShapeDtypeStruct((tokens, CHIP_COLS), BF16),
            jax.ShapeDtypeStruct((tiles, LOCAL_HEADS, 1, TILE), F32),
        ],
        in_specs=[SM, SM, VM, VM],
        out_specs=[VM] * 6,
        scratch_shapes=[
            pltpu.SMEM((blocks,), jnp.int32),
            pltpu.VMEM((tokens, width), BF16),
            pltpu.VMEM((queries, width), BF16),
            pltpu.VMEM((CHIP_COLS, tokens), BF16),
            pltpu.VMEM((tokens, TILE), F32),
            pltpu.VMEM((tokens, TILE), BF16),
        ],
        compiler_params=pltpu.CompilerParams(vmem_limit_bytes=VMEM_LIMIT),
        name="attention_forward",
    )(slots, lengths, all_rows, weights)


def attention_backward(hidden_rows, w_out, saved, slots, lengths):
    oT, q, k, v, lse = saved
    queries, width = hidden_rows.shape
    tokens = k.shape[0]
    tiles = queries // TILE
    blocks = tokens // BLK
    per_device = blocks // (2 * CHIPS)
    wide = LOCAL_HEADS * TILE

    def kernel(
        slots_ref, lengths_ref, h_ref, w_ref, oT_ref, q_ref, k_ref, v_ref, lse_ref,
        dq_ref, dk_ref, dv_ref, hq, kT, doT, dqT, q_stack, do_stack, p_buf, ds_buf, dk_acc, dv_acc,
    ):
        def gather_query(pair, _):
            _, second, _, _ = pair_blocks(slots_ref, pair, per_device)
            hq[aligned(pair, BLK), :] = h_ref[aligned(2 * pair + second, BLK), :]
            hq[aligned(pair + queries // (2 * BLK), BLK), :] = h_ref[
                aligned(2 * pair + 1 - second, BLK), :
            ]
            return 0

        lax.fori_loop(0, queries // (2 * BLK), gather_query, 0)

        def transpose_keys(i, _):
            rows = aligned(i, TILE)
            kT[:, rows] = k_ref[rows, :].T
            return 0

        lax.fori_loop(0, tokens // TILE, transpose_keys, 0)

        for kind in (1, 0):
            key_tiles = (PROMPT if kind == 0 else tokens) // TILE
            first_masked = 0 if kind == 0 else PROMPT // TILE

            def one_tile(step, _):
                tile = kind * (tiles // 2) + step
                q_tile = q_ref[aligned(tile, TILE), :]
                local, q_low, q_high = tile_tables(kind, step, slots_ref, lengths_ref, per_device)
                wide_do = lax.dot_general(
                    w_ref[...], hq[aligned(tile, TILE), :], NT, preferred_element_type=F32
                )
                do_tile = wide_do.T.astype(BF16)
                doT[...] = wide_do.astype(BF16).astype(F32) * oT_ref[tile]
                for head in range(LOCAL_HEADS):
                    lanes = pl.ds(head * TILE, TILE)
                    heads = pl.ds(head * HD, HD)
                    mask = head_mask(TILE, head)
                    q_head = jnp.where(mask, q_tile, jnp.zeros_like(q_tile))
                    do_head = jnp.where(mask, do_tile, jnp.zeros_like(do_tile))
                    q_stack[lanes, :] = q_head
                    do_stack[lanes, :] = do_head
                    delta = jnp.sum(doT[heads, :], axis=0, keepdims=True)
                    norm = lse_ref[tile, head]
                    for k_tile in range(key_tiles):
                        rows = pl.ds(k_tile * TILE, TILE)
                        s = lax.dot_general(k_ref[rows, :], q_head, NT, preferred_element_type=F32)
                        dp = lax.dot_general(v_ref[rows, :], do_head, NT, preferred_element_type=F32)
                        p = jnp.exp(s - norm)
                        if k_tile >= first_masked:
                            place = lax.broadcasted_iota(jnp.int32, (TILE, TILE), 0) + k_tile * TILE
                            seen = (place >= q_low) & (place <= q_high)
                            p = jnp.where(seen, p, 0.0)
                        p_buf[rows, lanes] = p.astype(BF16)
                        ds_buf[rows, lanes] = (p * (dp - delta)).astype(BF16)
                    keys = key_tiles * TILE
                    dqT[heads, :] = jnp.dot(
                        kT[heads, :keys], ds_buf[:keys, lanes], preferred_element_type=F32
                    )
                for k_tile in range(key_tiles):
                    rows = pl.ds(k_tile * TILE, TILE)
                    dv = jnp.dot(p_buf[rows, :], do_stack[...], preferred_element_type=F32)
                    dk = jnp.dot(ds_buf[rows, :], q_stack[...], preferred_element_type=F32)
                    if kind == 1:
                        fresh = step == 0
                        dv = dv + jnp.where(fresh, 0.0, dv_acc[rows, :])
                        dk = dk + jnp.where(fresh, 0.0, dk_acc[rows, :])
                    else:
                        dv = dv + dv_acc[rows, :]
                        dk = dk + dk_acc[rows, :]
                    dv_acc[rows, :] = dv
                    dk_acc[rows, :] = dk
                dq = dqT[...].T.astype(BF16)
                for b in range(TILE // BLK):
                    dq_ref[aligned(local[b], BLK), :] = dq[b * BLK : (b + 1) * BLK]
                return 0

            lax.fori_loop(0, tiles // 2, one_tile, 0)

        def give_block(slot, _):
            block = aligned(slots_ref[slot], BLK)
            dk_ref[aligned(slot, BLK), :] = dk_acc[block, :].astype(BF16)
            dv_ref[aligned(slot, BLK), :] = dv_acc[block, :].astype(BF16)
            return 0

        lax.fori_loop(0, blocks, give_block, 0)

    return pl.pallas_call(
        kernel,
        out_shape=[
            jax.ShapeDtypeStruct((queries, CHIP_COLS), BF16),
            jax.ShapeDtypeStruct((tokens, CHIP_COLS), BF16),
            jax.ShapeDtypeStruct((tokens, CHIP_COLS), BF16),
        ],
        in_specs=[SM, SM] + [VM] * 7,
        out_specs=[VM] * 3,
        scratch_shapes=[
            pltpu.VMEM((queries, width), BF16),
            pltpu.VMEM((CHIP_COLS, tokens), BF16),
            pltpu.VMEM((CHIP_COLS, TILE), F32),
            pltpu.VMEM((CHIP_COLS, TILE), F32),
            pltpu.VMEM((wide, CHIP_COLS), BF16),
            pltpu.VMEM((wide, CHIP_COLS), BF16),
            pltpu.VMEM((tokens, wide), BF16),
            pltpu.VMEM((tokens, wide), BF16),
            pltpu.VMEM((tokens, CHIP_COLS), F32),
            pltpu.VMEM((tokens, CHIP_COLS), F32),
        ],
        compiler_params=pltpu.CompilerParams(vmem_limit_bytes=VMEM_LIMIT),
        name="attention_backward",
    )(slots, lengths, hidden_rows, w_out, oT, q, k, v, lse)


TN = (((0,), (0,)), ((), ()))
ROWS = 32


def gelu_parts(v):
    scale = math.sqrt(2 / math.pi)
    square = v * v
    t = jnp.tanh(scale * v * (1.0 + 0.044715 * square))
    rise = 0.5 * (1.0 + t)
    return v * rise, rise + 0.5 * v * (1.0 - t * t) * scale * (1.0 + 0.134145 * square)


def middle(attended, out_w, piece, active, mixed_one, grads, teachers, weight, small, correct, collective_id):
    _, rows, width = attended.shape[0], active.shape[0], active.shape[1]
    depths, _, half, columns = piece.shape
    shard = 2 * half
    blocks = rows // ROWS
    col_tiles = columns // TILE

    def kernel(
        att_ref, wo_ref, piece_ref, a_ref, m_ref, g0_ref, g1_ref, t0_ref, t1_ref, wt_ref, small_ref, c_ref,
        out0_ref, out1_ref, up0_ref, up1_ref, hg_ref, h_rows, ff_ref, sums_ref,
        w_all, hidden, own, x_rows, r_rows, xT, innerT, inner, gate, up, gate_low, up_low,
        part0, part1, part2, got0, got1, got2, dw, dw_other,
        wsend, wrecv, wlocal, send0, recv0, send1, recv1, send2, recv2,
        ag1s, ag1r, ag2s, ag2r, ag3s, ag3r, dsend, drecv,
    ):
        depth, chip, core, chip_x, chip_y, chip_d = place_on_mesh()
        dev_x, dev_y, dev_d = ((2 * c + core, depth) for c in (chip_x, chip_y, chip_d))
        other = (2 * chip + 1 - core, depth)
        signal_and_wait([dev_x, dev_y, dev_d, other])
        near = ((chip_x, dev_x), (chip_y, dev_y), (chip_d, dev_d))

        w_copies = []
        for i in range(3):
            dst = w_all.at[i, :, core]
            w_copies.append(remote(piece_ref.at[:, i], dst, wsend, wrecv, i, other))
            w_copies.append(pltpu.make_async_copy(piece_ref.at[:, i], dst, wlocal.at[i]))
        for copy in w_copies:
            copy.start()

        def give(parts, got, send, recv):
            return [
                remote(parts.at[c], got.at[i], send, recv, i, device)
                for i, (c, device) in enumerate(near)
            ]

        def ring(source, target, send, recv):
            return ring_sends(
                source, target, lambda c: c, chip, core, depth, chip_x, chip_y, send, recv
            )

        sends0 = give(part0, got0, send0, recv0)
        for i in (2, 0, 1):
            part0[near[i][0]] = jnp.dot(
                att_ref[near[i][0]], wo_ref[...], preferred_element_type=F32
            ).astype(BF16)
            sends0[i].start()
        hidden[...] = a_ref[...] + jnp.dot(att_ref[chip], wo_ref[...], preferred_element_type=F32)
        for copy in sends0:
            copy.wait_recv()

        def first_norm(i, _):
            at = aligned(i, ROWS)
            h = hidden[at, :]
            for j in range(3):
                h = h + got0[j, at, :].astype(F32)
            hidden[at, :] = h
            factor = lax.rsqrt(jnp.mean(h * h, axis=1, keepdims=True) + EPSILON)
            own[0, at, :] = (h * factor * small_ref[1:2, :]).astype(BF16)
            return 0

        lax.fori_loop(0, blocks, first_norm, 0)
        ring1 = ring(own.at[0], x_rows, ag1s, ag1r)
        for copy in ring1[:4]:
            copy.start()
        x_rows[chip] = own[0]
        for copy in w_copies:
            copy.wait()

        def w_rows(i):
            return w_all[i].reshape(columns if i == 2 else width, width if i == 2 else columns)

        def forward(c):
            x = x_rows[c]
            for n in range(col_tiles):
                cols = slice(n * TILE, (n + 1) * TILE)
                g = jnp.dot(x, w_rows(0)[:, cols], preferred_element_type=F32)
                u = jnp.dot(x, w_rows(1)[:, cols], preferred_element_type=F32)
                gate[c, :, cols] = g
                up[c, :, cols] = u
                inner[c, :, cols] = (gelu_parts(g)[0] * u).astype(BF16)
            return jnp.dot(inner[c], w_rows(2), preferred_element_type=F32)

        sends1 = give(part1, got1, send1, recv1)
        mine = forward(chip)
        up0_ref[...] = mine
        ring1[0].wait_recv()
        ring1[4].start()
        ring1[1].wait_recv()
        ring1[5].start()
        for i, (c, _) in enumerate(near):
            if i < 2:
                ring1[2 + i].wait_recv()
            else:
                ring1[4].wait_recv()
                ring1[5].wait_recv()
            part1[c] = forward(c).astype(BF16)
            sends1[i].start()

        def turn(i, _):
            xT[:, aligned(i, rows)] = x_rows[i].T
            innerT[:, aligned(i, rows)] = inner[i].T
            return 0

        lax.fori_loop(0, CHIPS, turn, 0)
        for copy in sends1:
            copy.wait_recv()

        def outputs(i, sums):
            at = aligned(i, ROWS)
            h, a = hidden[at, :], a_ref[at, :]
            result = h + up0_ref[at, :]
            for j in range(3):
                result = result + got1[j, at, :].astype(F32)
            difference = result - a
            row_weight = wt_ref[at, :]
            c0, c1 = c_ref[0], c_ref[1]
            out0 = a + c0 * difference
            out1 = m_ref[at, :] + c1 * difference
            out0_ref[at, :] = out0.astype(BF16)
            out1_ref[at, :] = out1.astype(BF16)
            up0 = g0_ref[at, :].astype(F32) + row_weight * (out0 - t0_ref[at, :].astype(F32))
            up1 = g1_ref[at, :].astype(F32) + row_weight * (out1 - t1_ref[at, :].astype(F32))
            up0_ref[at, :] = up0
            up1_ref[at, :] = up1
            own[1, at, :] = (c0 * up0 + c1 * up1).astype(BF16)
            return (
                sums[0] + jnp.sum(up0 * difference, axis=0, keepdims=True),
                sums[1] + jnp.sum(up1 * difference, axis=0, keepdims=True),
            )

        zero = jnp.zeros((1, width), F32)
        correct_sums = lax.fori_loop(0, blocks, outputs, (zero, zero))
        sums_ref[...] = jnp.zeros_like(sums_ref)
        sums_ref[1:2, :] = correct_sums[0]
        sums_ref[2:3, :] = correct_sums[1]

        ring2 = ring(own.at[1], r_rows, ag2s, ag2r)
        for copy in ring2[:4]:
            copy.start()
        r_rows[chip] = own[1]

        def backward(c):
            r = r_rows[c]
            for n in range(col_tiles):
                cols = slice(n * TILE, (n + 1) * TILE)
                inner_grad = lax.dot_general(r, w_rows(2)[cols, :], NT, preferred_element_type=F32)
                value, slope = gelu_parts(gate[c, :, cols])
                gate_low[c, :, cols] = (inner_grad * up[c, :, cols] * slope).astype(BF16)
                up_low[c, :, cols] = (inner_grad * value).astype(BF16)
            return lax.dot_general(
                gate_low[c], w_rows(0), NT, preferred_element_type=F32
            ) + lax.dot_general(up_low[c], w_rows(1), NT, preferred_element_type=F32)

        sends2 = give(part2, got2, send2, recv2)
        hg_ref[...] = backward(chip)
        ring2[0].wait_recv()
        ring2[4].start()
        ring2[1].wait_recv()
        ring2[5].start()
        for i, (c, _) in enumerate(near):
            if i < 2:
                ring2[2 + i].wait_recv()
            else:
                ring2[4].wait_recv()
                ring2[5].wait_recv()
            part2[c] = backward(c).astype(BF16)
            sends2[i].start()

        def weight_grads(z, _):
            at = aligned(z, shard)
            for i, (left, right) in enumerate(((xT, gate_low), (xT, up_low), (innerT, r_rows))):
                wide = jnp.dot(
                    left[at, :], right[...].reshape(CHIPS * rows, -1), preferred_element_type=F32
                ).astype(BF16)
                dw[z, 0, i * half : (i + 1) * half, :] = wide[:half]
                dw[z, 1, i * half : (i + 1) * half, :] = wide[half:]
            return 0

        lax.fori_loop(0, depths, weight_grads, 0)
        swap = remote(dw.at[:, 1 - core], dw_other, dsend, drecv, 0, other)
        swap.start()
        for copy in sends2:
            copy.wait_recv()

        def second_norm(i, gain_sum):
            at = aligned(i, ROWS)
            h = hidden[at, :]
            dy = hg_ref[at, :]
            for j in range(3):
                dy = dy + got2[j, at, :].astype(F32)
            factor = lax.rsqrt(jnp.mean(h * h, axis=1, keepdims=True) + EPSILON)
            weighted = dy * small_ref[1:2, :]
            mean = jnp.mean(weighted * h, axis=1, keepdims=True)
            result_grad = c_ref[0] * up0_ref[at, :] + c_ref[1] * up1_ref[at, :]
            hidden_grad = result_grad + (factor * weighted - h * (factor * factor * factor * mean))
            hg_ref[at, :] = hidden_grad
            own[2, at, :] = hidden_grad.astype(BF16)
            return gain_sum + jnp.sum(dy * h * factor, axis=0, keepdims=True)

        sums_ref[0:1, :] = lax.fori_loop(0, blocks, second_norm, zero)
        ring3 = ring(own.at[2], h_rows, ag3s, ag3r)
        for copy in ring3[:4]:
            copy.start()
        h_rows[chip] = own[2]
        swap.wait_recv()

        def add_cores(z, _):
            ff_ref[z] = (dw[z, core].astype(F32) + dw_other[z].astype(F32)).astype(BF16)
            return 0

        lax.fori_loop(0, depths, add_cores, 0)
        ring3[0].wait_recv()
        ring3[4].start()
        ring3[1].wait_recv()
        ring3[5].start()
        for copy in ring3[2:]:
            copy.wait_recv()
        for copy in sends0 + sends1 + sends2 + ring1 + ring2 + ring3 + [swap]:
            copy.wait_send()

    dma = pltpu.SemaphoreType.DMA
    block = (rows, width)
    wide_rows = (CHIPS, rows, width)
    hid_rows = (CHIPS, rows, columns)
    return pl.pallas_call(
        kernel,
        out_shape=[
            jax.ShapeDtypeStruct(block, BF16),
            jax.ShapeDtypeStruct(block, BF16),
            jax.ShapeDtypeStruct(block, F32),
            jax.ShapeDtypeStruct(block, F32),
            jax.ShapeDtypeStruct(block, F32),
            jax.ShapeDtypeStruct(wide_rows, BF16),
            jax.ShapeDtypeStruct((depths, 3 * half, columns), BF16),
            jax.ShapeDtypeStruct((8, width), F32),
        ],
        in_specs=[VM, VM, ANY] + [VM] * 8 + [SM],
        out_specs=[VM] * 8,
        scratch_shapes=[
            pltpu.VMEM((3, depths, 2, half, columns), BF16),
            pltpu.VMEM(block, F32),
            pltpu.VMEM((3,) + block, BF16),
            pltpu.VMEM(wide_rows, BF16),
            pltpu.VMEM(wide_rows, BF16),
            pltpu.VMEM((width, CHIPS * rows), BF16),
            pltpu.VMEM((columns, CHIPS * rows), BF16),
            pltpu.VMEM(hid_rows, BF16),
            pltpu.VMEM(hid_rows, F32),
            pltpu.VMEM(hid_rows, F32),
            pltpu.VMEM(hid_rows, BF16),
            pltpu.VMEM(hid_rows, BF16),
            pltpu.VMEM(wide_rows, BF16),
            pltpu.VMEM(wide_rows, BF16),
            pltpu.VMEM(wide_rows, BF16),
            pltpu.VMEM((3,) + block, BF16),
            pltpu.VMEM((3,) + block, BF16),
            pltpu.VMEM((3,) + block, BF16),
            pltpu.VMEM((depths, 2, 3 * half, columns), BF16),
            pltpu.VMEM((depths, 3 * half, columns), BF16),
        ]
        + [dma((3,))] * 9
        + [dma((6,))] * 6
        + [dma((1,))] * 2,
        compiler_params=comm_params(collective_id),
        name="middle",
    )(attended, out_w, piece, active, mixed_one, *grads, *teachers, weight, small, correct)


def plane_shards(
    states, block_slot, cont_lengths, valid_mask, teacher, out_grad, predict, correct,
    norm_attn, w_query, w_key, w_value, w_out, norm_ffn, w_gate, w_up, w_down,
):
    depths = lax.axis_size("wsh")
    ctx, depth = lax.axis_index("ctx"), lax.axis_index("wsh")
    chip, core = ctx // 2, ctx % 2
    _, rows, _, width = states.shape
    shard = w_query.shape[0]
    half = shard // 2
    hidden_cols = w_gate.shape[1] // CHIPS
    group_len = block_slot.shape[1] * BLK
    slots, lengths = block_slot[0], cont_lengths[0]

    def columns(weight):
        return lax.dynamic_slice(weight, (core * half, chip * CHIP_COLS), (half, CHIP_COLS))

    qkv_piece = jnp.stack([columns(w) for w in (w_query, w_key, w_value)])
    out_half = lax.dynamic_slice_in_dim(w_out, core * half, half, 0)
    ff_split = hidden_cols // depths

    def ff_columns(weight):
        piece = lax.dynamic_slice_in_dim(weight, core * half, half, 0)
        piece = piece.reshape(half, depths, CHIPS, ff_split)
        return lax.dynamic_index_in_dim(piece, chip, 2, keepdims=False).reshape(half, hidden_cols)

    down_rows = lax.dynamic_slice_in_dim(w_down, chip * ff_split + core * (ff_split // 2), ff_split // 2, 0)
    ff_piece = jnp.concatenate([ff_columns(w_gate), ff_columns(w_up), down_rows], axis=0)
    valid_float = valid_mask.astype(F32)
    count = jnp.sum(valid_float)

    def own_columns(gain):
        return lax.dynamic_update_slice_in_dim(jnp.zeros((width,), F32), gain.astype(F32), depth * shard, 0)

    small = jnp.concatenate(
        [
            own_columns(norm_attn)[None],
            own_columns(norm_ffn)[None],
            jnp.full((1, width), count, F32),
            jnp.zeros((5, width), F32),
        ]
    )

    inputs = states[0].astype(F32)
    mixed = [predict[i, 0] * inputs[:, 0] + predict[i, 1] * inputs[:, 1] for i in range(2)]
    active = mixed[0]
    factor_one = lax.rsqrt(jnp.mean(active * active, axis=-1, keepdims=True) + EPSILON)
    all_rows, qkv, out_w, small = gather_inputs(active * factor_one, small, qkv_piece, out_half, 1)
    ff_piece, small = lax.optimization_barrier((ff_piece, small))
    ff_piece = lax.all_gather(ff_piece, "wsh", axis=0, tiled=True).reshape(depths, 3, half, hidden_cols)
    gain_one, valid_total = small[0], small[2, 0]
    all_rows = all_rows.reshape(-1, width)
    qkv = qkv.reshape(3, width, CHIP_COLS)
    out_w = out_w.reshape(CHIP_COLS, width)
    attended, *saved = attention_forward(all_rows, qkv, slots, lengths)
    weight = (depths * group_len / valid_total) * valid_float[0][:, None]
    out0, out1, up0, up1, hidden_grad, hidden_rows, ff_sum, sums = middle(
        attended.reshape(CHIPS, rows, CHIP_COLS), out_w, ff_piece, active, mixed[1],
        [out_grad[0, :, i] for i in range(2)], [teacher[0, :, i] for i in range(2)],
        weight, small, correct, 2,
    )
    ff_sum = lax.psum_scatter(
        ff_sum.reshape(depths * 3 * half, hidden_cols), "wsh", scatter_dimension=0, tiled=True
    )
    upstream = [up0, up1]
    result_grad = correct[0] * up0 + correct[1] * up1
    hidden_rows = hidden_rows.reshape(-1, width)

    def outer(left, right):
        return lax.dot_general(left, right, TN, preferred_element_type=F32).astype(BF16)

    def own_half(grad):
        return lax.dynamic_index_in_dim(grad, core, 1, keepdims=False)

    out_w_part = outer(attended, hidden_rows)
    dq, dk, dv = attention_backward(hidden_rows, out_w, saved, slots, lengths)
    by_core = [g.reshape(CHIPS, 2, rows, CHIP_COLS) for g in (dk, dv)]
    swapped = swap_cores(by_core, 10)
    dk, dv = (
        (own_half(g).astype(F32) + s.astype(F32)).astype(BF16).reshape(-1, CHIP_COLS)
        for g, s in zip(by_core, swapped)
    )
    part = (
        lax.dot_general(dq, qkv[0], NT, preferred_element_type=F32)
        + lax.dot_general(dk, qkv[1], NT, preferred_element_type=F32)
        + lax.dot_general(dv, qkv[2], NT, preferred_element_type=F32)
    )
    own_rows = lax.dynamic_index_in_dim(
        all_rows.reshape(CHIPS, 2, rows, width), core, 1, keepdims=False
    ).reshape(-1, width)
    qkv_grads = jnp.concatenate(
        [outer(own_rows, g).reshape(depths, 2, half, CHIP_COLS) for g in (dq, dk, dv)], axis=2
    )
    normed_grad, qkv_sum, out_sum = scatter_and_reduce(
        part.astype(BF16).reshape(CHIPS, rows, width), qkv_grads, out_w_part.reshape(2, half, width), 11
    )

    active_norm_grad, gain_one_grad = rms_backward(active, factor_one, gain_one, normed_grad)
    active_grad = hidden_grad + active_norm_grad - result_grad
    mixed_grad = [upstream[0] + active_grad, upstream[1]]
    predict_local = [jnp.sum(mixed_grad[i] * inputs[:, j]) for i in range(2) for j in range(2)]
    states_grad = jnp.stack(
        [predict[0, j] * mixed_grad[0] + predict[1, j] * mixed_grad[1] for j in range(2)], axis=1
    ).astype(BF16)
    scalars = jnp.concatenate([jnp.stack(predict_local), jnp.sum(sums[1:3], axis=1)])
    small = jnp.concatenate(
        [
            gain_one_grad[None],
            sums[0:1],
            jnp.pad(scalars, (0, width - scalars.shape[0]))[None],
            jnp.zeros((5, width), F32),
        ]
    )
    query_grad, key_grad, value_grad, out_w_grad, gate_out, up_out, down_out, small = finish_gradients(
        ff_sum, qkv_sum, out_sum, small, 12
    )

    def own_gain(grad):
        return lax.dynamic_slice_in_dim(grad, depth * shard, shard, 0)

    return (
        jnp.stack([out0, out1], axis=1)[None],
        states_grad[None],
        small[2, 0:4].reshape(2, 2),
        small[2, 4:6],
        own_gain(small[0]),
        query_grad,
        key_grad,
        value_grad,
        out_w_grad,
        own_gain(small[1]),
        gate_out,
        up_out,
        down_out,
    )


def fits_plane(mesh, states, block_slot, w_query, w_gate):
    ctx, depths = mesh.shape["ctx"], mesh.shape["wsh"]
    return (
        ctx == 2 * CHIPS
        and depths == CHIPS
        and states.shape[0] == depths
        and block_slot.shape[1] * BLK == 2 * PROMPT
        and states.shape[1] == 2 * PROMPT
        and w_query.shape[0] % (32 * depths) == 0
        and w_gate.shape[1] % (32 * CHIPS * depths) == 0
    )


def solution(mesh):
    in_specs = (
        P("wsh", "ctx", None, None),
        P("wsh", None),
        P("wsh", None),
        P("wsh", "ctx"),
        P("wsh", "ctx", None, None),
        P("wsh", "ctx", None, None),
        P(),
        P(),
        P("wsh"),
        P("wsh", None),
        P("wsh", None),
        P("wsh", None),
        P("wsh", None),
        P("wsh"),
        P("wsh", None),
        P("wsh", None),
        P("wsh", None),
    )
    out_specs = (
        P("wsh", "ctx", None, None),
        P("wsh", "ctx", None, None),
        P(),
        P(),
        P("wsh"),
        P("wsh", None),
        P("wsh", None),
        P("wsh", None),
        P("wsh", None),
        P("wsh"),
        P("wsh", None),
        P("wsh", None),
        P("wsh", None),
    )

    def step(*args):
        plane = fits_plane(mesh, args[0], args[1], args[9], args[14])
        body = plane_shards if plane else general_shards
        return jax.shard_map(
            body, mesh=mesh, in_specs=in_specs, out_specs=out_specs, check_vma=False
        )(*args)

    return step
```

```python
import functools
import math

import jax
import jax.numpy as jnp
from jax import lax
from jax.experimental import pallas as pl
from jax.experimental.pallas import tpu as pltpu
from jax.sharding import PartitionSpec as P

HEADS = 12
HD = 64
PROMPT = 1024
BLK = 64


EPSILON = 1e-06
NEGATIVE = -1e30
HIGHEST = lax.Precision.HIGHEST


def rms_forward(tensor, gain_vec):
    factor = lax.rsqrt(jnp.mean(tensor * tensor, axis=-1, keepdims=True) + EPSILON)
    return (tensor * factor * gain_vec, factor)


def rms_backward(tensor, factor, gain_vec, upstream):
    weighted = upstream * gain_vec
    gain_grad = jnp.sum(upstream * tensor * factor, axis=0)
    middle = jnp.mean(weighted * tensor, axis=-1, keepdims=True)
    return (factor * weighted - tensor * factor * factor * factor * middle, gain_grad)


def segment_starts(cont_lengths):
    count = cont_lengths.shape[1]
    index = jnp.arange(count, dtype=jnp.int32)
    before = index[:, None] < index[None, :]
    return PROMPT + jnp.sum(jnp.where(before[None], cont_lengths[:, :, None], 0), axis=1)


def token_places(block_slot, cont_lengths):
    groups, blocks = block_slot.shape
    offsets = jnp.arange(BLK, dtype=jnp.int32)
    places = (block_slot[:, :, None] * BLK + offsets[None, None, :]).reshape(groups, blocks * BLK)
    starts = segment_starts(cont_lengths)
    segments = jnp.sum((places[:, :, None] >= starts[:, None, :]).astype(jnp.int32), axis=2)
    return (places, segments)


def visible(query_place, query_segment, key_place, key_segment):
    earlier = key_place[:, None, :] <= query_place[:, :, None]
    shared = (key_segment[:, None, :] == 0) | (key_segment[:, None, :] == query_segment[:, :, None])
    return earlier & shared


def split_heads(tensor):
    return tensor.reshape(tensor.shape[0], tensor.shape[1], HEADS, HD)


def forward_block(running, query_part, key_part, value_part, allowed):

    def forward_compute(current):
        maximum, denominator, accumulated = current
        scores = jnp.einsum(
            "gqhd,gkhd->ghqk",
            split_heads(query_part),
            split_heads(key_part),
            preferred_element_type=jnp.float32,
        )
        masked = jnp.where(allowed[:, None], scores, NEGATIVE)
        new_max = jnp.maximum(maximum, jnp.max(masked, axis=-1))
        exponent = jnp.where(allowed[:, None], jnp.exp(masked - new_max[..., None]), 0.0)
        factor = jnp.exp(maximum - new_max)
        rescale = jnp.swapaxes(factor, 1, 2)[..., None]
        update = jnp.einsum(
            "ghqk,gkhd->gqhd",
            exponent.astype(jnp.bfloat16),
            split_heads(value_part),
            preferred_element_type=jnp.float32,
        )
        merged = (split_heads(accumulated) * rescale + update).reshape(accumulated.shape)
        return (new_max, denominator * factor + jnp.sum(exponent, axis=-1), merged)

    return lax.cond(jnp.any(allowed), forward_compute, lambda current: current, running)


def backward_block(
    query_part, grad_part, key_part, value_part, allowed, maximum, denominator, delta_sum
):
    scores = jnp.einsum(
        "gqhd,gkhd->ghqk",
        split_heads(query_part),
        split_heads(key_part),
        preferred_element_type=jnp.float32,
    )
    exponent = jnp.where(allowed[:, None], jnp.exp(scores - maximum[..., None]), 0.0)
    probability = exponent / denominator[..., None]
    prob_grad = jnp.einsum(
        "gqhd,gkhd->ghqk",
        split_heads(grad_part),
        split_heads(value_part),
        preferred_element_type=jnp.float32,
    )
    score_grad = (probability * (prob_grad - delta_sum[..., None])).astype(jnp.bfloat16)
    return (probability.astype(jnp.bfloat16), score_grad)


def general_shards(
    states,
    block_slot,
    cont_lengths,
    valid_mask,
    teacher,
    out_grad,
    predict,
    correct,
    norm_attn,
    w_query,
    w_key,
    w_value,
    w_out,
    norm_ffn,
    w_gate,
    w_up,
    w_down,
):
    groups, local_len = valid_mask.shape
    model_width = states.shape[3]
    row_count = groups * local_len
    group_len = block_slot.shape[1] * BLK
    gain_one, query_w, key_w, value_w, out_w, gain_two, gate_w, up_w, down_w = (
        lax.all_gather(norm_attn, "wsh", axis=0, tiled=True),
        lax.all_gather(w_query, "wsh", axis=0, tiled=True),
        lax.all_gather(w_key, "wsh", axis=0, tiled=True),
        lax.all_gather(w_value, "wsh", axis=0, tiled=True),
        lax.all_gather(w_out, "wsh", axis=0, tiled=True),
        lax.all_gather(norm_ffn, "wsh", axis=0, tiled=True),
        lax.all_gather(w_gate, "wsh", axis=0, tiled=True),
        lax.all_gather(w_up, "wsh", axis=0, tiled=True),
        lax.all_gather(w_down, "wsh", axis=0, tiled=True),
    )
    valid_float = valid_mask.astype(jnp.float32)
    valid_total = lax.psum(jnp.sum(valid_float), ("ctx", "wsh"))
    places, segments = token_places(block_slot, cont_lengths)
    offset = lax.axis_index("ctx") * local_len
    own_place = lax.dynamic_slice_in_dim(places, offset, local_len, 1)
    own_segment = lax.dynamic_slice_in_dim(segments, offset, local_len, 1)
    inputs = states.astype(jnp.float32)
    mixed_states = jnp.einsum("ij,gtjd->gtid", predict, inputs, precision=HIGHEST)
    active = mixed_states[:, :, 0].reshape(row_count, model_width)
    gain_first = gain_one.astype(jnp.float32)
    normed, factor_one = rms_forward(active, gain_first)
    normed_low = normed.astype(jnp.bfloat16)
    queries = (
        jnp.dot(normed_low, query_w, preferred_element_type=jnp.float32)
        .astype(jnp.bfloat16)
        .reshape(groups, local_len, model_width)
    )
    key_rows = (
        jnp.dot(normed_low, key_w, preferred_element_type=jnp.float32)
        .astype(jnp.bfloat16)
        .reshape(groups, local_len, model_width)
    )
    values = (
        jnp.dot(normed_low, value_w, preferred_element_type=jnp.float32)
        .astype(jnp.bfloat16)
        .reshape(groups, local_len, model_width)
    )
    initial = (
        jnp.full((groups, HEADS, local_len), NEGATIVE, jnp.float32),
        jnp.zeros((groups, HEADS, local_len), jnp.float32),
        jnp.zeros((groups, local_len, model_width), jnp.float32),
    )
    piece_keys = lax.all_gather(key_rows, "ctx", axis=1, tiled=True)
    piece_values = lax.all_gather(values, "ctx", axis=1, tiled=True)
    piece_len = piece_keys.shape[1]
    block_size = math.gcd(piece_len, local_len)

    def fold_one_block(current, block_index):
        begin = block_index * block_size
        key_part = lax.dynamic_slice_in_dim(piece_keys, begin, block_size, 1)
        value_part = lax.dynamic_slice_in_dim(piece_values, begin, block_size, 1)
        key_place = lax.dynamic_slice_in_dim(places, begin, block_size, 1)
        key_segment = lax.dynamic_slice_in_dim(segments, begin, block_size, 1)
        allowed = visible(own_place, own_segment, key_place, key_segment)
        return (forward_block(current, queries, key_part, value_part, allowed), None)

    finished, unused = lax.scan(
        fold_one_block, initial, jnp.arange(piece_len // block_size, dtype=jnp.int32)
    )
    maximum, denominator, accumulated = finished
    attended = (split_heads(accumulated) / jnp.swapaxes(denominator, 1, 2)[..., None]).reshape(
        row_count, model_width
    )
    attended_low = attended.astype(jnp.bfloat16)
    hidden = active + jnp.dot(attended_low, out_w, preferred_element_type=jnp.float32)
    gain_second = gain_two.astype(jnp.float32)
    normed_two, factor_two = rms_forward(hidden, gain_second)
    normed_two_low = normed_two.astype(jnp.bfloat16)
    gate_proj = jnp.dot(normed_two_low, gate_w, preferred_element_type=jnp.float32)
    up_proj = jnp.dot(normed_two_low, up_w, preferred_element_type=jnp.float32)
    inner_act, inner_pull = jax.vjp(
        lambda gate_in, up_in: jax.nn.gelu(gate_in, approximate=True) * up_in, gate_proj, up_proj
    )
    inner_low = inner_act.astype(jnp.bfloat16)
    result = hidden + jnp.dot(inner_low, down_w, preferred_element_type=jnp.float32)
    difference = (result - active).reshape(groups, local_len, 1, model_width)
    out_states = mixed_states + correct[None, None, :, None] * difference
    new_states = out_states.astype(jnp.bfloat16)
    loss_ratio = lax.axis_size("wsh") * groups * group_len / valid_total
    upstream = out_grad.astype(jnp.float32) + loss_ratio * valid_float[:, :, None, None] * (
        out_states - teacher.astype(jnp.float32)
    )
    correct_local = jnp.sum(upstream * difference, axis=(0, 1, 3))
    result_grad = jnp.einsum("i,gtid->gtd", correct, upstream, precision=HIGHEST).reshape(
        row_count, model_width
    )
    result_low = result_grad.astype(jnp.bfloat16)
    down_grad = jnp.einsum("rf,rd->fd", inner_low, result_low, preferred_element_type=jnp.float32)
    inner_grad = jnp.einsum("rd,fd->rf", result_low, down_w, preferred_element_type=jnp.float32)
    gate_grad, up_grad = inner_pull(inner_grad)
    gate_low = gate_grad.astype(jnp.bfloat16)
    up_low = up_grad.astype(jnp.bfloat16)
    gate_w_grad = jnp.einsum(
        "rd,rf->df", normed_two_low, gate_low, preferred_element_type=jnp.float32
    )
    up_w_grad = jnp.einsum("rd,rf->df", normed_two_low, up_low, preferred_element_type=jnp.float32)
    normed_two_grad = jnp.einsum(
        "rf,df->rd", gate_low, gate_w, preferred_element_type=jnp.float32
    ) + jnp.einsum("rf,df->rd", up_low, up_w, preferred_element_type=jnp.float32)
    hidden_norm_grad, gain_two_grad = rms_backward(hidden, factor_two, gain_second, normed_two_grad)
    hidden_grad = result_grad + hidden_norm_grad
    hidden_low = hidden_grad.astype(jnp.bfloat16)
    out_w_grad = jnp.einsum(
        "rc,rd->cd", attended_low, hidden_low, preferred_element_type=jnp.float32
    )
    attended_grad = jnp.einsum(
        "rd,cd->rc", hidden_low, out_w, preferred_element_type=jnp.float32
    ).astype(jnp.bfloat16)
    delta_sum = jnp.swapaxes(
        jnp.sum(
            split_heads(
                (attended_grad.astype(jnp.float32) * attended).reshape(
                    groups, local_len, model_width
                )
            ),
            axis=-1,
        ),
        1,
        2,
    )
    grad_local = attended_grad.reshape(groups, local_len, model_width)
    zero_grad = jnp.zeros((groups, local_len, model_width), jnp.float32)
    all_keys, all_values = (
        lax.all_gather(key_rows, "ctx", axis=1, tiled=True),
        lax.all_gather(values, "ctx", axis=1, tiled=True),
    )

    def query_step(current, block_index):
        begin = block_index * local_len
        key_part = lax.dynamic_slice_in_dim(all_keys, begin, local_len, 1)
        value_part = lax.dynamic_slice_in_dim(all_values, begin, local_len, 1)
        key_place = lax.dynamic_slice_in_dim(places, begin, local_len, 1)
        key_segment = lax.dynamic_slice_in_dim(segments, begin, local_len, 1)
        allowed = visible(own_place, own_segment, key_place, key_segment)

        def query_compute(query_sum):
            prob_low, score_grad = backward_block(
                queries, grad_local, key_part, value_part, allowed, maximum, denominator, delta_sum
            )
            return query_sum + jnp.einsum(
                "ghqk,gkhd->gqhd",
                score_grad,
                split_heads(key_part),
                preferred_element_type=jnp.float32,
            ).reshape(groups, local_len, model_width)

        return (
            lax.cond(jnp.any(allowed), query_compute, lambda query_sum: query_sum, current),
            None,
        )

    finished, unused = lax.scan(
        query_step, zero_grad, jnp.arange(group_len // local_len, dtype=jnp.int32)
    )
    term_rows = local_len * lax.axis_size("ctx")
    key_block_size = math.gcd(term_rows, local_len)

    def key_one_block(block_index):
        begin = block_index * key_block_size
        key_part = lax.dynamic_slice_in_dim(all_keys, begin, key_block_size, 1)
        value_part = lax.dynamic_slice_in_dim(all_values, begin, key_block_size, 1)
        key_place = lax.dynamic_slice_in_dim(places, begin, key_block_size, 1)
        key_segment = lax.dynamic_slice_in_dim(segments, begin, key_block_size, 1)
        allowed = visible(own_place, own_segment, key_place, key_segment)

        def one_compute(unused_arg):
            prob_low, score_grad = backward_block(
                queries, grad_local, key_part, value_part, allowed, maximum, denominator, delta_sum
            )
            key_add = jnp.einsum(
                "ghqk,gqhd->kghd",
                score_grad,
                split_heads(queries),
                preferred_element_type=jnp.float32,
            ).reshape(key_block_size, groups, model_width)
            value_add = jnp.einsum(
                "ghqk,gqhd->kghd",
                prob_low,
                split_heads(grad_local),
                preferred_element_type=jnp.float32,
            ).reshape(key_block_size, groups, model_width)
            return jnp.stack([key_add, value_add], axis=1)

        return lax.cond(
            jnp.any(allowed),
            one_compute,
            lambda unused_arg: jnp.zeros((key_block_size, 2, groups, model_width), jnp.float32),
            0,
        )

    summed = lax.psum_scatter(
        lax.map(key_one_block, jnp.arange(term_rows // key_block_size, dtype=jnp.int32))
        .reshape(term_rows, 2, groups, model_width)
        .astype(jnp.bfloat16),
        "ctx",
        scatter_dimension=0,
        tiled=True,
    ).astype(jnp.float32)
    key_grad = jnp.swapaxes(summed[:, 0], 0, 1)
    value_grad = jnp.swapaxes(summed[:, 1], 0, 1)
    query_low = finished.reshape(row_count, model_width).astype(jnp.bfloat16)
    key_low = key_grad.reshape(row_count, model_width).astype(jnp.bfloat16)
    value_low = value_grad.reshape(row_count, model_width).astype(jnp.bfloat16)
    query_w_grad = jnp.einsum(
        "rc,rd->cd", normed_low, query_low, preferred_element_type=jnp.float32
    )
    key_w_grad = jnp.einsum("rc,rd->cd", normed_low, key_low, preferred_element_type=jnp.float32)
    value_w_grad = jnp.einsum(
        "rc,rd->cd", normed_low, value_low, preferred_element_type=jnp.float32
    )
    normed_grad = (
        jnp.einsum("rd,cd->rc", query_low, query_w, preferred_element_type=jnp.float32)
        + jnp.einsum("rd,cd->rc", key_low, key_w, preferred_element_type=jnp.float32)
        + jnp.einsum("rd,cd->rc", value_low, value_w, preferred_element_type=jnp.float32)
    )
    active_norm_grad, gain_one_grad = rms_backward(active, factor_one, gain_first, normed_grad)
    active_grad = (hidden_grad + active_norm_grad - result_grad).reshape(
        groups, local_len, 1, model_width
    )
    mixed_grad = jnp.concatenate([upstream[:, :, :1] + active_grad, upstream[:, :, 1:]], axis=2)
    predict_local = jnp.einsum("gtid,gtjd->ij", mixed_grad, inputs, precision=HIGHEST)
    states_grad = jnp.einsum("ij,gtid->gtjd", predict, mixed_grad, precision=HIGHEST).astype(
        jnp.bfloat16
    )
    predict_grad, correct_grad = lax.psum((predict_local, correct_local), ("ctx", "wsh"))
    (
        gain_one_rows,
        query_rows,
        key_grad_rows,
        value_rows,
        out_rows,
        gain_two_rows,
        gate_rows,
        up_rows,
        down_rows,
    ) = (
        lax.psum_scatter(
            gain_one_grad.astype(jnp.bfloat16), "wsh", scatter_dimension=0, tiled=True
        ).astype(jnp.float32),
        lax.psum_scatter(
            query_w_grad.astype(jnp.bfloat16), "wsh", scatter_dimension=0, tiled=True
        ).astype(jnp.float32),
        lax.psum_scatter(
            key_w_grad.astype(jnp.bfloat16), "wsh", scatter_dimension=0, tiled=True
        ).astype(jnp.float32),
        lax.psum_scatter(
            value_w_grad.astype(jnp.bfloat16), "wsh", scatter_dimension=0, tiled=True
        ).astype(jnp.float32),
        lax.psum_scatter(
            out_w_grad.astype(jnp.bfloat16), "wsh", scatter_dimension=0, tiled=True
        ).astype(jnp.float32),
        lax.psum_scatter(
            gain_two_grad.astype(jnp.bfloat16), "wsh", scatter_dimension=0, tiled=True
        ).astype(jnp.float32),
        lax.psum_scatter(
            gate_w_grad.astype(jnp.bfloat16), "wsh", scatter_dimension=0, tiled=True
        ).astype(jnp.float32),
        lax.psum_scatter(
            up_w_grad.astype(jnp.bfloat16), "wsh", scatter_dimension=0, tiled=True
        ).astype(jnp.float32),
        lax.psum_scatter(
            down_grad.astype(jnp.bfloat16), "wsh", scatter_dimension=0, tiled=True
        ).astype(jnp.float32),
    )
    totals = (
        lax.psum(gain_one_rows.astype(jnp.bfloat16), "ctx").astype(jnp.float32),
        lax.psum(query_rows.astype(jnp.bfloat16), "ctx").astype(jnp.float32),
        lax.psum(key_grad_rows.astype(jnp.bfloat16), "ctx").astype(jnp.float32),
        lax.psum(value_rows.astype(jnp.bfloat16), "ctx").astype(jnp.float32),
        lax.psum(out_rows.astype(jnp.bfloat16), "ctx").astype(jnp.float32),
        lax.psum(gain_two_rows.astype(jnp.bfloat16), "ctx").astype(jnp.float32),
        lax.psum(gate_rows.astype(jnp.bfloat16), "ctx").astype(jnp.float32),
        lax.psum(up_rows.astype(jnp.bfloat16), "ctx").astype(jnp.float32),
        lax.psum(down_rows.astype(jnp.bfloat16), "ctx").astype(jnp.float32),
    )
    return (new_states, states_grad, predict_grad, correct_grad) + tuple(totals)


MESH = pl.DeviceIdType.MESH
F32 = jnp.float32
BF16 = jnp.bfloat16
CHIPS = 4
VMEM_LIMIT = 60 * 2**20
DMA = pltpu.SemaphoreType.DMA


def place_on_mesh():
    ctx = lax.axis_index("ctx")
    depth = lax.axis_index("wsh")
    chip = ctx // 2
    core = ctx % 2
    chip_x = chip + 1 - 2 * (chip % 2)
    chip_y = chip + 2 - 4 * (chip // 2)
    return depth, chip, core, chip_x, chip_y, 3 - chip


def signal_and_wait(devices):
    barrier = pltpu.get_barrier_semaphore()
    for device in devices:
        pl.semaphore_signal(barrier, inc=1, device_id=device, device_id_type=MESH)
    pl.semaphore_wait(barrier, len(devices))


def remote(src, dst, send, recv, index, device):
    return pltpu.make_async_remote_copy(
        src_ref=src,
        dst_ref=dst,
        send_sem=send.at[index],
        recv_sem=recv.at[index],
        device_id=device,
        device_id_type=MESH,
    )


def comm_params(collective_id):
    return pltpu.CompilerParams(
        collective_id=collective_id, has_side_effects=True, vmem_limit_bytes=VMEM_LIMIT
    )


ANY = pl.BlockSpec(memory_space=pl.ANY)
VM = pl.BlockSpec(memory_space=pltpu.VMEM)
SM = pl.BlockSpec(memory_space=pltpu.SMEM)


def ring_sends(own, out, slot_of, chip, core, depth, chip_x, chip_y, send, recv):
    half = own.shape[0] // 2
    top, low = pl.ds(0, half), pl.ds(half, half)
    dev_x, dev_y = (2 * chip_x + core, depth), (2 * chip_y + core, depth)
    here = slot_of(chip)
    return [
        remote(own.at[top], out.at[here, top], send, recv, 0, dev_x),
        remote(own.at[low], out.at[here, low], send, recv, 1, dev_y),
        remote(own.at[low], out.at[here, low], send, recv, 2, dev_x),
        remote(own.at[top], out.at[here, top], send, recv, 3, dev_y),
        remote(out.at[slot_of(chip_x), top], out.at[slot_of(chip_x), top], send, recv, 4, dev_y),
        remote(out.at[slot_of(chip_y), low], out.at[slot_of(chip_y), low], send, recv, 5, dev_x),
    ]


NT = (((1,), (1,)), ((), ()))
TILE = 256
LOCAL_HEADS = HEADS // CHIPS
CHIP_COLS = LOCAL_HEADS * HD


def head_mask(rows, head):
    lane = lax.broadcasted_iota(jnp.int32, (rows, CHIP_COLS), 1)
    return (lane >= head * HD) & (lane < (head + 1) * HD)


def spread_rows(pieces, target):
    depths, cores, rows, _ = pieces.shape
    half = rows // target.shape[0]
    for i in range(target.shape[0]):
        for z in range(depths):
            for c in range(cores):
                at = (z * cores + c) * half
                target[i, at : at + half, :] = pieces[z, c, i * half : (i + 1) * half, :]


def aligned(index, size):
    return pl.ds(pl.multiple_of(index * size, size), size)


def pair_blocks(slots_ref, pair, per_device):
    core = lax.axis_index("ctx") % 2
    pairs = per_device // 2
    slot = (pair // pairs) * (2 * per_device) + core * per_device + 2 * (pair % pairs)
    one, two = slots_ref[slot], slots_ref[slot + 1]
    second = (one >= PROMPT // BLK).astype(jnp.int32)
    return slot, second, jnp.minimum(one, two), jnp.maximum(one, two)


def tile_tables(kind, step, slots_ref, lengths_ref, per_device):
    lane = lax.broadcasted_iota(jnp.int32, (1, TILE), 1)
    high = jnp.zeros((1, TILE), jnp.int32)
    local = []
    per_tile = TILE // BLK
    for i in range(per_tile):
        pair = step * per_tile + i
        _, second, prompt, cont = pair_blocks(slots_ref, pair, per_device)
        block = prompt if kind == 0 else cont
        local.append(2 * pair + (second if kind == 0 else 1 - second))
        high = jnp.where(lane >= i * BLK, (block - i) * BLK + lane, high)
    low = jnp.zeros((1, TILE), jnp.int32)
    if kind == 1:
        start = PROMPT
        for i in range(lengths_ref.shape[0]):
            low = jnp.where(high >= start, start, low)
            start = start + lengths_ref[i]
    return local, low, high


def attention_forward(all_rows, weights, slots, lengths):
    tokens, width = all_rows.shape
    queries = tokens // 2
    tiles = queries // TILE
    blocks = tokens // BLK
    per_device = blocks // (2 * CHIPS)

    def kernel(
        slots_ref, lengths_ref, x_ref, w_ref,
        att_ref, oT_ref, q_ref, k_ref, v_ref, lse_ref, slot_of, w_all, xs, xq, vT, s_ref, p_ref,
    ):
        def place_slot(s, _):
            slot_of[slots_ref[s]] = s
            return 0

        lax.fori_loop(0, blocks, place_slot, 0)
        spread_rows(w_ref, w_all)
        def gather_block(b, _):
            xs[aligned(b, BLK), :] = x_ref[aligned(slot_of[b], BLK), :]
            return 0

        lax.fori_loop(0, blocks, gather_block, 0)

        def gather_query(pair, _):
            slot, second, _, _ = pair_blocks(slots_ref, pair, per_device)
            xq[aligned(pair, BLK), :] = x_ref[aligned(slot + second, BLK), :]
            xq[aligned(pair + queries // (2 * BLK), BLK), :] = x_ref[
                aligned(slot + 1 - second, BLK), :
            ]
            return 0

        lax.fori_loop(0, queries // (2 * BLK), gather_query, 0)

        def project_keys(i, _):
            rows = aligned(i, TILE)
            x = xs[rows, :]
            k_ref[rows, :] = jnp.dot(x, w_all[1], preferred_element_type=F32).astype(BF16)
            v = jnp.dot(x, w_all[2], preferred_element_type=F32).astype(BF16)
            v_ref[rows, :] = v
            vT[:, rows] = v.T
            return 0

        lax.fori_loop(0, tokens // TILE, project_keys, 0)

        def project_queries(i, _):
            rows = aligned(i, TILE)
            q_ref[rows, :] = jnp.dot(xq[rows, :], w_all[0], preferred_element_type=F32).astype(BF16)
            return 0

        lax.fori_loop(0, tiles, project_queries, 0)

        for kind in range(2):
            key_tiles = (PROMPT if kind == 0 else tokens) // TILE
            first_masked = 0 if kind == 0 else PROMPT // TILE

            def one_tile(step, _):
                tile = kind * (tiles // 2) + step
                q = q_ref[aligned(tile, TILE), :]
                local, q_low, q_high = tile_tables(kind, step, slots_ref, lengths_ref, per_device)
                for head in range(LOCAL_HEADS):
                    q_head = jnp.where(head_mask(TILE, head), q, jnp.zeros_like(q))
                    top = jnp.full((1, TILE), NEGATIVE, F32)
                    for k_tile in range(key_tiles):
                        rows = pl.ds(k_tile * TILE, TILE)
                        s = lax.dot_general(k_ref[rows, :], q_head, NT, preferred_element_type=F32)
                        if k_tile >= first_masked:
                            place = lax.broadcasted_iota(jnp.int32, (TILE, TILE), 0) + k_tile * TILE
                            seen = (place >= q_low) & (place <= q_high)
                            s = jnp.where(seen, s, NEGATIVE)
                        s_ref[rows, :] = s
                        top = jnp.maximum(top, jnp.max(s, axis=0, keepdims=True))
                    total = jnp.zeros((1, TILE), F32)
                    for k_tile in range(key_tiles):
                        rows = pl.ds(k_tile * TILE, TILE)
                        p = jnp.exp(s_ref[rows, :] - top)
                        total = total + jnp.sum(p, axis=0, keepdims=True)
                        p_ref[rows, :] = p.astype(BF16)
                    keys = key_tiles * TILE
                    out = jnp.dot(
                        vT[head * HD : (head + 1) * HD, :keys],
                        p_ref[:keys, :],
                        preferred_element_type=F32,
                    )
                    oT_ref[tile, head * HD : (head + 1) * HD, :] = out / total
                    lse_ref[tile, head] = top + jnp.log(total)
                att = oT_ref[tile].T.astype(BF16)
                for b in range(TILE // BLK):
                    att_ref[aligned(local[b], BLK), :] = att[b * BLK : (b + 1) * BLK]
                return 0

            lax.fori_loop(0, tiles // 2, one_tile, 0)

    return pl.pallas_call(
        kernel,
        out_shape=[
            jax.ShapeDtypeStruct((queries, CHIP_COLS), BF16),
            jax.ShapeDtypeStruct((tiles, CHIP_COLS, TILE), F32),
            jax.ShapeDtypeStruct((queries, CHIP_COLS), BF16),
            jax.ShapeDtypeStruct((tokens, CHIP_COLS), BF16),
            jax.ShapeDtypeStruct((tokens, CHIP_COLS), BF16),
            jax.ShapeDtypeStruct((tiles, LOCAL_HEADS, 1, TILE), F32),
        ],
        in_specs=[SM, SM, VM, VM],
        out_specs=[VM] * 6,
        scratch_shapes=[
            pltpu.SMEM((blocks,), jnp.int32),
            pltpu.VMEM((3, width, CHIP_COLS), BF16),
            pltpu.VMEM((tokens, width), BF16),
            pltpu.VMEM((queries, width), BF16),
            pltpu.VMEM((CHIP_COLS, tokens), BF16),
            pltpu.VMEM((tokens, TILE), F32),
            pltpu.VMEM((tokens, TILE), BF16),
        ],
        compiler_params=pltpu.CompilerParams(vmem_limit_bytes=VMEM_LIMIT),
        cost_estimate=pl.CostEstimate(
            flops=8 * queries * tokens * CHIP_COLS, bytes_accessed=12 * tokens * width, transcendentals=queries * tokens
        ),
        name="attention_forward",
    )(slots, lengths, all_rows, weights)


def attention_backward(att_grad, saved, slots, lengths):
    oT, q, k, v, lse = saved
    queries = att_grad.shape[0]
    tokens = k.shape[0]
    tiles = queries // TILE
    blocks = tokens // BLK
    per_device = blocks // (2 * CHIPS)
    wide = LOCAL_HEADS * TILE

    def kernel(
        slots_ref, lengths_ref, g_ref, oT_ref, q_ref, k_ref, v_ref, lse_ref,
        dq_ref, dk_ref, dv_ref, hq, kT, doT, dqT, q_stack, do_stack, p_buf, ds_buf, dk_acc, dv_acc,
    ):
        def gather_query(pair, _):
            _, second, _, _ = pair_blocks(slots_ref, pair, per_device)
            hq[aligned(pair, BLK), :] = g_ref[aligned(2 * pair + second, BLK), :]
            hq[aligned(pair + queries // (2 * BLK), BLK), :] = g_ref[
                aligned(2 * pair + 1 - second, BLK), :
            ]
            return 0

        lax.fori_loop(0, queries // (2 * BLK), gather_query, 0)

        def transpose_keys(i, _):
            rows = aligned(i, TILE)
            kT[:, rows] = k_ref[rows, :].T
            return 0

        lax.fori_loop(0, tokens // TILE, transpose_keys, 0)

        for kind in (1, 0):
            key_tiles = (PROMPT if kind == 0 else tokens) // TILE
            first_masked = 0 if kind == 0 else PROMPT // TILE

            def one_tile(step, _):
                tile = kind * (tiles // 2) + step
                q_tile = q_ref[aligned(tile, TILE), :]
                local, q_low, q_high = tile_tables(kind, step, slots_ref, lengths_ref, per_device)
                do_tile = hq[aligned(tile, TILE), :]
                doT[...] = do_tile.astype(F32).T * oT_ref[tile]
                for head in range(LOCAL_HEADS):
                    lanes = pl.ds(head * TILE, TILE)
                    heads = pl.ds(head * HD, HD)
                    mask = head_mask(TILE, head)
                    q_head = jnp.where(mask, q_tile, jnp.zeros_like(q_tile))
                    do_head = jnp.where(mask, do_tile, jnp.zeros_like(do_tile))
                    q_stack[lanes, :] = q_head
                    do_stack[lanes, :] = do_head
                    delta = jnp.sum(doT[heads, :], axis=0, keepdims=True)
                    norm = lse_ref[tile, head]
                    for k_tile in range(key_tiles):
                        rows = pl.ds(k_tile * TILE, TILE)
                        s = lax.dot_general(k_ref[rows, :], q_head, NT, preferred_element_type=F32)
                        dp = lax.dot_general(v_ref[rows, :], do_head, NT, preferred_element_type=F32)
                        p = jnp.exp(s - norm)
                        if k_tile >= first_masked:
                            place = lax.broadcasted_iota(jnp.int32, (TILE, TILE), 0) + k_tile * TILE
                            seen = (place >= q_low) & (place <= q_high)
                            p = jnp.where(seen, p, 0.0)
                        p_buf[rows, lanes] = p.astype(BF16)
                        ds_buf[rows, lanes] = (p * (dp - delta)).astype(BF16)
                    keys = key_tiles * TILE
                    dqT[heads, :] = jnp.dot(
                        kT[heads, :keys], ds_buf[:keys, lanes], preferred_element_type=F32
                    )
                for k_tile in range(key_tiles):
                    rows = pl.ds(k_tile * TILE, TILE)
                    dv = jnp.dot(p_buf[rows, :], do_stack[...], preferred_element_type=F32)
                    dk = jnp.dot(ds_buf[rows, :], q_stack[...], preferred_element_type=F32)
                    if kind == 1:
                        fresh = step == 0
                        dv = dv + jnp.where(fresh, 0.0, dv_acc[rows, :])
                        dk = dk + jnp.where(fresh, 0.0, dk_acc[rows, :])
                    else:
                        dv = dv + dv_acc[rows, :]
                        dk = dk + dk_acc[rows, :]
                    dv_acc[rows, :] = dv
                    dk_acc[rows, :] = dk
                dq = dqT[...].T.astype(BF16)
                for b in range(TILE // BLK):
                    dq_ref[aligned(local[b], BLK), :] = dq[b * BLK : (b + 1) * BLK]
                return 0

            lax.fori_loop(0, tiles // 2, one_tile, 0)

        def give_block(slot, _):
            block = aligned(slots_ref[slot], BLK)
            dk_ref[aligned(slot, BLK), :] = dk_acc[block, :].astype(BF16)
            dv_ref[aligned(slot, BLK), :] = dv_acc[block, :].astype(BF16)
            return 0

        lax.fori_loop(0, blocks, give_block, 0)

    return pl.pallas_call(
        kernel,
        out_shape=[
            jax.ShapeDtypeStruct((queries, CHIP_COLS), BF16),
            jax.ShapeDtypeStruct((tokens, CHIP_COLS), BF16),
            jax.ShapeDtypeStruct((tokens, CHIP_COLS), BF16),
        ],
        in_specs=[SM, SM] + [VM] * 6,
        out_specs=[VM] * 3,
        scratch_shapes=[
            pltpu.VMEM((queries, CHIP_COLS), BF16),
            pltpu.VMEM((CHIP_COLS, tokens), BF16),
            pltpu.VMEM((CHIP_COLS, TILE), F32),
            pltpu.VMEM((CHIP_COLS, TILE), F32),
            pltpu.VMEM((wide, CHIP_COLS), BF16),
            pltpu.VMEM((wide, CHIP_COLS), BF16),
            pltpu.VMEM((tokens, wide), BF16),
            pltpu.VMEM((tokens, wide), BF16),
            pltpu.VMEM((tokens, CHIP_COLS), F32),
            pltpu.VMEM((tokens, CHIP_COLS), F32),
        ],
        compiler_params=pltpu.CompilerParams(vmem_limit_bytes=VMEM_LIMIT),
        cost_estimate=pl.CostEstimate(
            flops=20 * queries * tokens * CHIP_COLS, bytes_accessed=20 * tokens * CHIP_COLS, transcendentals=queries * tokens
        ),
        name="attention_backward",
    )(slots, lengths, att_grad, oT, q, k, v, lse)


TN = (((0,), (0,)), ((), ()))
ROWS = 32


def norm_factor(rows):
    return lax.rsqrt(jnp.mean(rows * rows, axis=1, keepdims=True) + EPSILON)


def as_column(row):
    return jnp.broadcast_to(row, (8, row.shape[1])).T[:, 0:1]


def mix(states_ref, at, p_ref, i):
    return p_ref[i, 0] * states_ref[at, 0, :].astype(F32) + p_ref[i, 1] * states_ref[at, 1, :].astype(F32)


def prepare(states, predict, valid, gain_one, gain_two, w_query, w_key, w_value, w_gate, w_up, w_down):
    rows, _, width = states.shape
    shard = w_query.shape[0]
    half = shard // 2
    hidden_cols = w_gate.shape[1]
    columns = hidden_cols // CHIPS
    depths = width // shard
    split = columns // depths

    def kernel(
        s_ref, p_ref, v_ref, g1_ref, g2_ref, q_ref, k_ref, vw_ref, gate_ref, up_ref, down_ref,
        pre_ref, qkv_ref, ff_ref, count_ref, buf, wide, sems,
    ):
        _, chip, core, _, _, _ = place_on_mesh()
        mine = pl.ds(core * half, half)
        loads = [
            pltpu.make_async_copy(w.at[mine], buf.at[i], sems.at[i])
            for i, w in enumerate((q_ref, k_ref, vw_ref))
        ] + [
            pltpu.make_async_copy(gate_ref.at[mine], wide.at[0], sems.at[3]),
            pltpu.make_async_copy(up_ref.at[mine], wide.at[1], sems.at[4]),
            pltpu.make_async_copy(
                down_ref.at[pl.ds(chip * split + core * (split // 2), half)],
                ff_ref.at[pl.ds(2 * half, half)],
                sems.at[5],
            ),
        ]
        for copy in loads:
            copy.start()
        count_ref[...] = jnp.broadcast_to(
            jnp.sum(v_ref[...].astype(F32), axis=1, keepdims=True), count_ref.shape
        )

        def norm(i, _):
            at = aligned(i, ROWS)
            active = mix(s_ref, at, p_ref, 0)
            pre_ref[at, :] = (active * norm_factor(active)).astype(BF16)
            return 0

        lax.fori_loop(0, rows // ROWS, norm, 0)

        def gain_column(ref):
            both = jnp.broadcast_to(ref[...].astype(F32), (8, shard)).T
            return jnp.where(core == 0, both[:half, 0:1], both[half:, 0:1])

        one, two = gain_column(g1_ref), gain_column(g2_ref)
        for copy in loads:
            copy.wait()
        for p in range(CHIPS):

            @pl.when(chip == p)
            def _(p=p):
                for i in range(3):
                    cols = buf[i, :, p * CHIP_COLS : (p + 1) * CHIP_COLS]
                    qkv_ref[i * half : (i + 1) * half, :] = (cols.astype(F32) * one).astype(BF16)
                for i in range(2):
                    cols = jnp.concatenate(
                        [
                            wide[i, :, (z * CHIPS + p) * split : (z * CHIPS + p + 1) * split].astype(F32)
                            for z in range(depths)
                        ],
                        axis=1,
                    )
                    ff_ref[i * half : (i + 1) * half, :] = (cols * two).astype(BF16)

    return pl.pallas_call(
        kernel,
        out_shape=[
            jax.ShapeDtypeStruct((rows, width), BF16),
            jax.ShapeDtypeStruct((3 * half, CHIP_COLS), BF16),
            jax.ShapeDtypeStruct((3 * half, columns), BF16),
            jax.ShapeDtypeStruct((8, 128), F32),
        ],
        in_specs=[VM, SM] + [VM] * 3 + [ANY] * 6,
        out_specs=[VM] * 4,
        scratch_shapes=[
            pltpu.VMEM((3, half, width), BF16),
            pltpu.VMEM((2, half, hidden_cols), BF16),
            DMA((6,)),
        ],
        compiler_params=pltpu.CompilerParams(vmem_limit_bytes=VMEM_LIMIT),
        name="prepare",
    )(states, predict, valid, gain_one, gain_two, w_query, w_key, w_value, w_gate, w_up, w_down)


def plane_peers(chip, core, depth, chip_x, chip_y, chip_d):
    same = [(2 * c + core, depth) for c in (chip_x, chip_y, chip_d)]
    return same + [(2 * c + 1 - core, depth) for c in (chip, chip_x, chip_y, chip_d)]


def total_over_mesh(own_ref, arrived, staged, far, across, peers, bsend, brecv, csend, crecv):
    first = [remote(own_ref, arrived.at[i], bsend, brecv, i, d) for i, d in enumerate(across)]
    second = [remote(staged, far.at[i], csend, crecv, i, d) for i, d in enumerate(peers)]

    def start():
        for copy in first:
            copy.start()

    def turn():
        total = own_ref[...]
        for i, copy in enumerate(first):
            copy.wait_recv()
        for i in range(len(first)):
            total = total + arrived[i]
        staged[...] = total
        for copy in second:
            copy.start()

    def end():
        for copy in second:
            copy.wait_recv()
        total = staged[...]
        for i in range(len(second)):
            total = total + far[i]
        for copy in first + second:
            copy.wait_send()
        return total

    return start, turn, end


def total_scratch(shape, depths):
    return [
        pltpu.VMEM((depths - 1,) + shape, F32),
        pltpu.VMEM(shape, F32),
        pltpu.VMEM((2 * CHIPS - 1,) + shape, F32),
        DMA((depths - 1,)),
        DMA((depths - 1,)),
        DMA((2 * CHIPS - 1,)),
        DMA((2 * CHIPS - 1,)),
    ]


def gather_inputs(pre, qkv, w_out, count, collective_id):
    depths = lax.axis_size("wsh")
    out_rows = w_out.shape[0] // CHIPS

    def kernel(
        x_ref, w_ref, o_ref, c_ref, out_ref, wall_ref, oall_ref, total_ref,
        send, recv, wsend, wrecv, osend, orecv, ssend, srecv, local, *total_refs,
    ):
        depth, chip, core, chip_x, chip_y, chip_d = place_on_mesh()
        other = (2 * chip + 1 - core, depth)
        across = [
            (2 * chip + core, lax.rem(depth + step, depths)) for step in range(1, depths)
        ]
        peers = plane_peers(chip, core, depth, chip_x, chip_y, chip_d)
        signal_and_wait(peers + across)

        def slot(chip_index):
            return 2 * chip_index + core

        start, turn, end = total_over_mesh(c_ref, *total_refs[:3], across, peers, *total_refs[3:])
        start()
        copies = ring_sends(
            x_ref, out_ref, slot, chip, core, depth, chip_x, chip_y, send, recv
        )
        for copy in copies[:4]:
            copy.start()
        w_copies = [
            remote(w_ref, wall_ref.at[depth, core], wsend, wrecv, i, device)
            for i, device in enumerate(across)
        ]
        out_mine = o_ref.at[pl.ds(chip * out_rows, out_rows)]
        o_copies = [
            remote(out_mine, oall_ref.at[depth], osend, orecv, i, device)
            for i, device in enumerate(across)
        ]
        for copy in w_copies + o_copies:
            copy.start()

        def shared(index, ref, source=None):
            return remote(ref if source is None else source, ref, ssend, srecv, index, other)

        to_other = [
            shared(0, out_ref.at[slot(chip)], x_ref),
            shared(1, out_ref.at[slot(chip_x)]),
            shared(2, out_ref.at[slot(chip_y)]),
            shared(3, out_ref.at[slot(chip_d)]),
            shared(4, wall_ref.at[depth, core], w_ref),
        ] + [
            shared(5 + i, wall_ref.at[lax.rem(depth + depths - 1 - i, depths), core])
            for i in range(depths - 1)
        ]
        to_other[0].start()
        to_other[4].start()
        mine = pltpu.make_async_copy(x_ref, out_ref.at[slot(chip)], local)
        mine.start()
        wall_ref[depth, core] = w_ref[...]
        oall_ref[depth] = o_ref[aligned(chip, out_rows), :]
        turn()
        copies[0].wait_recv()
        copies[4].start()
        copies[1].wait_recv()
        copies[5].start()
        for i in range(depths - 1):
            w_copies[i].wait_recv()
            to_other[5 + i].start()
        copies[2].wait_recv()
        to_other[1].start()
        copies[3].wait_recv()
        to_other[2].start()
        copies[4].wait_recv()
        copies[5].wait_recv()
        to_other[3].start()
        for copy in o_copies:
            copy.wait_recv()
        total_ref[...] = end()
        for copy in to_other:
            copy.wait()
        for copy in copies + w_copies + o_copies:
            copy.wait_send()
        mine.wait()

    return pl.pallas_call(
        kernel,
        out_shape=[
            jax.ShapeDtypeStruct((2 * CHIPS,) + pre.shape, BF16),
            jax.ShapeDtypeStruct((depths, 2) + qkv.shape, BF16),
            jax.ShapeDtypeStruct((depths, out_rows, w_out.shape[1]), BF16),
            jax.ShapeDtypeStruct(count.shape, F32),
        ],
        in_specs=[VM] * 4,
        out_specs=[ANY, VM, VM, VM],
        scratch_shapes=[
            DMA((6,)),
            DMA((6,)),
            DMA((depths - 1,)),
            DMA((depths - 1,)),
            DMA((depths - 1,)),
            DMA((depths - 1,)),
            DMA((depths + 4,)),
            DMA((depths + 4,)),
            DMA,
        ]
        + total_scratch(count.shape, depths),
        compiler_params=comm_params(collective_id),
        name="gather_inputs",
    )(pre, qkv, w_out, count)


def gelu_parts(v):
    scale = math.sqrt(2 / math.pi)
    square = v * v
    t = jnp.tanh(scale * v * (1.0 + 0.044715 * square))
    rise = 0.5 * (1.0 + t)
    return v * rise, rise + 0.5 * v * (1.0 - t * t) * scale * (1.0 + 0.134145 * square)


def middle(attended, out_pieces, ff_pieces, states, out_grad, teacher, valid, count, predict, correct, collective_id):
    rows, _, width = states.shape
    _, half, columns = ff_pieces[0].shape
    depths, out_rows, _ = out_pieces[0].shape
    shard = 2 * half
    blocks = rows // ROWS
    col_tiles = columns // TILE
    tokens = 2 * CHIPS * rows * depths

    def kernel(
        att_ref, o0, o1, o2, o3, f0, f1, f2, f3, f4, f5, s_ref, g_ref, t_ref, v_ref, n_ref, p_ref, c_ref,
        new_ref, up0_ref, up1_ref, hg_ref, da_ref, dw0_ref, dw1_ref, dw2_ref, dw3_ref, ff_ref, sums_ref,
        w_all, w_out, att_all, hidden, own, x_rows, r_rows, xT, innerT, inner, gate, up, gate_low, up_low,
        part0, part1, part2, got1, got2, dw, dw_other,
        wsend, wrecv, wlocal, olocal, send0, recv0, send1, recv1, send2, recv2, send3, recv3,
        ag1s, ag1r, ag2s, ag2r, dsend, drecv,
    ):
        depth, chip, core, chip_x, chip_y, chip_d = place_on_mesh()
        near = [(c, (2 * c + core, depth)) for c in (chip_x, chip_y, chip_d)]
        other = (2 * chip + 1 - core, depth)
        signal_and_wait([device for _, device in near] + [other])

        def exchange(source_of, target, send, recv):
            return [
                remote(source_of(c), target, send, recv, i, device)
                for i, (c, device) in enumerate(near)
            ]

        def ring(source, target, send, recv):
            return ring_sends(
                source, target, lambda c: c, chip, core, depth, chip_x, chip_y, send, recv
            )

        sends0 = exchange(lambda c: att_ref.at[c], att_all.at[chip], send0, recv0)
        for copy in sends0:
            copy.start()
        out_loads = [
            pltpu.make_async_copy(piece, w_out.at[:, c], olocal.at[i])
            for i, (piece, c) in enumerate(zip((o0, o1, o2, o3), (chip, chip_x, chip_y, chip_d)))
        ]
        for copy in out_loads:
            copy.start()
        sources = (
            (f0, 0, None),
            (f1, -1, depth >= 1),
            (f2, -2, depth >= 2),
            (f3, 1, depth <= depths - 2),
            (f4, 2, depth <= depths - 3),
            (f5, None, (depth == 0) | (depth == depths - 1)),
        )

        def each_source(act):
            for i, (ref, shift, present) in enumerate(sources):
                z = depths - 1 - depth if shift is None else depth + shift
                z = jnp.clip(z, 0, depths - 1)
                dst = w_all.at[:, z, core]
                copies = (
                    remote(ref, dst, wsend, wrecv, i, other),
                    pltpu.make_async_copy(ref, dst, wlocal.at[i]),
                )
                if present is None:
                    act(copies)
                else:

                    @pl.when(present)
                    def _(copies=copies):
                        act(copies)

        each_source(lambda copies: [copy.start() for copy in copies])
        att_all[chip] = att_ref[chip]
        for copy in out_loads:
            copy.wait()
        for copy in sends0:
            copy.wait_recv()

        def w_out_rows(p):
            return w_out[p].reshape(CHIP_COLS, width)

        for p in range(CHIPS):
            term = jnp.dot(att_all[p], w_out_rows(p), preferred_element_type=F32)
            hidden[...] = term if p == 0 else hidden[...] + term

        def first_norm(i, _):
            at = aligned(i, ROWS)
            h = hidden[at, :] + mix(s_ref, at, p_ref, 0)
            hidden[at, :] = h
            own[0, at, :] = (h * norm_factor(h)).astype(BF16)
            return 0

        lax.fori_loop(0, blocks, first_norm, 0)
        ring1 = ring(own.at[0], x_rows, ag1s, ag1r)
        for copy in ring1[:4]:
            copy.start()
        x_rows[chip] = own[0]
        each_source(lambda copies: [copy.wait() for copy in copies])

        def w_rows(i):
            return w_all[i].reshape(width, columns)

        def forward(c):
            x = x_rows[c]
            for n in range(col_tiles):
                cols = slice(n * TILE, (n + 1) * TILE)
                g = jnp.dot(x, w_rows(0)[:, cols], preferred_element_type=F32)
                u = jnp.dot(x, w_rows(1)[:, cols], preferred_element_type=F32)
                gate[c, :, cols] = g
                up[c, :, cols] = u
                inner[c, :, cols] = (gelu_parts(g)[0] * u).astype(BF16)
            return jnp.dot(inner[c], w_rows(2), preferred_element_type=F32)

        sends1 = [
            remote(part1.at[c], got1.at[i], send1, recv1, i, device) for i, (c, device) in enumerate(near)
        ]
        up0_ref[...] = forward(chip)
        ring1[0].wait_recv()
        ring1[4].start()
        ring1[1].wait_recv()
        ring1[5].start()
        for i, (c, _) in enumerate(near):
            if i < 2:
                ring1[2 + i].wait_recv()
            else:
                ring1[4].wait_recv()
                ring1[5].wait_recv()
            part1[c] = forward(c).astype(BF16)
            sends1[i].start()

        def turn(i, _):
            xT[:, aligned(i, rows)] = x_rows[i].T
            innerT[:, aligned(i, rows)] = inner[i].T
            return 0

        lax.fori_loop(0, CHIPS, turn, 0)
        weight = as_column(v_ref[...].astype(F32)) * (tokens / n_ref[0:1, 0:1])
        own_weight = part0
        own_weight[...] = jnp.broadcast_to(weight, own_weight.shape)
        for copy in sends1:
            copy.wait_recv()

        def outputs(i, sums):
            at = aligned(i, ROWS)
            a = mix(s_ref, at, p_ref, 0)
            result = hidden[at, :] + up0_ref[at, :]
            for j in range(3):
                result = result + got1[j, at, :].astype(F32)
            difference = result - a
            row_weight = own_weight[at, 0:1]
            c0, c1 = c_ref[0], c_ref[1]
            out0 = a + c0 * difference
            out1 = mix(s_ref, at, p_ref, 1) + c1 * difference
            new_ref[at, 0, :] = out0.astype(BF16)
            new_ref[at, 1, :] = out1.astype(BF16)
            up0 = g_ref[at, 0, :].astype(F32) + row_weight * (out0 - t_ref[at, 0, :].astype(F32))
            up1 = g_ref[at, 1, :].astype(F32) + row_weight * (out1 - t_ref[at, 1, :].astype(F32))
            up0_ref[at, :] = up0
            up1_ref[at, :] = up1
            own[1, at, :] = (c0 * up0 + c1 * up1).astype(BF16)
            return (
                sums[0] + jnp.sum(up0 * difference, axis=0, keepdims=True),
                sums[1] + jnp.sum(up1 * difference, axis=0, keepdims=True),
            )

        zero = jnp.zeros((1, width), F32)
        correct_sums = lax.fori_loop(0, blocks, outputs, (zero, zero))
        sums_ref[...] = jnp.zeros_like(sums_ref)
        sums_ref[2:3, :] = correct_sums[0]
        sums_ref[3:4, :] = correct_sums[1]

        ring2 = ring(own.at[1], r_rows, ag2s, ag2r)
        for copy in ring2[:4]:
            copy.start()
        r_rows[chip] = own[1]

        def backward(c):
            r = r_rows[c]
            for n in range(col_tiles):
                cols = slice(n * TILE, (n + 1) * TILE)
                inner_grad = lax.dot_general(r, w_rows(2)[cols, :], NT, preferred_element_type=F32)
                value, slope = gelu_parts(gate[c, :, cols])
                gate_low[c, :, cols] = (inner_grad * up[c, :, cols] * slope).astype(BF16)
                up_low[c, :, cols] = (inner_grad * value).astype(BF16)
            return lax.dot_general(
                gate_low[c], w_rows(0), NT, preferred_element_type=F32
            ) + lax.dot_general(up_low[c], w_rows(1), NT, preferred_element_type=F32)

        sends2 = [
            remote(part2.at[c], got2.at[i], send2, recv2, i, device) for i, (c, device) in enumerate(near)
        ]
        hg_ref[...] = backward(chip)
        ring2[0].wait_recv()
        ring2[4].start()
        ring2[1].wait_recv()
        ring2[5].start()
        for i, (c, _) in enumerate(near):
            if i < 2:
                ring2[2 + i].wait_recv()
            else:
                ring2[4].wait_recv()
                ring2[5].wait_recv()
            part2[c] = backward(c).astype(BF16)
            sends2[i].start()

        def weight_grads(z, _):
            at = aligned(z, shard)
            for i, (left, right) in enumerate(((xT, gate_low), (xT, up_low), (innerT, r_rows))):
                wide = jnp.dot(
                    left[at, :], right[...].reshape(CHIPS * rows, -1), preferred_element_type=F32
                ).astype(BF16)
                dw[z, 0, i * half : (i + 1) * half, :] = wide[:half]
                dw[z, 1, i * half : (i + 1) * half, :] = wide[half:]
            return 0

        lax.fori_loop(0, depths, weight_grads, 0)
        swap = remote(dw.at[:, 1 - core], dw_other, dsend, drecv, 0, other)
        swap.start()
        for copy in sends2:
            copy.wait_recv()

        def second_norm(i, gain_sum):
            at = aligned(i, ROWS)
            h = hidden[at, :]
            weighted = hg_ref[at, :]
            for j in range(3):
                weighted = weighted + got2[j, at, :].astype(F32)
            factor = norm_factor(h)
            mean = jnp.mean(weighted * h, axis=1, keepdims=True)
            result_grad = c_ref[0] * up0_ref[at, :] + c_ref[1] * up1_ref[at, :]
            hidden_grad = result_grad + (factor * weighted - h * (factor * factor * factor * mean))
            hg_ref[at, :] = hidden_grad
            own[2, at, :] = hidden_grad.astype(BF16)
            return gain_sum + jnp.sum(weighted * h * factor, axis=0, keepdims=True)

        sums_ref[1:2, :] = lax.fori_loop(0, blocks, second_norm, zero)

        sends3 = exchange(lambda c: att_all.at[CHIPS + c], da_ref.at[chip], send3, recv3)

        def att_grad(c):
            return lax.dot_general(own[2], w_out_rows(c), NT, preferred_element_type=F32).astype(BF16)

        for i in (2, 0, 1):
            att_all[CHIPS + near[i][0]] = att_grad(near[i][0])
            sends3[i].start()
        da_ref[chip] = att_grad(chip)
        for c, ref in zip((chip, chip_x, chip_y, chip_d), (dw0_ref, dw1_ref, dw2_ref, dw3_ref)):
            ref[...] = jnp.dot(att_all[c].T, own[2], preferred_element_type=F32).astype(BF16)
        swap.wait_recv()

        def add_cores(z, _):
            ff_ref[z] = (dw[z, core].astype(F32) + dw_other[z].astype(F32)).astype(BF16)
            return 0

        lax.fori_loop(0, depths, add_cores, 0)
        for copy in sends3:
            copy.wait_recv()
        for copy in sends0 + sends1 + sends2 + sends3 + ring1 + ring2 + [swap]:
            copy.wait_send()

    block = (rows, width)
    pair = (rows, 2, width)
    wide_rows = (CHIPS, rows, width)
    hid_rows = (CHIPS, rows, columns)
    return pl.pallas_call(
        kernel,
        out_shape=[
            jax.ShapeDtypeStruct(pair, BF16),
            jax.ShapeDtypeStruct(block, F32),
            jax.ShapeDtypeStruct(block, F32),
            jax.ShapeDtypeStruct(block, F32),
            jax.ShapeDtypeStruct((CHIPS, rows, CHIP_COLS), BF16),
            jax.ShapeDtypeStruct((CHIP_COLS, width), BF16),
            jax.ShapeDtypeStruct((CHIP_COLS, width), BF16),
            jax.ShapeDtypeStruct((CHIP_COLS, width), BF16),
            jax.ShapeDtypeStruct((CHIP_COLS, width), BF16),
            jax.ShapeDtypeStruct((depths, 3 * half, columns), BF16),
            jax.ShapeDtypeStruct((8, width), F32),
        ],
        in_specs=[VM] + [ANY] * 10 + [VM] * 5 + [SM] * 2,
        out_specs=[VM] * 11,
        scratch_shapes=[
            pltpu.VMEM((3, depths, 2, half, columns), BF16),
            pltpu.VMEM((depths, CHIPS, out_rows, width), BF16),
            pltpu.VMEM((2 * CHIPS, rows, CHIP_COLS), BF16),
            pltpu.VMEM(block, F32),
            pltpu.VMEM((3,) + block, BF16),
            pltpu.VMEM(wide_rows, BF16),
            pltpu.VMEM(wide_rows, BF16),
            pltpu.VMEM((width, CHIPS * rows), BF16),
            pltpu.VMEM((columns, CHIPS * rows), BF16),
            pltpu.VMEM(hid_rows, BF16),
            pltpu.VMEM(hid_rows, F32),
            pltpu.VMEM(hid_rows, F32),
            pltpu.VMEM(hid_rows, BF16),
            pltpu.VMEM(hid_rows, BF16),
            pltpu.VMEM((rows, 128), F32),
            pltpu.VMEM(wide_rows, BF16),
            pltpu.VMEM(wide_rows, BF16),
            pltpu.VMEM((3,) + block, BF16),
            pltpu.VMEM((3,) + block, BF16),
            pltpu.VMEM((depths, 2, 3 * half, columns), BF16),
            pltpu.VMEM((depths, 3 * half, columns), BF16),
        ]
        + [DMA((6,))] * 3
        + [DMA((CHIPS,))]
        + [DMA((3,))] * 8
        + [DMA((6,))] * 4
        + [DMA((1,))] * 2,
        compiler_params=comm_params(collective_id),
        name="middle",
    )(attended, *out_pieces, *ff_pieces, states, out_grad, teacher, valid, count, predict, correct)


def input_gradients(
    dq, dk, dv, qkv, all_rows, out_grads, states, up0, up1, hidden_grad, sums, predict, correct, collective_id
):
    rows, _, width = states.shape
    depths, _, part_rows, columns = qkv.shape
    half = part_rows // 3
    blocks = rows // ROWS

    def kernel(
        dq_ref, dk_ref, dv_ref, qkv_ref, rows_ref, o0, o1, o2, o3, s_ref, up0_ref, up1_ref, hg_ref, sums_ref,
        p_ref, c_ref,
        grad_ref, qsum_ref, osum_ref, all_sums,
        w_all, x_own, xT, dk_other, dv_other, dkv, part, got, mine, q_grad, q_other, q_mine, q_far,
        o_grad, o_other, o_mine, o_far,
        xload, ksend, krecv, send, recv, ssend, srecv, zsend, zrecv, osend, orecv,
    ):
        depth, chip, core, chip_x, chip_y, chip_d = place_on_mesh()
        near = [(c, (2 * c + core, depth)) for c in (chip_x, chip_y, chip_d)]
        other = (2 * chip + 1 - core, depth)
        across = [
            (2 * chip + core, lax.rem(depth + step, depths)) for step in range(1, depths)
        ]
        signal_and_wait([device for _, device in near] + [other] + across)
        swaps = [
            remote(dk_ref.at[:, 1 - core], dk_other, ksend, krecv, 0, other),
            remote(dv_ref.at[:, 1 - core], dv_other, ksend, krecv, 1, other),
        ]
        for copy in swaps:
            copy.start()
        load = pltpu.make_async_copy(rows_ref.at[:, core], x_own, xload)
        load.start()
        spread_rows(qkv_ref, w_all)
        for copy in swaps:
            copy.wait_recv()

        def add_cores(c, _):
            dkv[0, c] = (dk_ref[c, core].astype(F32) + dk_other[c].astype(F32)).astype(BF16)
            dkv[1, c] = (dv_ref[c, core].astype(F32) + dv_other[c].astype(F32)).astype(BF16)
            return 0

        lax.fori_loop(0, CHIPS, add_cores, 0)

        def rows_grad(c):
            return (
                lax.dot_general(dq_ref[c], w_all[0], NT, preferred_element_type=F32)
                + lax.dot_general(dkv[0, c], w_all[1], NT, preferred_element_type=F32)
                + lax.dot_general(dkv[1, c], w_all[2], NT, preferred_element_type=F32)
            )

        sends = [
            remote(part.at[c], got.at[i], send, recv, i, device) for i, (c, device) in enumerate(near)
        ]
        for i in (2, 0, 1):
            part[near[i][0]] = rows_grad(near[i][0]).astype(BF16)
            sends[i].start()
        mine[...] = rows_grad(chip)
        load.wait()

        def turn(c, _):
            xT[:, aligned(c, rows)] = x_own[c].T
            return 0

        lax.fori_loop(0, CHIPS, turn, 0)

        def weight_grads(z, _):
            at = aligned(z, 2 * half)
            for i in range(3):
                right = dq_ref[...] if i == 0 else dkv[i - 1]
                wide = jnp.dot(
                    xT[at, :], right.reshape(CHIPS * rows, columns), preferred_element_type=F32
                ).astype(BF16)
                q_grad[z, 0, i * half : (i + 1) * half, :] = wide[:half]
                q_grad[z, 1, i * half : (i + 1) * half, :] = wide[half:]
            return 0

        lax.fori_loop(0, depths, weight_grads, 0)
        wide = (
            o0[...].astype(F32) + o1[...].astype(F32) + o2[...].astype(F32) + o3[...].astype(F32)
        ).astype(BF16)
        o_grad[0] = wide[:half]
        o_grad[1] = wide[half:]
        core_swaps = [
            remote(q_grad.at[:, 1 - core], q_other, ssend, srecv, 0, other),
            remote(o_grad.at[1 - core], o_other, ssend, srecv, 1, other),
        ]
        for copy in core_swaps:
            copy.start()
        for copy in core_swaps:
            copy.wait_recv()
        for i in range(depths):
            q_mine[i] = (q_grad[i, core].astype(F32) + q_other[i].astype(F32)).astype(BF16)
        q_copies = [
            remote(q_mine.at[lax.rem(depth + i + 1, depths)], q_far.at[i], zsend, zrecv, i, device)
            for i, device in enumerate(across)
        ]
        for copy in q_copies:
            copy.start()
        o_mine[...] = (o_grad[core].astype(F32) + o_other[...].astype(F32)).astype(BF16)
        distance = lax.rem(chip + depths - depth, depths)
        o_copies = [
            remote(o_mine, o_far.at[i], osend, orecv, i, device) for i, device in enumerate(across)
        ]
        for i in range(depths - 1):

            @pl.when(distance == i + 1)
            def _(i=i):
                o_copies[i].start()

        for copy in sends:
            copy.wait_recv()

        def state_grads(i, totals):
            at = aligned(i, ROWS)
            s0, s1 = s_ref[at, 0, :].astype(F32), s_ref[at, 1, :].astype(F32)
            a = p_ref[0, 0] * s0 + p_ref[0, 1] * s1
            weighted = mine[at, :]
            for j in range(3):
                weighted = weighted + got[j, at, :].astype(F32)
            factor = norm_factor(a)
            mean = jnp.mean(weighted * a, axis=1, keepdims=True)
            up0, up1 = up0_ref[at, :], up1_ref[at, :]
            result_grad = c_ref[0] * up0 + c_ref[1] * up1
            norm_grad = factor * weighted - a * (factor * factor * factor * mean)
            mixed0 = up0 + (hg_ref[at, :] + norm_grad - result_grad)
            grad_ref[at, 0, :] = (p_ref[0, 0] * mixed0 + p_ref[1, 0] * up1).astype(BF16)
            grad_ref[at, 1, :] = (p_ref[0, 1] * mixed0 + p_ref[1, 1] * up1).astype(BF16)
            terms = (weighted * a * factor, mixed0 * s0, mixed0 * s1, up1 * s0, up1 * s1)
            return tuple(t + jnp.sum(v, axis=0, keepdims=True) for t, v in zip(totals, terms))

        totals = lax.fori_loop(
            0, blocks, state_grads, tuple(jnp.zeros((1, width), F32) for _ in range(5))
        )
        all_sums[...] = sums_ref[...]
        all_sums[0:1, :] = totals[0]
        for i in range(4):
            all_sums[4 + i : 5 + i, :] = totals[1 + i]
        for copy in q_copies:
            copy.wait_recv()
        total = q_mine[depth].astype(F32)
        for i in range(depths - 1):
            total = total + q_far[i].astype(F32)
        qsum_ref[...] = total.astype(BF16)
        osum_ref[...] = jnp.zeros_like(osum_ref)

        @pl.when(distance == 0)
        def _():
            for copy in o_copies:
                copy.wait_recv()
            total = o_mine[...].astype(F32)
            for i in range(depths - 1):
                total = total + o_far[i].astype(F32)
            osum_ref[...] = total.astype(BF16)

        for copy in swaps + sends + core_swaps + q_copies:
            copy.wait_send()
        for i in range(depths - 1):

            @pl.when(distance == i + 1)
            def _(i=i):
                o_copies[i].wait_send()

    block = (rows, width)
    q_block, o_block = (part_rows, columns), (half, width)
    return pl.pallas_call(
        kernel,
        out_shape=[
            jax.ShapeDtypeStruct((rows, 2, width), BF16),
            jax.ShapeDtypeStruct(q_block, BF16),
            jax.ShapeDtypeStruct(o_block, BF16),
            jax.ShapeDtypeStruct((8, width), F32),
        ],
        in_specs=[VM] * 4 + [ANY] + [VM] * 9 + [SM] * 2,
        out_specs=[VM] * 4,
        scratch_shapes=[
            pltpu.VMEM((3, width, columns), BF16),
            pltpu.VMEM((CHIPS,) + block, BF16),
            pltpu.VMEM((width, CHIPS * rows), BF16),
            pltpu.VMEM((CHIPS, rows, columns), BF16),
            pltpu.VMEM((CHIPS, rows, columns), BF16),
            pltpu.VMEM((2, CHIPS, rows, columns), BF16),
            pltpu.VMEM((CHIPS,) + block, BF16),
            pltpu.VMEM((3,) + block, BF16),
            pltpu.VMEM(block, F32),
            pltpu.VMEM((depths, 2) + q_block, BF16),
            pltpu.VMEM((depths,) + q_block, BF16),
            pltpu.VMEM((depths,) + q_block, BF16),
            pltpu.VMEM((depths - 1,) + q_block, BF16),
            pltpu.VMEM((2,) + o_block, BF16),
            pltpu.VMEM(o_block, BF16),
            pltpu.VMEM(o_block, BF16),
            pltpu.VMEM((depths - 1,) + o_block, BF16),
            DMA,
            DMA((2,)),
            DMA((2,)),
            DMA((3,)),
            DMA((3,)),
            DMA((2,)),
            DMA((2,)),
            DMA((depths - 1,)),
            DMA((depths - 1,)),
            DMA((depths - 1,)),
            DMA((depths - 1,)),
        ],
        compiler_params=comm_params(collective_id),
        name="input_gradients",
    )(dq, dk, dv, qkv, all_rows, *out_grads, states, up0, up1, hidden_grad, sums, predict, correct)


def gather_gradients(ff, qkv, out, sums, collective_id):
    depths = lax.axis_size("wsh")
    half, width = out.shape

    def kernel(
        f_ref, q_ref, o_ref, s_ref, f_all, q_all, o_all, total_ref,
        fsend, frecv, qsend, qrecv, osend, orecv, ssend, srecv, *total_refs,
    ):
        depth, chip, core, chip_x, chip_y, chip_d = place_on_mesh()
        dev_x, dev_y = (2 * chip_x + core, depth), (2 * chip_y + core, depth)
        other = (2 * chip + 1 - core, depth)
        across = [
            (2 * chip + core, lax.rem(depth + step, depths)) for step in range(1, depths)
        ]
        peers = plane_peers(chip, core, depth, chip_x, chip_y, chip_d)
        signal_and_wait(peers + across)

        def slot(chip_index):
            return 2 * chip_index + core

        start, turn, end = total_over_mesh(s_ref, *total_refs[:3], across, peers, *total_refs[3:])
        start()
        f_copies = ring_sends(
            f_ref, f_all, slot, chip, core, depth, chip_x, chip_y, fsend, frecv
        )
        q_copies = ring_sends(
            q_ref, q_all, slot, chip, core, depth, chip_x, chip_y, qsend, qrecv
        )
        for copy in f_copies[:2] + q_copies[:2]:
            copy.start()
        quarter = half // 2
        o_top, o_low = o_all.at[core, pl.ds(0, quarter)], o_all.at[core, pl.ds(quarter, quarter)]
        o_source_top, o_source_low = o_ref.at[pl.ds(0, quarter)], o_ref.at[pl.ds(quarter, quarter)]
        o_copies = [
            remote(o_source_top, o_top, osend, orecv, 0, dev_x),
            remote(o_source_low, o_low, osend, orecv, 1, dev_y),
            remote(o_source_low, o_low, osend, orecv, 2, dev_x),
            remote(o_source_top, o_top, osend, orecv, 3, dev_y),
            remote(o_top, o_top, osend, orecv, 4, dev_y),
            remote(o_low, o_low, osend, orecv, 5, dev_x),
        ]
        source, from_x, from_y = chip == depth, chip_x == depth, chip_y == depth

        @pl.when(source)
        def _():
            for copy in o_copies[:4]:
                copy.start()
            o_all[core] = o_ref[...]

        for copy in f_copies[2:4] + q_copies[2:4]:
            copy.start()
        f_all[slot(chip)] = f_ref[...]
        q_all[slot(chip)] = q_ref[...]

        def shared(index, ref):
            return remote(ref, ref, ssend, srecv, index, other)

        f_shared = [shared(i, f_all.at[slot(c)]) for i, c in enumerate((chip, chip_x, chip_y, chip_d))]
        q_shared = [shared(4 + i, q_all.at[slot(c)]) for i, c in enumerate((chip, chip_x, chip_y, chip_d))]
        o_shared = shared(8, o_all.at[core])
        f_shared[0].start()
        q_shared[0].start()
        turn()
        for copies in (f_copies, q_copies):
            copies[0].wait_recv()
            copies[4].start()
            copies[1].wait_recv()
            copies[5].start()

        @pl.when(from_x)
        def _():
            o_copies[0].wait_recv()
            o_copies[4].start()
            o_copies[2].wait_recv()

        @pl.when(from_y)
        def _():
            o_copies[1].wait_recv()
            o_copies[5].start()
            o_copies[3].wait_recv()

        for copies, passed in ((f_copies, f_shared), (q_copies, q_shared)):
            copies[2].wait_recv()
            passed[1].start()
            copies[3].wait_recv()
            passed[2].start()
        for copies, passed in ((f_copies, f_shared), (q_copies, q_shared)):
            copies[4].wait_recv()
            copies[5].wait_recv()
            passed[3].start()

        @pl.when(chip_d == depth)
        def _():
            o_copies[4].wait_recv()
            o_copies[5].wait_recv()

        o_shared.start()
        total_ref[...] = end()
        for copy in f_shared + q_shared + [o_shared]:
            copy.wait()
        for copy in f_copies + q_copies:
            copy.wait_send()

        @pl.when(source)
        def _():
            for copy in o_copies[:4]:
                copy.wait_send()

        @pl.when(from_x)
        def _():
            o_copies[4].wait_send()

        @pl.when(from_y)
        def _():
            o_copies[5].wait_send()

    return pl.pallas_call(
        kernel,
        out_shape=[
            jax.ShapeDtypeStruct((2 * CHIPS,) + ff.shape, BF16),
            jax.ShapeDtypeStruct((2 * CHIPS,) + qkv.shape, BF16),
            jax.ShapeDtypeStruct((2,) + out.shape, BF16),
            jax.ShapeDtypeStruct(sums.shape, F32),
        ],
        in_specs=[VM] * 4,
        out_specs=[VM] * 4,
        scratch_shapes=[DMA((6,))] * 6 + [DMA((9,))] * 2 + total_scratch(sums.shape, depths),
        compiler_params=comm_params(collective_id),
        name="gather_gradients",
    )(ff, qkv, out, sums)


def lay_out(ff, qkv, out, sums, gain_one, gain_two):
    ctx, part_rows, columns = ff.shape
    half, width = out.shape[1:]
    shard = 2 * half
    depths = width // shard
    split = columns // depths

    def kernel(
        f_ref, q_ref, o_ref, s_ref, g1_ref, g2_ref,
        dq_ref, dk_ref, dv_ref, do_ref, dg_ref, du_ref, dd_ref, g1_out, g2_out, p_out, c_out,
    ):
        depth = lax.axis_index("wsh")
        one, two = g1_ref[...].astype(F32), g2_ref[...].astype(F32)
        one_column, two_column = as_column(one), as_column(two)
        for c in range(2):
            rows = slice(c * half, (c + 1) * half)
            do_ref[rows, :] = o_ref[c].astype(F32)
            for i, ref in enumerate((dq_ref, dk_ref, dv_ref)):
                wide = jnp.concatenate(
                    [q_ref[2 * p + c, i * half : (i + 1) * half, :].astype(F32) for p in range(CHIPS)],
                    axis=1,
                )
                ref[rows, :] = wide * one_column[rows]
            for i, ref in enumerate((dg_ref, du_ref)):
                for z in range(depths):
                    wide = jnp.concatenate(
                        [
                            f_ref[
                                2 * p + c, i * half : (i + 1) * half, z * split : (z + 1) * split
                            ].astype(F32)
                            for p in range(CHIPS)
                        ],
                        axis=1,
                    )
                    ref[rows, z * CHIPS * split : (z + 1) * CHIPS * split] = wide * two_column[rows]
            for p in range(CHIPS):
                at = (2 * p + c) * half
                dd_ref[at : at + half, :] = f_ref[2 * p + c, 2 * half :, :].astype(F32)
        for z in range(depths):

            @pl.when(depth == z)
            def _(z=z):
                g1_out[...] = s_ref[0:1, z * shard : (z + 1) * shard] / one
                g2_out[...] = s_ref[1:2, z * shard : (z + 1) * shard] / two

        scalars = jnp.sum(s_ref[...], axis=1, keepdims=True)
        for i in range(2):
            c_out[:, i : i + 1] = scalars[2 + i : 3 + i]
            for j in range(2):
                at = 4 + 2 * i + j
                p_out[i : i + 1, j : j + 1] = scalars[at : at + 1]

    square = jax.ShapeDtypeStruct((shard, width), F32)
    tall = jax.ShapeDtypeStruct((shard, columns * CHIPS), F32)
    row = jax.ShapeDtypeStruct((1, shard), F32)
    return pl.pallas_call(
        kernel,
        out_shape=[
            square,
            square,
            square,
            square,
            tall,
            tall,
            jax.ShapeDtypeStruct((ctx * half, width), F32),
            row,
            row,
            jax.ShapeDtypeStruct((2, 2), F32),
            jax.ShapeDtypeStruct((1, 2), F32),
        ],
        in_specs=[VM] * 6,
        out_specs=[VM] * 11,
        compiler_params=pltpu.CompilerParams(vmem_limit_bytes=VMEM_LIMIT),
        name="lay_out",
    )(ff, qkv, out, sums, gain_one, gain_two)


def plane_shards(
    states, block_slot, cont_lengths, valid_mask, teacher, out_grad, predict, correct,
    norm_attn, w_query, w_key, w_value, w_out, norm_ffn, w_gate, w_up, w_down,
):
    depths = lax.axis_size("wsh")
    _, rows, _, width = states.shape
    half = w_query.shape[0] // 2
    hidden_cols = w_gate.shape[1] // CHIPS
    slots, lengths = block_slot[0], cont_lengths[0]
    states, out_grad, teacher = states[0], out_grad[0], teacher[0]
    gain_one, gain_two = norm_attn[None], norm_ffn[None]

    def along_depth(value, pairs):
        return lax.ppermute(value, "wsh", pairs)

    def over_plane(value, step):
        pairs = [(2 * c + k, 2 * (c ^ step) + k) for c in range(CHIPS) for k in range(2)]
        return lax.ppermute(value, "ctx", pairs)

    pre, qkv_piece, ff_piece, count = prepare(
        states, predict, valid_mask, gain_one, gain_two, w_query, w_key, w_value, w_gate, w_up, w_down
    )
    ff_piece = ff_piece.reshape(3, half, hidden_cols)
    above = [(z, z + 1) for z in range(depths - 1)]
    below = [(z + 1, z) for z in range(depths - 1)]
    from_below = along_depth(ff_piece, above)
    from_above = along_depth(ff_piece, below)
    all_rows, qkv, out_piece, count = gather_inputs(pre, qkv_piece, w_out, count, 1)
    ff_pieces = [
        ff_piece,
        from_below,
        along_depth(from_below, above[1:]),
        from_above,
        along_depth(from_above, below[:-1]),
        along_depth(ff_piece, [(0, depths - 1), (depths - 1, 0)]),
    ]
    out_pieces = [out_piece] + [over_plane(out_piece, step) for step in (1, 2, 3)]
    attended, *saved = attention_forward(all_rows.reshape(-1, width), qkv, slots, lengths)
    new_states, up0, up1, hidden_grad, att_grad, *rest = middle(
        attended.reshape(CHIPS, rows, CHIP_COLS), out_pieces, ff_pieces, states, out_grad, teacher,
        valid_mask, count, predict, correct, 2,
    )
    out_grads, (ff_sum, sums) = rest[:4], rest[4:]
    ff_sum = lax.psum_scatter(
        ff_sum.reshape(depths * 3 * half, hidden_cols), "wsh", scatter_dimension=0, tiled=True
    )
    out_grads = [out_grads[0]] + [over_plane(g, step) for step, g in zip((1, 2, 3), out_grads[1:])]
    dq, dk, dv = attention_backward(att_grad.reshape(-1, CHIP_COLS), saved, slots, lengths)
    states_grad, qkv_sum, out_sum, sums = input_gradients(
        dq.reshape(CHIPS, rows, CHIP_COLS),
        dk.reshape(CHIPS, 2, rows, CHIP_COLS),
        dv.reshape(CHIPS, 2, rows, CHIP_COLS),
        qkv, all_rows.reshape(CHIPS, 2, rows, width), out_grads,
        states, up0, up1, hidden_grad, sums, predict, correct, 3,
    )
    gathered = gather_gradients(ff_sum, qkv_sum, out_sum, sums, 4)
    dq, dk, dv, do, dg, du, dd, g_one, g_two, predict_grad, correct_grad = lay_out(
        *gathered, gain_one, gain_two
    )
    return (
        new_states[None], states_grad[None], predict_grad, correct_grad[0],
        g_one[0], dq, dk, dv, do, g_two[0], dg, du, dd,
    )


def fits_plane(mesh, states, block_slot, w_query, w_gate):
    ctx, depths = mesh.shape["ctx"], mesh.shape["wsh"]
    return (
        ctx == 2 * CHIPS
        and depths == CHIPS
        and states.shape[0] == depths
        and block_slot.shape[1] * BLK == 2 * PROMPT
        and states.shape[1] == 2 * PROMPT
        and w_query.shape[0] % (32 * depths) == 0
        and w_gate.shape[1] % (32 * CHIPS * depths) == 0
    )


def solution(mesh):
    in_specs = (
        P("wsh", "ctx", None, None),
        P("wsh", None),
        P("wsh", None),
        P("wsh", "ctx"),
        P("wsh", "ctx", None, None),
        P("wsh", "ctx", None, None),
        P(),
        P(),
        P("wsh"),
        P("wsh", None),
        P("wsh", None),
        P("wsh", None),
        P("wsh", None),
        P("wsh"),
        P("wsh", None),
        P("wsh", None),
        P("wsh", None),
    )
    out_specs = (
        P("wsh", "ctx", None, None),
        P("wsh", "ctx", None, None),
        P(),
        P(),
        P("wsh"),
        P("wsh", None),
        P("wsh", None),
        P("wsh", None),
        P("wsh", None),
        P("wsh"),
        P("wsh", None),
        P("wsh", None),
        P("wsh", None),
    )

    def step(*args):
        plane = fits_plane(mesh, args[0], args[1], args[9], args[14])
        body = plane_shards if plane else general_shards
        return jax.shard_map(
            body, mesh=mesh, in_specs=in_specs, out_specs=out_specs, check_vma=False
        )(*args)

    return step
```

```python
import functools
import math

import jax
import jax.numpy as jnp
from jax import lax
from jax.experimental import pallas as pl
from jax.experimental.pallas import tpu as pltpu
from jax.sharding import PartitionSpec as P

HEADS = 12
HD = 64
PROMPT = 1024
BLK = 64


EPSILON = 1e-06
NEGATIVE = -1e30
HIGHEST = lax.Precision.HIGHEST


def rms_forward(tensor, gain_vec):
    factor = lax.rsqrt(jnp.mean(tensor * tensor, axis=-1, keepdims=True) + EPSILON)
    return (tensor * factor * gain_vec, factor)


def rms_backward(tensor, factor, gain_vec, upstream):
    weighted = upstream * gain_vec
    gain_grad = jnp.sum(upstream * tensor * factor, axis=0)
    middle = jnp.mean(weighted * tensor, axis=-1, keepdims=True)
    return (factor * weighted - tensor * factor * factor * factor * middle, gain_grad)


def segment_starts(cont_lengths):
    count = cont_lengths.shape[1]
    index = jnp.arange(count, dtype=jnp.int32)
    before = index[:, None] < index[None, :]
    return PROMPT + jnp.sum(jnp.where(before[None], cont_lengths[:, :, None], 0), axis=1)


def token_places(block_slot, cont_lengths):
    groups, blocks = block_slot.shape
    offsets = jnp.arange(BLK, dtype=jnp.int32)
    places = (block_slot[:, :, None] * BLK + offsets[None, None, :]).reshape(groups, blocks * BLK)
    starts = segment_starts(cont_lengths)
    segments = jnp.sum((places[:, :, None] >= starts[:, None, :]).astype(jnp.int32), axis=2)
    return (places, segments)


def visible(query_place, query_segment, key_place, key_segment):
    earlier = key_place[:, None, :] <= query_place[:, :, None]
    shared = (key_segment[:, None, :] == 0) | (key_segment[:, None, :] == query_segment[:, :, None])
    return earlier & shared


def split_heads(tensor):
    return tensor.reshape(tensor.shape[0], tensor.shape[1], HEADS, HD)


def forward_block(running, query_part, key_part, value_part, allowed):

    def forward_compute(current):
        maximum, denominator, accumulated = current
        scores = jnp.einsum(
            "gqhd,gkhd->ghqk",
            split_heads(query_part),
            split_heads(key_part),
            preferred_element_type=jnp.float32,
        )
        masked = jnp.where(allowed[:, None], scores, NEGATIVE)
        new_max = jnp.maximum(maximum, jnp.max(masked, axis=-1))
        exponent = jnp.where(allowed[:, None], jnp.exp(masked - new_max[..., None]), 0.0)
        factor = jnp.exp(maximum - new_max)
        rescale = jnp.swapaxes(factor, 1, 2)[..., None]
        update = jnp.einsum(
            "ghqk,gkhd->gqhd",
            exponent.astype(jnp.bfloat16),
            split_heads(value_part),
            preferred_element_type=jnp.float32,
        )
        merged = (split_heads(accumulated) * rescale + update).reshape(accumulated.shape)
        return (new_max, denominator * factor + jnp.sum(exponent, axis=-1), merged)

    return lax.cond(jnp.any(allowed), forward_compute, lambda current: current, running)


def backward_block(
    query_part, grad_part, key_part, value_part, allowed, maximum, denominator, delta_sum
):
    scores = jnp.einsum(
        "gqhd,gkhd->ghqk",
        split_heads(query_part),
        split_heads(key_part),
        preferred_element_type=jnp.float32,
    )
    exponent = jnp.where(allowed[:, None], jnp.exp(scores - maximum[..., None]), 0.0)
    probability = exponent / denominator[..., None]
    prob_grad = jnp.einsum(
        "gqhd,gkhd->ghqk",
        split_heads(grad_part),
        split_heads(value_part),
        preferred_element_type=jnp.float32,
    )
    score_grad = (probability * (prob_grad - delta_sum[..., None])).astype(jnp.bfloat16)
    return (probability.astype(jnp.bfloat16), score_grad)


def general_shards(
    states,
    block_slot,
    cont_lengths,
    valid_mask,
    teacher,
    out_grad,
    predict,
    correct,
    norm_attn,
    w_query,
    w_key,
    w_value,
    w_out,
    norm_ffn,
    w_gate,
    w_up,
    w_down,
):
    groups, local_len = valid_mask.shape
    model_width = states.shape[3]
    row_count = groups * local_len
    group_len = block_slot.shape[1] * BLK
    gain_one, query_w, key_w, value_w, out_w, gain_two, gate_w, up_w, down_w = (
        lax.all_gather(norm_attn, "wsh", axis=0, tiled=True),
        lax.all_gather(w_query, "wsh", axis=0, tiled=True),
        lax.all_gather(w_key, "wsh", axis=0, tiled=True),
        lax.all_gather(w_value, "wsh", axis=0, tiled=True),
        lax.all_gather(w_out, "wsh", axis=0, tiled=True),
        lax.all_gather(norm_ffn, "wsh", axis=0, tiled=True),
        lax.all_gather(w_gate, "wsh", axis=0, tiled=True),
        lax.all_gather(w_up, "wsh", axis=0, tiled=True),
        lax.all_gather(w_down, "wsh", axis=0, tiled=True),
    )
    valid_float = valid_mask.astype(jnp.float32)
    valid_total = lax.psum(jnp.sum(valid_float), ("ctx", "wsh"))
    places, segments = token_places(block_slot, cont_lengths)
    offset = lax.axis_index("ctx") * local_len
    own_place = lax.dynamic_slice_in_dim(places, offset, local_len, 1)
    own_segment = lax.dynamic_slice_in_dim(segments, offset, local_len, 1)
    inputs = states.astype(jnp.float32)
    mixed_states = jnp.einsum("ij,gtjd->gtid", predict, inputs, precision=HIGHEST)
    active = mixed_states[:, :, 0].reshape(row_count, model_width)
    gain_first = gain_one.astype(jnp.float32)
    normed, factor_one = rms_forward(active, gain_first)
    normed_low = normed.astype(jnp.bfloat16)
    queries = (
        jnp.dot(normed_low, query_w, preferred_element_type=jnp.float32)
        .astype(jnp.bfloat16)
        .reshape(groups, local_len, model_width)
    )
    key_rows = (
        jnp.dot(normed_low, key_w, preferred_element_type=jnp.float32)
        .astype(jnp.bfloat16)
        .reshape(groups, local_len, model_width)
    )
    values = (
        jnp.dot(normed_low, value_w, preferred_element_type=jnp.float32)
        .astype(jnp.bfloat16)
        .reshape(groups, local_len, model_width)
    )
    initial = (
        jnp.full((groups, HEADS, local_len), NEGATIVE, jnp.float32),
        jnp.zeros((groups, HEADS, local_len), jnp.float32),
        jnp.zeros((groups, local_len, model_width), jnp.float32),
    )
    piece_keys = lax.all_gather(key_rows, "ctx", axis=1, tiled=True)
    piece_values = lax.all_gather(values, "ctx", axis=1, tiled=True)
    piece_len = piece_keys.shape[1]
    block_size = math.gcd(piece_len, local_len)

    def fold_one_block(current, block_index):
        begin = block_index * block_size
        key_part = lax.dynamic_slice_in_dim(piece_keys, begin, block_size, 1)
        value_part = lax.dynamic_slice_in_dim(piece_values, begin, block_size, 1)
        key_place = lax.dynamic_slice_in_dim(places, begin, block_size, 1)
        key_segment = lax.dynamic_slice_in_dim(segments, begin, block_size, 1)
        allowed = visible(own_place, own_segment, key_place, key_segment)
        return (forward_block(current, queries, key_part, value_part, allowed), None)

    finished, unused = lax.scan(
        fold_one_block, initial, jnp.arange(piece_len // block_size, dtype=jnp.int32)
    )
    maximum, denominator, accumulated = finished
    attended = (split_heads(accumulated) / jnp.swapaxes(denominator, 1, 2)[..., None]).reshape(
        row_count, model_width
    )
    attended_low = attended.astype(jnp.bfloat16)
    hidden = active + jnp.dot(attended_low, out_w, preferred_element_type=jnp.float32)
    gain_second = gain_two.astype(jnp.float32)
    normed_two, factor_two = rms_forward(hidden, gain_second)
    normed_two_low = normed_two.astype(jnp.bfloat16)
    gate_proj = jnp.dot(normed_two_low, gate_w, preferred_element_type=jnp.float32)
    up_proj = jnp.dot(normed_two_low, up_w, preferred_element_type=jnp.float32)
    inner_act, inner_pull = jax.vjp(
        lambda gate_in, up_in: jax.nn.gelu(gate_in, approximate=True) * up_in, gate_proj, up_proj
    )
    inner_low = inner_act.astype(jnp.bfloat16)
    result = hidden + jnp.dot(inner_low, down_w, preferred_element_type=jnp.float32)
    difference = (result - active).reshape(groups, local_len, 1, model_width)
    out_states = mixed_states + correct[None, None, :, None] * difference
    new_states = out_states.astype(jnp.bfloat16)
    loss_ratio = lax.axis_size("wsh") * groups * group_len / valid_total
    upstream = out_grad.astype(jnp.float32) + loss_ratio * valid_float[:, :, None, None] * (
        out_states - teacher.astype(jnp.float32)
    )
    correct_local = jnp.sum(upstream * difference, axis=(0, 1, 3))
    result_grad = jnp.einsum("i,gtid->gtd", correct, upstream, precision=HIGHEST).reshape(
        row_count, model_width
    )
    result_low = result_grad.astype(jnp.bfloat16)
    down_grad = jnp.einsum("rf,rd->fd", inner_low, result_low, preferred_element_type=jnp.float32)
    inner_grad = jnp.einsum("rd,fd->rf", result_low, down_w, preferred_element_type=jnp.float32)
    gate_grad, up_grad = inner_pull(inner_grad)
    gate_low = gate_grad.astype(jnp.bfloat16)
    up_low = up_grad.astype(jnp.bfloat16)
    gate_w_grad = jnp.einsum(
        "rd,rf->df", normed_two_low, gate_low, preferred_element_type=jnp.float32
    )
    up_w_grad = jnp.einsum("rd,rf->df", normed_two_low, up_low, preferred_element_type=jnp.float32)
    normed_two_grad = jnp.einsum(
        "rf,df->rd", gate_low, gate_w, preferred_element_type=jnp.float32
    ) + jnp.einsum("rf,df->rd", up_low, up_w, preferred_element_type=jnp.float32)
    hidden_norm_grad, gain_two_grad = rms_backward(hidden, factor_two, gain_second, normed_two_grad)
    hidden_grad = result_grad + hidden_norm_grad
    hidden_low = hidden_grad.astype(jnp.bfloat16)
    out_w_grad = jnp.einsum(
        "rc,rd->cd", attended_low, hidden_low, preferred_element_type=jnp.float32
    )
    attended_grad = jnp.einsum(
        "rd,cd->rc", hidden_low, out_w, preferred_element_type=jnp.float32
    ).astype(jnp.bfloat16)
    delta_sum = jnp.swapaxes(
        jnp.sum(
            split_heads(
                (attended_grad.astype(jnp.float32) * attended).reshape(
                    groups, local_len, model_width
                )
            ),
            axis=-1,
        ),
        1,
        2,
    )
    grad_local = attended_grad.reshape(groups, local_len, model_width)
    zero_grad = jnp.zeros((groups, local_len, model_width), jnp.float32)
    all_keys, all_values = (
        lax.all_gather(key_rows, "ctx", axis=1, tiled=True),
        lax.all_gather(values, "ctx", axis=1, tiled=True),
    )

    def query_step(current, block_index):
        begin = block_index * local_len
        key_part = lax.dynamic_slice_in_dim(all_keys, begin, local_len, 1)
        value_part = lax.dynamic_slice_in_dim(all_values, begin, local_len, 1)
        key_place = lax.dynamic_slice_in_dim(places, begin, local_len, 1)
        key_segment = lax.dynamic_slice_in_dim(segments, begin, local_len, 1)
        allowed = visible(own_place, own_segment, key_place, key_segment)

        def query_compute(query_sum):
            prob_low, score_grad = backward_block(
                queries, grad_local, key_part, value_part, allowed, maximum, denominator, delta_sum
            )
            return query_sum + jnp.einsum(
                "ghqk,gkhd->gqhd",
                score_grad,
                split_heads(key_part),
                preferred_element_type=jnp.float32,
            ).reshape(groups, local_len, model_width)

        return (
            lax.cond(jnp.any(allowed), query_compute, lambda query_sum: query_sum, current),
            None,
        )

    finished, unused = lax.scan(
        query_step, zero_grad, jnp.arange(group_len // local_len, dtype=jnp.int32)
    )
    term_rows = local_len * lax.axis_size("ctx")
    key_block_size = math.gcd(term_rows, local_len)

    def key_one_block(block_index):
        begin = block_index * key_block_size
        key_part = lax.dynamic_slice_in_dim(all_keys, begin, key_block_size, 1)
        value_part = lax.dynamic_slice_in_dim(all_values, begin, key_block_size, 1)
        key_place = lax.dynamic_slice_in_dim(places, begin, key_block_size, 1)
        key_segment = lax.dynamic_slice_in_dim(segments, begin, key_block_size, 1)
        allowed = visible(own_place, own_segment, key_place, key_segment)

        def one_compute(unused_arg):
            prob_low, score_grad = backward_block(
                queries, grad_local, key_part, value_part, allowed, maximum, denominator, delta_sum
            )
            key_add = jnp.einsum(
                "ghqk,gqhd->kghd",
                score_grad,
                split_heads(queries),
                preferred_element_type=jnp.float32,
            ).reshape(key_block_size, groups, model_width)
            value_add = jnp.einsum(
                "ghqk,gqhd->kghd",
                prob_low,
                split_heads(grad_local),
                preferred_element_type=jnp.float32,
            ).reshape(key_block_size, groups, model_width)
            return jnp.stack([key_add, value_add], axis=1)

        return lax.cond(
            jnp.any(allowed),
            one_compute,
            lambda unused_arg: jnp.zeros((key_block_size, 2, groups, model_width), jnp.float32),
            0,
        )

    summed = lax.psum_scatter(
        lax.map(key_one_block, jnp.arange(term_rows // key_block_size, dtype=jnp.int32))
        .reshape(term_rows, 2, groups, model_width)
        .astype(jnp.bfloat16),
        "ctx",
        scatter_dimension=0,
        tiled=True,
    ).astype(jnp.float32)
    key_grad = jnp.swapaxes(summed[:, 0], 0, 1)
    value_grad = jnp.swapaxes(summed[:, 1], 0, 1)
    query_low = finished.reshape(row_count, model_width).astype(jnp.bfloat16)
    key_low = key_grad.reshape(row_count, model_width).astype(jnp.bfloat16)
    value_low = value_grad.reshape(row_count, model_width).astype(jnp.bfloat16)
    query_w_grad = jnp.einsum(
        "rc,rd->cd", normed_low, query_low, preferred_element_type=jnp.float32
    )
    key_w_grad = jnp.einsum("rc,rd->cd", normed_low, key_low, preferred_element_type=jnp.float32)
    value_w_grad = jnp.einsum(
        "rc,rd->cd", normed_low, value_low, preferred_element_type=jnp.float32
    )
    normed_grad = (
        jnp.einsum("rd,cd->rc", query_low, query_w, preferred_element_type=jnp.float32)
        + jnp.einsum("rd,cd->rc", key_low, key_w, preferred_element_type=jnp.float32)
        + jnp.einsum("rd,cd->rc", value_low, value_w, preferred_element_type=jnp.float32)
    )
    active_norm_grad, gain_one_grad = rms_backward(active, factor_one, gain_first, normed_grad)
    active_grad = (hidden_grad + active_norm_grad - result_grad).reshape(
        groups, local_len, 1, model_width
    )
    mixed_grad = jnp.concatenate([upstream[:, :, :1] + active_grad, upstream[:, :, 1:]], axis=2)
    predict_local = jnp.einsum("gtid,gtjd->ij", mixed_grad, inputs, precision=HIGHEST)
    states_grad = jnp.einsum("ij,gtid->gtjd", predict, mixed_grad, precision=HIGHEST).astype(
        jnp.bfloat16
    )
    predict_grad, correct_grad = lax.psum((predict_local, correct_local), ("ctx", "wsh"))
    (
        gain_one_rows,
        query_rows,
        key_grad_rows,
        value_rows,
        out_rows,
        gain_two_rows,
        gate_rows,
        up_rows,
        down_rows,
    ) = (
        lax.psum_scatter(
            gain_one_grad.astype(jnp.bfloat16), "wsh", scatter_dimension=0, tiled=True
        ).astype(jnp.float32),
        lax.psum_scatter(
            query_w_grad.astype(jnp.bfloat16), "wsh", scatter_dimension=0, tiled=True
        ).astype(jnp.float32),
        lax.psum_scatter(
            key_w_grad.astype(jnp.bfloat16), "wsh", scatter_dimension=0, tiled=True
        ).astype(jnp.float32),
        lax.psum_scatter(
            value_w_grad.astype(jnp.bfloat16), "wsh", scatter_dimension=0, tiled=True
        ).astype(jnp.float32),
        lax.psum_scatter(
            out_w_grad.astype(jnp.bfloat16), "wsh", scatter_dimension=0, tiled=True
        ).astype(jnp.float32),
        lax.psum_scatter(
            gain_two_grad.astype(jnp.bfloat16), "wsh", scatter_dimension=0, tiled=True
        ).astype(jnp.float32),
        lax.psum_scatter(
            gate_w_grad.astype(jnp.bfloat16), "wsh", scatter_dimension=0, tiled=True
        ).astype(jnp.float32),
        lax.psum_scatter(
            up_w_grad.astype(jnp.bfloat16), "wsh", scatter_dimension=0, tiled=True
        ).astype(jnp.float32),
        lax.psum_scatter(
            down_grad.astype(jnp.bfloat16), "wsh", scatter_dimension=0, tiled=True
        ).astype(jnp.float32),
    )
    totals = (
        lax.psum(gain_one_rows.astype(jnp.bfloat16), "ctx").astype(jnp.float32),
        lax.psum(query_rows.astype(jnp.bfloat16), "ctx").astype(jnp.float32),
        lax.psum(key_grad_rows.astype(jnp.bfloat16), "ctx").astype(jnp.float32),
        lax.psum(value_rows.astype(jnp.bfloat16), "ctx").astype(jnp.float32),
        lax.psum(out_rows.astype(jnp.bfloat16), "ctx").astype(jnp.float32),
        lax.psum(gain_two_rows.astype(jnp.bfloat16), "ctx").astype(jnp.float32),
        lax.psum(gate_rows.astype(jnp.bfloat16), "ctx").astype(jnp.float32),
        lax.psum(up_rows.astype(jnp.bfloat16), "ctx").astype(jnp.float32),
        lax.psum(down_rows.astype(jnp.bfloat16), "ctx").astype(jnp.float32),
    )
    return (new_states, states_grad, predict_grad, correct_grad) + tuple(totals)


MESH = pl.DeviceIdType.MESH
F32 = jnp.float32
BF16 = jnp.bfloat16
CHIPS = 4
VMEM_LIMIT = 60 * 2**20
DMA = pltpu.SemaphoreType.DMA


def place_on_mesh():
    ctx = lax.axis_index("ctx")
    depth = lax.axis_index("wsh")
    chip = ctx // 2
    core = ctx % 2
    chip_x = chip + 1 - 2 * (chip % 2)
    chip_y = chip + 2 - 4 * (chip // 2)
    return depth, chip, core, chip_x, chip_y, 3 - chip


def signal_all(devices):
    barrier = pltpu.get_barrier_semaphore()
    for device in devices:
        pl.semaphore_signal(barrier, inc=1, device_id=device, device_id_type=MESH)


def wait_all(devices):
    pl.semaphore_wait(pltpu.get_barrier_semaphore(), len(devices))


def remote(src, dst, send, recv, index, device):
    return pltpu.make_async_remote_copy(
        src_ref=src,
        dst_ref=dst,
        send_sem=send.at[index],
        recv_sem=recv.at[index],
        device_id=device,
        device_id_type=MESH,
    )


def comm_params(collective_id):
    return pltpu.CompilerParams(
        collective_id=collective_id, has_side_effects=True, vmem_limit_bytes=VMEM_LIMIT
    )


ANY = pl.BlockSpec(memory_space=pl.ANY)
VM = pl.BlockSpec(memory_space=pltpu.VMEM)
SM = pl.BlockSpec(memory_space=pltpu.SMEM)


def ring_sends(own, out, slot_of, chip, core, depth, chip_x, chip_y, send, recv):
    half = own.shape[0] // 2
    top, low = pl.ds(0, half), pl.ds(half, half)
    dev_x, dev_y = (2 * chip_x + core, depth), (2 * chip_y + core, depth)
    here = slot_of(chip)
    return [
        remote(own.at[top], out.at[here, top], send, recv, 0, dev_x),
        remote(own.at[low], out.at[here, low], send, recv, 1, dev_y),
        remote(own.at[low], out.at[here, low], send, recv, 2, dev_x),
        remote(own.at[top], out.at[here, top], send, recv, 3, dev_y),
        remote(out.at[slot_of(chip_x), top], out.at[slot_of(chip_x), top], send, recv, 4, dev_y),
        remote(out.at[slot_of(chip_y), low], out.at[slot_of(chip_y), low], send, recv, 5, dev_x),
    ]


NT = (((1,), (1,)), ((), ()))
TN = (((0,), (0,)), ((), ()))
TILE = 256
ROWS = 32
LOCAL_HEADS = HEADS // CHIPS
CHIP_COLS = LOCAL_HEADS * HD


def head_mask(rows, head):
    lane = lax.broadcasted_iota(jnp.int32, (rows, CHIP_COLS), 1)
    return (lane >= head * HD) & (lane < (head + 1) * HD)


def aligned(index, size):
    return pl.ds(pl.multiple_of(index * size, size), size)


def norm_factor(rows):
    return lax.rsqrt(jnp.mean(rows * rows, axis=1, keepdims=True) + EPSILON)


def as_column(row):
    return jnp.broadcast_to(row, (8, row.shape[1])).T[:, 0:1]


def mix(states_ref, at, p_ref, i):
    return p_ref[i, 0] * states_ref[at, 0, :].astype(F32) + p_ref[i, 1] * states_ref[at, 1, :].astype(F32)


def plane_peers(chip, core, depth, chip_x, chip_y, chip_d):
    same = [(2 * c + core, depth) for c in (chip_x, chip_y, chip_d)]
    return same + [(2 * c + 1 - core, depth) for c in (chip, chip_x, chip_y, chip_d)]


def total_over_mesh(own_ref, arrived, staged, far, across, peers, bsend, brecv, csend, crecv):
    first = [remote(own_ref, arrived.at[i], bsend, brecv, i, d) for i, d in enumerate(across)]
    second = [remote(staged, far.at[i], csend, crecv, i, d) for i, d in enumerate(peers)]

    def start():
        for copy in first:
            copy.start()

    def turn():
        total = own_ref[...]
        for i, copy in enumerate(first):
            copy.wait_recv()
        for i in range(len(first)):
            total = total + arrived[i]
        staged[...] = total
        for copy in second:
            copy.start()

    def end():
        for copy in second:
            copy.wait_recv()
        total = staged[...]
        for i in range(len(second)):
            total = total + far[i]
        for copy in first + second:
            copy.wait_send()
        return total

    return start, turn, end


def total_scratch(shape, depths):
    return [
        pltpu.VMEM((depths - 1,) + shape, F32),
        pltpu.VMEM(shape, F32),
        pltpu.VMEM((2 * CHIPS - 1,) + shape, F32),
        DMA((depths - 1,)),
        DMA((depths - 1,)),
        DMA((2 * CHIPS - 1,)),
        DMA((2 * CHIPS - 1,)),
    ]


def gelu_parts(v):
    scale = math.sqrt(2 / math.pi)
    square = v * v
    t = jnp.tanh(scale * v * (1.0 + 0.044715 * square))
    rise = 0.5 * (1.0 + t)
    return v * rise, rise + 0.5 * v * (1.0 - t * t) * scale * (1.0 + 0.134145 * square)


def pair_places(slots_ref, pair):
    one, two = slots_ref[2 * pair], slots_ref[2 * pair + 1]
    second = (one >= PROMPT // BLK).astype(jnp.int32)
    return second, jnp.minimum(one, two), jnp.maximum(one, two)


def own_pair(pair, per_device):
    core = lax.axis_index("ctx") % 2
    pairs = per_device // 2
    return (pair // pairs) * per_device + core * pairs + pair % pairs


PER_TILE = TILE // BLK


def fill_bias(bias, kind, tile_step, slots_ref, lengths_ref, per_device, group_pairs):
    lane = lax.broadcasted_iota(jnp.int32, (1, TILE), 1)
    high = jnp.zeros((1, TILE), jnp.int32)
    for i in range(PER_TILE):
        _, prompt, cont = pair_places(slots_ref, own_pair(tile_step * PER_TILE + i, per_device))
        block = prompt if kind == 0 else cont
        high = jnp.where(lane >= i * BLK, (block - i) * BLK + lane, high)
    low = jnp.zeros((1, TILE), jnp.int32)
    if kind == 1:
        start = PROMPT
        for i in range(lengths_ref.shape[0]):
            low = jnp.where(high >= start, start, low)
            start = start + lengths_ref[i]
    offset = lax.broadcasted_iota(jnp.int32, (BLK, TILE), 0)

    def one_block(pair, _):
        _, prompt, cont = pair_places(slots_ref, pair)
        base = (prompt if kind == 0 else cont) * BLK
        seen = offset <= high - base
        if kind == 1:
            seen = seen & (offset >= low - base)
        bias[pair // PER_TILE, aligned(pair % PER_TILE, BLK), 0:TILE] = jnp.where(seen, 0.0, NEGATIVE)
        return 0

    lax.fori_loop(0, group_pairs, one_block, 0)


def either(second, one, two):
    swap = second == 1
    return jnp.where(swap, two, one), jnp.where(swap, one, two)


def to_pair_order(source, target, slots_ref, group_pairs):
    def one_pair(pair, _):
        second, _, _ = pair_places(slots_ref, pair)
        first, last = either(second, source[aligned(2 * pair, BLK), :], source[aligned(2 * pair + 1, BLK), :])
        target[aligned(pair, BLK), :] = first
        target[aligned(group_pairs + pair, BLK), :] = last
        return 0

    lax.fori_loop(0, group_pairs, one_pair, 0)


def own_to_pair_order(source, target, slots_ref, pairs, per_device):
    def one_pair(pair, _):
        second, _, _ = pair_places(slots_ref, own_pair(pair, per_device))
        first, last = either(second, source[aligned(2 * pair, BLK), :], source[aligned(2 * pair + 1, BLK), :])
        target[aligned(pair, BLK), :] = first
        target[aligned(pairs + pair, BLK), :] = last
        return 0

    lax.fori_loop(0, pairs, one_pair, 0)


def own_to_slot_order(source, target, slots_ref, pairs, per_device):
    def one_pair(pair, _):
        second, _, _ = pair_places(slots_ref, own_pair(pair, per_device))
        first, last = either(second, source[aligned(pair, BLK), :], source[aligned(pairs + pair, BLK), :])
        target[aligned(2 * pair, BLK), :] = first
        target[aligned(2 * pair + 1, BLK), :] = last
        return 0

    lax.fori_loop(0, pairs, one_pair, 0)


def forward(
    slots, lengths, predict, correct, states, out_grad, teacher, valid, gain_one, gain_two,
    w_query, w_key, w_value, w_out, w_gate, w_up, w_down, collective_id,
):
    rows, _, width = states.shape
    shard = w_query.shape[0]
    half = shard // 2
    depths = width // shard
    hidden_cols = w_gate.shape[1]
    columns = hidden_cols // CHIPS
    split = columns // depths
    out_rows = shard // CHIPS
    blocks = rows // ROWS
    col_tiles = columns // TILE
    tokens = 2 * CHIPS * rows
    queries = CHIPS * rows
    tiles = queries // TILE
    per_device = rows // BLK
    group_pairs = tokens // (2 * BLK)
    pairs = queries // (2 * BLK)
    mesh_tokens = tokens * depths
    piece_lanes = 3 * CHIP_COLS

    def kernel(
        slots_ref, lengths_ref, p_ref, c_ref, s_ref, g_ref, t_ref, v_ref, g1_ref, g2_ref,
        wq_ref, wk_ref, wv_ref, wo_ref, wg_ref, wu_ref, wd_ref,
        new_ref, up0_ref, up1_ref, hg_ref, da_ref, dw0_ref, dw1_ref, dw2_ref, dw3_ref, ff_ref, sums_ref,
        all_rows, w_all, q_pairs, k_pairs, v_pairs, oT_ref, lse_ref,
        w_ff, w_wo, qkv, att_all, hidden, own, x_rows, r_rows, xT, innerT, inner, gate, up, gate_low, up_low,
        own_weight, part1, part2, got1, got2, dw, dw_other, buf, wide, count, q_slot, k_slot, v_slot, vT,
        lsend, fsend, frecv, fosend, forecv, qsend, qrecv, qosend, qorecv,
        osend, orecv, oosend, oorecv, opsend, oprecv,
        rsend, rrecv, rosend, rorecv, send0, recv0, send1, recv1, send2, recv2, send3, recv3,
        ag1s, ag1r, ag2s, ag2r, dsend, drecv, *total_refs,
    ):
        depth, chip, core, chip_x, chip_y, chip_d = place_on_mesh()
        near = [(c, (2 * c + core, depth)) for c in (chip_x, chip_y, chip_d)]
        other = (2 * chip + 1 - core, depth)
        across = [
            (2 * chip + core, lax.rem(depth + step, depths)) for step in range(1, depths)
        ]
        peers = plane_peers(chip, core, depth, chip_x, chip_y, chip_d)
        signal_all(peers + across)

        mine = pl.ds(core * half, half)
        loads = [
            pltpu.make_async_copy(w.at[mine], buf.at[i], lsend.at[i])
            for i, w in enumerate((wq_ref, wk_ref, wv_ref))
        ] + [
            pltpu.make_async_copy(wg_ref.at[mine], wide.at[0], lsend.at[3]),
            pltpu.make_async_copy(wu_ref.at[mine], wide.at[1], lsend.at[4]),
            pltpu.make_async_copy(
                wd_ref.at[pl.ds(chip * split + core * half, half)], w_ff.at[2, depth, core], lsend.at[5]
            ),
            pltpu.make_async_copy(
                wo_ref.at[pl.ds(chip * out_rows, out_rows)], w_wo.at[depth, chip], lsend.at[6]
            ),
        ]
        for copy in loads:
            copy.start()
        count[...] = jnp.broadcast_to(
            jnp.sum(v_ref[...].astype(F32), axis=1, keepdims=True), count.shape
        )

        def input_norm(i, _):
            at = aligned(i, ROWS)
            active = mix(s_ref, at, p_ref, 0)
            own[0, at, :] = (active * norm_factor(active)).astype(BF16)
            return 0

        lax.fori_loop(0, blocks, input_norm, 0)

        def gain_column(ref):
            both = jnp.broadcast_to(ref[...].astype(F32), (8, shard)).T
            return jnp.where(core == 0, both[:half, 0:1], both[half:, 0:1])

        one, two = gain_column(g1_ref), gain_column(g2_ref)
        wait_all(peers + across)

        def slot(chip_index):
            return 2 * chip_index + core

        start_count, turn_count, end_count = total_over_mesh(
            count, *total_refs[:3], across, peers, *total_refs[3:]
        )
        start_count()
        ring0 = ring_sends(
            own.at[0], all_rows, slot, chip, core, depth, chip_x, chip_y, rsend, rrecv
        )
        for copy in ring0[:4]:
            copy.start()

        def rows_to_other(index, chip_index):
            ref = all_rows.at[slot(chip_index)]
            return remote(own.at[0] if index == 0 else ref, ref, rosend, rorecv, index, other)

        shared0 = [rows_to_other(i, c) for i, c in enumerate((chip, chip_x, chip_y, chip_d))]
        shared0[0].start()
        all_rows[slot(chip)] = own[0]

        for copy in loads[:3]:
            copy.wait()
        for p in range(CHIPS):

            @pl.when(chip == p)
            def _(p=p):
                cols = jnp.concatenate(
                    [buf[i, :, p * CHIP_COLS : (p + 1) * CHIP_COLS].astype(F32) for i in range(3)], axis=1
                )
                qkv[depth, core] = (cols * one).astype(BF16)

        qkv_mine = qkv.at[depth, core]
        q_copies = [
            remote(qkv_mine, qkv_mine, qsend, qrecv, i, device) for i, device in enumerate(across)
        ]
        q_shared = [remote(qkv_mine, qkv_mine, qosend, qorecv, 0, other)]
        for copy in q_copies + q_shared:
            copy.start()

        loads[6].wait()
        o_copies = [
            remote(w_wo.at[depth, chip], w_wo.at[depth, chip], osend, orecv, i, device)
            for i, device in enumerate(across)
        ]
        o_shared = []
        for i in range(depths - 1):
            came = w_wo.at[lax.rem(depth + depths - 1 - i, depths), chip]
            o_shared.append(remote(came, came, oosend, oorecv, i, other))

        def carried(i, act):
            pl.when(core == (i + 1) % 2)(act)

        def not_carried(i, act):
            pl.when(core != (i + 1) % 2)(act)

        for i in range(depths - 1):
            carried(i, o_copies[i].start)

        for copy in loads[3:6]:
            copy.wait()
        for p in range(CHIPS):

            @pl.when(chip == p)
            def _(p=p):
                for i in range(2):
                    cols = jnp.concatenate(
                        [
                            wide[i, :, (z * CHIPS + p) * split : (z * CHIPS + p + 1) * split].astype(F32)
                            for z in range(depths)
                        ],
                        axis=1,
                    )
                    w_ff[i, depth, core] = (cols * two).astype(BF16)

        line_up = (2 * chip + core, lax.rem(depth + 1, depths))
        line_down = (2 * chip + core, lax.rem(depth + depths - 1, depths))
        hops = []
        for stage in range(1, depths):
            for direction, device, index in ((1, line_up, stage - 1), (-1, line_down, depths + stage - 2)):
                goes = jnp.clip(depth - direction * (stage - 1), 0, depths - 1)
                comes = jnp.clip(depth - direction * stage, 0, depths - 1)
                piece, came = w_ff.at[:, goes, core], w_ff.at[:, comes, core]
                if direction == 1:
                    sends, receives = (depth >= stage - 1) & (depth < depths - 1), depth >= stage
                else:
                    sends, receives = (depth <= depths - stage) & (depth > 0), depth < depths - stage
                hops.append(
                    (
                        stage,
                        sends,
                        receives,
                        remote(piece, piece, fsend, frecv, index, device),
                        remote(came, came, fosend, forecv, index, other),
                    )
                )
        ff_mine = remote(w_ff.at[:, depth, core], w_ff.at[:, depth, core], fosend, forecv, 2 * depths - 2, other)
        ff_mine.start()

        def send_hop(stage):
            for at, sends, _, hop, _ in hops:
                if at == stage:
                    pl.when(sends)(hop.start)

        def take_hop(stage):
            for at, _, receives, hop, share in hops:
                if at == stage:

                    @pl.when(receives)
                    def _(hop=hop, share=share):
                        hop.wait_recv()
                        share.start()

        send_hop(1)
        turn_count()
        ring0[0].wait_recv()
        ring0[4].start()
        ring0[1].wait_recv()
        ring0[5].start()
        for i in range(depths - 1):
            q_copies[i].wait_recv()
            came = qkv.at[lax.rem(depth + depths - 1 - i, depths), core]
            share = remote(came, came, qosend, qorecv, 1 + i, other)
            share.start()
            q_shared.append(share)
        ring0[2].wait_recv()
        shared0[1].start()
        ring0[3].wait_recv()
        shared0[2].start()
        for copy in q_shared:
            copy.wait_recv()
        for i in range(3):
            for z in range(depths):
                for c in range(2):
                    at = (z * 2 + c) * half
                    w_all[i, at : at + half, :] = qkv[z, c, :, i * CHIP_COLS : (i + 1) * CHIP_COLS]

        def project(device_slot, with_queries):
            x = all_rows[device_slot]
            at = aligned(device_slot, rows)
            k_slot[at, :] = jnp.dot(x, w_all[1], preferred_element_type=F32).astype(BF16)
            v_slot[at, :] = jnp.dot(x, w_all[2], preferred_element_type=F32).astype(BF16)
            if with_queries:
                q_slot[aligned(device_slot // 2, rows), :] = jnp.dot(
                    x, w_all[0], preferred_element_type=F32
                ).astype(BF16)

        for c in (chip, chip_x, chip_y):
            project(slot(c), True)
        for i, c in enumerate((chip, chip_x, chip_y)):
            shared0[i].wait_recv()
            project(2 * c + 1 - core, False)
        ring0[4].wait_recv()
        ring0[5].wait_recv()
        shared0[3].start()
        project(slot(chip_d), True)
        for i in range(depths - 1):

            def came_here(i=i):
                o_copies[i].wait_recv()
                o_shared[i].start()

            carried(i, came_here)
        for i in range(depths - 1):
            not_carried(i, o_shared[i].wait_recv)
        o_plane = [
            remote(w_wo.at[:, chip], w_wo.at[:, chip], opsend, oprecv, i, device)
            for i, (_, device) in enumerate(near)
        ]
        for copy in o_plane:
            copy.start()
        shared0[3].wait_recv()
        project(2 * chip_d + 1 - core, False)

        to_pair_order(k_slot, k_pairs, slots_ref, group_pairs)
        to_pair_order(v_slot, v_pairs, slots_ref, group_pairs)
        own_to_pair_order(q_slot, q_pairs, slots_ref, pairs, per_device)

        def turn_values(i, _):
            vT[:, aligned(i, TILE)] = v_pairs[aligned(i, TILE), :].T
            return 0

        lax.fori_loop(0, tokens // TILE, turn_values, 0)
        half_keys = group_pairs * BLK
        half_tiles = half_keys // TILE
        scores, bias = gate, up

        def cell(k_tile):
            lanes = (k_tile // CHIPS) * TILE
            return k_tile % CHIPS, slice(lanes, lanes + TILE)

        def attend(kind, step):
            tile = kind * (tiles // 2) + step
            key_tiles = half_tiles * (kind + 1)
            q = q_pairs[aligned(tile, TILE), :]
            fill_bias(bias, kind, step, slots_ref, lengths_ref, per_device, group_pairs)
            for head in range(LOCAL_HEADS):
                heads = slice(head * HD, (head + 1) * HD)
                q_head = jnp.where(head_mask(TILE, head), q, jnp.zeros_like(q))
                top = jnp.full((1, TILE), NEGATIVE, F32)
                for k_tile in range(key_tiles):
                    s = lax.dot_general(
                        k_pairs[k_tile * TILE : (k_tile + 1) * TILE, :], q_head, NT, preferred_element_type=F32
                    )
                    if k_tile >= key_tiles - half_tiles:
                        s = s + bias[k_tile - (key_tiles - half_tiles), :, 0:TILE]
                    index, lanes = cell(k_tile)
                    scores[index, :, lanes] = s
                    top = jnp.maximum(top, jnp.max(s, axis=0, keepdims=True))
                total = jnp.zeros((1, TILE), F32)
                out = jnp.zeros((HD, TILE), F32)
                for k_tile in range(key_tiles):
                    index, lanes = cell(k_tile)
                    e = jnp.exp(scores[index, :, lanes] - top)
                    total = total + jnp.sum(e, axis=0, keepdims=True)
                    out = out + jnp.dot(
                        vT[heads, k_tile * TILE : (k_tile + 1) * TILE], e.astype(BF16), preferred_element_type=F32
                    )
                oT_ref[tile, heads, :] = out / total
                lse_ref[tile, head] = top + jnp.log(total)
            q_slot[aligned(tile, TILE), :] = oT_ref[tile].T.astype(BF16)

        def both_steps(kind):
            def body(step, _):
                attend(kind, step)
                return 0

            lax.fori_loop(0, tiles // 2, body, 0)

        both_steps(1)
        take_hop(1)
        send_hop(2)
        both_steps(0)

        own_to_slot_order(q_slot, k_slot, slots_ref, pairs, per_device)
        for c in range(CHIPS):
            att_all[CHIPS + c] = k_slot[c * rows : (c + 1) * rows, :]
        sends0 = [
            remote(att_all.at[CHIPS + c], att_all.at[chip], send0, recv0, i, device)
            for i, (c, device) in enumerate(near)
        ]
        for copy in sends0:
            copy.start()
        att_all[chip] = att_all[CHIPS + chip]
        take_hop(2)
        send_hop(3)
        for copy in o_plane:
            copy.wait_recv()
        for copy in sends0:
            copy.wait()

        def w_out_rows(p):
            return w_wo[p].reshape(CHIP_COLS, width)

        for p in range(CHIPS):
            term = jnp.dot(att_all[p], w_out_rows(p), preferred_element_type=F32)
            hidden[...] = term if p == 0 else hidden[...] + term

        def first_norm(i, _):
            at = aligned(i, ROWS)
            h = hidden[at, :] + mix(s_ref, at, p_ref, 0)
            hidden[at, :] = h
            own[1, at, :] = (h * norm_factor(h)).astype(BF16)
            return 0

        lax.fori_loop(0, blocks, first_norm, 0)

        def ring(source, target, send, recv):
            return ring_sends(
                source, target, lambda c: c, chip, core, depth, chip_x, chip_y, send, recv
            )

        ring1 = ring(own.at[1], x_rows, ag1s, ag1r)
        for copy in ring1[:4]:
            copy.start()
        x_rows[chip] = own[1]
        ring1[0].wait_recv()
        ring1[4].start()
        ring1[1].wait_recv()
        ring1[5].start()
        take_hop(3)
        ff_mine.wait_recv()
        for _, _, receives, _, share in hops:
            pl.when(receives)(share.wait_recv)

        def w_rows(i):
            return w_ff[i].reshape(width, columns)

        def ff_forward(c):
            x = x_rows[c]
            for n in range(col_tiles):
                cols = slice(n * TILE, (n + 1) * TILE)
                g = jnp.dot(x, w_rows(0)[:, cols], preferred_element_type=F32)
                u = jnp.dot(x, w_rows(1)[:, cols], preferred_element_type=F32)
                gate[c, :, cols] = g
                up[c, :, cols] = u
                inner[c, :, cols] = (gelu_parts(g)[0] * u).astype(BF16)
            return jnp.dot(inner[c], w_rows(2), preferred_element_type=F32)

        sends1 = [
            remote(part1.at[c], got1.at[i], send1, recv1, i, device) for i, (c, device) in enumerate(near)
        ]
        up0_ref[...] = ff_forward(chip)
        for i, (c, _) in enumerate(near):
            if i < 2:
                ring1[2 + i].wait_recv()
            else:
                ring1[4].wait_recv()
                ring1[5].wait_recv()
            part1[c] = ff_forward(c).astype(BF16)
            sends1[i].start()

        def turn(i, _):
            xT[:, aligned(i, rows)] = x_rows[i].T
            innerT[:, aligned(i, rows)] = inner[i].T
            return 0

        lax.fori_loop(0, CHIPS, turn, 0)
        valid_count = end_count()
        weight = as_column(v_ref[...].astype(F32)) * (mesh_tokens / valid_count[0:1, 0:1])
        own_weight[...] = jnp.broadcast_to(weight, own_weight.shape)
        for copy in sends1:
            copy.wait_recv()

        def outputs(i, sums):
            at = aligned(i, ROWS)
            a = mix(s_ref, at, p_ref, 0)
            result = hidden[at, :] + up0_ref[at, :]
            for j in range(3):
                result = result + got1[j, at, :].astype(F32)
            difference = result - a
            row_weight = own_weight[at, 0:1]
            c0, c1 = c_ref[0], c_ref[1]
            out0 = a + c0 * difference
            out1 = mix(s_ref, at, p_ref, 1) + c1 * difference
            new_ref[at, 0, :] = out0.astype(BF16)
            new_ref[at, 1, :] = out1.astype(BF16)
            up0 = g_ref[at, 0, :].astype(F32) + row_weight * (out0 - t_ref[at, 0, :].astype(F32))
            up1 = g_ref[at, 1, :].astype(F32) + row_weight * (out1 - t_ref[at, 1, :].astype(F32))
            up0_ref[at, :] = up0
            up1_ref[at, :] = up1
            own[2, at, :] = (c0 * up0 + c1 * up1).astype(BF16)
            return (
                sums[0] + jnp.sum(up0 * difference, axis=0, keepdims=True),
                sums[1] + jnp.sum(up1 * difference, axis=0, keepdims=True),
            )

        zero = jnp.zeros((1, width), F32)
        correct_sums = lax.fori_loop(0, blocks, outputs, (zero, zero))
        sums_ref[...] = jnp.zeros_like(sums_ref)
        sums_ref[2:3, :] = correct_sums[0]
        sums_ref[3:4, :] = correct_sums[1]

        ring2 = ring(own.at[2], r_rows, ag2s, ag2r)
        for copy in ring2[:4]:
            copy.start()
        r_rows[chip] = own[2]

        def ff_backward(c):
            r = r_rows[c]
            for n in range(col_tiles):
                cols = slice(n * TILE, (n + 1) * TILE)
                inner_grad = lax.dot_general(r, w_rows(2)[cols, :], NT, preferred_element_type=F32)
                value, slope = gelu_parts(gate[c, :, cols])
                gate_low[c, :, cols] = (inner_grad * up[c, :, cols] * slope).astype(BF16)
                up_low[c, :, cols] = (inner_grad * value).astype(BF16)
            return lax.dot_general(
                gate_low[c], w_rows(0), NT, preferred_element_type=F32
            ) + lax.dot_general(up_low[c], w_rows(1), NT, preferred_element_type=F32)

        sends2 = [
            remote(part2.at[c], got2.at[i], send2, recv2, i, device) for i, (c, device) in enumerate(near)
        ]
        hg_ref[...] = ff_backward(chip)
        ring2[0].wait_recv()
        ring2[4].start()
        ring2[1].wait_recv()
        ring2[5].start()
        for i, (c, _) in enumerate(near):
            if i < 2:
                ring2[2 + i].wait_recv()
            else:
                ring2[4].wait_recv()
                ring2[5].wait_recv()
            part2[c] = ff_backward(c).astype(BF16)
            sends2[i].start()

        def weight_grads(z, _):
            at = aligned(z, shard)
            for i, (left, right) in enumerate(((xT, gate_low), (xT, up_low), (innerT, r_rows))):
                grad = jnp.dot(
                    left[at, :], right[...].reshape(queries, -1), preferred_element_type=F32
                ).astype(BF16)
                dw[z, 0, i * half : (i + 1) * half, :] = grad[:half]
                dw[z, 1, i * half : (i + 1) * half, :] = grad[half:]
            return 0

        lax.fori_loop(0, depths, weight_grads, 0)
        swap = remote(dw.at[:, 1 - core], dw_other, dsend, drecv, 0, other)
        swap.start()
        for copy in sends2:
            copy.wait_recv()

        def second_norm(i, gain_sum):
            at = aligned(i, ROWS)
            h = hidden[at, :]
            weighted = hg_ref[at, :]
            for j in range(3):
                weighted = weighted + got2[j, at, :].astype(F32)
            factor = norm_factor(h)
            mean = jnp.mean(weighted * h, axis=1, keepdims=True)
            result_grad = c_ref[0] * up0_ref[at, :] + c_ref[1] * up1_ref[at, :]
            hidden_grad = result_grad + (factor * weighted - h * (factor * factor * factor * mean))
            hg_ref[at, :] = hidden_grad
            own[3, at, :] = hidden_grad.astype(BF16)
            return gain_sum + jnp.sum(weighted * h * factor, axis=0, keepdims=True)

        sums_ref[1:2, :] = lax.fori_loop(0, blocks, second_norm, zero)

        sends3 = [
            remote(att_all.at[CHIPS + c], da_ref.at[chip], send3, recv3, i, device)
            for i, (c, device) in enumerate(near)
        ]

        def att_grad(c):
            return lax.dot_general(own[3], w_out_rows(c), NT, preferred_element_type=F32).astype(BF16)

        for i in (2, 0, 1):
            att_all[CHIPS + near[i][0]] = att_grad(near[i][0])
            sends3[i].start()
        da_ref[chip] = att_grad(chip)
        for c, ref in zip((chip, chip_x, chip_y, chip_d), (dw0_ref, dw1_ref, dw2_ref, dw3_ref)):
            ref[...] = jnp.dot(att_all[c].T, own[3], preferred_element_type=F32).astype(BF16)
        swap.wait_recv()

        def add_cores(z, _):
            ff_ref[z] = (dw[z, core].astype(F32) + dw_other[z].astype(F32)).astype(BF16)
            return 0

        lax.fori_loop(0, depths, add_cores, 0)
        for copy in sends3:
            copy.wait_recv()
        sent = ring0 + shared0 + q_copies + q_shared + o_plane + sends1 + sends2 + sends3
        for copy in sent + ring1 + ring2 + [swap, ff_mine]:
            copy.wait_send()
        for i in range(depths - 1):
            carried(i, o_copies[i].wait_send)
            carried(i, o_shared[i].wait_send)
        for _, sends, receives, hop, share in hops:
            pl.when(sends)(hop.wait_send)
            pl.when(receives)(share.wait_send)

    block = (rows, width)
    pair = (rows, 2, width)
    wide_rows = (CHIPS, rows, width)
    hid_rows = (CHIPS, rows, columns)

    def out(shape, dtype):
        return jax.ShapeDtypeStruct(shape, dtype)

    vmem = pltpu.VMEM
    outs = [
        out(pair, BF16),
        out(block, F32),
        out(block, F32),
        out(block, F32),
        out((CHIPS, rows, CHIP_COLS), BF16),
        out((CHIP_COLS, width), BF16),
        out((CHIP_COLS, width), BF16),
        out((CHIP_COLS, width), BF16),
        out((CHIP_COLS, width), BF16),
        out((depths, 3 * half, columns), BF16),
        out((8, width), F32),
        out((2 * CHIPS, rows, width), BF16),
        out((3, width, CHIP_COLS), BF16),
        out((queries, CHIP_COLS), BF16),
        out((tokens, CHIP_COLS), BF16),
        out((tokens, CHIP_COLS), BF16),
        out((tiles, CHIP_COLS, TILE), F32),
        out((tiles, LOCAL_HEADS, 1, TILE), F32),
    ]
    return pl.pallas_call(
        kernel,
        out_shape=outs,
        in_specs=[SM] * 4 + [VM] * 6 + [ANY] * 7,
        out_specs=[VM] * len(outs),
        scratch_shapes=[
            vmem((3, depths, 2, half, columns), BF16),
            vmem((depths, CHIPS, out_rows, width), BF16),
            vmem((depths, 2, half, piece_lanes), BF16),
            vmem((2 * CHIPS, rows, CHIP_COLS), BF16),
            vmem(block, F32),
            vmem((4,) + block, BF16),
            vmem(wide_rows, BF16),
            vmem(wide_rows, BF16),
            vmem((width, queries), BF16),
            vmem((columns, queries), BF16),
            vmem(hid_rows, BF16),
            vmem(hid_rows, F32),
            vmem(hid_rows, F32),
            vmem(hid_rows, BF16),
            vmem(hid_rows, BF16),
            vmem((rows, 128), F32),
            vmem(wide_rows, BF16),
            vmem(wide_rows, BF16),
            vmem((3,) + block, BF16),
            vmem((3,) + block, BF16),
            vmem((depths, 2, 3 * half, columns), BF16),
            vmem((depths, 3 * half, columns), BF16),
            vmem((3, half, width), BF16),
            vmem((2, half, hidden_cols), BF16),
            vmem((8, 128), F32),
            vmem((queries, CHIP_COLS), BF16),
            vmem((tokens, CHIP_COLS), BF16),
            vmem((tokens, CHIP_COLS), BF16),
            vmem((CHIP_COLS, tokens), BF16),
        ]
        + [DMA((7,))]
        + [DMA((2 * depths - 2,))] * 2
        + [DMA((2 * depths - 1,))] * 2
        + [DMA((depths - 1,))] * 2
        + [DMA((depths,))] * 2
        + [DMA((depths - 1,))] * 4
        + [DMA((3,))] * 2
        + [DMA((6,))] * 2
        + [DMA((4,))] * 2
        + [DMA((3,))] * 8
        + [DMA((6,))] * 4
        + [DMA((1,))] * 2
        + total_scratch((8, 128), depths),
        compiler_params=comm_params(collective_id),
        name="forward",
    )(
        slots, lengths, predict, correct, states, out_grad, teacher, valid, gain_one, gain_two,
        w_query, w_key, w_value, w_out, w_gate, w_up, w_down,
    )


def backward(
    slots, lengths, predict, correct, att_grad, q_pairs, k_pairs, v_pairs, oT, lse, weights, states, up0, up1,
    hidden_grad, sums, out_grads, all_rows, collective_id,
):
    rows, _, width = states.shape
    depths = lax.axis_size("wsh")
    columns = CHIP_COLS
    half = width // (2 * depths)
    part_rows = 3 * half
    blocks = rows // ROWS
    tokens = k_pairs.shape[0]
    queries = q_pairs.shape[0]
    tiles = queries // TILE
    per_device = rows // BLK
    group_pairs = tokens // (2 * BLK)
    pairs = queries // (2 * BLK)
    half_tiles = group_pairs * BLK // TILE
    wide_lanes = LOCAL_HEADS * TILE

    def kernel(
        slots_ref, lengths_ref, p_ref, c_ref, g_ref, q_ref, k_ref, v_ref, oT_ref, lse_ref, w_all, s_ref,
        up0_ref, up1_ref, hg_ref, sums_ref, o0, o1, o2, o3, rows_ref,
        grad_ref, qsum_ref, osum_ref, all_sums,
        g_pairs, kT, doT, dqT, q_stack, do_stack, p_buf, ds_buf, dk_acc, dv_acc, bias, dq_pairs, dq_rows,
        give, kept, came, x_own, xT, part, got, mine, q_grad, q_other, q_mine, q_far,
        o_near, o_grad, o_other, o_mine, o_far,
        xload, nsend, nrecv, ksend, krecv, send, recv, ssend, srecv, zsend, zrecv, osend, orecv,
    ):
        depth, chip, core, chip_x, chip_y, chip_d = place_on_mesh()
        near = [(c, (2 * c + core, depth)) for c in (chip_x, chip_y, chip_d)]
        other = (2 * chip + 1 - core, depth)
        across = [
            (2 * chip + core, lax.rem(depth + step, depths)) for step in range(1, depths)
        ]
        everyone = [device for _, device in near] + [other] + across
        signal_all(everyone)
        load = pltpu.make_async_copy(rows_ref.at[:, core], x_own, xload)
        load.start()
        own_to_pair_order(g_ref, g_pairs, slots_ref, pairs, per_device)

        def turn_keys(i, _):
            at = aligned(i, TILE)
            kT[:, at] = k_ref[at, :].T
            return 0

        lax.fori_loop(0, tokens // TILE, turn_keys, 0)
        wait_all(everyone)
        near_grads = [
            remote(ref, o_near.at[i], nsend, nrecv, i, near[i][1]) for i, ref in enumerate((o1, o2, o3))
        ]
        for copy in near_grads:
            copy.start()

        def attend(kind, step):
            tile = kind * (tiles // 2) + step
            key_tiles = half_tiles * (kind + 1)
            q_tile = q_ref[aligned(tile, TILE), :]
            fill_bias(bias, kind, step, slots_ref, lengths_ref, per_device, group_pairs)
            do_tile = g_pairs[aligned(tile, TILE), :]
            doT[...] = do_tile.astype(F32).T * oT_ref[tile]
            for head in range(LOCAL_HEADS):
                lanes = slice(head * TILE, (head + 1) * TILE)
                heads = slice(head * HD, (head + 1) * HD)
                mask = head_mask(TILE, head)
                q_head = jnp.where(mask, q_tile, jnp.zeros_like(q_tile))
                do_head = jnp.where(mask, do_tile, jnp.zeros_like(do_tile))
                q_stack[lanes, :] = q_head
                do_stack[lanes, :] = do_head
                delta = jnp.sum(doT[heads, :], axis=0, keepdims=True)
                norm = lse_ref[tile, head]
                total = jnp.zeros((HD, TILE), F32)
                for k_tile in range(key_tiles):
                    at = slice(k_tile * TILE, (k_tile + 1) * TILE)
                    s = lax.dot_general(k_ref[at, :], q_head, NT, preferred_element_type=F32)
                    if k_tile >= key_tiles - half_tiles:
                        s = s + bias[k_tile - (key_tiles - half_tiles), :, 0:TILE]
                    dp = lax.dot_general(v_ref[at, :], do_head, NT, preferred_element_type=F32)
                    e = jnp.exp(s - norm)
                    p_buf[at, lanes] = e.astype(BF16)
                    ds = (e * (dp - delta)).astype(BF16)
                    ds_buf[at, lanes] = ds
                    total = total + jnp.dot(kT[heads, at], ds, preferred_element_type=F32)
                dqT[heads, :] = total
            for k_tile in range(key_tiles):
                at = slice(k_tile * TILE, (k_tile + 1) * TILE)
                dv = jnp.dot(p_buf[at, :], do_stack[...], preferred_element_type=F32)
                dk = jnp.dot(ds_buf[at, :], q_stack[...], preferred_element_type=F32)
                if kind == 1:
                    fresh = step == 0
                    dv_acc[at, :] = dv + jnp.where(fresh, 0.0, dv_acc[at, :])
                    dk_acc[at, :] = dk + jnp.where(fresh, 0.0, dk_acc[at, :])
                else:
                    dv_acc[at, :] = dv + dv_acc[at, :]
                    dk_acc[at, :] = dk + dk_acc[at, :]
            dq_pairs[aligned(tile, TILE), :] = dqT[...].T.astype(BF16)

        for kind in (1, 0):

            def body(step, _, kind=kind):
                attend(kind, step)
                return 0

            lax.fori_loop(0, tiles // 2, body, 0)

        def slot_rows(target, side, chip_index, pair_index):
            pair = chip_index * per_device + side * (per_device // 2) + pair_index
            second, _, _ = pair_places(slots_ref, pair)
            at = 2 * pair_index * BLK
            for i, acc in enumerate((dk_acc, dv_acc)):
                both = either(second, acc[aligned(pair, BLK), :], acc[aligned(group_pairs + pair, BLK), :])
                for j in range(2):
                    target[i, chip_index, at + j * BLK : at + (j + 1) * BLK, :] = both[j].astype(BF16)

        for c in range(CHIPS):
            for i in range(per_device // 2):
                slot_rows(give, 1 - core, c, i)
        swap = remote(give, came, ksend, krecv, 0, other)
        swap.start()
        for c in range(CHIPS):
            for i in range(per_device // 2):
                slot_rows(kept, core, c, i)
        own_to_slot_order(dq_pairs, dq_rows, slots_ref, pairs, per_device)
        swap.wait_recv()

        def add_cores(c, _):
            for i in range(2):
                kept[i, c] = (kept[i, c].astype(F32) + came[i, c].astype(F32)).astype(BF16)
            return 0

        lax.fori_loop(0, CHIPS, add_cores, 0)

        def rows_grad(c):
            return (
                lax.dot_general(
                    dq_rows[aligned(c, rows), :], w_all[0], NT, preferred_element_type=F32
                )
                + lax.dot_general(kept[0, c], w_all[1], NT, preferred_element_type=F32)
                + lax.dot_general(kept[1, c], w_all[2], NT, preferred_element_type=F32)
            )

        sends = [
            remote(part.at[c], got.at[i], send, recv, i, device) for i, (c, device) in enumerate(near)
        ]
        for i in (2, 0, 1):
            part[near[i][0]] = rows_grad(near[i][0]).astype(BF16)
            sends[i].start()
        mine[...] = rows_grad(chip)
        load.wait()

        def turn(c, _):
            xT[:, aligned(c, rows)] = x_own[c].T
            return 0

        lax.fori_loop(0, CHIPS, turn, 0)

        def weight_grads(z, _):
            at = aligned(z, 2 * half)
            for i in range(3):
                right = dq_rows[...] if i == 0 else kept[i - 1].reshape(queries, columns)
                grad = jnp.dot(xT[at, :], right, preferred_element_type=F32).astype(BF16)
                q_grad[z, 0, i * half : (i + 1) * half, :] = grad[:half]
                q_grad[z, 1, i * half : (i + 1) * half, :] = grad[half:]
            return 0

        lax.fori_loop(0, depths, weight_grads, 0)
        for copy in near_grads:
            copy.wait_recv()
        whole = o0[...].astype(F32)
        for i in range(3):
            whole = whole + o_near[i].astype(F32)
        whole = whole.astype(BF16)
        o_grad[0] = whole[:half]
        o_grad[1] = whole[half:]
        core_swaps = [
            remote(q_grad.at[:, 1 - core], q_other, ssend, srecv, 0, other),
            remote(o_grad.at[1 - core], o_other, ssend, srecv, 1, other),
        ]
        for copy in core_swaps:
            copy.start()
        for copy in core_swaps:
            copy.wait_recv()
        for i in range(depths):
            q_mine[i] = (q_grad[i, core].astype(F32) + q_other[i].astype(F32)).astype(BF16)
        q_copies = [
            remote(q_mine.at[lax.rem(depth + i + 1, depths)], q_far.at[i], zsend, zrecv, i, device)
            for i, device in enumerate(across)
        ]
        for copy in q_copies:
            copy.start()
        o_mine[...] = (o_grad[core].astype(F32) + o_other[...].astype(F32)).astype(BF16)
        distance = lax.rem(chip + depths - depth, depths)
        o_copies = [
            remote(o_mine, o_far.at[i], osend, orecv, i, device) for i, device in enumerate(across)
        ]
        for i in range(depths - 1):
            pl.when(distance == i + 1)(o_copies[i].start)
        for copy in sends:
            copy.wait_recv()

        def state_grads(i, totals):
            at = aligned(i, ROWS)
            s0, s1 = s_ref[at, 0, :].astype(F32), s_ref[at, 1, :].astype(F32)
            a = p_ref[0, 0] * s0 + p_ref[0, 1] * s1
            weighted = mine[at, :]
            for j in range(3):
                weighted = weighted + got[j, at, :].astype(F32)
            factor = norm_factor(a)
            mean = jnp.mean(weighted * a, axis=1, keepdims=True)
            up0, up1 = up0_ref[at, :], up1_ref[at, :]
            result_grad = c_ref[0] * up0 + c_ref[1] * up1
            norm_grad = factor * weighted - a * (factor * factor * factor * mean)
            mixed0 = up0 + (hg_ref[at, :] + norm_grad - result_grad)
            grad_ref[at, 0, :] = (p_ref[0, 0] * mixed0 + p_ref[1, 0] * up1).astype(BF16)
            grad_ref[at, 1, :] = (p_ref[0, 1] * mixed0 + p_ref[1, 1] * up1).astype(BF16)
            terms = (weighted * a * factor, mixed0 * s0, mixed0 * s1, up1 * s0, up1 * s1)
            return tuple(t + jnp.sum(v, axis=0, keepdims=True) for t, v in zip(totals, terms))

        totals = lax.fori_loop(
            0, blocks, state_grads, tuple(jnp.zeros((1, width), F32) for _ in range(5))
        )
        all_sums[...] = sums_ref[...]
        all_sums[0:1, :] = totals[0]
        for i in range(4):
            all_sums[4 + i : 5 + i, :] = totals[1 + i]
        for copy in q_copies:
            copy.wait_recv()
        total = q_mine[depth].astype(F32)
        for i in range(depths - 1):
            total = total + q_far[i].astype(F32)
        qsum_ref[...] = total.astype(BF16)
        osum_ref[...] = jnp.zeros_like(osum_ref)

        @pl.when(distance == 0)
        def _():
            for copy in o_copies:
                copy.wait_recv()
            total = o_mine[...].astype(F32)
            for i in range(depths - 1):
                total = total + o_far[i].astype(F32)
            osum_ref[...] = total.astype(BF16)

        for copy in near_grads + [swap] + sends + core_swaps + q_copies:
            copy.wait_send()
        for i in range(depths - 1):
            pl.when(distance == i + 1)(o_copies[i].wait_send)

    vmem = pltpu.VMEM
    block = (rows, width)
    wide_rows = (CHIPS, rows, width)
    q_block, o_block = (part_rows, columns), (half, width)
    kv_half = (2, CHIPS, rows, columns)
    return pl.pallas_call(
        kernel,
        out_shape=[
            jax.ShapeDtypeStruct((rows, 2, width), BF16),
            jax.ShapeDtypeStruct(q_block, BF16),
            jax.ShapeDtypeStruct(o_block, BF16),
            jax.ShapeDtypeStruct((8, width), F32),
        ],
        in_specs=[SM] * 4 + [VM] * 16 + [ANY],
        out_specs=[VM] * 4,
        scratch_shapes=[
            vmem((queries, columns), BF16),
            vmem((columns, tokens), BF16),
            vmem((columns, TILE), F32),
            vmem((columns, TILE), F32),
            vmem((wide_lanes, columns), BF16),
            vmem((wide_lanes, columns), BF16),
            vmem((tokens, wide_lanes), BF16),
            vmem((tokens, wide_lanes), BF16),
            vmem((tokens, columns), F32),
            vmem((tokens, columns), F32),
            vmem((half_tiles, TILE, TILE), F32),
            vmem((queries, columns), BF16),
            vmem((queries, columns), BF16),
            vmem(kv_half, BF16),
            vmem(kv_half, BF16),
            vmem(kv_half, BF16),
            vmem(wide_rows, BF16),
            vmem((width, queries), BF16),
            vmem(wide_rows, BF16),
            vmem((3,) + block, BF16),
            vmem(block, F32),
            vmem((depths, 2) + q_block, BF16),
            vmem((depths,) + q_block, BF16),
            vmem((depths,) + q_block, BF16),
            vmem((depths - 1,) + q_block, BF16),
            vmem((3, columns, width), BF16),
            vmem((2,) + o_block, BF16),
            vmem(o_block, BF16),
            vmem(o_block, BF16),
            vmem((depths - 1,) + o_block, BF16),
            DMA,
            DMA((3,)),
            DMA((3,)),
            DMA((1,)),
            DMA((1,)),
            DMA((3,)),
            DMA((3,)),
            DMA((2,)),
            DMA((2,)),
            DMA((depths - 1,)),
            DMA((depths - 1,)),
            DMA((depths - 1,)),
            DMA((depths - 1,)),
        ],
        compiler_params=comm_params(collective_id),
        name="backward",
    )(
        slots, lengths, predict, correct, att_grad, q_pairs, k_pairs, v_pairs, oT, lse, weights, states, up0, up1,
        hidden_grad, sums, *out_grads, all_rows,
    )


def gather_gradients(ff, qkv, out, sums, collective_id):
    depths = lax.axis_size("wsh")
    half, width = out.shape

    def kernel(
        f_ref, q_ref, o_ref, s_ref, f_all, q_all, o_all, total_ref,
        fsend, frecv, qsend, qrecv, osend, orecv, ssend, srecv, *total_refs,
    ):
        depth, chip, core, chip_x, chip_y, chip_d = place_on_mesh()
        dev_x, dev_y = (2 * chip_x + core, depth), (2 * chip_y + core, depth)
        other = (2 * chip + 1 - core, depth)
        across = [
            (2 * chip + core, lax.rem(depth + step, depths)) for step in range(1, depths)
        ]
        peers = plane_peers(chip, core, depth, chip_x, chip_y, chip_d)
        signal_all(peers + across)
        wait_all(peers + across)

        def slot(chip_index):
            return 2 * chip_index + core

        start, turn, end = total_over_mesh(s_ref, *total_refs[:3], across, peers, *total_refs[3:])
        start()
        f_copies = ring_sends(
            f_ref, f_all, slot, chip, core, depth, chip_x, chip_y, fsend, frecv
        )
        q_copies = ring_sends(
            q_ref, q_all, slot, chip, core, depth, chip_x, chip_y, qsend, qrecv
        )
        for copy in f_copies[:2] + q_copies[:2]:
            copy.start()
        quarter = half // 2
        o_top, o_low = o_all.at[core, pl.ds(0, quarter)], o_all.at[core, pl.ds(quarter, quarter)]
        o_source_top, o_source_low = o_ref.at[pl.ds(0, quarter)], o_ref.at[pl.ds(quarter, quarter)]
        o_copies = [
            remote(o_source_top, o_top, osend, orecv, 0, dev_x),
            remote(o_source_low, o_low, osend, orecv, 1, dev_y),
            remote(o_source_low, o_low, osend, orecv, 2, dev_x),
            remote(o_source_top, o_top, osend, orecv, 3, dev_y),
            remote(o_top, o_top, osend, orecv, 4, dev_y),
            remote(o_low, o_low, osend, orecv, 5, dev_x),
        ]
        source, from_x, from_y = chip == depth, chip_x == depth, chip_y == depth

        @pl.when(source)
        def _():
            for copy in o_copies[:4]:
                copy.start()
            o_all[core] = o_ref[...]

        for copy in f_copies[2:4] + q_copies[2:4]:
            copy.start()
        f_all[slot(chip)] = f_ref[...]
        q_all[slot(chip)] = q_ref[...]

        def shared(index, ref):
            return remote(ref, ref, ssend, srecv, index, other)

        f_shared = [shared(i, f_all.at[slot(c)]) for i, c in enumerate((chip, chip_x, chip_y, chip_d))]
        q_shared = [shared(4 + i, q_all.at[slot(c)]) for i, c in enumerate((chip, chip_x, chip_y, chip_d))]
        o_shared = shared(8, o_all.at[core])
        f_shared[0].start()
        q_shared[0].start()
        turn()
        for copies in (f_copies, q_copies):
            copies[0].wait_recv()
            copies[4].start()
            copies[1].wait_recv()
            copies[5].start()

        @pl.when(from_x)
        def _():
            o_copies[0].wait_recv()
            o_copies[4].start()
            o_copies[2].wait_recv()

        @pl.when(from_y)
        def _():
            o_copies[1].wait_recv()
            o_copies[5].start()
            o_copies[3].wait_recv()

        for copies, passed in ((f_copies, f_shared), (q_copies, q_shared)):
            copies[2].wait_recv()
            passed[1].start()
            copies[3].wait_recv()
            passed[2].start()
        for copies, passed in ((f_copies, f_shared), (q_copies, q_shared)):
            copies[4].wait_recv()
            copies[5].wait_recv()
            passed[3].start()

        @pl.when(chip_d == depth)
        def _():
            o_copies[4].wait_recv()
            o_copies[5].wait_recv()

        o_shared.start()
        total_ref[...] = end()
        for copy in f_shared + q_shared + [o_shared]:
            copy.wait()
        for copy in f_copies + q_copies:
            copy.wait_send()

        @pl.when(source)
        def _():
            for copy in o_copies[:4]:
                copy.wait_send()

        @pl.when(from_x)
        def _():
            o_copies[4].wait_send()

        @pl.when(from_y)
        def _():
            o_copies[5].wait_send()

    return pl.pallas_call(
        kernel,
        out_shape=[
            jax.ShapeDtypeStruct((2 * CHIPS,) + ff.shape, BF16),
            jax.ShapeDtypeStruct((2 * CHIPS,) + qkv.shape, BF16),
            jax.ShapeDtypeStruct((2,) + out.shape, BF16),
            jax.ShapeDtypeStruct(sums.shape, F32),
        ],
        in_specs=[VM] * 4,
        out_specs=[VM] * 4,
        scratch_shapes=[DMA((6,))] * 6 + [DMA((9,))] * 2 + total_scratch(sums.shape, depths),
        compiler_params=comm_params(collective_id),
        name="gather_gradients",
    )(ff, qkv, out, sums)


def lay_out(ff, qkv, out, sums, gain_one, gain_two):
    ctx, part_rows, columns = ff.shape
    half, width = out.shape[1:]
    shard = 2 * half
    depths = width // shard
    split = columns // depths

    def kernel(
        f_ref, q_ref, o_ref, s_ref, g1_ref, g2_ref,
        dq_ref, dk_ref, dv_ref, do_ref, dg_ref, du_ref, dd_ref, g1_out, g2_out, p_out, c_out,
    ):
        depth = lax.axis_index("wsh")
        one, two = g1_ref[...].astype(F32), g2_ref[...].astype(F32)
        one_column, two_column = as_column(one), as_column(two)
        for c in range(2):
            rows = slice(c * half, (c + 1) * half)
            do_ref[rows, :] = o_ref[c].astype(F32)
            for i, ref in enumerate((dq_ref, dk_ref, dv_ref)):
                wide = jnp.concatenate(
                    [q_ref[2 * p + c, i * half : (i + 1) * half, :].astype(F32) for p in range(CHIPS)],
                    axis=1,
                )
                ref[rows, :] = wide * one_column[rows]
            for i, ref in enumerate((dg_ref, du_ref)):
                for z in range(depths):
                    wide = jnp.concatenate(
                        [
                            f_ref[
                                2 * p + c, i * half : (i + 1) * half, z * split : (z + 1) * split
                            ].astype(F32)
                            for p in range(CHIPS)
                        ],
                        axis=1,
                    )
                    ref[rows, z * CHIPS * split : (z + 1) * CHIPS * split] = wide * two_column[rows]
            for p in range(CHIPS):
                at = (2 * p + c) * half
                dd_ref[at : at + half, :] = f_ref[2 * p + c, 2 * half :, :].astype(F32)
        for z in range(depths):

            @pl.when(depth == z)
            def _(z=z):
                g1_out[...] = s_ref[0:1, z * shard : (z + 1) * shard] / one
                g2_out[...] = s_ref[1:2, z * shard : (z + 1) * shard] / two

        scalars = jnp.sum(s_ref[...], axis=1, keepdims=True)
        for i in range(2):
            c_out[:, i : i + 1] = scalars[2 + i : 3 + i]
            for j in range(2):
                at = 4 + 2 * i + j
                p_out[i : i + 1, j : j + 1] = scalars[at : at + 1]

    square = jax.ShapeDtypeStruct((shard, width), F32)
    tall = jax.ShapeDtypeStruct((shard, columns * CHIPS), F32)
    row = jax.ShapeDtypeStruct((1, shard), F32)
    return pl.pallas_call(
        kernel,
        out_shape=[
            square,
            square,
            square,
            square,
            tall,
            tall,
            jax.ShapeDtypeStruct((ctx * half, width), F32),
            row,
            row,
            jax.ShapeDtypeStruct((2, 2), F32),
            jax.ShapeDtypeStruct((1, 2), F32),
        ],
        in_specs=[VM] * 6,
        out_specs=[VM] * 11,
        compiler_params=pltpu.CompilerParams(vmem_limit_bytes=VMEM_LIMIT),
        name="lay_out",
    )(ff, qkv, out, sums, gain_one, gain_two)


def plane_shards(
    states, block_slot, cont_lengths, valid_mask, teacher, out_grad, predict, correct,
    norm_attn, w_query, w_key, w_value, w_out, norm_ffn, w_gate, w_up, w_down,
):
    depths = lax.axis_size("wsh")
    _, rows, _, width = states.shape
    half = w_query.shape[0] // 2
    hidden_cols = w_gate.shape[1] // CHIPS
    slots, lengths = block_slot[0], cont_lengths[0]
    gain_one, gain_two = norm_attn[None], norm_ffn[None]
    states = states[0]
    new_states, up0, up1, hidden_grad, att_grad, *rest = forward(
        slots, lengths, predict, correct, states, out_grad[0], teacher[0], valid_mask, gain_one, gain_two,
        w_query, w_key, w_value, w_out, w_gate, w_up, w_down, 1,
    )
    out_grads, (ff_sum, sums, all_rows, weights, q_pairs, k_pairs, v_pairs, oT, lse) = rest[:4], rest[4:]
    ff_sum = lax.psum_scatter(
        ff_sum.reshape(depths * 3 * half, hidden_cols), "wsh", scatter_dimension=0, tiled=True
    )
    states_grad, qkv_sum, out_sum, sums = backward(
        slots, lengths, predict, correct, att_grad.reshape(-1, CHIP_COLS), q_pairs, k_pairs, v_pairs, oT, lse,
        weights, states, up0, up1, hidden_grad, sums, out_grads, all_rows.reshape(CHIPS, 2, rows, width), 2,
    )
    gathered = gather_gradients(ff_sum, qkv_sum, out_sum, sums, 3)
    dq, dk, dv, do, dg, du, dd, g_one, g_two, predict_grad, correct_grad = lay_out(
        *gathered, gain_one, gain_two
    )
    return (
        new_states[None], states_grad[None], predict_grad, correct_grad[0],
        g_one[0], dq, dk, dv, do, g_two[0], dg, du, dd,
    )


def fits_plane(mesh, states, block_slot, w_query, w_gate):
    ctx, depths = mesh.shape["ctx"], mesh.shape["wsh"]
    return (
        ctx == 2 * CHIPS
        and depths == CHIPS
        and states.shape[0] == depths
        and block_slot.shape[1] * BLK == 2 * PROMPT
        and states.shape[1] == 2 * PROMPT
        and w_query.shape[0] % (32 * depths) == 0
        and w_gate.shape[1] % (32 * CHIPS * depths) == 0
    )


def solution(mesh):
    in_specs = (
        P("wsh", "ctx", None, None),
        P("wsh", None),
        P("wsh", None),
        P("wsh", "ctx"),
        P("wsh", "ctx", None, None),
        P("wsh", "ctx", None, None),
        P(),
        P(),
        P("wsh"),
        P("wsh", None),
        P("wsh", None),
        P("wsh", None),
        P("wsh", None),
        P("wsh"),
        P("wsh", None),
        P("wsh", None),
        P("wsh", None),
    )
    out_specs = (
        P("wsh", "ctx", None, None),
        P("wsh", "ctx", None, None),
        P(),
        P(),
        P("wsh"),
        P("wsh", None),
        P("wsh", None),
        P("wsh", None),
        P("wsh", None),
        P("wsh"),
        P("wsh", None),
        P("wsh", None),
        P("wsh", None),
    )

    def step(*args):
        plane = fits_plane(mesh, args[0], args[1], args[9], args[14])
        body = plane_shards if plane else general_shards
        return jax.shard_map(
            body, mesh=mesh, in_specs=in_specs, out_specs=out_specs, check_vma=False
        )(*args)

    return step
```

```python
import functools
import math

import jax
import jax.numpy as jnp
from jax import lax
from jax.experimental import pallas as pl
from jax.experimental.pallas import tpu as pltpu
from jax.sharding import PartitionSpec as P

HEADS = 12
HD = 64
PROMPT = 1024
BLK = 64


EPSILON = 1e-06
NEGATIVE = -1e30
HIGHEST = lax.Precision.HIGHEST


def rms_forward(tensor, gain_vec):
    factor = lax.rsqrt(jnp.mean(tensor * tensor, axis=-1, keepdims=True) + EPSILON)
    return (tensor * factor * gain_vec, factor)


def rms_backward(tensor, factor, gain_vec, upstream):
    weighted = upstream * gain_vec
    gain_grad = jnp.sum(upstream * tensor * factor, axis=0)
    middle = jnp.mean(weighted * tensor, axis=-1, keepdims=True)
    return (factor * weighted - tensor * factor * factor * factor * middle, gain_grad)


def segment_starts(cont_lengths):
    count = cont_lengths.shape[1]
    index = jnp.arange(count, dtype=jnp.int32)
    before = index[:, None] < index[None, :]
    return PROMPT + jnp.sum(jnp.where(before[None], cont_lengths[:, :, None], 0), axis=1)


def token_places(block_slot, cont_lengths):
    groups, blocks = block_slot.shape
    offsets = jnp.arange(BLK, dtype=jnp.int32)
    places = (block_slot[:, :, None] * BLK + offsets[None, None, :]).reshape(groups, blocks * BLK)
    starts = segment_starts(cont_lengths)
    segments = jnp.sum((places[:, :, None] >= starts[:, None, :]).astype(jnp.int32), axis=2)
    return (places, segments)


def visible(query_place, query_segment, key_place, key_segment):
    earlier = key_place[:, None, :] <= query_place[:, :, None]
    shared = (key_segment[:, None, :] == 0) | (key_segment[:, None, :] == query_segment[:, :, None])
    return earlier & shared


def split_heads(tensor):
    return tensor.reshape(tensor.shape[0], tensor.shape[1], HEADS, HD)


def forward_block(running, query_part, key_part, value_part, allowed):

    def forward_compute(current):
        maximum, denominator, accumulated = current
        scores = jnp.einsum(
            "gqhd,gkhd->ghqk",
            split_heads(query_part),
            split_heads(key_part),
            preferred_element_type=jnp.float32,
        )
        masked = jnp.where(allowed[:, None], scores, NEGATIVE)
        new_max = jnp.maximum(maximum, jnp.max(masked, axis=-1))
        exponent = jnp.where(allowed[:, None], jnp.exp(masked - new_max[..., None]), 0.0)
        factor = jnp.exp(maximum - new_max)
        rescale = jnp.swapaxes(factor, 1, 2)[..., None]
        update = jnp.einsum(
            "ghqk,gkhd->gqhd",
            exponent.astype(jnp.bfloat16),
            split_heads(value_part),
            preferred_element_type=jnp.float32,
        )
        merged = (split_heads(accumulated) * rescale + update).reshape(accumulated.shape)
        return (new_max, denominator * factor + jnp.sum(exponent, axis=-1), merged)

    return lax.cond(jnp.any(allowed), forward_compute, lambda current: current, running)


def backward_block(
    query_part, grad_part, key_part, value_part, allowed, maximum, denominator, delta_sum
):
    scores = jnp.einsum(
        "gqhd,gkhd->ghqk",
        split_heads(query_part),
        split_heads(key_part),
        preferred_element_type=jnp.float32,
    )
    exponent = jnp.where(allowed[:, None], jnp.exp(scores - maximum[..., None]), 0.0)
    probability = exponent / denominator[..., None]
    prob_grad = jnp.einsum(
        "gqhd,gkhd->ghqk",
        split_heads(grad_part),
        split_heads(value_part),
        preferred_element_type=jnp.float32,
    )
    score_grad = (probability * (prob_grad - delta_sum[..., None])).astype(jnp.bfloat16)
    return (probability.astype(jnp.bfloat16), score_grad)


def general_shards(
    states,
    block_slot,
    cont_lengths,
    valid_mask,
    teacher,
    out_grad,
    predict,
    correct,
    norm_attn,
    w_query,
    w_key,
    w_value,
    w_out,
    norm_ffn,
    w_gate,
    w_up,
    w_down,
):
    groups, local_len = valid_mask.shape
    model_width = states.shape[3]
    row_count = groups * local_len
    group_len = block_slot.shape[1] * BLK
    gain_one, query_w, key_w, value_w, out_w, gain_two, gate_w, up_w, down_w = (
        lax.all_gather(norm_attn, "wsh", axis=0, tiled=True),
        lax.all_gather(w_query, "wsh", axis=0, tiled=True),
        lax.all_gather(w_key, "wsh", axis=0, tiled=True),
        lax.all_gather(w_value, "wsh", axis=0, tiled=True),
        lax.all_gather(w_out, "wsh", axis=0, tiled=True),
        lax.all_gather(norm_ffn, "wsh", axis=0, tiled=True),
        lax.all_gather(w_gate, "wsh", axis=0, tiled=True),
        lax.all_gather(w_up, "wsh", axis=0, tiled=True),
        lax.all_gather(w_down, "wsh", axis=0, tiled=True),
    )
    valid_float = valid_mask.astype(jnp.float32)
    valid_total = lax.psum(jnp.sum(valid_float), ("ctx", "wsh"))
    places, segments = token_places(block_slot, cont_lengths)
    offset = lax.axis_index("ctx") * local_len
    own_place = lax.dynamic_slice_in_dim(places, offset, local_len, 1)
    own_segment = lax.dynamic_slice_in_dim(segments, offset, local_len, 1)
    inputs = states.astype(jnp.float32)
    mixed_states = jnp.einsum("ij,gtjd->gtid", predict, inputs, precision=HIGHEST)
    active = mixed_states[:, :, 0].reshape(row_count, model_width)
    gain_first = gain_one.astype(jnp.float32)
    normed, factor_one = rms_forward(active, gain_first)
    normed_low = normed.astype(jnp.bfloat16)
    queries = (
        jnp.dot(normed_low, query_w, preferred_element_type=jnp.float32)
        .astype(jnp.bfloat16)
        .reshape(groups, local_len, model_width)
    )
    key_rows = (
        jnp.dot(normed_low, key_w, preferred_element_type=jnp.float32)
        .astype(jnp.bfloat16)
        .reshape(groups, local_len, model_width)
    )
    values = (
        jnp.dot(normed_low, value_w, preferred_element_type=jnp.float32)
        .astype(jnp.bfloat16)
        .reshape(groups, local_len, model_width)
    )
    initial = (
        jnp.full((groups, HEADS, local_len), NEGATIVE, jnp.float32),
        jnp.zeros((groups, HEADS, local_len), jnp.float32),
        jnp.zeros((groups, local_len, model_width), jnp.float32),
    )
    piece_keys = lax.all_gather(key_rows, "ctx", axis=1, tiled=True)
    piece_values = lax.all_gather(values, "ctx", axis=1, tiled=True)
    piece_len = piece_keys.shape[1]
    block_size = math.gcd(piece_len, local_len)

    def fold_one_block(current, block_index):
        begin = block_index * block_size
        key_part = lax.dynamic_slice_in_dim(piece_keys, begin, block_size, 1)
        value_part = lax.dynamic_slice_in_dim(piece_values, begin, block_size, 1)
        key_place = lax.dynamic_slice_in_dim(places, begin, block_size, 1)
        key_segment = lax.dynamic_slice_in_dim(segments, begin, block_size, 1)
        allowed = visible(own_place, own_segment, key_place, key_segment)
        return (forward_block(current, queries, key_part, value_part, allowed), None)

    finished, unused = lax.scan(
        fold_one_block, initial, jnp.arange(piece_len // block_size, dtype=jnp.int32)
    )
    maximum, denominator, accumulated = finished
    attended = (split_heads(accumulated) / jnp.swapaxes(denominator, 1, 2)[..., None]).reshape(
        row_count, model_width
    )
    attended_low = attended.astype(jnp.bfloat16)
    hidden = active + jnp.dot(attended_low, out_w, preferred_element_type=jnp.float32)
    gain_second = gain_two.astype(jnp.float32)
    normed_two, factor_two = rms_forward(hidden, gain_second)
    normed_two_low = normed_two.astype(jnp.bfloat16)
    gate_proj = jnp.dot(normed_two_low, gate_w, preferred_element_type=jnp.float32)
    up_proj = jnp.dot(normed_two_low, up_w, preferred_element_type=jnp.float32)
    inner_act, inner_pull = jax.vjp(
        lambda gate_in, up_in: jax.nn.gelu(gate_in, approximate=True) * up_in, gate_proj, up_proj
    )
    inner_low = inner_act.astype(jnp.bfloat16)
    result = hidden + jnp.dot(inner_low, down_w, preferred_element_type=jnp.float32)
    difference = (result - active).reshape(groups, local_len, 1, model_width)
    out_states = mixed_states + correct[None, None, :, None] * difference
    new_states = out_states.astype(jnp.bfloat16)
    loss_ratio = lax.axis_size("wsh") * groups * group_len / valid_total
    upstream = out_grad.astype(jnp.float32) + loss_ratio * valid_float[:, :, None, None] * (
        out_states - teacher.astype(jnp.float32)
    )
    correct_local = jnp.sum(upstream * difference, axis=(0, 1, 3))
    result_grad = jnp.einsum("i,gtid->gtd", correct, upstream, precision=HIGHEST).reshape(
        row_count, model_width
    )
    result_low = result_grad.astype(jnp.bfloat16)
    down_grad = jnp.einsum("rf,rd->fd", inner_low, result_low, preferred_element_type=jnp.float32)
    inner_grad = jnp.einsum("rd,fd->rf", result_low, down_w, preferred_element_type=jnp.float32)
    gate_grad, up_grad = inner_pull(inner_grad)
    gate_low = gate_grad.astype(jnp.bfloat16)
    up_low = up_grad.astype(jnp.bfloat16)
    gate_w_grad = jnp.einsum(
        "rd,rf->df", normed_two_low, gate_low, preferred_element_type=jnp.float32
    )
    up_w_grad = jnp.einsum("rd,rf->df", normed_two_low, up_low, preferred_element_type=jnp.float32)
    normed_two_grad = jnp.einsum(
        "rf,df->rd", gate_low, gate_w, preferred_element_type=jnp.float32
    ) + jnp.einsum("rf,df->rd", up_low, up_w, preferred_element_type=jnp.float32)
    hidden_norm_grad, gain_two_grad = rms_backward(hidden, factor_two, gain_second, normed_two_grad)
    hidden_grad = result_grad + hidden_norm_grad
    hidden_low = hidden_grad.astype(jnp.bfloat16)
    out_w_grad = jnp.einsum(
        "rc,rd->cd", attended_low, hidden_low, preferred_element_type=jnp.float32
    )
    attended_grad = jnp.einsum(
        "rd,cd->rc", hidden_low, out_w, preferred_element_type=jnp.float32
    ).astype(jnp.bfloat16)
    delta_sum = jnp.swapaxes(
        jnp.sum(
            split_heads(
                (attended_grad.astype(jnp.float32) * attended).reshape(
                    groups, local_len, model_width
                )
            ),
            axis=-1,
        ),
        1,
        2,
    )
    grad_local = attended_grad.reshape(groups, local_len, model_width)
    zero_grad = jnp.zeros((groups, local_len, model_width), jnp.float32)
    all_keys, all_values = (
        lax.all_gather(key_rows, "ctx", axis=1, tiled=True),
        lax.all_gather(values, "ctx", axis=1, tiled=True),
    )

    def query_step(current, block_index):
        begin = block_index * local_len
        key_part = lax.dynamic_slice_in_dim(all_keys, begin, local_len, 1)
        value_part = lax.dynamic_slice_in_dim(all_values, begin, local_len, 1)
        key_place = lax.dynamic_slice_in_dim(places, begin, local_len, 1)
        key_segment = lax.dynamic_slice_in_dim(segments, begin, local_len, 1)
        allowed = visible(own_place, own_segment, key_place, key_segment)

        def query_compute(query_sum):
            prob_low, score_grad = backward_block(
                queries, grad_local, key_part, value_part, allowed, maximum, denominator, delta_sum
            )
            return query_sum + jnp.einsum(
                "ghqk,gkhd->gqhd",
                score_grad,
                split_heads(key_part),
                preferred_element_type=jnp.float32,
            ).reshape(groups, local_len, model_width)

        return (
            lax.cond(jnp.any(allowed), query_compute, lambda query_sum: query_sum, current),
            None,
        )

    finished, unused = lax.scan(
        query_step, zero_grad, jnp.arange(group_len // local_len, dtype=jnp.int32)
    )
    term_rows = local_len * lax.axis_size("ctx")
    key_block_size = math.gcd(term_rows, local_len)

    def key_one_block(block_index):
        begin = block_index * key_block_size
        key_part = lax.dynamic_slice_in_dim(all_keys, begin, key_block_size, 1)
        value_part = lax.dynamic_slice_in_dim(all_values, begin, key_block_size, 1)
        key_place = lax.dynamic_slice_in_dim(places, begin, key_block_size, 1)
        key_segment = lax.dynamic_slice_in_dim(segments, begin, key_block_size, 1)
        allowed = visible(own_place, own_segment, key_place, key_segment)

        def one_compute(unused_arg):
            prob_low, score_grad = backward_block(
                queries, grad_local, key_part, value_part, allowed, maximum, denominator, delta_sum
            )
            key_add = jnp.einsum(
                "ghqk,gqhd->kghd",
                score_grad,
                split_heads(queries),
                preferred_element_type=jnp.float32,
            ).reshape(key_block_size, groups, model_width)
            value_add = jnp.einsum(
                "ghqk,gqhd->kghd",
                prob_low,
                split_heads(grad_local),
                preferred_element_type=jnp.float32,
            ).reshape(key_block_size, groups, model_width)
            return jnp.stack([key_add, value_add], axis=1)

        return lax.cond(
            jnp.any(allowed),
            one_compute,
            lambda unused_arg: jnp.zeros((key_block_size, 2, groups, model_width), jnp.float32),
            0,
        )

    summed = lax.psum_scatter(
        lax.map(key_one_block, jnp.arange(term_rows // key_block_size, dtype=jnp.int32))
        .reshape(term_rows, 2, groups, model_width)
        .astype(jnp.bfloat16),
        "ctx",
        scatter_dimension=0,
        tiled=True,
    ).astype(jnp.float32)
    key_grad = jnp.swapaxes(summed[:, 0], 0, 1)
    value_grad = jnp.swapaxes(summed[:, 1], 0, 1)
    query_low = finished.reshape(row_count, model_width).astype(jnp.bfloat16)
    key_low = key_grad.reshape(row_count, model_width).astype(jnp.bfloat16)
    value_low = value_grad.reshape(row_count, model_width).astype(jnp.bfloat16)
    query_w_grad = jnp.einsum(
        "rc,rd->cd", normed_low, query_low, preferred_element_type=jnp.float32
    )
    key_w_grad = jnp.einsum("rc,rd->cd", normed_low, key_low, preferred_element_type=jnp.float32)
    value_w_grad = jnp.einsum(
        "rc,rd->cd", normed_low, value_low, preferred_element_type=jnp.float32
    )
    normed_grad = (
        jnp.einsum("rd,cd->rc", query_low, query_w, preferred_element_type=jnp.float32)
        + jnp.einsum("rd,cd->rc", key_low, key_w, preferred_element_type=jnp.float32)
        + jnp.einsum("rd,cd->rc", value_low, value_w, preferred_element_type=jnp.float32)
    )
    active_norm_grad, gain_one_grad = rms_backward(active, factor_one, gain_first, normed_grad)
    active_grad = (hidden_grad + active_norm_grad - result_grad).reshape(
        groups, local_len, 1, model_width
    )
    mixed_grad = jnp.concatenate([upstream[:, :, :1] + active_grad, upstream[:, :, 1:]], axis=2)
    predict_local = jnp.einsum("gtid,gtjd->ij", mixed_grad, inputs, precision=HIGHEST)
    states_grad = jnp.einsum("ij,gtid->gtjd", predict, mixed_grad, precision=HIGHEST).astype(
        jnp.bfloat16
    )
    predict_grad, correct_grad = lax.psum((predict_local, correct_local), ("ctx", "wsh"))
    (
        gain_one_rows,
        query_rows,
        key_grad_rows,
        value_rows,
        out_rows,
        gain_two_rows,
        gate_rows,
        up_rows,
        down_rows,
    ) = (
        lax.psum_scatter(
            gain_one_grad.astype(jnp.bfloat16), "wsh", scatter_dimension=0, tiled=True
        ).astype(jnp.float32),
        lax.psum_scatter(
            query_w_grad.astype(jnp.bfloat16), "wsh", scatter_dimension=0, tiled=True
        ).astype(jnp.float32),
        lax.psum_scatter(
            key_w_grad.astype(jnp.bfloat16), "wsh", scatter_dimension=0, tiled=True
        ).astype(jnp.float32),
        lax.psum_scatter(
            value_w_grad.astype(jnp.bfloat16), "wsh", scatter_dimension=0, tiled=True
        ).astype(jnp.float32),
        lax.psum_scatter(
            out_w_grad.astype(jnp.bfloat16), "wsh", scatter_dimension=0, tiled=True
        ).astype(jnp.float32),
        lax.psum_scatter(
            gain_two_grad.astype(jnp.bfloat16), "wsh", scatter_dimension=0, tiled=True
        ).astype(jnp.float32),
        lax.psum_scatter(
            gate_w_grad.astype(jnp.bfloat16), "wsh", scatter_dimension=0, tiled=True
        ).astype(jnp.float32),
        lax.psum_scatter(
            up_w_grad.astype(jnp.bfloat16), "wsh", scatter_dimension=0, tiled=True
        ).astype(jnp.float32),
        lax.psum_scatter(
            down_grad.astype(jnp.bfloat16), "wsh", scatter_dimension=0, tiled=True
        ).astype(jnp.float32),
    )
    totals = (
        lax.psum(gain_one_rows.astype(jnp.bfloat16), "ctx").astype(jnp.float32),
        lax.psum(query_rows.astype(jnp.bfloat16), "ctx").astype(jnp.float32),
        lax.psum(key_grad_rows.astype(jnp.bfloat16), "ctx").astype(jnp.float32),
        lax.psum(value_rows.astype(jnp.bfloat16), "ctx").astype(jnp.float32),
        lax.psum(out_rows.astype(jnp.bfloat16), "ctx").astype(jnp.float32),
        lax.psum(gain_two_rows.astype(jnp.bfloat16), "ctx").astype(jnp.float32),
        lax.psum(gate_rows.astype(jnp.bfloat16), "ctx").astype(jnp.float32),
        lax.psum(up_rows.astype(jnp.bfloat16), "ctx").astype(jnp.float32),
        lax.psum(down_rows.astype(jnp.bfloat16), "ctx").astype(jnp.float32),
    )
    return (new_states, states_grad, predict_grad, correct_grad) + tuple(totals)


MESH = pl.DeviceIdType.MESH
F32 = jnp.float32
BF16 = jnp.bfloat16
CHIPS = 4
VMEM_LIMIT = 60 * 2**20
DMA = pltpu.SemaphoreType.DMA


def place_on_mesh():
    ctx = lax.axis_index("ctx")
    depth = lax.axis_index("wsh")
    chip = ctx // 2
    core = ctx % 2
    chip_x = chip + 1 - 2 * (chip % 2)
    chip_y = chip + 2 - 4 * (chip // 2)
    return depth, chip, core, chip_x, chip_y, 3 - chip


def signal_all(devices):
    barrier = pltpu.get_barrier_semaphore()
    for device in devices:
        pl.semaphore_signal(barrier, inc=1, device_id=device, device_id_type=MESH)


def wait_all(devices):
    pl.semaphore_wait(pltpu.get_barrier_semaphore(), len(devices))


def remote(src, dst, send, recv, index, device):
    return pltpu.make_async_remote_copy(
        src_ref=src,
        dst_ref=dst,
        send_sem=send.at[index],
        recv_sem=recv.at[index],
        device_id=device,
        device_id_type=MESH,
    )


def comm_params(collective_id):
    return pltpu.CompilerParams(
        collective_id=collective_id, has_side_effects=True, vmem_limit_bytes=VMEM_LIMIT
    )


ANY = pl.BlockSpec(memory_space=pl.ANY)
VM = pl.BlockSpec(memory_space=pltpu.VMEM)
SM = pl.BlockSpec(memory_space=pltpu.SMEM)


def ring_sends(own, out, slot_of, chip, core, depth, chip_x, chip_y, send, recv):
    half = own.shape[0] // 2
    top, low = pl.ds(0, half), pl.ds(half, half)
    dev_x, dev_y = (2 * chip_x + core, depth), (2 * chip_y + core, depth)
    here = slot_of(chip)
    return [
        remote(own.at[top], out.at[here, top], send, recv, 0, dev_x),
        remote(own.at[low], out.at[here, low], send, recv, 1, dev_y),
        remote(own.at[low], out.at[here, low], send, recv, 2, dev_x),
        remote(own.at[top], out.at[here, top], send, recv, 3, dev_y),
        remote(out.at[slot_of(chip_x), top], out.at[slot_of(chip_x), top], send, recv, 4, dev_y),
        remote(out.at[slot_of(chip_y), low], out.at[slot_of(chip_y), low], send, recv, 5, dev_x),
    ]


NT = (((1,), (1,)), ((), ()))
TN = (((0,), (0,)), ((), ()))
TILE = 256
ROWS = 32
LOCAL_HEADS = HEADS // CHIPS
CHIP_COLS = LOCAL_HEADS * HD


def head_mask(rows, head):
    lane = lax.broadcasted_iota(jnp.int32, (rows, CHIP_COLS), 1)
    return (lane >= head * HD) & (lane < (head + 1) * HD)


def aligned(index, size):
    return pl.ds(pl.multiple_of(index * size, size), size)


def norm_factor(rows):
    return lax.rsqrt(jnp.mean(rows * rows, axis=1, keepdims=True) + EPSILON)


def as_column(row):
    return jnp.broadcast_to(row, (8, row.shape[1])).T[:, 0:1]


def mix(states_ref, at, p_ref, i):
    return p_ref[i, 0] * states_ref[at, 0, :].astype(F32) + p_ref[i, 1] * states_ref[at, 1, :].astype(F32)


def plane_peers(chip, core, depth, chip_x, chip_y, chip_d):
    same = [(2 * c + core, depth) for c in (chip_x, chip_y, chip_d)]
    return same + [(2 * c + 1 - core, depth) for c in (chip, chip_x, chip_y, chip_d)]


def total_over_mesh(own_ref, arrived, staged, far, across, peers, bsend, brecv, csend, crecv):
    first = [remote(own_ref, arrived.at[i], bsend, brecv, i, d) for i, d in enumerate(across)]
    second = [remote(staged, far.at[i], csend, crecv, i, d) for i, d in enumerate(peers)]

    def start():
        for copy in first:
            copy.start()

    def turn():
        total = own_ref[...]
        for i, copy in enumerate(first):
            copy.wait_recv()
        for i in range(len(first)):
            total = total + arrived[i]
        staged[...] = total
        for copy in second:
            copy.start()

    def end():
        for copy in second:
            copy.wait_recv()
        total = staged[...]
        for i in range(len(second)):
            total = total + far[i]
        for copy in first + second:
            copy.wait_send()
        return total

    return start, turn, end


def total_scratch(shape, depths):
    return [
        pltpu.VMEM((depths - 1,) + shape, F32),
        pltpu.VMEM(shape, F32),
        pltpu.VMEM((2 * CHIPS - 1,) + shape, F32),
        DMA((depths - 1,)),
        DMA((depths - 1,)),
        DMA((2 * CHIPS - 1,)),
        DMA((2 * CHIPS - 1,)),
    ]


def gelu_parts(v):
    scale = math.sqrt(2 / math.pi)
    square = v * v
    t = jnp.tanh(scale * v * (1.0 + 0.044715 * square))
    rise = 0.5 * (1.0 + t)
    return v * rise, rise + 0.5 * v * (1.0 - t * t) * scale * (1.0 + 0.134145 * square)


def pair_places(slots_ref, pair):
    one, two = slots_ref[2 * pair], slots_ref[2 * pair + 1]
    second = (one >= PROMPT // BLK).astype(jnp.int32)
    return second, jnp.minimum(one, two), jnp.maximum(one, two)


def own_pair(pair, per_device):
    core = lax.axis_index("ctx") % 2
    pairs = per_device // 2
    return (pair // pairs) * per_device + core * pairs + pair % pairs


PER_TILE = TILE // BLK


def fill_bias(bias, kind, tile_step, slots_ref, lengths_ref, per_device, group_pairs):
    lane = lax.broadcasted_iota(jnp.int32, (1, TILE), 1)
    high = jnp.zeros((1, TILE), jnp.int32)
    for i in range(PER_TILE):
        _, prompt, cont = pair_places(slots_ref, own_pair(tile_step * PER_TILE + i, per_device))
        block = prompt if kind == 0 else cont
        high = jnp.where(lane >= i * BLK, (block - i) * BLK + lane, high)
    low = jnp.zeros((1, TILE), jnp.int32)
    if kind == 1:
        start = PROMPT
        for i in range(lengths_ref.shape[0]):
            low = jnp.where(high >= start, start, low)
            start = start + lengths_ref[i]
    offset = lax.broadcasted_iota(jnp.int32, (BLK, TILE), 0)

    def one_block(pair, _):
        _, prompt, cont = pair_places(slots_ref, pair)
        base = (prompt if kind == 0 else cont) * BLK
        seen = offset <= high - base
        if kind == 1:
            seen = seen & (offset >= low - base)
        bias[pair // PER_TILE, aligned(pair % PER_TILE, BLK), 0:TILE] = jnp.where(seen, 0.0, NEGATIVE)
        return 0

    lax.fori_loop(0, group_pairs, one_block, 0)


def either(second, one, two):
    swap = second == 1
    return jnp.where(swap, two, one), jnp.where(swap, one, two)


def to_pair_order(source, target, slots_ref, group_pairs):
    def one_pair(pair, _):
        second, _, _ = pair_places(slots_ref, pair)
        first, last = either(second, source[aligned(2 * pair, BLK), :], source[aligned(2 * pair + 1, BLK), :])
        target[aligned(pair, BLK), :] = first
        target[aligned(group_pairs + pair, BLK), :] = last
        return 0

    lax.fori_loop(0, group_pairs, one_pair, 0)


def own_to_pair_order(source, target, slots_ref, pairs, per_device):
    def one_pair(pair, _):
        second, _, _ = pair_places(slots_ref, own_pair(pair, per_device))
        first, last = either(second, source[aligned(2 * pair, BLK), :], source[aligned(2 * pair + 1, BLK), :])
        target[aligned(pair, BLK), :] = first
        target[aligned(pairs + pair, BLK), :] = last
        return 0

    lax.fori_loop(0, pairs, one_pair, 0)


def own_to_slot_order(source, target, slots_ref, pairs, per_device):
    def one_pair(pair, _):
        second, _, _ = pair_places(slots_ref, own_pair(pair, per_device))
        first, last = either(second, source[aligned(pair, BLK), :], source[aligned(pairs + pair, BLK), :])
        target[aligned(2 * pair, BLK), :] = first
        target[aligned(2 * pair + 1, BLK), :] = last
        return 0

    lax.fori_loop(0, pairs, one_pair, 0)


def line_reduce(pieces, acc, up_in, down_in, up_out, down_out, sems):
    depth, chip, core, _, _, _ = place_on_mesh()
    depths = pieces.shape[0]
    last = depths - 1
    up_send, up_recv, down_send, down_recv = sems
    above = (2 * chip + core, lax.rem(depth + 1, depths))
    below = (2 * chip + core, lax.rem(depth + last, depths))

    def up(source, k):
        return remote(source, up_in.at[k], up_send, up_recv, k, above)

    def down(source, k):
        return remote(source, down_in.at[k], down_send, down_recv, k, below)

    def start():
        @pl.when(depth == 0)
        def _():
            for k in range(last):
                up(pieces.at[last - k], k).start()

        @pl.when(depth == last)
        def _():
            for k in range(last):
                down(pieces.at[k], k).start()

    def hop(k):
        @pl.when((depth >= 1) & (depth <= k))
        def _():
            up(up_in.at[k - 1], k - 1).wait_recv()
            mine = pieces[jnp.clip(depth + last - k, 0, last)]
            up_out[k - 1] = (mine.astype(F32) + up_in[k - 1].astype(F32)).astype(BF16)
            up(up_out.at[k - 1], k).start()

        @pl.when((depth <= last - 1) & (depth >= last - k))
        def _():
            down(down_in.at[k - 1], k - 1).wait_recv()
            mine = pieces[jnp.clip(depth + k - last, 0, last)]
            down_out[k - 1] = (mine.astype(F32) + down_in[k - 1].astype(F32)).astype(BF16)
            down(down_out.at[k - 1], k).start()

    def result():
        acc[...] = pieces[depth].astype(F32)

        @pl.when(depth >= 1)
        def _():
            up(up_in.at[last - 1], last - 1).wait_recv()
            acc[...] += up_in[last - 1].astype(F32)

        @pl.when(depth <= last - 1)
        def _():
            down(down_in.at[last - 1], last - 1).wait_recv()
            acc[...] += down_in[last - 1].astype(F32)

    def finish():
        @pl.when(depth == 0)
        def _():
            for k in range(last):
                up(pieces.at[last - k], k).wait_send()

        @pl.when(depth == last)
        def _():
            for k in range(last):
                down(pieces.at[k], k).wait_send()

        for k in range(1, last):

            @pl.when((depth >= 1) & (depth <= k))
            def _(k=k):
                up(up_out.at[k - 1], k).wait_send()

            @pl.when((depth <= last - 1) & (depth >= last - k))
            def _(k=k):
                down(down_out.at[k - 1], k).wait_send()

    return start, hop, result, finish


def line_reduce_scratch(shape, depths):
    buffers = [(depths - 1,), (depths - 1,), (depths - 2,), (depths - 2,)]
    return [pltpu.VMEM(shape, F32)] + [pltpu.VMEM(lead + shape, BF16) for lead in buffers], [
        DMA((depths - 1,))
    ] * 4


def forward(
    slots, lengths, predict, correct, states, out_grad, teacher, valid, gain_one, gain_two,
    w_query, w_key, w_value, w_out, w_gate, w_up, w_down, collective_id,
):
    rows, _, width = states.shape
    shard = w_query.shape[0]
    half = shard // 2
    depths = width // shard
    hidden_cols = w_gate.shape[1]
    columns = hidden_cols // CHIPS
    split = columns // depths
    out_rows = shard // CHIPS
    blocks = rows // ROWS
    col_tiles = columns // TILE
    tokens = 2 * CHIPS * rows
    queries = CHIPS * rows
    tiles = queries // TILE
    per_device = rows // BLK
    group_pairs = tokens // (2 * BLK)
    pairs = queries // (2 * BLK)
    mesh_tokens = tokens * depths
    piece_lanes = 3 * CHIP_COLS

    def kernel(
        slots_ref, lengths_ref, p_ref, c_ref, s_ref, g_ref, t_ref, v_ref, g1_ref, g2_ref,
        wq_ref, wk_ref, wv_ref, wo_ref, wg_ref, wu_ref, wd_ref,
        new_ref, up0_ref, up1_ref, hg_ref, da_ref, dw0_ref, dw1_ref, dw2_ref, dw3_ref, ff_ref, sums_ref,
        all_rows, w_all, q_pairs, k_pairs, v_pairs, oT_ref, lse_ref,
        w_ff, w_wo, qkv, att_all, hidden, own, x_rows, r_rows, xT, innerT, inner, gate, up, gate_low, up_low,
        own_weight, part1, part2, got1, got2, dw, dw_other, buf, wide, count, q_slot, k_slot, v_slot, vT,
        lsend, fsend, frecv, fosend, forecv, qsend, qrecv, qosend, qorecv,
        osend, orecv, oosend, oorecv, opsend, oprecv,
        rsend, rrecv, rosend, rorecv, send0, recv0, send1, recv1, send2, recv2, send3, recv3,
        ag1s, ag1r, ag2s, ag2r, dsend, drecv, *total_refs,
    ):
        depth, chip, core, chip_x, chip_y, chip_d = place_on_mesh()
        near = [(c, (2 * c + core, depth)) for c in (chip_x, chip_y, chip_d)]
        other = (2 * chip + 1 - core, depth)
        across = [
            (2 * chip + core, lax.rem(depth + step, depths)) for step in range(1, depths)
        ]
        peers = plane_peers(chip, core, depth, chip_x, chip_y, chip_d)
        signal_all(peers + across)

        mine = pl.ds(core * half, half)
        loads = [
            pltpu.make_async_copy(w.at[mine], buf.at[i], lsend.at[i])
            for i, w in enumerate((wq_ref, wk_ref, wv_ref))
        ] + [
            pltpu.make_async_copy(wg_ref.at[mine], wide.at[0], lsend.at[3]),
            pltpu.make_async_copy(wu_ref.at[mine], wide.at[1], lsend.at[4]),
            pltpu.make_async_copy(
                wd_ref.at[pl.ds(chip * split + core * half, half)], w_ff.at[2, depth, core], lsend.at[5]
            ),
            pltpu.make_async_copy(
                wo_ref.at[pl.ds(chip * out_rows, out_rows)], w_wo.at[depth, chip], lsend.at[6]
            ),
        ]
        for copy in loads:
            copy.start()
        count[...] = jnp.broadcast_to(
            jnp.sum(v_ref[...].astype(F32), axis=1, keepdims=True), count.shape
        )

        def input_norm(i, _):
            at = aligned(i, ROWS)
            active = mix(s_ref, at, p_ref, 0)
            own[0, at, :] = (active * norm_factor(active)).astype(BF16)
            return 0

        lax.fori_loop(0, blocks, input_norm, 0)

        def gain_column(ref):
            both = jnp.broadcast_to(ref[...].astype(F32), (8, shard)).T
            return jnp.where(core == 0, both[:half, 0:1], both[half:, 0:1])

        one, two = gain_column(g1_ref), gain_column(g2_ref)
        wait_all(peers + across)

        def slot(chip_index):
            return 2 * chip_index + core

        start_count, turn_count, end_count = total_over_mesh(
            count, *total_refs[:3], across, peers, *total_refs[3:]
        )
        start_count()
        ring0 = ring_sends(
            own.at[0], all_rows, slot, chip, core, depth, chip_x, chip_y, rsend, rrecv
        )
        for copy in ring0[:4]:
            copy.start()

        def rows_to_other(index, chip_index):
            ref = all_rows.at[slot(chip_index)]
            return remote(own.at[0] if index == 0 else ref, ref, rosend, rorecv, index, other)

        shared0 = [rows_to_other(i, c) for i, c in enumerate((chip, chip_x, chip_y, chip_d))]
        shared0[0].start()
        all_rows[slot(chip)] = own[0]

        for copy in loads[:3]:
            copy.wait()
        for p in range(CHIPS):

            @pl.when(chip == p)
            def _(p=p):
                cols = jnp.concatenate(
                    [buf[i, :, p * CHIP_COLS : (p + 1) * CHIP_COLS].astype(F32) for i in range(3)], axis=1
                )
                qkv[depth, core] = (cols * one).astype(BF16)

        qkv_mine = qkv.at[depth, core]
        q_copies = [
            remote(qkv_mine, qkv_mine, qsend, qrecv, i, device) for i, device in enumerate(across)
        ]
        q_shared = [remote(qkv_mine, qkv_mine, qosend, qorecv, 0, other)]
        for copy in q_copies + q_shared:
            copy.start()

        loads[6].wait()
        o_copies = [
            remote(w_wo.at[depth, chip], w_wo.at[depth, chip], osend, orecv, i, device)
            for i, device in enumerate(across)
        ]
        o_shared = []
        for i in range(depths - 1):
            came = w_wo.at[lax.rem(depth + depths - 1 - i, depths), chip]
            o_shared.append(remote(came, came, oosend, oorecv, i, other))

        def carried(i, act):
            pl.when(core == (i + 1) % 2)(act)

        def not_carried(i, act):
            pl.when(core != (i + 1) % 2)(act)

        for i in range(depths - 1):
            carried(i, o_copies[i].start)

        for copy in loads[3:6]:
            copy.wait()
        for p in range(CHIPS):

            @pl.when(chip == p)
            def _(p=p):
                for i in range(2):
                    cols = jnp.concatenate(
                        [
                            wide[i, :, (z * CHIPS + p) * split : (z * CHIPS + p + 1) * split].astype(F32)
                            for z in range(depths)
                        ],
                        axis=1,
                    )
                    w_ff[i, depth, core] = (cols * two).astype(BF16)

        line_up = (2 * chip + core, lax.rem(depth + 1, depths))
        line_down = (2 * chip + core, lax.rem(depth + depths - 1, depths))
        hops = []
        for stage in range(1, depths):
            for direction, device, index in ((1, line_up, stage - 1), (-1, line_down, depths + stage - 2)):
                goes = jnp.clip(depth - direction * (stage - 1), 0, depths - 1)
                comes = jnp.clip(depth - direction * stage, 0, depths - 1)
                piece, came = w_ff.at[:, goes, core], w_ff.at[:, comes, core]
                if direction == 1:
                    sends, receives = (depth >= stage - 1) & (depth < depths - 1), depth >= stage
                else:
                    sends, receives = (depth <= depths - stage) & (depth > 0), depth < depths - stage
                hops.append(
                    (
                        stage,
                        sends,
                        receives,
                        remote(piece, piece, fsend, frecv, index, device),
                        remote(came, came, fosend, forecv, index, other),
                    )
                )
        ff_mine = remote(w_ff.at[:, depth, core], w_ff.at[:, depth, core], fosend, forecv, 2 * depths - 2, other)
        ff_mine.start()

        def send_hop(stage):
            for at, sends, _, hop, _ in hops:
                if at == stage:
                    pl.when(sends)(hop.start)

        def take_hop(stage):
            for at, _, receives, hop, share in hops:
                if at == stage:

                    @pl.when(receives)
                    def _(hop=hop, share=share):
                        hop.wait_recv()
                        share.start()

        send_hop(1)
        turn_count()
        ring0[0].wait_recv()
        ring0[4].start()
        ring0[1].wait_recv()
        ring0[5].start()
        for i in range(depths - 1):
            q_copies[i].wait_recv()
            came = qkv.at[lax.rem(depth + depths - 1 - i, depths), core]
            share = remote(came, came, qosend, qorecv, 1 + i, other)
            share.start()
            q_shared.append(share)
        ring0[2].wait_recv()
        shared0[1].start()
        ring0[3].wait_recv()
        shared0[2].start()
        for copy in q_shared:
            copy.wait_recv()
        for i in range(3):
            for z in range(depths):
                for c in range(2):
                    at = (z * 2 + c) * half
                    w_all[i, at : at + half, :] = qkv[z, c, :, i * CHIP_COLS : (i + 1) * CHIP_COLS]

        def project(device_slot, with_queries):
            x = all_rows[device_slot]
            at = aligned(device_slot, rows)
            k_slot[at, :] = jnp.dot(x, w_all[1], preferred_element_type=F32).astype(BF16)
            v_slot[at, :] = jnp.dot(x, w_all[2], preferred_element_type=F32).astype(BF16)
            if with_queries:
                q_slot[aligned(device_slot // 2, rows), :] = jnp.dot(
                    x, w_all[0], preferred_element_type=F32
                ).astype(BF16)

        for c in (chip, chip_x, chip_y):
            project(slot(c), True)
        for i, c in enumerate((chip, chip_x, chip_y)):
            shared0[i].wait_recv()
            project(2 * c + 1 - core, False)
        ring0[4].wait_recv()
        ring0[5].wait_recv()
        shared0[3].start()
        project(slot(chip_d), True)
        for i in range(depths - 1):

            def came_here(i=i):
                o_copies[i].wait_recv()
                o_shared[i].start()

            carried(i, came_here)
        for i in range(depths - 1):
            not_carried(i, o_shared[i].wait_recv)
        o_plane = [
            remote(w_wo.at[:, chip], w_wo.at[:, chip], opsend, oprecv, i, device)
            for i, (_, device) in enumerate(near)
        ]
        for copy in o_plane:
            copy.start()
        shared0[3].wait_recv()
        project(2 * chip_d + 1 - core, False)

        to_pair_order(k_slot, k_pairs, slots_ref, group_pairs)
        to_pair_order(v_slot, v_pairs, slots_ref, group_pairs)
        own_to_pair_order(q_slot, q_pairs, slots_ref, pairs, per_device)

        def turn_values(i, _):
            vT[:, aligned(i, TILE)] = v_pairs[aligned(i, TILE), :].T
            return 0

        lax.fori_loop(0, tokens // TILE, turn_values, 0)
        half_keys = group_pairs * BLK
        half_tiles = half_keys // TILE
        scores, bias = gate, up

        def cell(k_tile):
            lanes = (k_tile // CHIPS) * TILE
            return k_tile % CHIPS, slice(lanes, lanes + TILE)

        def attend(kind, step):
            tile = kind * (tiles // 2) + step
            key_tiles = half_tiles * (kind + 1)
            q = q_pairs[aligned(tile, TILE), :]
            fill_bias(bias, kind, step, slots_ref, lengths_ref, per_device, group_pairs)
            for head in range(LOCAL_HEADS):
                heads = slice(head * HD, (head + 1) * HD)
                q_head = jnp.where(head_mask(TILE, head), q, jnp.zeros_like(q))
                top = jnp.full((1, TILE), NEGATIVE, F32)
                for k_tile in range(key_tiles):
                    s = lax.dot_general(
                        k_pairs[k_tile * TILE : (k_tile + 1) * TILE, :], q_head, NT, preferred_element_type=F32
                    )
                    if k_tile >= key_tiles - half_tiles:
                        s = s + bias[k_tile - (key_tiles - half_tiles), :, 0:TILE]
                    index, lanes = cell(k_tile)
                    scores[index, :, lanes] = s
                    top = jnp.maximum(top, jnp.max(s, axis=0, keepdims=True))
                total = jnp.zeros((1, TILE), F32)
                out = jnp.zeros((HD, TILE), F32)
                for k_tile in range(key_tiles):
                    index, lanes = cell(k_tile)
                    e = jnp.exp(scores[index, :, lanes] - top)
                    total = total + jnp.sum(e, axis=0, keepdims=True)
                    out = out + jnp.dot(
                        vT[heads, k_tile * TILE : (k_tile + 1) * TILE], e.astype(BF16), preferred_element_type=F32
                    )
                oT_ref[tile, heads, :] = out / total
                lse_ref[tile, head] = top + jnp.log(total)
            q_slot[aligned(tile, TILE), :] = oT_ref[tile].T.astype(BF16)

        def both_steps(kind):
            def body(step, _):
                attend(kind, step)
                return 0

            lax.fori_loop(0, tiles // 2, body, 0)

        both_steps(1)
        take_hop(1)
        send_hop(2)
        both_steps(0)

        own_to_slot_order(q_slot, k_slot, slots_ref, pairs, per_device)
        for c in range(CHIPS):
            att_all[CHIPS + c] = k_slot[c * rows : (c + 1) * rows, :]
        sends0 = [
            remote(att_all.at[CHIPS + c], att_all.at[chip], send0, recv0, i, device)
            for i, (c, device) in enumerate(near)
        ]
        for copy in sends0:
            copy.start()
        att_all[chip] = att_all[CHIPS + chip]
        take_hop(2)
        send_hop(3)
        for copy in o_plane:
            copy.wait_recv()
        for copy in sends0:
            copy.wait()

        def w_out_rows(p):
            return w_wo[p].reshape(CHIP_COLS, width)

        for p in range(CHIPS):
            term = jnp.dot(att_all[p], w_out_rows(p), preferred_element_type=F32)
            hidden[...] = term if p == 0 else hidden[...] + term

        def first_norm(i, _):
            at = aligned(i, ROWS)
            h = hidden[at, :] + mix(s_ref, at, p_ref, 0)
            hidden[at, :] = h
            own[1, at, :] = (h * norm_factor(h)).astype(BF16)
            return 0

        lax.fori_loop(0, blocks, first_norm, 0)

        def ring(source, target, send, recv):
            return ring_sends(
                source, target, lambda c: c, chip, core, depth, chip_x, chip_y, send, recv
            )

        ring1 = ring(own.at[1], x_rows, ag1s, ag1r)
        for copy in ring1[:4]:
            copy.start()
        x_rows[chip] = own[1]
        ring1[0].wait_recv()
        ring1[4].start()
        ring1[1].wait_recv()
        ring1[5].start()
        take_hop(3)
        ff_mine.wait_recv()
        for _, _, receives, _, share in hops:
            pl.when(receives)(share.wait_recv)

        def w_rows(i):
            return w_ff[i].reshape(width, columns)

        def ff_forward(c):
            x = x_rows[c]
            for n in range(col_tiles):
                cols = slice(n * TILE, (n + 1) * TILE)
                g = jnp.dot(x, w_rows(0)[:, cols], preferred_element_type=F32)
                u = jnp.dot(x, w_rows(1)[:, cols], preferred_element_type=F32)
                gate[c, :, cols] = g
                up[c, :, cols] = u
                inner[c, :, cols] = (gelu_parts(g)[0] * u).astype(BF16)
            return jnp.dot(inner[c], w_rows(2), preferred_element_type=F32)

        sends1 = [
            remote(part1.at[c], got1.at[i], send1, recv1, i, device) for i, (c, device) in enumerate(near)
        ]
        up0_ref[...] = ff_forward(chip)
        for i, (c, _) in enumerate(near):
            if i < 2:
                ring1[2 + i].wait_recv()
            else:
                ring1[4].wait_recv()
                ring1[5].wait_recv()
            part1[c] = ff_forward(c).astype(BF16)
            sends1[i].start()

        def turn(i, _):
            xT[:, aligned(i, rows)] = x_rows[i].T
            innerT[:, aligned(i, rows)] = inner[i].T
            return 0

        lax.fori_loop(0, CHIPS, turn, 0)
        valid_count = end_count()
        weight = as_column(v_ref[...].astype(F32)) * (mesh_tokens / valid_count[0:1, 0:1])
        own_weight[...] = jnp.broadcast_to(weight, own_weight.shape)
        for copy in sends1:
            copy.wait_recv()

        def outputs(i, sums):
            at = aligned(i, ROWS)
            a = mix(s_ref, at, p_ref, 0)
            result = hidden[at, :] + up0_ref[at, :]
            for j in range(3):
                result = result + got1[j, at, :].astype(F32)
            difference = result - a
            row_weight = own_weight[at, 0:1]
            c0, c1 = c_ref[0], c_ref[1]
            out0 = a + c0 * difference
            out1 = mix(s_ref, at, p_ref, 1) + c1 * difference
            new_ref[at, 0, :] = out0.astype(BF16)
            new_ref[at, 1, :] = out1.astype(BF16)
            up0 = g_ref[at, 0, :].astype(F32) + row_weight * (out0 - t_ref[at, 0, :].astype(F32))
            up1 = g_ref[at, 1, :].astype(F32) + row_weight * (out1 - t_ref[at, 1, :].astype(F32))
            up0_ref[at, :] = up0
            up1_ref[at, :] = up1
            own[2, at, :] = (c0 * up0 + c1 * up1).astype(BF16)
            return (
                sums[0] + jnp.sum(up0 * difference, axis=0, keepdims=True),
                sums[1] + jnp.sum(up1 * difference, axis=0, keepdims=True),
            )

        zero = jnp.zeros((1, width), F32)
        correct_sums = lax.fori_loop(0, blocks, outputs, (zero, zero))
        sums_ref[...] = jnp.zeros_like(sums_ref)
        sums_ref[2:3, :] = correct_sums[0]
        sums_ref[3:4, :] = correct_sums[1]

        ring2 = ring(own.at[2], r_rows, ag2s, ag2r)
        for copy in ring2[:4]:
            copy.start()
        r_rows[chip] = own[2]

        def ff_backward(c):
            r = r_rows[c]
            for n in range(col_tiles):
                cols = slice(n * TILE, (n + 1) * TILE)
                inner_grad = lax.dot_general(r, w_rows(2)[cols, :], NT, preferred_element_type=F32)
                value, slope = gelu_parts(gate[c, :, cols])
                gate_low[c, :, cols] = (inner_grad * up[c, :, cols] * slope).astype(BF16)
                up_low[c, :, cols] = (inner_grad * value).astype(BF16)
            return lax.dot_general(
                gate_low[c], w_rows(0), NT, preferred_element_type=F32
            ) + lax.dot_general(up_low[c], w_rows(1), NT, preferred_element_type=F32)

        sends2 = [
            remote(part2.at[c], got2.at[i], send2, recv2, i, device) for i, (c, device) in enumerate(near)
        ]
        hg_ref[...] = ff_backward(chip)
        ring2[0].wait_recv()
        ring2[4].start()
        ring2[1].wait_recv()
        ring2[5].start()
        for i, (c, _) in enumerate(near):
            if i < 2:
                ring2[2 + i].wait_recv()
            else:
                ring2[4].wait_recv()
                ring2[5].wait_recv()
            part2[c] = ff_backward(c).astype(BF16)
            sends2[i].start()

        def weight_grads(z, _):
            at = aligned(z, shard)
            for i, (left, right) in enumerate(((xT, gate_low), (xT, up_low), (innerT, r_rows))):
                grad = jnp.dot(
                    left[at, :], right[...].reshape(queries, -1), preferred_element_type=F32
                ).astype(BF16)
                dw[z, 0, i * half : (i + 1) * half, :] = grad[:half]
                dw[z, 1, i * half : (i + 1) * half, :] = grad[half:]
            return 0

        lax.fori_loop(0, depths, weight_grads, 0)
        swap = remote(dw.at[:, 1 - core], dw_other, dsend, drecv, 0, other)
        swap.start()
        for copy in sends2:
            copy.wait_recv()

        def second_norm(i, gain_sum):
            at = aligned(i, ROWS)
            h = hidden[at, :]
            weighted = hg_ref[at, :]
            for j in range(3):
                weighted = weighted + got2[j, at, :].astype(F32)
            factor = norm_factor(h)
            mean = jnp.mean(weighted * h, axis=1, keepdims=True)
            result_grad = c_ref[0] * up0_ref[at, :] + c_ref[1] * up1_ref[at, :]
            hidden_grad = result_grad + (factor * weighted - h * (factor * factor * factor * mean))
            hg_ref[at, :] = hidden_grad
            own[3, at, :] = hidden_grad.astype(BF16)
            return gain_sum + jnp.sum(weighted * h * factor, axis=0, keepdims=True)

        sums_ref[1:2, :] = lax.fori_loop(0, blocks, second_norm, zero)

        sends3 = [
            remote(att_all.at[CHIPS + c], da_ref.at[chip], send3, recv3, i, device)
            for i, (c, device) in enumerate(near)
        ]

        def att_grad(c):
            return lax.dot_general(own[3], w_out_rows(c), NT, preferred_element_type=F32).astype(BF16)

        for i in (2, 0, 1):
            att_all[CHIPS + near[i][0]] = att_grad(near[i][0])
            sends3[i].start()
        da_ref[chip] = att_grad(chip)
        for c, ref in zip((chip, chip_x, chip_y, chip_d), (dw0_ref, dw1_ref, dw2_ref, dw3_ref)):
            ref[...] = jnp.dot(att_all[c].T, own[3], preferred_element_type=F32).astype(BF16)
        swap.wait_recv()

        def add_cores(z, _):
            ff_ref[z] = (dw[z, core].astype(F32) + dw_other[z].astype(F32)).astype(BF16)
            return 0

        lax.fori_loop(0, depths, add_cores, 0)
        for copy in sends3:
            copy.wait_recv()
        sent = ring0 + shared0 + q_copies + q_shared + o_plane + sends1 + sends2 + sends3
        for copy in sent + ring1 + ring2 + [swap, ff_mine]:
            copy.wait_send()
        for i in range(depths - 1):
            carried(i, o_copies[i].wait_send)
            carried(i, o_shared[i].wait_send)
        for _, sends, receives, hop, share in hops:
            pl.when(sends)(hop.wait_send)
            pl.when(receives)(share.wait_send)

    block = (rows, width)
    pair = (rows, 2, width)
    wide_rows = (CHIPS, rows, width)
    hid_rows = (CHIPS, rows, columns)

    def out(shape, dtype):
        return jax.ShapeDtypeStruct(shape, dtype)

    vmem = pltpu.VMEM
    outs = [
        out(pair, BF16),
        out(block, F32),
        out(block, F32),
        out(block, F32),
        out((CHIPS, rows, CHIP_COLS), BF16),
        out((CHIP_COLS, width), BF16),
        out((CHIP_COLS, width), BF16),
        out((CHIP_COLS, width), BF16),
        out((CHIP_COLS, width), BF16),
        out((depths, 3 * half, columns), BF16),
        out((8, width), F32),
        out((2 * CHIPS, rows, width), BF16),
        out((3, width, CHIP_COLS), BF16),
        out((queries, CHIP_COLS), BF16),
        out((tokens, CHIP_COLS), BF16),
        out((tokens, CHIP_COLS), BF16),
        out((tiles, CHIP_COLS, TILE), F32),
        out((tiles, LOCAL_HEADS, 1, TILE), F32),
    ]
    return pl.pallas_call(
        kernel,
        out_shape=outs,
        in_specs=[SM] * 4 + [VM] * 6 + [ANY] * 7,
        out_specs=[VM] * len(outs),
        scratch_shapes=[
            vmem((3, depths, 2, half, columns), BF16),
            vmem((depths, CHIPS, out_rows, width), BF16),
            vmem((depths, 2, half, piece_lanes), BF16),
            vmem((2 * CHIPS, rows, CHIP_COLS), BF16),
            vmem(block, F32),
            vmem((4,) + block, BF16),
            vmem(wide_rows, BF16),
            vmem(wide_rows, BF16),
            vmem((width, queries), BF16),
            vmem((columns, queries), BF16),
            vmem(hid_rows, BF16),
            vmem(hid_rows, F32),
            vmem(hid_rows, F32),
            vmem(hid_rows, BF16),
            vmem(hid_rows, BF16),
            vmem((rows, 128), F32),
            vmem(wide_rows, BF16),
            vmem(wide_rows, BF16),
            vmem((3,) + block, BF16),
            vmem((3,) + block, BF16),
            vmem((depths, 2, 3 * half, columns), BF16),
            vmem((depths, 3 * half, columns), BF16),
            vmem((3, half, width), BF16),
            vmem((2, half, hidden_cols), BF16),
            vmem((8, 128), F32),
            vmem((queries, CHIP_COLS), BF16),
            vmem((tokens, CHIP_COLS), BF16),
            vmem((tokens, CHIP_COLS), BF16),
            vmem((CHIP_COLS, tokens), BF16),
        ]
        + [DMA((7,))]
        + [DMA((2 * depths - 2,))] * 2
        + [DMA((2 * depths - 1,))] * 2
        + [DMA((depths - 1,))] * 2
        + [DMA((depths,))] * 2
        + [DMA((depths - 1,))] * 4
        + [DMA((3,))] * 2
        + [DMA((6,))] * 2
        + [DMA((4,))] * 2
        + [DMA((3,))] * 8
        + [DMA((6,))] * 4
        + [DMA((1,))] * 2
        + total_scratch((8, 128), depths),
        compiler_params=comm_params(collective_id),
        name="forward",
    )(
        slots, lengths, predict, correct, states, out_grad, teacher, valid, gain_one, gain_two,
        w_query, w_key, w_value, w_out, w_gate, w_up, w_down,
    )


def backward(
    slots, lengths, predict, correct, att_grad, q_pairs, k_pairs, v_pairs, oT, lse, weights, states, up0, up1,
    hidden_grad, sums, ff_grads, out_grads, all_rows, collective_id,
):
    rows, _, width = states.shape
    depths = lax.axis_size("wsh")
    columns = CHIP_COLS
    half = width // (2 * depths)
    part_rows = 3 * half
    blocks = rows // ROWS
    tokens = k_pairs.shape[0]
    queries = q_pairs.shape[0]
    tiles = queries // TILE
    per_device = rows // BLK
    group_pairs = tokens // (2 * BLK)
    pairs = queries // (2 * BLK)
    half_tiles = group_pairs * BLK // TILE
    wide_lanes = LOCAL_HEADS * TILE

    def kernel(
        slots_ref, lengths_ref, p_ref, c_ref, g_ref, q_ref, k_ref, v_ref, oT_ref, lse_ref, w_all, s_ref,
        up0_ref, up1_ref, hg_ref, sums_ref, ff_ref, o0, o1, o2, o3, rows_ref,
        grad_ref, f_all, q_all, o_all, total_ref,
        g_pairs, kT, doT, dqT, q_stack, do_stack, p_buf, ds_buf, dk_acc, dv_acc, bias, dq_pairs, dq_rows,
        give, kept, came, x_own, xT, part, got, mine, q_grad, q_other, q_mine, q_far,
        o_near, o_grad, o_other, o_mine, o_far, f_mine, q_sum, o_sum, all_sums, *rest,
    ):
        (
            f_acc, f_up_in, f_down_in, f_up_out, f_down_out, f_us, f_ur, f_ds, f_dr,
            xload, nsend, nrecv, ksend, krecv, send, recv, ssend, srecv, zsend, zrecv, osend, orecv,
            fsend, frecv, gsend, grecv, bsend, brecv, psend, precv, *total_refs,
        ) = rest
        depth, chip, core, chip_x, chip_y, chip_d = place_on_mesh()
        near = [(c, (2 * c + core, depth)) for c in (chip_x, chip_y, chip_d)]
        other = (2 * chip + 1 - core, depth)
        across = [
            (2 * chip + core, lax.rem(depth + step, depths)) for step in range(1, depths)
        ]
        peers = plane_peers(chip, core, depth, chip_x, chip_y, chip_d)
        everyone = peers + across
        signal_all(everyone)
        load = pltpu.make_async_copy(rows_ref.at[:, core], x_own, xload)
        load.start()
        own_to_pair_order(g_ref, g_pairs, slots_ref, pairs, per_device)

        def turn_keys(i, _):
            at = aligned(i, TILE)
            kT[:, at] = k_ref[at, :].T
            return 0

        lax.fori_loop(0, tokens // TILE, turn_keys, 0)
        wait_all(everyone)
        near_grads = [
            remote(ref, o_near.at[i], nsend, nrecv, i, near[i][1]) for i, ref in enumerate((o1, o2, o3))
        ]
        for copy in near_grads:
            copy.start()
        ff_start, ff_hop, ff_result, ff_finish = line_reduce(
            ff_ref, f_acc, f_up_in, f_down_in, f_up_out, f_down_out, (f_us, f_ur, f_ds, f_dr)
        )
        ff_start()

        def attend(kind, step):
            tile = kind * (tiles // 2) + step
            key_tiles = half_tiles * (kind + 1)
            q_tile = q_ref[aligned(tile, TILE), :]
            fill_bias(bias, kind, step, slots_ref, lengths_ref, per_device, group_pairs)
            do_tile = g_pairs[aligned(tile, TILE), :]
            doT[...] = do_tile.astype(F32).T * oT_ref[tile]
            for head in range(LOCAL_HEADS):
                lanes = slice(head * TILE, (head + 1) * TILE)
                heads = slice(head * HD, (head + 1) * HD)
                mask = head_mask(TILE, head)
                q_head = jnp.where(mask, q_tile, jnp.zeros_like(q_tile))
                do_head = jnp.where(mask, do_tile, jnp.zeros_like(do_tile))
                q_stack[lanes, :] = q_head
                do_stack[lanes, :] = do_head
                delta = jnp.sum(doT[heads, :], axis=0, keepdims=True)
                norm = lse_ref[tile, head]
                total = jnp.zeros((HD, TILE), F32)
                for k_tile in range(key_tiles):
                    at = slice(k_tile * TILE, (k_tile + 1) * TILE)
                    s = lax.dot_general(k_ref[at, :], q_head, NT, preferred_element_type=F32)
                    if k_tile >= key_tiles - half_tiles:
                        s = s + bias[k_tile - (key_tiles - half_tiles), :, 0:TILE]
                    dp = lax.dot_general(v_ref[at, :], do_head, NT, preferred_element_type=F32)
                    e = jnp.exp(s - norm)
                    p_buf[at, lanes] = e.astype(BF16)
                    ds = (e * (dp - delta)).astype(BF16)
                    ds_buf[at, lanes] = ds
                    total = total + jnp.dot(kT[heads, at], ds, preferred_element_type=F32)
                dqT[heads, :] = total
            for k_tile in range(key_tiles):
                at = slice(k_tile * TILE, (k_tile + 1) * TILE)
                dv = jnp.dot(p_buf[at, :], do_stack[...], preferred_element_type=F32)
                dk = jnp.dot(ds_buf[at, :], q_stack[...], preferred_element_type=F32)
                if kind == 1:
                    fresh = step == 0
                    dv_acc[at, :] = dv + jnp.where(fresh, 0.0, dv_acc[at, :])
                    dk_acc[at, :] = dk + jnp.where(fresh, 0.0, dk_acc[at, :])
                else:
                    dv_acc[at, :] = dv + dv_acc[at, :]
                    dk_acc[at, :] = dk + dk_acc[at, :]
            dq_pairs[aligned(tile, TILE), :] = dqT[...].T.astype(BF16)

        for kind in (1, 0):

            def body(step, _, kind=kind):
                attend(kind, step)
                return 0

            lax.fori_loop(0, tiles // 2, body, 0)
            ff_hop(2 - kind)

        def slot_rows(target, side, chip_index, pair_index):
            pair = chip_index * per_device + side * (per_device // 2) + pair_index
            second, _, _ = pair_places(slots_ref, pair)
            at = 2 * pair_index * BLK
            for i, acc in enumerate((dk_acc, dv_acc)):
                both = either(second, acc[aligned(pair, BLK), :], acc[aligned(group_pairs + pair, BLK), :])
                for j in range(2):
                    target[i, chip_index, at + j * BLK : at + (j + 1) * BLK, :] = both[j].astype(BF16)

        for c in range(CHIPS):
            for i in range(per_device // 2):
                slot_rows(give, 1 - core, c, i)
        swap = remote(give, came, ksend, krecv, 0, other)
        swap.start()
        for c in range(CHIPS):
            for i in range(per_device // 2):
                slot_rows(kept, core, c, i)
        own_to_slot_order(dq_pairs, dq_rows, slots_ref, pairs, per_device)
        swap.wait_recv()

        def add_cores(c, _):
            for i in range(2):
                kept[i, c] = (kept[i, c].astype(F32) + came[i, c].astype(F32)).astype(BF16)
            return 0

        lax.fori_loop(0, CHIPS, add_cores, 0)

        def rows_grad(c):
            return (
                lax.dot_general(
                    dq_rows[aligned(c, rows), :], w_all[0], NT, preferred_element_type=F32
                )
                + lax.dot_general(kept[0, c], w_all[1], NT, preferred_element_type=F32)
                + lax.dot_general(kept[1, c], w_all[2], NT, preferred_element_type=F32)
            )

        sends = [
            remote(part.at[c], got.at[i], send, recv, i, device) for i, (c, device) in enumerate(near)
        ]
        for i in (2, 0, 1):
            part[near[i][0]] = rows_grad(near[i][0]).astype(BF16)
            sends[i].start()
        mine[...] = rows_grad(chip)
        load.wait()

        def turn(c, _):
            xT[:, aligned(c, rows)] = x_own[c].T
            return 0

        lax.fori_loop(0, CHIPS, turn, 0)

        def weight_grads(z, _):
            at = aligned(z, 2 * half)
            for i in range(3):
                right = dq_rows[...] if i == 0 else kept[i - 1].reshape(queries, columns)
                grad = jnp.dot(xT[at, :], right, preferred_element_type=F32).astype(BF16)
                q_grad[z, 0, i * half : (i + 1) * half, :] = grad[:half]
                q_grad[z, 1, i * half : (i + 1) * half, :] = grad[half:]
            return 0

        lax.fori_loop(0, depths, weight_grads, 0)
        for copy in near_grads:
            copy.wait_recv()
        whole = o0[...].astype(F32)
        for i in range(3):
            whole = whole + o_near[i].astype(F32)
        whole = whole.astype(BF16)
        o_grad[0] = whole[:half]
        o_grad[1] = whole[half:]
        core_swaps = [
            remote(q_grad.at[:, 1 - core], q_other, ssend, srecv, 0, other),
            remote(o_grad.at[1 - core], o_other, ssend, srecv, 1, other),
        ]
        for copy in core_swaps:
            copy.start()
        for copy in core_swaps:
            copy.wait_recv()
        for i in range(depths):
            q_mine[i] = (q_grad[i, core].astype(F32) + q_other[i].astype(F32)).astype(BF16)
        q_copies = [
            remote(q_mine.at[lax.rem(depth + i + 1, depths)], q_far.at[i], zsend, zrecv, i, device)
            for i, device in enumerate(across)
        ]
        for copy in q_copies:
            copy.start()
        o_mine[...] = (o_grad[core].astype(F32) + o_other[...].astype(F32)).astype(BF16)
        distance = lax.rem(chip + depths - depth, depths)
        o_copies = [
            remote(o_mine, o_far.at[i], osend, orecv, i, device) for i, device in enumerate(across)
        ]
        for i in range(depths - 1):
            pl.when(distance == i + 1)(o_copies[i].start)
        ff_result()
        f_mine[...] = f_acc[...].astype(BF16)

        def slot(chip_index):
            return 2 * chip_index + core

        f_copies = ring_sends(
            f_mine, f_all, slot, chip, core, depth, chip_x, chip_y, fsend, frecv
        )
        for copy in f_copies[:4]:
            copy.start()
        f_all[slot(chip)] = f_mine[...]

        def shared(index, ref):
            return remote(ref, ref, psend, precv, index, other)

        f_shared = [shared(i, f_all.at[slot(c)]) for i, c in enumerate((chip, chip_x, chip_y, chip_d))]
        q_shared = [shared(4 + i, q_all.at[slot(c)]) for i, c in enumerate((chip, chip_x, chip_y, chip_d))]
        o_shared = shared(8, o_all.at[core])
        f_shared[0].start()
        for copy in sends:
            copy.wait_recv()

        def state_grads(i, totals):
            at = aligned(i, ROWS)
            s0, s1 = s_ref[at, 0, :].astype(F32), s_ref[at, 1, :].astype(F32)
            a = p_ref[0, 0] * s0 + p_ref[0, 1] * s1
            weighted = mine[at, :]
            for j in range(3):
                weighted = weighted + got[j, at, :].astype(F32)
            factor = norm_factor(a)
            mean = jnp.mean(weighted * a, axis=1, keepdims=True)
            up0, up1 = up0_ref[at, :], up1_ref[at, :]
            result_grad = c_ref[0] * up0 + c_ref[1] * up1
            norm_grad = factor * weighted - a * (factor * factor * factor * mean)
            mixed0 = up0 + (hg_ref[at, :] + norm_grad - result_grad)
            grad_ref[at, 0, :] = (p_ref[0, 0] * mixed0 + p_ref[1, 0] * up1).astype(BF16)
            grad_ref[at, 1, :] = (p_ref[0, 1] * mixed0 + p_ref[1, 1] * up1).astype(BF16)
            terms = (weighted * a * factor, mixed0 * s0, mixed0 * s1, up1 * s0, up1 * s1)
            return tuple(t + jnp.sum(v, axis=0, keepdims=True) for t, v in zip(totals, terms))

        totals = lax.fori_loop(
            0, blocks, state_grads, tuple(jnp.zeros((1, width), F32) for _ in range(5))
        )
        all_sums[...] = sums_ref[...]
        all_sums[0:1, :] = totals[0]
        for i in range(4):
            all_sums[4 + i : 5 + i, :] = totals[1 + i]
        start, turn_sums, end = total_over_mesh(
            all_sums, *total_refs[:3], across, peers, *total_refs[3:]
        )
        start()
        f_copies[0].wait_recv()
        f_copies[4].start()
        f_copies[1].wait_recv()
        f_copies[5].start()
        for copy in q_copies:
            copy.wait_recv()
        total = q_mine[depth].astype(F32)
        for i in range(depths - 1):
            total = total + q_far[i].astype(F32)
        q_sum[...] = total.astype(BF16)
        r_copies = ring_sends(
            q_sum, q_all, slot, chip, core, depth, chip_x, chip_y, gsend, grecv
        )
        for copy in r_copies[:4]:
            copy.start()
        q_all[slot(chip)] = q_sum[...]
        q_shared[0].start()
        quarter = half // 2
        o_top, o_low = o_all.at[core, pl.ds(0, quarter)], o_all.at[core, pl.ds(quarter, quarter)]
        o_source_top, o_source_low = o_sum.at[pl.ds(0, quarter)], o_sum.at[pl.ds(quarter, quarter)]
        dev_x, dev_y = near[0][1], near[1][1]
        b_copies = [
            remote(o_source_top, o_top, bsend, brecv, 0, dev_x),
            remote(o_source_low, o_low, bsend, brecv, 1, dev_y),
            remote(o_source_low, o_low, bsend, brecv, 2, dev_x),
            remote(o_source_top, o_top, bsend, brecv, 3, dev_y),
            remote(o_top, o_top, bsend, brecv, 4, dev_y),
            remote(o_low, o_low, bsend, brecv, 5, dev_x),
        ]
        source, from_x, from_y = chip == depth, chip_x == depth, chip_y == depth

        @pl.when(source)
        def _():
            for copy in o_copies:
                copy.wait_recv()
            total = o_mine[...].astype(F32)
            for i in range(depths - 1):
                total = total + o_far[i].astype(F32)
            o_sum[...] = total.astype(BF16)
            for copy in b_copies[:4]:
                copy.start()
            o_all[core] = o_sum[...]

        turn_sums()
        r_copies[0].wait_recv()
        r_copies[4].start()
        r_copies[1].wait_recv()
        r_copies[5].start()

        @pl.when(from_x)
        def _():
            b_copies[0].wait_recv()
            b_copies[4].start()
            b_copies[2].wait_recv()

        @pl.when(from_y)
        def _():
            b_copies[1].wait_recv()
            b_copies[5].start()
            b_copies[3].wait_recv()

        for copies, passed in ((f_copies, f_shared), (r_copies, q_shared)):
            copies[2].wait_recv()
            passed[1].start()
            copies[3].wait_recv()
            passed[2].start()
            copies[4].wait_recv()
            copies[5].wait_recv()
            passed[3].start()

        @pl.when(chip_d == depth)
        def _():
            b_copies[4].wait_recv()
            b_copies[5].wait_recv()

        o_shared.start()
        total_ref[...] = end()
        for copy in f_shared + q_shared + [o_shared]:
            copy.wait()
        for copy in near_grads + [swap] + sends + core_swaps + q_copies + f_copies + r_copies:
            copy.wait_send()
        for i in range(depths - 1):
            pl.when(distance == i + 1)(o_copies[i].wait_send)
        ff_finish()

        @pl.when(source)
        def _():
            for copy in b_copies[:4]:
                copy.wait_send()

        pl.when(from_x)(b_copies[4].wait_send)
        pl.when(from_y)(b_copies[5].wait_send)

    vmem = pltpu.VMEM
    block = (rows, width)
    wide_rows = (CHIPS, rows, width)
    q_block, o_block = (part_rows, columns), (half, width)
    kv_half = (2, CHIPS, rows, columns)
    f_block = ff_grads.shape[1:]
    line_buffers, line_sems = line_reduce_scratch(f_block, depths)
    return pl.pallas_call(
        kernel,
        out_shape=[
            jax.ShapeDtypeStruct((rows, 2, width), BF16),
            jax.ShapeDtypeStruct((2 * CHIPS,) + f_block, BF16),
            jax.ShapeDtypeStruct((2 * CHIPS,) + q_block, BF16),
            jax.ShapeDtypeStruct((2,) + o_block, BF16),
            jax.ShapeDtypeStruct((8, width), F32),
        ],
        in_specs=[SM] * 4 + [VM] * 17 + [ANY],
        out_specs=[VM] * 5,
        scratch_shapes=[
            vmem((queries, columns), BF16),
            vmem((columns, tokens), BF16),
            vmem((columns, TILE), F32),
            vmem((columns, TILE), F32),
            vmem((wide_lanes, columns), BF16),
            vmem((wide_lanes, columns), BF16),
            vmem((tokens, wide_lanes), BF16),
            vmem((tokens, wide_lanes), BF16),
            vmem((tokens, columns), F32),
            vmem((tokens, columns), F32),
            vmem((half_tiles, TILE, TILE), F32),
            vmem((queries, columns), BF16),
            vmem((queries, columns), BF16),
            vmem(kv_half, BF16),
            vmem(kv_half, BF16),
            vmem(kv_half, BF16),
            vmem(wide_rows, BF16),
            vmem((width, queries), BF16),
            vmem(wide_rows, BF16),
            vmem((3,) + block, BF16),
            vmem(block, F32),
            vmem((depths, 2) + q_block, BF16),
            vmem((depths,) + q_block, BF16),
            vmem((depths,) + q_block, BF16),
            vmem((depths - 1,) + q_block, BF16),
            vmem((3, columns, width), BF16),
            vmem((2,) + o_block, BF16),
            vmem(o_block, BF16),
            vmem(o_block, BF16),
            vmem((depths - 1,) + o_block, BF16),
            vmem(f_block, BF16),
            vmem(q_block, BF16),
            vmem(o_block, BF16),
            vmem((8, width), F32),
            *line_buffers,
            *line_sems,
            DMA,
            DMA((3,)),
            DMA((3,)),
            DMA((1,)),
            DMA((1,)),
            DMA((3,)),
            DMA((3,)),
            DMA((2,)),
            DMA((2,)),
            DMA((depths - 1,)),
            DMA((depths - 1,)),
            DMA((depths - 1,)),
            DMA((depths - 1,)),
            *[DMA((6,))] * 6,
            *[DMA((9,))] * 2,
            *total_scratch((8, width), depths),
        ],
        compiler_params=comm_params(collective_id),
        name="backward",
    )(
        slots, lengths, predict, correct, att_grad, q_pairs, k_pairs, v_pairs, oT, lse, weights, states, up0, up1,
        hidden_grad, sums, ff_grads, *out_grads, all_rows,
    )


def lay_out(ff, qkv, out, sums, gain_one, gain_two):
    ctx, part_rows, columns = ff.shape
    half, width = out.shape[1:]
    shard = 2 * half
    depths = width // shard
    split = columns // depths

    def kernel(
        f_ref, q_ref, o_ref, s_ref, g1_ref, g2_ref,
        dq_ref, dk_ref, dv_ref, do_ref, dg_ref, du_ref, dd_ref, g1_out, g2_out, p_out, c_out,
    ):
        depth = lax.axis_index("wsh")
        one, two = g1_ref[...].astype(F32), g2_ref[...].astype(F32)
        one_column, two_column = as_column(one), as_column(two)
        for c in range(2):
            rows = slice(c * half, (c + 1) * half)
            do_ref[rows, :] = o_ref[c].astype(F32)
            for i, ref in enumerate((dq_ref, dk_ref, dv_ref)):
                wide = jnp.concatenate(
                    [q_ref[2 * p + c, i * half : (i + 1) * half, :].astype(F32) for p in range(CHIPS)],
                    axis=1,
                )
                ref[rows, :] = wide * one_column[rows]
            for i, ref in enumerate((dg_ref, du_ref)):
                for z in range(depths):
                    wide = jnp.concatenate(
                        [
                            f_ref[
                                2 * p + c, i * half : (i + 1) * half, z * split : (z + 1) * split
                            ].astype(F32)
                            for p in range(CHIPS)
                        ],
                        axis=1,
                    )
                    ref[rows, z * CHIPS * split : (z + 1) * CHIPS * split] = wide * two_column[rows]
            for p in range(CHIPS):
                at = (2 * p + c) * half
                dd_ref[at : at + half, :] = f_ref[2 * p + c, 2 * half :, :].astype(F32)
        for z in range(depths):

            @pl.when(depth == z)
            def _(z=z):
                g1_out[...] = s_ref[0:1, z * shard : (z + 1) * shard] / one
                g2_out[...] = s_ref[1:2, z * shard : (z + 1) * shard] / two

        scalars = jnp.sum(s_ref[...], axis=1, keepdims=True)
        for i in range(2):
            c_out[:, i : i + 1] = scalars[2 + i : 3 + i]
            for j in range(2):
                at = 4 + 2 * i + j
                p_out[i : i + 1, j : j + 1] = scalars[at : at + 1]

    square = jax.ShapeDtypeStruct((shard, width), F32)
    tall = jax.ShapeDtypeStruct((shard, columns * CHIPS), F32)
    row = jax.ShapeDtypeStruct((1, shard), F32)
    return pl.pallas_call(
        kernel,
        out_shape=[
            square,
            square,
            square,
            square,
            tall,
            tall,
            jax.ShapeDtypeStruct((ctx * half, width), F32),
            row,
            row,
            jax.ShapeDtypeStruct((2, 2), F32),
            jax.ShapeDtypeStruct((1, 2), F32),
        ],
        in_specs=[VM] * 6,
        out_specs=[VM] * 11,
        compiler_params=pltpu.CompilerParams(vmem_limit_bytes=VMEM_LIMIT),
        name="lay_out",
    )(ff, qkv, out, sums, gain_one, gain_two)


def plane_shards(
    states, block_slot, cont_lengths, valid_mask, teacher, out_grad, predict, correct,
    norm_attn, w_query, w_key, w_value, w_out, norm_ffn, w_gate, w_up, w_down,
):
    _, rows, _, width = states.shape
    slots, lengths = block_slot[0], cont_lengths[0]
    gain_one, gain_two = norm_attn[None], norm_ffn[None]
    states = states[0]
    new_states, up0, up1, hidden_grad, att_grad, *rest = forward(
        slots, lengths, predict, correct, states, out_grad[0], teacher[0], valid_mask, gain_one, gain_two,
        w_query, w_key, w_value, w_out, w_gate, w_up, w_down, 1,
    )
    out_grads, (ff_sum, sums, all_rows, weights, q_pairs, k_pairs, v_pairs, oT, lse) = rest[:4], rest[4:]
    states_grad, *gathered = backward(
        slots, lengths, predict, correct, att_grad.reshape(-1, CHIP_COLS), q_pairs, k_pairs, v_pairs, oT, lse,
        weights, states, up0, up1, hidden_grad, sums, ff_sum, out_grads, all_rows.reshape(CHIPS, 2, rows, width), 2,
    )
    dq, dk, dv, do, dg, du, dd, g_one, g_two, predict_grad, correct_grad = lay_out(
        *gathered, gain_one, gain_two
    )
    return (
        new_states[None], states_grad[None], predict_grad, correct_grad[0],
        g_one[0], dq, dk, dv, do, g_two[0], dg, du, dd,
    )


def fits_plane(mesh, states, block_slot, w_query, w_gate):
    ctx, depths = mesh.shape["ctx"], mesh.shape["wsh"]
    return (
        ctx == 2 * CHIPS
        and depths == CHIPS
        and states.shape[0] == depths
        and block_slot.shape[1] * BLK == 2 * PROMPT
        and states.shape[1] == 2 * PROMPT
        and w_query.shape[0] % (32 * depths) == 0
        and w_gate.shape[1] % (32 * CHIPS * depths) == 0
    )


def solution(mesh):
    in_specs = (
        P("wsh", "ctx", None, None),
        P("wsh", None),
        P("wsh", None),
        P("wsh", "ctx"),
        P("wsh", "ctx", None, None),
        P("wsh", "ctx", None, None),
        P(),
        P(),
        P("wsh"),
        P("wsh", None),
        P("wsh", None),
        P("wsh", None),
        P("wsh", None),
        P("wsh"),
        P("wsh", None),
        P("wsh", None),
        P("wsh", None),
    )
    out_specs = (
        P("wsh", "ctx", None, None),
        P("wsh", "ctx", None, None),
        P(),
        P(),
        P("wsh"),
        P("wsh", None),
        P("wsh", None),
        P("wsh", None),
        P("wsh", None),
        P("wsh"),
        P("wsh", None),
        P("wsh", None),
        P("wsh", None),
    )

    def step(*args):
        plane = fits_plane(mesh, args[0], args[1], args[9], args[14])
        body = plane_shards if plane else general_shards
        return jax.shard_map(
            body, mesh=mesh, in_specs=in_specs, out_specs=out_specs, check_vma=False
        )(*args)

    return step
```

```python
import functools
import math

import jax
import jax.numpy as jnp
from jax import lax
from jax.experimental import pallas as pl
from jax.experimental.pallas import tpu as pltpu
from jax.sharding import PartitionSpec as P

HEADS = 12
HD = 64
PROMPT = 1024
BLK = 64


EPSILON = 1e-06
NEGATIVE = -1e30
HIGHEST = lax.Precision.HIGHEST


def rms_forward(tensor, gain_vec):
    factor = lax.rsqrt(jnp.mean(tensor * tensor, axis=-1, keepdims=True) + EPSILON)
    return (tensor * factor * gain_vec, factor)


def rms_backward(tensor, factor, gain_vec, upstream):
    weighted = upstream * gain_vec
    gain_grad = jnp.sum(upstream * tensor * factor, axis=0)
    middle = jnp.mean(weighted * tensor, axis=-1, keepdims=True)
    return (factor * weighted - tensor * factor * factor * factor * middle, gain_grad)


def segment_starts(cont_lengths):
    count = cont_lengths.shape[1]
    index = jnp.arange(count, dtype=jnp.int32)
    before = index[:, None] < index[None, :]
    return PROMPT + jnp.sum(jnp.where(before[None], cont_lengths[:, :, None], 0), axis=1)


def token_places(block_slot, cont_lengths):
    groups, blocks = block_slot.shape
    offsets = jnp.arange(BLK, dtype=jnp.int32)
    places = (block_slot[:, :, None] * BLK + offsets[None, None, :]).reshape(groups, blocks * BLK)
    starts = segment_starts(cont_lengths)
    segments = jnp.sum((places[:, :, None] >= starts[:, None, :]).astype(jnp.int32), axis=2)
    return (places, segments)


def visible(query_place, query_segment, key_place, key_segment):
    earlier = key_place[:, None, :] <= query_place[:, :, None]
    shared = (key_segment[:, None, :] == 0) | (key_segment[:, None, :] == query_segment[:, :, None])
    return earlier & shared


def split_heads(tensor):
    return tensor.reshape(tensor.shape[0], tensor.shape[1], HEADS, HD)


def forward_block(running, query_part, key_part, value_part, allowed):

    def forward_compute(current):
        maximum, denominator, accumulated = current
        scores = jnp.einsum(
            "gqhd,gkhd->ghqk",
            split_heads(query_part),
            split_heads(key_part),
            preferred_element_type=jnp.float32,
        )
        masked = jnp.where(allowed[:, None], scores, NEGATIVE)
        new_max = jnp.maximum(maximum, jnp.max(masked, axis=-1))
        exponent = jnp.where(allowed[:, None], jnp.exp(masked - new_max[..., None]), 0.0)
        factor = jnp.exp(maximum - new_max)
        rescale = jnp.swapaxes(factor, 1, 2)[..., None]
        update = jnp.einsum(
            "ghqk,gkhd->gqhd",
            exponent.astype(jnp.bfloat16),
            split_heads(value_part),
            preferred_element_type=jnp.float32,
        )
        merged = (split_heads(accumulated) * rescale + update).reshape(accumulated.shape)
        return (new_max, denominator * factor + jnp.sum(exponent, axis=-1), merged)

    return lax.cond(jnp.any(allowed), forward_compute, lambda current: current, running)


def backward_block(
    query_part, grad_part, key_part, value_part, allowed, maximum, denominator, delta_sum
):
    scores = jnp.einsum(
        "gqhd,gkhd->ghqk",
        split_heads(query_part),
        split_heads(key_part),
        preferred_element_type=jnp.float32,
    )
    exponent = jnp.where(allowed[:, None], jnp.exp(scores - maximum[..., None]), 0.0)
    probability = exponent / denominator[..., None]
    prob_grad = jnp.einsum(
        "gqhd,gkhd->ghqk",
        split_heads(grad_part),
        split_heads(value_part),
        preferred_element_type=jnp.float32,
    )
    score_grad = (probability * (prob_grad - delta_sum[..., None])).astype(jnp.bfloat16)
    return (probability.astype(jnp.bfloat16), score_grad)


def general_shards(
    states,
    block_slot,
    cont_lengths,
    valid_mask,
    teacher,
    out_grad,
    predict,
    correct,
    norm_attn,
    w_query,
    w_key,
    w_value,
    w_out,
    norm_ffn,
    w_gate,
    w_up,
    w_down,
):
    groups, local_len = valid_mask.shape
    model_width = states.shape[3]
    row_count = groups * local_len
    group_len = block_slot.shape[1] * BLK
    gain_one, query_w, key_w, value_w, out_w, gain_two, gate_w, up_w, down_w = (
        lax.all_gather(norm_attn, "wsh", axis=0, tiled=True),
        lax.all_gather(w_query, "wsh", axis=0, tiled=True),
        lax.all_gather(w_key, "wsh", axis=0, tiled=True),
        lax.all_gather(w_value, "wsh", axis=0, tiled=True),
        lax.all_gather(w_out, "wsh", axis=0, tiled=True),
        lax.all_gather(norm_ffn, "wsh", axis=0, tiled=True),
        lax.all_gather(w_gate, "wsh", axis=0, tiled=True),
        lax.all_gather(w_up, "wsh", axis=0, tiled=True),
        lax.all_gather(w_down, "wsh", axis=0, tiled=True),
    )
    valid_float = valid_mask.astype(jnp.float32)
    valid_total = lax.psum(jnp.sum(valid_float), ("ctx", "wsh"))
    places, segments = token_places(block_slot, cont_lengths)
    offset = lax.axis_index("ctx") * local_len
    own_place = lax.dynamic_slice_in_dim(places, offset, local_len, 1)
    own_segment = lax.dynamic_slice_in_dim(segments, offset, local_len, 1)
    inputs = states.astype(jnp.float32)
    mixed_states = jnp.einsum("ij,gtjd->gtid", predict, inputs, precision=HIGHEST)
    active = mixed_states[:, :, 0].reshape(row_count, model_width)
    gain_first = gain_one.astype(jnp.float32)
    normed, factor_one = rms_forward(active, gain_first)
    normed_low = normed.astype(jnp.bfloat16)
    queries = (
        jnp.dot(normed_low, query_w, preferred_element_type=jnp.float32)
        .astype(jnp.bfloat16)
        .reshape(groups, local_len, model_width)
    )
    key_rows = (
        jnp.dot(normed_low, key_w, preferred_element_type=jnp.float32)
        .astype(jnp.bfloat16)
        .reshape(groups, local_len, model_width)
    )
    values = (
        jnp.dot(normed_low, value_w, preferred_element_type=jnp.float32)
        .astype(jnp.bfloat16)
        .reshape(groups, local_len, model_width)
    )
    initial = (
        jnp.full((groups, HEADS, local_len), NEGATIVE, jnp.float32),
        jnp.zeros((groups, HEADS, local_len), jnp.float32),
        jnp.zeros((groups, local_len, model_width), jnp.float32),
    )
    piece_keys = lax.all_gather(key_rows, "ctx", axis=1, tiled=True)
    piece_values = lax.all_gather(values, "ctx", axis=1, tiled=True)
    piece_len = piece_keys.shape[1]
    block_size = math.gcd(piece_len, local_len)

    def fold_one_block(current, block_index):
        begin = block_index * block_size
        key_part = lax.dynamic_slice_in_dim(piece_keys, begin, block_size, 1)
        value_part = lax.dynamic_slice_in_dim(piece_values, begin, block_size, 1)
        key_place = lax.dynamic_slice_in_dim(places, begin, block_size, 1)
        key_segment = lax.dynamic_slice_in_dim(segments, begin, block_size, 1)
        allowed = visible(own_place, own_segment, key_place, key_segment)
        return (forward_block(current, queries, key_part, value_part, allowed), None)

    finished, unused = lax.scan(
        fold_one_block, initial, jnp.arange(piece_len // block_size, dtype=jnp.int32)
    )
    maximum, denominator, accumulated = finished
    attended = (split_heads(accumulated) / jnp.swapaxes(denominator, 1, 2)[..., None]).reshape(
        row_count, model_width
    )
    attended_low = attended.astype(jnp.bfloat16)
    hidden = active + jnp.dot(attended_low, out_w, preferred_element_type=jnp.float32)
    gain_second = gain_two.astype(jnp.float32)
    normed_two, factor_two = rms_forward(hidden, gain_second)
    normed_two_low = normed_two.astype(jnp.bfloat16)
    gate_proj = jnp.dot(normed_two_low, gate_w, preferred_element_type=jnp.float32)
    up_proj = jnp.dot(normed_two_low, up_w, preferred_element_type=jnp.float32)
    inner_act, inner_pull = jax.vjp(
        lambda gate_in, up_in: jax.nn.gelu(gate_in, approximate=True) * up_in, gate_proj, up_proj
    )
    inner_low = inner_act.astype(jnp.bfloat16)
    result = hidden + jnp.dot(inner_low, down_w, preferred_element_type=jnp.float32)
    difference = (result - active).reshape(groups, local_len, 1, model_width)
    out_states = mixed_states + correct[None, None, :, None] * difference
    new_states = out_states.astype(jnp.bfloat16)
    loss_ratio = lax.axis_size("wsh") * groups * group_len / valid_total
    upstream = out_grad.astype(jnp.float32) + loss_ratio * valid_float[:, :, None, None] * (
        out_states - teacher.astype(jnp.float32)
    )
    correct_local = jnp.sum(upstream * difference, axis=(0, 1, 3))
    result_grad = jnp.einsum("i,gtid->gtd", correct, upstream, precision=HIGHEST).reshape(
        row_count, model_width
    )
    result_low = result_grad.astype(jnp.bfloat16)
    down_grad = jnp.einsum("rf,rd->fd", inner_low, result_low, preferred_element_type=jnp.float32)
    inner_grad = jnp.einsum("rd,fd->rf", result_low, down_w, preferred_element_type=jnp.float32)
    gate_grad, up_grad = inner_pull(inner_grad)
    gate_low = gate_grad.astype(jnp.bfloat16)
    up_low = up_grad.astype(jnp.bfloat16)
    gate_w_grad = jnp.einsum(
        "rd,rf->df", normed_two_low, gate_low, preferred_element_type=jnp.float32
    )
    up_w_grad = jnp.einsum("rd,rf->df", normed_two_low, up_low, preferred_element_type=jnp.float32)
    normed_two_grad = jnp.einsum(
        "rf,df->rd", gate_low, gate_w, preferred_element_type=jnp.float32
    ) + jnp.einsum("rf,df->rd", up_low, up_w, preferred_element_type=jnp.float32)
    hidden_norm_grad, gain_two_grad = rms_backward(hidden, factor_two, gain_second, normed_two_grad)
    hidden_grad = result_grad + hidden_norm_grad
    hidden_low = hidden_grad.astype(jnp.bfloat16)
    out_w_grad = jnp.einsum(
        "rc,rd->cd", attended_low, hidden_low, preferred_element_type=jnp.float32
    )
    attended_grad = jnp.einsum(
        "rd,cd->rc", hidden_low, out_w, preferred_element_type=jnp.float32
    ).astype(jnp.bfloat16)
    delta_sum = jnp.swapaxes(
        jnp.sum(
            split_heads(
                (attended_grad.astype(jnp.float32) * attended).reshape(
                    groups, local_len, model_width
                )
            ),
            axis=-1,
        ),
        1,
        2,
    )
    grad_local = attended_grad.reshape(groups, local_len, model_width)
    zero_grad = jnp.zeros((groups, local_len, model_width), jnp.float32)
    all_keys, all_values = (
        lax.all_gather(key_rows, "ctx", axis=1, tiled=True),
        lax.all_gather(values, "ctx", axis=1, tiled=True),
    )

    def query_step(current, block_index):
        begin = block_index * local_len
        key_part = lax.dynamic_slice_in_dim(all_keys, begin, local_len, 1)
        value_part = lax.dynamic_slice_in_dim(all_values, begin, local_len, 1)
        key_place = lax.dynamic_slice_in_dim(places, begin, local_len, 1)
        key_segment = lax.dynamic_slice_in_dim(segments, begin, local_len, 1)
        allowed = visible(own_place, own_segment, key_place, key_segment)

        def query_compute(query_sum):
            prob_low, score_grad = backward_block(
                queries, grad_local, key_part, value_part, allowed, maximum, denominator, delta_sum
            )
            return query_sum + jnp.einsum(
                "ghqk,gkhd->gqhd",
                score_grad,
                split_heads(key_part),
                preferred_element_type=jnp.float32,
            ).reshape(groups, local_len, model_width)

        return (
            lax.cond(jnp.any(allowed), query_compute, lambda query_sum: query_sum, current),
            None,
        )

    finished, unused = lax.scan(
        query_step, zero_grad, jnp.arange(group_len // local_len, dtype=jnp.int32)
    )
    term_rows = local_len * lax.axis_size("ctx")
    key_block_size = math.gcd(term_rows, local_len)

    def key_one_block(block_index):
        begin = block_index * key_block_size
        key_part = lax.dynamic_slice_in_dim(all_keys, begin, key_block_size, 1)
        value_part = lax.dynamic_slice_in_dim(all_values, begin, key_block_size, 1)
        key_place = lax.dynamic_slice_in_dim(places, begin, key_block_size, 1)
        key_segment = lax.dynamic_slice_in_dim(segments, begin, key_block_size, 1)
        allowed = visible(own_place, own_segment, key_place, key_segment)

        def one_compute(unused_arg):
            prob_low, score_grad = backward_block(
                queries, grad_local, key_part, value_part, allowed, maximum, denominator, delta_sum
            )
            key_add = jnp.einsum(
                "ghqk,gqhd->kghd",
                score_grad,
                split_heads(queries),
                preferred_element_type=jnp.float32,
            ).reshape(key_block_size, groups, model_width)
            value_add = jnp.einsum(
                "ghqk,gqhd->kghd",
                prob_low,
                split_heads(grad_local),
                preferred_element_type=jnp.float32,
            ).reshape(key_block_size, groups, model_width)
            return jnp.stack([key_add, value_add], axis=1)

        return lax.cond(
            jnp.any(allowed),
            one_compute,
            lambda unused_arg: jnp.zeros((key_block_size, 2, groups, model_width), jnp.float32),
            0,
        )

    summed = lax.psum_scatter(
        lax.map(key_one_block, jnp.arange(term_rows // key_block_size, dtype=jnp.int32))
        .reshape(term_rows, 2, groups, model_width)
        .astype(jnp.bfloat16),
        "ctx",
        scatter_dimension=0,
        tiled=True,
    ).astype(jnp.float32)
    key_grad = jnp.swapaxes(summed[:, 0], 0, 1)
    value_grad = jnp.swapaxes(summed[:, 1], 0, 1)
    query_low = finished.reshape(row_count, model_width).astype(jnp.bfloat16)
    key_low = key_grad.reshape(row_count, model_width).astype(jnp.bfloat16)
    value_low = value_grad.reshape(row_count, model_width).astype(jnp.bfloat16)
    query_w_grad = jnp.einsum(
        "rc,rd->cd", normed_low, query_low, preferred_element_type=jnp.float32
    )
    key_w_grad = jnp.einsum("rc,rd->cd", normed_low, key_low, preferred_element_type=jnp.float32)
    value_w_grad = jnp.einsum(
        "rc,rd->cd", normed_low, value_low, preferred_element_type=jnp.float32
    )
    normed_grad = (
        jnp.einsum("rd,cd->rc", query_low, query_w, preferred_element_type=jnp.float32)
        + jnp.einsum("rd,cd->rc", key_low, key_w, preferred_element_type=jnp.float32)
        + jnp.einsum("rd,cd->rc", value_low, value_w, preferred_element_type=jnp.float32)
    )
    active_norm_grad, gain_one_grad = rms_backward(active, factor_one, gain_first, normed_grad)
    active_grad = (hidden_grad + active_norm_grad - result_grad).reshape(
        groups, local_len, 1, model_width
    )
    mixed_grad = jnp.concatenate([upstream[:, :, :1] + active_grad, upstream[:, :, 1:]], axis=2)
    predict_local = jnp.einsum("gtid,gtjd->ij", mixed_grad, inputs, precision=HIGHEST)
    states_grad = jnp.einsum("ij,gtid->gtjd", predict, mixed_grad, precision=HIGHEST).astype(
        jnp.bfloat16
    )
    predict_grad, correct_grad = lax.psum((predict_local, correct_local), ("ctx", "wsh"))
    (
        gain_one_rows,
        query_rows,
        key_grad_rows,
        value_rows,
        out_rows,
        gain_two_rows,
        gate_rows,
        up_rows,
        down_rows,
    ) = (
        lax.psum_scatter(
            gain_one_grad.astype(jnp.bfloat16), "wsh", scatter_dimension=0, tiled=True
        ).astype(jnp.float32),
        lax.psum_scatter(
            query_w_grad.astype(jnp.bfloat16), "wsh", scatter_dimension=0, tiled=True
        ).astype(jnp.float32),
        lax.psum_scatter(
            key_w_grad.astype(jnp.bfloat16), "wsh", scatter_dimension=0, tiled=True
        ).astype(jnp.float32),
        lax.psum_scatter(
            value_w_grad.astype(jnp.bfloat16), "wsh", scatter_dimension=0, tiled=True
        ).astype(jnp.float32),
        lax.psum_scatter(
            out_w_grad.astype(jnp.bfloat16), "wsh", scatter_dimension=0, tiled=True
        ).astype(jnp.float32),
        lax.psum_scatter(
            gain_two_grad.astype(jnp.bfloat16), "wsh", scatter_dimension=0, tiled=True
        ).astype(jnp.float32),
        lax.psum_scatter(
            gate_w_grad.astype(jnp.bfloat16), "wsh", scatter_dimension=0, tiled=True
        ).astype(jnp.float32),
        lax.psum_scatter(
            up_w_grad.astype(jnp.bfloat16), "wsh", scatter_dimension=0, tiled=True
        ).astype(jnp.float32),
        lax.psum_scatter(
            down_grad.astype(jnp.bfloat16), "wsh", scatter_dimension=0, tiled=True
        ).astype(jnp.float32),
    )
    totals = (
        lax.psum(gain_one_rows.astype(jnp.bfloat16), "ctx").astype(jnp.float32),
        lax.psum(query_rows.astype(jnp.bfloat16), "ctx").astype(jnp.float32),
        lax.psum(key_grad_rows.astype(jnp.bfloat16), "ctx").astype(jnp.float32),
        lax.psum(value_rows.astype(jnp.bfloat16), "ctx").astype(jnp.float32),
        lax.psum(out_rows.astype(jnp.bfloat16), "ctx").astype(jnp.float32),
        lax.psum(gain_two_rows.astype(jnp.bfloat16), "ctx").astype(jnp.float32),
        lax.psum(gate_rows.astype(jnp.bfloat16), "ctx").astype(jnp.float32),
        lax.psum(up_rows.astype(jnp.bfloat16), "ctx").astype(jnp.float32),
        lax.psum(down_rows.astype(jnp.bfloat16), "ctx").astype(jnp.float32),
    )
    return (new_states, states_grad, predict_grad, correct_grad) + tuple(totals)


MESH = pl.DeviceIdType.MESH
F32 = jnp.float32
BF16 = jnp.bfloat16
CHIPS = 4
VMEM_LIMIT = 60 * 2**20
DMA = pltpu.SemaphoreType.DMA


def place_on_mesh():
    ctx = lax.axis_index("ctx")
    depth = lax.axis_index("wsh")
    chip = ctx // 2
    core = ctx % 2
    chip_x = chip + 1 - 2 * (chip % 2)
    chip_y = chip + 2 - 4 * (chip // 2)
    return depth, chip, core, chip_x, chip_y, 3 - chip


def signal_all(devices):
    barrier = pltpu.get_barrier_semaphore()
    for device in devices:
        pl.semaphore_signal(barrier, inc=1, device_id=device, device_id_type=MESH)


def wait_all(devices):
    pl.semaphore_wait(pltpu.get_barrier_semaphore(), len(devices))


def remote(src, dst, send, recv, index, device):
    return pltpu.make_async_remote_copy(
        src_ref=src,
        dst_ref=dst,
        send_sem=send.at[index],
        recv_sem=recv.at[index],
        device_id=device,
        device_id_type=MESH,
    )


def comm_params(collective_id):
    return pltpu.CompilerParams(
        collective_id=collective_id, has_side_effects=True, vmem_limit_bytes=VMEM_LIMIT
    )


ANY = pl.BlockSpec(memory_space=pl.ANY)
VM = pl.BlockSpec(memory_space=pltpu.VMEM)
SM = pl.BlockSpec(memory_space=pltpu.SMEM)


def ring_sends(own, out, slot_of, chip, core, depth, chip_x, chip_y, send, recv):
    half = own.shape[0] // 2
    top, low = pl.ds(0, half), pl.ds(half, half)
    dev_x, dev_y = (2 * chip_x + core, depth), (2 * chip_y + core, depth)
    here = slot_of(chip)
    return [
        remote(own.at[top], out.at[here, top], send, recv, 0, dev_x),
        remote(own.at[low], out.at[here, low], send, recv, 1, dev_y),
        remote(own.at[low], out.at[here, low], send, recv, 2, dev_x),
        remote(own.at[top], out.at[here, top], send, recv, 3, dev_y),
        remote(out.at[slot_of(chip_x), top], out.at[slot_of(chip_x), top], send, recv, 4, dev_y),
        remote(out.at[slot_of(chip_y), low], out.at[slot_of(chip_y), low], send, recv, 5, dev_x),
    ]


NT = (((1,), (1,)), ((), ()))
TN = (((0,), (0,)), ((), ()))
TILE = 256
ROWS = 32
LOCAL_HEADS = HEADS // CHIPS
CHIP_COLS = LOCAL_HEADS * HD


def head_mask(rows, head):
    lane = lax.broadcasted_iota(jnp.int32, (rows, CHIP_COLS), 1)
    return (lane >= head * HD) & (lane < (head + 1) * HD)


def aligned(index, size):
    return pl.ds(pl.multiple_of(index * size, size), size)


def norm_factor(rows):
    return lax.rsqrt(jnp.mean(rows * rows, axis=1, keepdims=True) + EPSILON)


def as_column(row):
    return jnp.broadcast_to(row, (8, row.shape[1])).T[:, 0:1]


def mix(states_ref, at, p_ref, i):
    return p_ref[i, 0] * states_ref[at, 0, :].astype(F32) + p_ref[i, 1] * states_ref[at, 1, :].astype(F32)


def plane_sum(parts, near_in, far_in, chip, core, depth, chip_x, chip_y, chip_d, send, recv):
    half = parts.shape[1] // 2
    top, low = pl.ds(0, half), pl.ds(half, half)
    dev_x, dev_y = (2 * chip_x + core, depth), (2 * chip_y + core, depth)
    copies = [
        remote(parts.at[chip_d, top], far_in.at[0], send, recv, 0, dev_x),
        remote(parts.at[chip_d, low], far_in.at[1], send, recv, 1, dev_y),
        remote(parts.at[chip_x, top], near_in.at[0, top], send, recv, 2, dev_x),
        remote(parts.at[chip_y, low], near_in.at[1, low], send, recv, 3, dev_y),
        remote(parts.at[chip_y, top], near_in.at[1, top], send, recv, 4, dev_y),
        remote(parts.at[chip_x, low], near_in.at[0, low], send, recv, 5, dev_x),
    ]

    def give(i):
        for copy in (copies[:2] if i == 2 else copies[2 + i : 3 + i]):
            copy.start()

    def relay():
        for i, (c, rows) in enumerate(((chip_y, slice(0, half)), (chip_x, slice(half, 2 * half)))):
            copies[i].wait_recv()
            parts[c, rows] = (parts[c, rows].astype(F32) + far_in[i].astype(F32)).astype(BF16)
            copies[4 + i].start()

    def receive():
        for copy in copies[2:]:
            copy.wait_recv()

    return give, relay, receive, copies


def plane_peers(chip, core, depth, chip_x, chip_y, chip_d):
    same = [(2 * c + core, depth) for c in (chip_x, chip_y, chip_d)]
    return same + [(2 * c + 1 - core, depth) for c in (chip, chip_x, chip_y, chip_d)]


def total_over_mesh(own_ref, arrived, staged, far, across, peers, bsend, brecv, csend, crecv):
    first = [remote(own_ref, arrived.at[i], bsend, brecv, i, d) for i, d in enumerate(across)]
    second = [remote(staged, far.at[i], csend, crecv, i, d) for i, d in enumerate(peers)]

    def start():
        for copy in first:
            copy.start()

    def turn():
        total = own_ref[...]
        for i, copy in enumerate(first):
            copy.wait_recv()
        for i in range(len(first)):
            total = total + arrived[i]
        staged[...] = total
        for copy in second:
            copy.start()

    def end():
        for copy in second:
            copy.wait_recv()
        total = staged[...]
        for i in range(len(second)):
            total = total + far[i]
        for copy in first + second:
            copy.wait_send()
        return total

    return start, turn, end


def total_scratch(shape, depths):
    return [
        pltpu.VMEM((depths - 1,) + shape, F32),
        pltpu.VMEM(shape, F32),
        pltpu.VMEM((2 * CHIPS - 1,) + shape, F32),
        DMA((depths - 1,)),
        DMA((depths - 1,)),
        DMA((2 * CHIPS - 1,)),
        DMA((2 * CHIPS - 1,)),
    ]


def gelu_parts(v):
    scale = math.sqrt(2 / math.pi)
    square = v * v
    t = jnp.tanh(scale * v * (1.0 + 0.044715 * square))
    rise = 0.5 * (1.0 + t)
    return v * rise, rise + 0.5 * v * (1.0 - t * t) * scale * (1.0 + 0.134145 * square)


def pair_places(slots_ref, pair):
    one, two = slots_ref[2 * pair], slots_ref[2 * pair + 1]
    second = (one >= PROMPT // BLK).astype(jnp.int32)
    return second, jnp.minimum(one, two), jnp.maximum(one, two)


def own_pair(pair, per_device):
    core = lax.axis_index("ctx") % 2
    pairs = per_device // 2
    return (pair // pairs) * per_device + core * pairs + pair % pairs


PER_TILE = TILE // BLK


def fill_bias(bias, kind, tile_step, slots_ref, lengths_ref, per_device, group_pairs):
    lane = lax.broadcasted_iota(jnp.int32, (1, TILE), 1)
    high = jnp.zeros((1, TILE), jnp.int32)
    for i in range(PER_TILE):
        _, prompt, cont = pair_places(slots_ref, own_pair(tile_step * PER_TILE + i, per_device))
        block = prompt if kind == 0 else cont
        high = jnp.where(lane >= i * BLK, (block - i) * BLK + lane, high)
    low = jnp.zeros((1, TILE), jnp.int32)
    if kind == 1:
        start = PROMPT
        for i in range(lengths_ref.shape[0]):
            low = jnp.where(high >= start, start, low)
            start = start + lengths_ref[i]
    offset = lax.broadcasted_iota(jnp.int32, (BLK, TILE), 0)

    def one_block(pair, _):
        _, prompt, cont = pair_places(slots_ref, pair)
        base = (prompt if kind == 0 else cont) * BLK
        seen = offset <= high - base
        if kind == 1:
            seen = seen & (offset >= low - base)
        bias[pair // PER_TILE, aligned(pair % PER_TILE, BLK), 0:TILE] = jnp.where(seen, 0.0, NEGATIVE)
        return 0

    lax.fori_loop(0, group_pairs, one_block, 0)


def either(second, one, two):
    swap = second == 1
    return jnp.where(swap, two, one), jnp.where(swap, one, two)


def to_pair_order(source, target, slots_ref, group_pairs):
    def one_pair(pair, _):
        second, _, _ = pair_places(slots_ref, pair)
        first, last = either(second, source[aligned(2 * pair, BLK), :], source[aligned(2 * pair + 1, BLK), :])
        target[aligned(pair, BLK), :] = first
        target[aligned(group_pairs + pair, BLK), :] = last
        return 0

    lax.fori_loop(0, group_pairs, one_pair, 0)


def own_to_pair_order(source, target, slots_ref, pairs, per_device):
    def one_pair(pair, _):
        second, _, _ = pair_places(slots_ref, own_pair(pair, per_device))
        first, last = either(second, source[aligned(2 * pair, BLK), :], source[aligned(2 * pair + 1, BLK), :])
        target[aligned(pair, BLK), :] = first
        target[aligned(pairs + pair, BLK), :] = last
        return 0

    lax.fori_loop(0, pairs, one_pair, 0)


def own_to_slot_order(source, target, slots_ref, pairs, per_device):
    def one_pair(pair, _):
        second, _, _ = pair_places(slots_ref, own_pair(pair, per_device))
        first, last = either(second, source[aligned(pair, BLK), :], source[aligned(pairs + pair, BLK), :])
        target[aligned(2 * pair, BLK), :] = first
        target[aligned(2 * pair + 1, BLK), :] = last
        return 0

    lax.fori_loop(0, pairs, one_pair, 0)


def line_reduce(pieces, acc, up_in, down_in, up_out, down_out, sems):
    depth, chip, core, _, _, _ = place_on_mesh()
    depths = pieces.shape[0]
    last = depths - 1
    up_send, up_recv, down_send, down_recv = sems
    above = (2 * chip + core, lax.rem(depth + 1, depths))
    below = (2 * chip + core, lax.rem(depth + last, depths))

    def up(source, k):
        return remote(source, up_in.at[k], up_send, up_recv, k, above)

    def down(source, k):
        return remote(source, down_in.at[k], down_send, down_recv, k, below)

    def start():
        @pl.when(depth == 0)
        def _():
            for k in range(last):
                up(pieces.at[last - k], k).start()

        @pl.when(depth == last)
        def _():
            for k in range(last):
                down(pieces.at[k], k).start()

    def hop(k):
        @pl.when((depth >= 1) & (depth <= k))
        def _():
            up(up_in.at[k - 1], k - 1).wait_recv()
            mine = pieces[jnp.clip(depth + last - k, 0, last)]
            up_out[k - 1] = (mine.astype(F32) + up_in[k - 1].astype(F32)).astype(BF16)
            up(up_out.at[k - 1], k).start()

        @pl.when((depth <= last - 1) & (depth >= last - k))
        def _():
            down(down_in.at[k - 1], k - 1).wait_recv()
            mine = pieces[jnp.clip(depth + k - last, 0, last)]
            down_out[k - 1] = (mine.astype(F32) + down_in[k - 1].astype(F32)).astype(BF16)
            down(down_out.at[k - 1], k).start()

    def result():
        acc[...] = pieces[depth].astype(F32)

        @pl.when(depth >= 1)
        def _():
            up(up_in.at[last - 1], last - 1).wait_recv()
            acc[...] += up_in[last - 1].astype(F32)

        @pl.when(depth <= last - 1)
        def _():
            down(down_in.at[last - 1], last - 1).wait_recv()
            acc[...] += down_in[last - 1].astype(F32)

    def finish():
        @pl.when(depth == 0)
        def _():
            for k in range(last):
                up(pieces.at[last - k], k).wait_send()

        @pl.when(depth == last)
        def _():
            for k in range(last):
                down(pieces.at[k], k).wait_send()

        for k in range(1, last):

            @pl.when((depth >= 1) & (depth <= k))
            def _(k=k):
                up(up_out.at[k - 1], k).wait_send()

            @pl.when((depth <= last - 1) & (depth >= last - k))
            def _(k=k):
                down(down_out.at[k - 1], k).wait_send()

    return start, hop, result, finish


def forward(
    slots, lengths, predict, correct, states, out_grad, teacher, valid, gain_one, gain_two,
    w_query, w_key, w_value, w_out, w_gate, w_up, w_down, collective_id,
):
    rows, _, width = states.shape
    shard = w_query.shape[0]
    half = shard // 2
    depths = width // shard
    hidden_cols = w_gate.shape[1]
    columns = hidden_cols // CHIPS
    split = columns // depths
    out_rows = shard // CHIPS
    blocks = rows // ROWS
    col_tiles = columns // TILE
    tokens = 2 * CHIPS * rows
    queries = CHIPS * rows
    tiles = queries // TILE
    per_device = rows // BLK
    group_pairs = tokens // (2 * BLK)
    pairs = queries // (2 * BLK)
    mesh_tokens = tokens * depths
    piece_lanes = 3 * CHIP_COLS

    def kernel(
        slots_ref, lengths_ref, p_ref, c_ref, s_ref, g_ref, t_ref, v_ref, g1_ref, g2_ref,
        wq_ref, wk_ref, wv_ref, wo_ref, wg_ref, wu_ref, wd_ref,
        new_out, up0_out, up1_out, hg_out, da_ref, dwo_ref, ffa_ref, ffb_ref, sums_ref,
        x_out, w_out_ref, q_out, k_out, v_out, oT_out, lse_ref,
        new_ref, up0_ref, up1_ref, hg_ref, all_rows, w_all, q_pairs, k_pairs, v_pairs, oT_ref, dwo, dwo_other,
        w_ff, w_wo, qkv, att_all, hidden, own, x_rows, r_rows, xT, innerT, inner, gate, up, gate_low, up_low,
        own_weight, part1, part2, got1, got2, far1, far2, dw, dw_other, a_up, a_down, buf, wide, count, q_slot, k_slot, v_slot, vT,
        lsend, fsend, frecv, fosend, forecv, qsend, qrecv, qosend, qorecv,
        osend, orecv, oosend, oorecv, opsend, oprecv,
        rsend, rrecv, rosend, rorecv, send0, recv0, send1, recv1, send2, recv2, send3, recv3,
        ag1s, ag1r, ag2s, ag2r, dsend, drecv, osems, xsems, *rest,
    ):
        a_sems, total_refs = rest[:4], rest[4:]
        stores = []

        def store(index, source, target):
            copy = pltpu.make_async_copy(source, target, osems.at[index])
            copy.start()
            stores.append(copy)

        depth, chip, core, chip_x, chip_y, chip_d = place_on_mesh()
        near = [(c, (2 * c + core, depth)) for c in (chip_x, chip_y, chip_d)]
        other = (2 * chip + 1 - core, depth)
        across = [
            (2 * chip + core, lax.rem(depth + step, depths)) for step in range(1, depths)
        ]
        peers = plane_peers(chip, core, depth, chip_x, chip_y, chip_d)
        signal_all(peers + across)

        mine = pl.ds(core * half, half)
        loads = [
            pltpu.make_async_copy(w.at[mine], buf.at[i], lsend.at[i])
            for i, w in enumerate((wq_ref, wk_ref, wv_ref))
        ] + [
            pltpu.make_async_copy(wg_ref.at[mine], wide.at[0], lsend.at[3]),
            pltpu.make_async_copy(wu_ref.at[mine], wide.at[1], lsend.at[4]),
            pltpu.make_async_copy(
                wd_ref.at[pl.ds(chip * split + core * half, half)], w_ff.at[2, depth, core], lsend.at[5]
            ),
            pltpu.make_async_copy(
                wo_ref.at[pl.ds(chip * out_rows, out_rows)], w_wo.at[depth, chip], lsend.at[6]
            ),
        ]
        for copy in loads:
            copy.start()
        count[...] = jnp.broadcast_to(
            jnp.sum(v_ref[...].astype(F32), axis=1, keepdims=True), count.shape
        )

        def input_norm(i, _):
            at = aligned(i, ROWS)
            active = mix(s_ref, at, p_ref, 0)
            own[0, at, :] = (active * norm_factor(active)).astype(BF16)
            return 0

        lax.fori_loop(0, blocks, input_norm, 0)

        def gain_column(ref):
            both = jnp.broadcast_to(ref[...].astype(F32), (8, shard)).T
            return jnp.where(core == 0, both[:half, 0:1], both[half:, 0:1])

        one, two = gain_column(g1_ref), gain_column(g2_ref)
        wait_all(peers + across)

        def slot(chip_index):
            return 2 * chip_index + core

        start_count, turn_count, end_count = total_over_mesh(
            count, *total_refs[:3], across, peers, *total_refs[3:]
        )
        start_count()
        ring0 = ring_sends(
            own.at[0], all_rows, slot, chip, core, depth, chip_x, chip_y, rsend, rrecv
        )
        for copy in ring0[:4]:
            copy.start()

        def rows_to_other(index, chip_index):
            ref = all_rows.at[slot(chip_index)]
            return remote(own.at[0] if index == 0 else ref, ref, rosend, rorecv, index, other)

        shared0 = [rows_to_other(i, c) for i, c in enumerate((chip, chip_x, chip_y, chip_d))]
        shared0[0].start()
        all_rows[slot(chip)] = own[0]

        for copy in loads[:3]:
            copy.wait()
        for p in range(CHIPS):

            @pl.when(chip == p)
            def _(p=p):
                cols = jnp.concatenate(
                    [buf[i, :, p * CHIP_COLS : (p + 1) * CHIP_COLS].astype(F32) for i in range(3)], axis=1
                )
                qkv[depth, core] = (cols * one).astype(BF16)

        qkv_mine = qkv.at[depth, core]
        q_copies = [
            remote(qkv_mine, qkv_mine, qsend, qrecv, i, device) for i, device in enumerate(across)
        ]
        q_shared = [remote(qkv_mine, qkv_mine, qosend, qorecv, 0, other)]
        for copy in q_copies + q_shared:
            copy.start()

        loads[6].wait()
        o_copies = [
            remote(w_wo.at[depth, chip], w_wo.at[depth, chip], osend, orecv, i, device)
            for i, device in enumerate(across)
        ]
        o_shared = []
        for i in range(depths - 1):
            came = w_wo.at[lax.rem(depth + depths - 1 - i, depths), chip]
            o_shared.append(remote(came, came, oosend, oorecv, i, other))

        def carried(i, act):
            pl.when(core == (i + 1) % 2)(act)

        def not_carried(i, act):
            pl.when(core != (i + 1) % 2)(act)

        for i in range(depths - 1):
            carried(i, o_copies[i].start)

        for copy in loads[3:6]:
            copy.wait()
        for p in range(CHIPS):

            @pl.when(chip == p)
            def _(p=p):
                for i in range(2):
                    cols = jnp.concatenate(
                        [
                            wide[i, :, (z * CHIPS + p) * split : (z * CHIPS + p + 1) * split].astype(F32)
                            for z in range(depths)
                        ],
                        axis=1,
                    )
                    w_ff[i, depth, core] = (cols * two).astype(BF16)

        line_up = (2 * chip + core, lax.rem(depth + 1, depths))
        line_down = (2 * chip + core, lax.rem(depth + depths - 1, depths))
        hops = []
        for stage in range(1, depths):
            for direction, device, index in ((1, line_up, stage - 1), (-1, line_down, depths + stage - 2)):
                goes = jnp.clip(depth - direction * (stage - 1), 0, depths - 1)
                comes = jnp.clip(depth - direction * stage, 0, depths - 1)
                piece, came = w_ff.at[:, goes, core], w_ff.at[:, comes, core]
                if direction == 1:
                    sends, receives = (depth >= stage - 1) & (depth < depths - 1), depth >= stage
                else:
                    sends, receives = (depth <= depths - stage) & (depth > 0), depth < depths - stage
                hops.append(
                    (
                        stage,
                        sends,
                        receives,
                        remote(piece, piece, fsend, frecv, index, device),
                        remote(came, came, fosend, forecv, index, other),
                    )
                )
        ff_mine = remote(w_ff.at[:, depth, core], w_ff.at[:, depth, core], fosend, forecv, 2 * depths - 2, other)
        ff_mine.start()

        def send_hop(stage):
            for at, sends, _, hop, _ in hops:
                if at == stage:
                    pl.when(sends)(hop.start)

        def take_hop(stage):
            for at, _, receives, hop, share in hops:
                if at == stage:

                    @pl.when(receives)
                    def _(hop=hop, share=share):
                        hop.wait_recv()
                        share.start()

        send_hop(1)
        turn_count()
        ring0[0].wait_recv()
        ring0[4].start()
        ring0[1].wait_recv()
        ring0[5].start()
        for i in range(depths - 1):
            q_copies[i].wait_recv()
            came = qkv.at[lax.rem(depth + depths - 1 - i, depths), core]
            share = remote(came, came, qosend, qorecv, 1 + i, other)
            share.start()
            q_shared.append(share)
        ring0[2].wait_recv()
        shared0[1].start()
        ring0[3].wait_recv()
        shared0[2].start()
        for copy in q_shared:
            copy.wait_recv()
        for i in range(3):
            for z in range(depths):
                for c in range(2):
                    at = (z * 2 + c) * half
                    w_all[i, at : at + half, :] = qkv[z, c, :, i * CHIP_COLS : (i + 1) * CHIP_COLS]

        def project(device_slot, with_queries):
            x = all_rows[device_slot]
            at = aligned(device_slot, rows)
            k_slot[at, :] = jnp.dot(x, w_all[1], preferred_element_type=F32).astype(BF16)
            v_slot[at, :] = jnp.dot(x, w_all[2], preferred_element_type=F32).astype(BF16)
            if with_queries:
                q_slot[aligned(device_slot // 2, rows), :] = jnp.dot(
                    x, w_all[0], preferred_element_type=F32
                ).astype(BF16)

        for c in (chip, chip_x, chip_y):
            project(slot(c), True)
        for i, c in enumerate((chip, chip_x, chip_y)):
            shared0[i].wait_recv()
            project(2 * c + 1 - core, False)
        ring0[4].wait_recv()
        ring0[5].wait_recv()
        shared0[3].start()
        project(slot(chip_d), True)
        for i in range(depths - 1):

            def came_here(i=i):
                o_copies[i].wait_recv()
                o_shared[i].start()

            carried(i, came_here)
        for i in range(depths - 1):
            not_carried(i, o_shared[i].wait_recv)
        carry = pl.ds(core * (depths // 2), depths // 2)
        o_plane = [
            remote(w_wo.at[carry, chip], w_wo.at[carry, chip], opsend, oprecv, i, device)
            for i, (_, device) in enumerate(near)
        ]
        for copy in o_plane:
            copy.start()
        o_across = [
            remote(w_wo.at[carry, c], w_wo.at[carry, c], opsend, oprecv, 3 + i, other)
            for i, (c, _) in enumerate(near)
        ]
        shared0[3].wait_recv()
        project(2 * chip_d + 1 - core, False)

        for i in range(CHIPS):
            x_copy = pltpu.make_async_copy(all_rows.at[2 * i + core], x_out.at[i], xsems.at[i])
            x_copy.start()
            stores.append(x_copy)
        store(0, w_all, w_out_ref)

        to_pair_order(k_slot, k_pairs, slots_ref, group_pairs)
        to_pair_order(v_slot, v_pairs, slots_ref, group_pairs)
        own_to_pair_order(q_slot, q_pairs, slots_ref, pairs, per_device)

        store(1, q_pairs, q_out)
        store(2, k_pairs, k_out)
        store(3, v_pairs, v_out)

        def turn_values(i, _):
            vT[:, aligned(i, TILE)] = v_pairs[aligned(i, TILE), :].T
            return 0

        lax.fori_loop(0, tokens // TILE, turn_values, 0)
        half_keys = group_pairs * BLK
        half_tiles = half_keys // TILE
        scores, bias = gate, up

        def cell(k_tile):
            lanes = (k_tile // CHIPS) * TILE
            return k_tile % CHIPS, slice(lanes, lanes + TILE)

        def attend(kind, step):
            tile = kind * (tiles // 2) + step
            key_tiles = half_tiles * (kind + 1)
            q = q_pairs[aligned(tile, TILE), :]
            fill_bias(bias, kind, step, slots_ref, lengths_ref, per_device, group_pairs)
            for head in range(LOCAL_HEADS):
                heads = slice(head * HD, (head + 1) * HD)
                q_head = jnp.where(head_mask(TILE, head), q, jnp.zeros_like(q))
                top = jnp.full((1, TILE), NEGATIVE, F32)
                for k_tile in range(key_tiles):
                    s = lax.dot_general(
                        k_pairs[k_tile * TILE : (k_tile + 1) * TILE, :], q_head, NT, preferred_element_type=F32
                    )
                    if k_tile >= key_tiles - half_tiles:
                        s = s + bias[k_tile - (key_tiles - half_tiles), :, 0:TILE]
                    index, lanes = cell(k_tile)
                    scores[index, :, lanes] = s
                    top = jnp.maximum(top, jnp.max(s, axis=0, keepdims=True))
                total = jnp.zeros((1, TILE), F32)
                out = jnp.zeros((HD, TILE), F32)
                for k_tile in range(key_tiles):
                    index, lanes = cell(k_tile)
                    e = jnp.exp(scores[index, :, lanes] - top)
                    total = total + jnp.sum(e, axis=0, keepdims=True)
                    out = out + jnp.dot(
                        vT[heads, k_tile * TILE : (k_tile + 1) * TILE], e.astype(BF16), preferred_element_type=F32
                    )
                oT_ref[tile, heads, :] = out / total
                lse_ref[tile, head] = top + jnp.log(total)
            q_slot[aligned(tile, TILE), :] = oT_ref[tile].T.astype(BF16)

        def both_steps(kind):
            def body(step, _):
                attend(kind, step)
                return 0

            lax.fori_loop(0, tiles // 2, body, 0)

        both_steps(1)
        take_hop(1)
        send_hop(2)
        for copy, passed in zip(o_plane, o_across):
            copy.wait_recv()
            passed.start()
        both_steps(0)

        store(4, oT_ref, oT_out)
        own_to_slot_order(q_slot, k_slot, slots_ref, pairs, per_device)
        for c in range(CHIPS):
            att_all[CHIPS + c] = k_slot[c * rows : (c + 1) * rows, :]
        sends0 = [
            remote(att_all.at[CHIPS + c], att_all.at[chip], send0, recv0, i, device)
            for i, (c, device) in enumerate(near)
        ]
        for copy in sends0:
            copy.start()
        att_all[chip] = att_all[CHIPS + chip]
        take_hop(2)
        send_hop(3)
        for copy in o_across:
            copy.wait_recv()
        for copy in sends0:
            copy.wait()

        def w_out_rows(p):
            return w_wo[p].reshape(CHIP_COLS, width)

        for p in range(CHIPS):
            term = jnp.dot(att_all[p], w_out_rows(p), preferred_element_type=F32)
            hidden[...] = term if p == 0 else hidden[...] + term

        def first_norm(i, _):
            at = aligned(i, ROWS)
            h = hidden[at, :] + mix(s_ref, at, p_ref, 0)
            hidden[at, :] = h
            own[1, at, :] = (h * norm_factor(h)).astype(BF16)
            return 0

        lax.fori_loop(0, blocks, first_norm, 0)

        def ring(source, target, send, recv):
            return ring_sends(
                source, target, lambda c: c, chip, core, depth, chip_x, chip_y, send, recv
            )

        ring1 = ring(own.at[1], x_rows, ag1s, ag1r)
        for copy in ring1[:4]:
            copy.start()
        x_rows[chip] = own[1]
        ring1[0].wait_recv()
        ring1[4].start()
        ring1[1].wait_recv()
        ring1[5].start()
        take_hop(3)
        ff_mine.wait_recv()
        for _, _, receives, _, share in hops:
            pl.when(receives)(share.wait_recv)

        def w_rows(i):
            return w_ff[i].reshape(width, columns)

        def ff_forward(c):
            x = x_rows[c]
            for n in range(col_tiles):
                cols = slice(n * TILE, (n + 1) * TILE)
                g = jnp.dot(x, w_rows(0)[:, cols], preferred_element_type=F32)
                u = jnp.dot(x, w_rows(1)[:, cols], preferred_element_type=F32)
                gate[c, :, cols] = g
                up[c, :, cols] = u
                inner[c, :, cols] = (gelu_parts(g)[0] * u).astype(BF16)
            return jnp.dot(inner[c], w_rows(2), preferred_element_type=F32)

        give1, relay1, receive1, sends1 = plane_sum(
            part1, got1, far1, chip, core, depth, chip_x, chip_y, chip_d, send1, recv1
        )
        up0_ref[...] = ff_forward(chip)
        for i, (c, _) in enumerate(near):
            if i < 2:
                ring1[2 + i].wait_recv()
            else:
                ring1[4].wait_recv()
                ring1[5].wait_recv()
            part1[c] = ff_forward(c).astype(BF16)
            give1(i)
        relay1()

        def turn(i, _):
            xT[:, aligned(i, rows)] = x_rows[i].T
            innerT[:, aligned(i, rows)] = inner[i].T
            return 0

        lax.fori_loop(0, CHIPS, turn, 0)
        valid_count = end_count()
        weight = as_column(v_ref[...].astype(F32)) * (mesh_tokens / valid_count[0:1, 0:1])
        own_weight[...] = jnp.broadcast_to(weight, own_weight.shape)
        receive1()

        def outputs(i, sums):
            at = aligned(i, ROWS)
            a = mix(s_ref, at, p_ref, 0)
            result = hidden[at, :] + up0_ref[at, :]
            for j in range(2):
                result = result + got1[j, at, :].astype(F32)
            difference = result - a
            row_weight = own_weight[at, 0:1]
            c0, c1 = c_ref[0], c_ref[1]
            out0 = a + c0 * difference
            out1 = mix(s_ref, at, p_ref, 1) + c1 * difference
            new_ref[at, 0, :] = out0.astype(BF16)
            new_ref[at, 1, :] = out1.astype(BF16)
            up0 = g_ref[at, 0, :].astype(F32) + row_weight * (out0 - t_ref[at, 0, :].astype(F32))
            up1 = g_ref[at, 1, :].astype(F32) + row_weight * (out1 - t_ref[at, 1, :].astype(F32))
            up0_ref[at, :] = up0
            up1_ref[at, :] = up1
            own[2, at, :] = (c0 * up0 + c1 * up1).astype(BF16)
            return (
                sums[0] + jnp.sum(up0 * difference, axis=0, keepdims=True),
                sums[1] + jnp.sum(up1 * difference, axis=0, keepdims=True),
            )

        zero = jnp.zeros((1, width), F32)
        correct_sums = lax.fori_loop(0, blocks, outputs, (zero, zero))
        sums_ref[...] = jnp.zeros_like(sums_ref)
        sums_ref[2:3, :] = correct_sums[0]
        sums_ref[3:4, :] = correct_sums[1]
        store(5, new_ref, new_out)
        store(6, up0_ref, up0_out)
        store(7, up1_ref, up1_out)

        ring2 = ring(own.at[2], r_rows, ag2s, ag2r)
        for copy in ring2[:4]:
            copy.start()
        r_rows[chip] = own[2]

        def ff_backward(c):
            r = r_rows[c]
            for n in range(col_tiles):
                cols = slice(n * TILE, (n + 1) * TILE)
                inner_grad = lax.dot_general(r, w_rows(2)[cols, :], NT, preferred_element_type=F32)
                value, slope = gelu_parts(gate[c, :, cols])
                gate_low[c, :, cols] = (inner_grad * up[c, :, cols] * slope).astype(BF16)
                up_low[c, :, cols] = (inner_grad * value).astype(BF16)
            return lax.dot_general(
                gate_low[c], w_rows(0), NT, preferred_element_type=F32
            ) + lax.dot_general(up_low[c], w_rows(1), NT, preferred_element_type=F32)

        give2, relay2, receive2, sends2 = plane_sum(
            part2, got2, far2, chip, core, depth, chip_x, chip_y, chip_d, send2, recv2
        )
        hg_ref[...] = ff_backward(chip)
        ring2[0].wait_recv()
        ring2[4].start()
        ring2[1].wait_recv()
        ring2[5].start()
        for i, (c, _) in enumerate(near):
            if i < 2:
                ring2[2 + i].wait_recv()
            else:
                ring2[4].wait_recv()
                ring2[5].wait_recv()
            part2[c] = ff_backward(c).astype(BF16)
            give2(i)

        def weight_grads(terms):
            def body(z, _):
                at = aligned(z, shard)
                for i, left, right in terms:
                    grad = jnp.dot(
                        left[at, :], right[...].reshape(queries, -1), preferred_element_type=F32
                    ).astype(BF16)
                    dw[z, 0, i * half : (i + 1) * half, :] = grad[:half]
                    dw[z, 1, i * half : (i + 1) * half, :] = grad[half:]
                return 0

            lax.fori_loop(0, depths, body, 0)

        early, late = pl.ds(0, half), pl.ds(half, 2 * half)

        def swap_rows(index, part):
            return remote(dw.at[:, 1 - core, part], dw_other.at[:, part], dsend, drecv, index, other)

        def add_cores(part):
            def body(z, _):
                dw_other[z, part, :] = (
                    dw[z, core, part, :].astype(F32) + dw_other[z, part, :].astype(F32)
                ).astype(BF16)
                return 0

            lax.fori_loop(0, depths, body, 0)

        swaps = [swap_rows(0, early), swap_rows(1, late)]
        weight_grads(((0, innerT, r_rows),))
        swaps[0].start()
        for copy in sends1:
            copy.wait_send()
        a_start, a_hop, a_result, a_finish = line_reduce(
            dw_other.at[:, early], gate.at[0, pl.ds(0, half)], a_up, a_down,
            part1.at[pl.ds(0, 2), pl.ds(0, half)], part1.at[pl.ds(2, 2), pl.ds(0, half)], a_sems,
        )
        swaps[0].wait_recv()
        add_cores(early)
        a_start()
        relay2()
        weight_grads(((1, xT, gate_low), (2, xT, up_low)))
        swaps[1].start()
        a_hop(1)
        receive2()

        def second_norm(i, gain_sum):
            at = aligned(i, ROWS)
            h = hidden[at, :]
            weighted = hg_ref[at, :]
            for j in range(2):
                weighted = weighted + got2[j, at, :].astype(F32)
            factor = norm_factor(h)
            mean = jnp.mean(weighted * h, axis=1, keepdims=True)
            result_grad = c_ref[0] * up0_ref[at, :] + c_ref[1] * up1_ref[at, :]
            hidden_grad = result_grad + (factor * weighted - h * (factor * factor * factor * mean))
            hg_ref[at, :] = hidden_grad
            own[3, at, :] = hidden_grad.astype(BF16)
            return gain_sum + jnp.sum(weighted * h * factor, axis=0, keepdims=True)

        sums_ref[1:2, :] = lax.fori_loop(0, blocks, second_norm, zero)
        store(10, hg_ref, hg_out)

        sends3 = [
            remote(att_all.at[CHIPS + c], da_ref.at[chip], send3, recv3, i, device)
            for i, (c, device) in enumerate(near)
        ]

        def att_grad(c):
            return lax.dot_general(own[3], w_out_rows(c), NT, preferred_element_type=F32).astype(BF16)

        for i in (2, 0, 1):
            att_all[CHIPS + near[i][0]] = att_grad(near[i][0])
            sends3[i].start()
        da_ref[chip] = att_grad(chip)
        for i, c in enumerate((chip, chip_x, chip_y, chip_d)):
            grad = jnp.dot(att_all[c].T, own[3], preferred_element_type=F32).astype(BF16)
            dwo[i, 0] = grad[:half]
            dwo[i, 1] = grad[half:]
        out_swap = remote(dwo.at[:, 1 - core], dwo_other, dsend, drecv, 2, other)
        out_swap.start()
        swaps[1].wait_recv()
        add_cores(late)
        store(8, dw_other.at[:, late], ffb_ref)
        a_hop(2)
        out_swap.wait_recv()
        for i in range(CHIPS):
            dwo_other[i] = (dwo[i, core].astype(F32) + dwo_other[i].astype(F32)).astype(BF16)
        store(9, dwo_other, dwo_ref)
        a_result()
        ffa_ref[...] = gate[0, 0:half, :].astype(BF16)
        for copy in sends3:
            copy.wait_recv()
        sent = ring0 + shared0 + q_copies + q_shared + o_plane + o_across + sends2 + sends3
        for copy in sent + ring1 + ring2 + swaps + [out_swap, ff_mine]:
            copy.wait_send()
        a_finish()
        for i in range(depths - 1):
            carried(i, o_copies[i].wait_send)
            carried(i, o_shared[i].wait_send)
        for _, sends, receives, hop, share in hops:
            pl.when(sends)(hop.wait_send)
            pl.when(receives)(share.wait_send)
        for copy in stores:
            copy.wait()

    block = (rows, width)
    pair = (rows, 2, width)
    wide_rows = (CHIPS, rows, width)
    hid_rows = (CHIPS, rows, columns)

    def out(shape, dtype):
        return jax.ShapeDtypeStruct(shape, dtype)

    vmem = pltpu.VMEM
    outs = [
        out(pair, BF16),
        out(block, F32),
        out(block, F32),
        out(block, F32),
        out((CHIPS, rows, CHIP_COLS), BF16),
        out((CHIPS, half, width), BF16),
        out((half, columns), BF16),
        out((depths, 2 * half, columns), BF16),
        out((8, width), F32),
        out(wide_rows, BF16),
        out((3, width, CHIP_COLS), BF16),
        out((queries, CHIP_COLS), BF16),
        out((tokens, CHIP_COLS), BF16),
        out((tokens, CHIP_COLS), BF16),
        out((tiles, CHIP_COLS, TILE), F32),
        out((tiles, LOCAL_HEADS, 1, TILE), F32),
    ]
    return pl.pallas_call(
        kernel,
        out_shape=outs,
        in_specs=[SM] * 4 + [VM] * 6 + [ANY] * 7,
        out_specs=[ANY] * 4 + [VM, ANY, VM, ANY, VM] + [ANY] * 6 + [VM],
        scratch_shapes=[
            vmem(pair, BF16),
            vmem(block, F32),
            vmem(block, F32),
            vmem(block, F32),
            vmem((2 * CHIPS, rows, width), BF16),
            vmem((3, width, CHIP_COLS), BF16),
            vmem((queries, CHIP_COLS), BF16),
            vmem((tokens, CHIP_COLS), BF16),
            vmem((tokens, CHIP_COLS), BF16),
            vmem((tiles, CHIP_COLS, TILE), F32),
            vmem((CHIPS, 2, half, width), BF16),
            vmem((CHIPS, half, width), BF16),
            vmem((3, depths, 2, half, columns), BF16),
            vmem((depths, CHIPS, out_rows, width), BF16),
            vmem((depths, 2, half, piece_lanes), BF16),
            vmem((2 * CHIPS, rows, CHIP_COLS), BF16),
            vmem(block, F32),
            vmem((4,) + block, BF16),
            vmem(wide_rows, BF16),
            vmem(wide_rows, BF16),
            vmem((width, queries), BF16),
            vmem((columns, queries), BF16),
            vmem(hid_rows, BF16),
            vmem(hid_rows, F32),
            vmem(hid_rows, F32),
            vmem(hid_rows, BF16),
            vmem(hid_rows, BF16),
            vmem((rows, 128), F32),
            vmem(wide_rows, BF16),
            vmem(wide_rows, BF16),
            vmem((2,) + block, BF16),
            vmem((2,) + block, BF16),
            vmem((2, rows // 2, width), BF16),
            vmem((2, rows // 2, width), BF16),
            vmem((depths, 2, 3 * half, columns), BF16),
            vmem((depths, 3 * half, columns), BF16),
            vmem((depths - 1, half, columns), BF16),
            vmem((depths - 1, half, columns), BF16),
            vmem((3, half, width), BF16),
            vmem((2, half, hidden_cols), BF16),
            vmem((8, 128), F32),
            vmem((queries, CHIP_COLS), BF16),
            vmem((tokens, CHIP_COLS), BF16),
            vmem((tokens, CHIP_COLS), BF16),
            vmem((CHIP_COLS, tokens), BF16),
        ]
        + [DMA((7,))]
        + [DMA((2 * depths - 2,))] * 2
        + [DMA((2 * depths - 1,))] * 2
        + [DMA((depths - 1,))] * 2
        + [DMA((depths,))] * 2
        + [DMA((depths - 1,))] * 4
        + [DMA((6,))] * 2
        + [DMA((6,))] * 2
        + [DMA((4,))] * 2
        + [DMA((3,))] * 2
        + [DMA((6,))] * 4
        + [DMA((3,))] * 2
        + [DMA((6,))] * 4
        + [DMA((3,))] * 2
        + [DMA((11,)), DMA((CHIPS,))]
        + [DMA((depths - 1,))] * 4
        + total_scratch((8, 128), depths),
        compiler_params=comm_params(collective_id),
        name="forward",
    )(
        slots, lengths, predict, correct, states, out_grad, teacher, valid, gain_one, gain_two,
        w_query, w_key, w_value, w_out, w_gate, w_up, w_down,
    )


def backward(
    slots, lengths, predict, correct, att_grad, q_pairs, k_pairs, v_pairs, oT, lse, sums, up_grads,
    out_grads, ff_early, weights, states, up0, up1, hidden_grad, own_rows, collective_id,
):
    rows, _, width = states.shape
    depths, late_rows, ff_columns = up_grads.shape
    half = late_rows // 2
    columns = CHIP_COLS
    lanes_all = 3 * columns
    blocks = rows // ROWS
    tokens = k_pairs.shape[0]
    queries = q_pairs.shape[0]
    tiles = queries // TILE
    per_device = rows // BLK
    group_pairs = tokens // (2 * BLK)
    pairs = queries // (2 * BLK)
    half_tiles = group_pairs * BLK // TILE
    wide_lanes = LOCAL_HEADS * TILE

    def kernel(
        slots_ref, lengths_ref, p_ref, c_ref, g_ref, q_ref, k_ref, v_ref, oT_ref, lse_ref, sums_ref, u_ref,
        og_ref, fa_ref, w_in, s_in, up0_in, up1_in, hg_in, x_in,
        grad_ref, fa_all, fb_all, q_all, o_all, total_ref,
        w_all, s_ref, up0_ref, up1_ref, hg_ref, x_own, fa_own,
        g_pairs, kT, doT, dqT, q_stack, do_stack, p_buf, ds_buf, dk_acc, dv_acc, bias, dq_pairs, dq_rows,
        give, kept, came, xT, part, got, far, mine, q_grad, q_other, q_mine, q_far, q_sum,
        o_near, o_mine, o_far, o_sum, u_far, u_sum, all_sums,
        loads, nsend, nrecv, ksend, krecv, send, recv, ssend, srecv, zsend, zrecv, osend, orecv, usend, urecv,
        asend, arecv, fsend, frecv, gsend, grecv, bsend, brecv, psend, precv, *total_refs,
    ):
        depth, chip, core, chip_x, chip_y, chip_d = place_on_mesh()
        near = [(c, (2 * c + core, depth)) for c in (chip_x, chip_y, chip_d)]
        other = (2 * chip + 1 - core, depth)
        across = [
            (2 * chip + core, lax.rem(depth + step, depths)) for step in range(1, depths)
        ]
        peers = plane_peers(chip, core, depth, chip_x, chip_y, chip_d)
        everyone = peers + across
        signal_all(everyone)

        def slot(chip_index):
            return 2 * chip_index + core

        def load(index, source, target):
            copy = pltpu.make_async_copy(source, target, loads.at[index])
            copy.start()
            return copy

        early_load = load(0, fa_ref, fa_own)
        other_loads = [
            load(1 + i, source, target)
            for i, (source, target) in enumerate(
                (
                    (w_in, w_all), (x_in, x_own), (s_in, s_ref), (up0_in, up0_ref), (up1_in, up1_ref), (hg_in, hg_ref)
                )
            )
        ]

        def depth_sum(source_of, inbox, sends, receives):
            return [
                remote(source_of(lax.rem(depth + i + 1, depths)), inbox.at[i], sends, receives, i, device)
                for i, device in enumerate(across)
            ]

        own_to_pair_order(g_ref, g_pairs, slots_ref, pairs, per_device)
        early_load.wait()
        wait_all(everyone)
        u_copies = depth_sum(lambda z: u_ref.at[z], u_far, usend, urecv)
        near_grads = [
            remote(og_ref.at[1 + i], o_near.at[i], nsend, nrecv, i, device)
            for i, (_, device) in enumerate(near)
        ]
        a_ring = ring_sends(
            fa_own, fa_all, slot, chip, core, depth, chip_x, chip_y, asend, arecv
        )
        for copy in u_copies + near_grads + a_ring[:4]:
            copy.start()

        def shared(index, ref):
            return remote(ref, ref, psend, precv, index, other)

        in_plane = (chip, chip_x, chip_y, chip_d)
        a_shared = [shared(i, fa_all.at[slot(c)]) for i, c in enumerate(in_plane)]
        b_shared = [shared(4 + i, fb_all.at[slot(c)]) for i, c in enumerate(in_plane)]
        q_shared = [shared(8 + i, q_all.at[slot(c)]) for i, c in enumerate(in_plane)]
        o_shared = shared(12, o_all.at[core])
        fa_all[slot(chip)] = fa_own[...]
        a_shared[0].start()

        def turn_keys(i, _):
            at = aligned(i, TILE)
            kT[:, at] = k_ref[at, :].T
            return 0

        lax.fori_loop(0, tokens // TILE, turn_keys, 0)

        def attend(kind, step):
            tile = kind * (tiles // 2) + step
            key_tiles = half_tiles * (kind + 1)
            q_tile = q_ref[aligned(tile, TILE), :]
            fill_bias(bias, kind, step, slots_ref, lengths_ref, per_device, group_pairs)
            do_tile = g_pairs[aligned(tile, TILE), :]
            doT[...] = do_tile.astype(F32).T * oT_ref[tile]
            for head in range(LOCAL_HEADS):
                lanes = slice(head * TILE, (head + 1) * TILE)
                heads = slice(head * HD, (head + 1) * HD)
                mask = head_mask(TILE, head)
                q_head = jnp.where(mask, q_tile, jnp.zeros_like(q_tile))
                do_head = jnp.where(mask, do_tile, jnp.zeros_like(do_tile))
                q_stack[lanes, :] = q_head
                do_stack[lanes, :] = do_head
                delta = jnp.sum(doT[heads, :], axis=0, keepdims=True)
                norm = lse_ref[tile, head]
                total = jnp.zeros((HD, TILE), F32)
                for k_tile in range(key_tiles):
                    at = slice(k_tile * TILE, (k_tile + 1) * TILE)
                    s = lax.dot_general(k_ref[at, :], q_head, NT, preferred_element_type=F32)
                    if k_tile >= key_tiles - half_tiles:
                        s = s + bias[k_tile - (key_tiles - half_tiles), :, 0:TILE]
                    dp = lax.dot_general(v_ref[at, :], do_head, NT, preferred_element_type=F32)
                    e = jnp.exp(s - norm)
                    p_buf[at, lanes] = e.astype(BF16)
                    ds = (e * (dp - delta)).astype(BF16)
                    ds_buf[at, lanes] = ds
                    total = total + jnp.dot(kT[heads, at], ds, preferred_element_type=F32)
                dqT[heads, :] = total
            for k_tile in range(key_tiles):
                at = slice(k_tile * TILE, (k_tile + 1) * TILE)
                dv = jnp.dot(p_buf[at, :], do_stack[...], preferred_element_type=F32)
                dk = jnp.dot(ds_buf[at, :], q_stack[...], preferred_element_type=F32)
                if kind == 1:
                    fresh = step == 0
                    dv_acc[at, :] = dv + jnp.where(fresh, 0.0, dv_acc[at, :])
                    dk_acc[at, :] = dk + jnp.where(fresh, 0.0, dk_acc[at, :])
                else:
                    dv_acc[at, :] = dv + dv_acc[at, :]
                    dk_acc[at, :] = dk + dk_acc[at, :]
            dq_pairs[aligned(tile, TILE), :] = dqT[...].T.astype(BF16)

        for kind in (1, 0):

            def body(step, _, kind=kind):
                attend(kind, step)
                return 0

            lax.fori_loop(0, tiles // 2, body, 0)
            if kind == 1:
                a_ring[0].wait_recv()
                a_ring[4].start()
                a_ring[1].wait_recv()
                a_ring[5].start()

        def slot_rows(target, side, chip_index, pair_index):
            pair = chip_index * per_device + side * (per_device // 2) + pair_index
            second, _, _ = pair_places(slots_ref, pair)
            at = 2 * pair_index * BLK
            for i, acc in enumerate((dk_acc, dv_acc)):
                both = either(second, acc[aligned(pair, BLK), :], acc[aligned(group_pairs + pair, BLK), :])
                for j in range(2):
                    target[i, chip_index, at + j * BLK : at + (j + 1) * BLK, :] = both[j].astype(BF16)

        for c in range(CHIPS):
            for i in range(per_device // 2):
                slot_rows(give, 1 - core, c, i)
        swap = remote(give, came, ksend, krecv, 0, other)
        swap.start()
        for c in range(CHIPS):
            for i in range(per_device // 2):
                slot_rows(kept, core, c, i)
        own_to_slot_order(dq_pairs, dq_rows, slots_ref, pairs, per_device)

        for copy in near_grads:
            copy.wait_recv()
        whole = og_ref[0].astype(F32)
        for i in range(3):
            whole = whole + o_near[i].astype(F32)
        o_mine[...] = whole.astype(BF16)
        distance = lax.rem(chip + depths - depth, depths)
        o_copies = [
            remote(o_mine, o_far.at[i], osend, orecv, i, device) for i, device in enumerate(across)
        ]
        for i in range(depths - 1):
            pl.when(distance == i + 1)(o_copies[i].start)
        swap.wait_recv()

        def add_cores(c, _):
            for i in range(2):
                kept[i, c] = (kept[i, c].astype(F32) + came[i, c].astype(F32)).astype(BF16)
            return 0

        lax.fori_loop(0, CHIPS, add_cores, 0)
        for copy in other_loads:
            copy.wait()

        def rows_grad(c):
            return (
                lax.dot_general(
                    dq_rows[aligned(c, rows), :], w_all[0], NT, preferred_element_type=F32
                )
                + lax.dot_general(kept[0, c], w_all[1], NT, preferred_element_type=F32)
                + lax.dot_general(kept[1, c], w_all[2], NT, preferred_element_type=F32)
            )

        give_rows, relay_rows, receive_rows, sends = plane_sum(
            part, got, far, chip, core, depth, chip_x, chip_y, chip_d, send, recv
        )
        for i in (2, 0, 1):
            part[near[i][0]] = rows_grad(near[i][0]).astype(BF16)
            give_rows(i)
        mine[...] = rows_grad(chip)

        def turn(c, _):
            xT[:, aligned(c, rows)] = x_own[c].T
            return 0

        lax.fori_loop(0, CHIPS, turn, 0)

        def weight_grads(z, _):
            at = aligned(z, 2 * half)
            grads = []
            for i in range(3):
                right = dq_rows[...] if i == 0 else kept[i - 1].reshape(queries, columns)
                grads.append(jnp.dot(xT[at, :], right, preferred_element_type=F32))
            grad = jnp.concatenate(grads, axis=1).astype(BF16)
            q_grad[z, 0] = grad[:half]
            q_grad[z, 1] = grad[half:]
            return 0

        for copy in u_copies:
            copy.wait_recv()
        whole = u_ref[depth].astype(F32)
        for i in range(depths - 1):
            whole = whole + u_far[i].astype(F32)
        u_sum[...] = whole.astype(BF16)
        b_ring = ring_sends(
            u_sum, fb_all, slot, chip, core, depth, chip_x, chip_y, fsend, frecv
        )
        for copy in b_ring[:4]:
            copy.start()
        fb_all[slot(chip)] = u_sum[...]
        b_shared[0].start()

        lax.fori_loop(0, depths, weight_grads, 0)
        core_swap = remote(q_grad.at[:, 1 - core], q_other, ssend, srecv, 0, other)
        core_swap.start()
        relay_rows()
        core_swap.wait_recv()
        for i in range(depths):
            q_mine[i] = (q_grad[i, core].astype(F32) + q_other[i].astype(F32)).astype(BF16)
        q_copies = depth_sum(lambda z: q_mine.at[z], q_far, zsend, zrecv)
        for copy in q_copies:
            copy.start()
        b_ring[0].wait_recv()
        b_ring[4].start()
        b_ring[1].wait_recv()
        b_ring[5].start()
        a_ring[2].wait_recv()
        a_shared[1].start()
        a_ring[3].wait_recv()
        a_shared[2].start()
        a_ring[4].wait_recv()
        a_ring[5].wait_recv()
        a_shared[3].start()
        receive_rows()

        def state_grads(i, totals):
            at = aligned(i, ROWS)
            s0, s1 = s_ref[at, 0, :].astype(F32), s_ref[at, 1, :].astype(F32)
            a = p_ref[0, 0] * s0 + p_ref[0, 1] * s1
            weighted = mine[at, :]
            for j in range(2):
                weighted = weighted + got[j, at, :].astype(F32)
            factor = norm_factor(a)
            mean = jnp.mean(weighted * a, axis=1, keepdims=True)
            up0, up1 = up0_ref[at, :], up1_ref[at, :]
            result_grad = c_ref[0] * up0 + c_ref[1] * up1
            norm_grad = factor * weighted - a * (factor * factor * factor * mean)
            mixed0 = up0 + (hg_ref[at, :] + norm_grad - result_grad)
            grad_ref[at, 0, :] = (p_ref[0, 0] * mixed0 + p_ref[1, 0] * up1).astype(BF16)
            grad_ref[at, 1, :] = (p_ref[0, 1] * mixed0 + p_ref[1, 1] * up1).astype(BF16)
            terms = (weighted * a * factor, mixed0 * s0, mixed0 * s1, up1 * s0, up1 * s1)
            return tuple(t + jnp.sum(v, axis=0, keepdims=True) for t, v in zip(totals, terms))

        totals = lax.fori_loop(
            0, blocks, state_grads, tuple(jnp.zeros((1, width), F32) for _ in range(5))
        )
        all_sums[...] = sums_ref[...]
        all_sums[0:1, :] = totals[0]
        for i in range(4):
            all_sums[4 + i : 5 + i, :] = totals[1 + i]
        start, turn_sums, end = total_over_mesh(
            all_sums, *total_refs[:3], across, peers, *total_refs[3:]
        )
        start()
        for copy in q_copies:
            copy.wait_recv()
        whole = q_mine[depth].astype(F32)
        for i in range(depths - 1):
            whole = whole + q_far[i].astype(F32)
        q_sum[...] = whole.astype(BF16)
        q_ring = ring_sends(
            q_sum, q_all, slot, chip, core, depth, chip_x, chip_y, gsend, grecv
        )
        for copy in q_ring[:4]:
            copy.start()
        q_all[slot(chip)] = q_sum[...]
        q_shared[0].start()
        quarter = half // 2
        o_top, o_low = o_all.at[core, pl.ds(0, quarter)], o_all.at[core, pl.ds(quarter, quarter)]
        o_source_top, o_source_low = o_sum.at[pl.ds(0, quarter)], o_sum.at[pl.ds(quarter, quarter)]
        dev_x, dev_y = near[0][1], near[1][1]
        o_ring = [
            remote(o_source_top, o_top, bsend, brecv, 0, dev_x),
            remote(o_source_low, o_low, bsend, brecv, 1, dev_y),
            remote(o_source_low, o_low, bsend, brecv, 2, dev_x),
            remote(o_source_top, o_top, bsend, brecv, 3, dev_y),
            remote(o_top, o_top, bsend, brecv, 4, dev_y),
            remote(o_low, o_low, bsend, brecv, 5, dev_x),
        ]
        source, from_x, from_y = chip == depth, chip_x == depth, chip_y == depth

        @pl.when(source)
        def _():
            for copy in o_copies:
                copy.wait_recv()
            whole = o_mine[...].astype(F32)
            for i in range(depths - 1):
                whole = whole + o_far[i].astype(F32)
            o_sum[...] = whole.astype(BF16)
            for copy in o_ring[:4]:
                copy.start()
            o_all[core] = o_sum[...]

        turn_sums()
        q_ring[0].wait_recv()
        q_ring[4].start()
        q_ring[1].wait_recv()
        q_ring[5].start()

        @pl.when(from_x)
        def _():
            o_ring[0].wait_recv()
            o_ring[4].start()
            o_ring[2].wait_recv()

        @pl.when(from_y)
        def _():
            o_ring[1].wait_recv()
            o_ring[5].start()
            o_ring[3].wait_recv()

        for copies, passed in ((b_ring, b_shared), (q_ring, q_shared)):
            copies[2].wait_recv()
            passed[1].start()
            copies[3].wait_recv()
            passed[2].start()
            copies[4].wait_recv()
            copies[5].wait_recv()
            passed[3].start()

        @pl.when(chip_d == depth)
        def _():
            o_ring[4].wait_recv()
            o_ring[5].wait_recv()

        o_shared.start()
        total_ref[...] = end()
        for copy in a_shared + b_shared + q_shared + [o_shared]:
            copy.wait()
        for copy in u_copies + near_grads + [swap] + sends + [core_swap] + q_copies + a_ring + b_ring + q_ring:
            copy.wait_send()
        for i in range(depths - 1):
            pl.when(distance == i + 1)(o_copies[i].wait_send)

        @pl.when(source)
        def _():
            for copy in o_ring[:4]:
                copy.wait_send()

        pl.when(from_x)(o_ring[4].wait_send)
        pl.when(from_y)(o_ring[5].wait_send)

    vmem = pltpu.VMEM
    block = (rows, width)
    wide_rows = (CHIPS, rows, width)
    q_block, o_block = (half, lanes_all), (half, width)
    kv_half = (2, CHIPS, rows, columns)
    a_block, b_block = ff_early.shape, (late_rows, ff_columns)
    ctx = 2 * CHIPS
    return pl.pallas_call(
        kernel,
        out_shape=[
            jax.ShapeDtypeStruct((rows, 2, width), BF16),
            jax.ShapeDtypeStruct((ctx,) + a_block, BF16),
            jax.ShapeDtypeStruct((ctx,) + b_block, BF16),
            jax.ShapeDtypeStruct((ctx,) + q_block, BF16),
            jax.ShapeDtypeStruct((2,) + o_block, BF16),
            jax.ShapeDtypeStruct((8, width), F32),
        ],
        in_specs=[SM] * 4 + [VM] * 9 + [ANY] * 7,
        out_specs=[VM] * 6,
        scratch_shapes=[
            vmem((3, width, columns), BF16),
            vmem((rows, 2, width), BF16),
            vmem(block, F32),
            vmem(block, F32),
            vmem(block, F32),
            vmem(wide_rows, BF16),
            vmem(a_block, BF16),
            vmem((queries, columns), BF16),
            vmem((columns, tokens), BF16),
            vmem((columns, TILE), F32),
            vmem((columns, TILE), F32),
            vmem((wide_lanes, columns), BF16),
            vmem((wide_lanes, columns), BF16),
            vmem((tokens, wide_lanes), BF16),
            vmem((tokens, wide_lanes), BF16),
            vmem((tokens, columns), F32),
            vmem((tokens, columns), F32),
            vmem((half_tiles, TILE, TILE), F32),
            vmem((queries, columns), BF16),
            vmem((queries, columns), BF16),
            vmem(kv_half, BF16),
            vmem(kv_half, BF16),
            vmem(kv_half, BF16),
            vmem((width, queries), BF16),
            vmem(wide_rows, BF16),
            vmem((2,) + block, BF16),
            vmem((2, rows // 2, width), BF16),
            vmem(block, F32),
            vmem((depths, 2) + q_block, BF16),
            vmem((depths,) + q_block, BF16),
            vmem((depths,) + q_block, BF16),
            vmem((depths - 1,) + q_block, BF16),
            vmem(q_block, BF16),
            vmem((3,) + o_block, BF16),
            vmem(o_block, BF16),
            vmem((depths - 1,) + o_block, BF16),
            vmem(o_block, BF16),
            vmem((depths - 1,) + b_block, BF16),
            vmem(b_block, BF16),
            vmem((8, width), F32),
            DMA((7,)),
            *[DMA((3,))] * 2,
            *[DMA((1,))] * 2,
            *[DMA((6,))] * 2,
            *[DMA((1,))] * 2,
            *[DMA((depths - 1,))] * 6,
            *[DMA((6,))] * 8,
            *[DMA((13,))] * 2,
            *total_scratch((8, width), depths),
        ],
        compiler_params=comm_params(collective_id),
        name="backward",
    )(
        slots, lengths, predict, correct, att_grad, q_pairs, k_pairs, v_pairs, oT, lse, sums, up_grads,
        out_grads, ff_early, weights, states, up0, up1, hidden_grad, own_rows,
    )


def lay_out(early, late, qkv, out, sums, gain_one, gain_two):
    ctx, half, columns = early.shape
    width = out.shape[2]
    shard = 2 * half
    depths = width // shard
    split = columns // depths
    steps = 3
    strip = half // steps

    def kernel(
        d_ref, g_ref, u_ref, q_ref, o_ref, s_ref, g1_ref, g2_ref,
        dq_ref, dk_ref, dv_ref, do_ref, dg_ref, du_ref, dd_ref, g1_out, g2_out, p_out, c_out, columns_ref,
    ):
        core, step = pl.program_id(0), pl.program_id(1)
        depth = lax.axis_index("wsh")

        @pl.when((core == 0) & (step == 0))
        def _():
            one, two = g1_ref[...].astype(F32), g2_ref[...].astype(F32)
            columns_ref[0] = jnp.broadcast_to(as_column(one), (shard, 128))
            columns_ref[1] = jnp.broadcast_to(as_column(two), (shard, 128))
            for z in range(depths):

                @pl.when(depth == z)
                def _(z=z):
                    g1_out[...] = s_ref[0:1, z * shard : (z + 1) * shard] / one
                    g2_out[...] = s_ref[1:2, z * shard : (z + 1) * shard] / two

            scalars = jnp.sum(s_ref[...], axis=1, keepdims=True)
            for i in range(2):
                c_out[:, i : i + 1] = scalars[2 + i : 3 + i]
                for j in range(2):
                    at = 4 + 2 * i + j
                    p_out[i : i + 1, j : j + 1] = scalars[at : at + 1]

        rows = aligned(core * steps + step, strip)
        one, two = columns_ref[0, rows, 0:1], columns_ref[1, rows, 0:1]
        do_ref[...] = o_ref[...].astype(F32)
        for i, ref in enumerate((dq_ref, dk_ref, dv_ref)):
            wide = jnp.concatenate(
                [q_ref[p, :, i * CHIP_COLS : (i + 1) * CHIP_COLS].astype(F32) for p in range(CHIPS)], axis=1
            )
            ref[...] = wide * one
        for source, ref in ((g_ref, dg_ref), (u_ref, du_ref)):
            for z in range(depths):
                wide = jnp.concatenate(
                    [source[p, :, z * split : (z + 1) * split].astype(F32) for p in range(CHIPS)], axis=1
                )
                ref[:, z * CHIPS * split : (z + 1) * CHIPS * split] = wide * two
        dd_ref[...] = d_ref[...].astype(F32)

    early = early.reshape(CHIPS, 2, half, columns)
    late = late.reshape(CHIPS, 2, 2, half, columns)
    qkv = qkv.reshape(CHIPS, 2, half, -1)
    square = jax.ShapeDtypeStruct((shard, width), F32)
    tall = jax.ShapeDtypeStruct((shard, columns * CHIPS), F32)
    row = jax.ShapeDtypeStruct((1, shard), F32)

    def whole(shape):
        return pl.BlockSpec(shape, lambda c, r: (0,) * len(shape))

    def piece(lanes):
        return pl.BlockSpec((CHIPS, None, strip, lanes), lambda c, r: (0, c, r, 0))

    def part(i):
        return pl.BlockSpec((CHIPS, None, None, strip, columns), lambda c, r: (0, c, i, r, 0))

    def strip_of(lanes):
        return pl.BlockSpec((strip, lanes), lambda c, r: (c * steps + r, 0))

    outs = pl.pallas_call(
        kernel,
        grid=(2, steps),
        out_shape=[
            square,
            square,
            square,
            square,
            tall,
            tall,
            jax.ShapeDtypeStruct((CHIPS, 2, half, width), F32),
            row,
            row,
            jax.ShapeDtypeStruct((2, 2), F32),
            jax.ShapeDtypeStruct((1, 2), F32),
        ],
        in_specs=[
            piece(columns),
            part(0),
            part(1),
            piece(3 * CHIP_COLS),
            pl.BlockSpec((None, strip, width), lambda c, r: (c, r, 0)),
            whole((8, width)),
            whole((1, shard)),
            whole((1, shard)),
        ],
        out_specs=[
            strip_of(width),
            strip_of(width),
            strip_of(width),
            strip_of(width),
            strip_of(columns * CHIPS),
            strip_of(columns * CHIPS),
            piece(width),
            whole((1, shard)),
            whole((1, shard)),
            whole((2, 2)),
            whole((1, 2)),
        ],
        scratch_shapes=[pltpu.VMEM((2, shard, 128), F32)],
        compiler_params=pltpu.CompilerParams(vmem_limit_bytes=VMEM_LIMIT),
        name="lay_out",
    )(early, late, late, qkv, out, sums, gain_one, gain_two)
    return (*outs[:6], outs[6].reshape(ctx * half, width), *outs[7:])


def plane_shards(
    states, block_slot, cont_lengths, valid_mask, teacher, out_grad, predict, correct,
    norm_attn, w_query, w_key, w_value, w_out, norm_ffn, w_gate, w_up, w_down,
):
    slots, lengths = block_slot[0], cont_lengths[0]
    gain_one, gain_two = norm_attn[None], norm_ffn[None]
    states = states[0]
    new_states, up0, up1, hidden_grad, att_grad, out_grads, ff_early, up_grads, sums, *saved = forward(
        slots, lengths, predict, correct, states, out_grad[0], teacher[0], valid_mask, gain_one, gain_two,
        w_query, w_key, w_value, w_out, w_gate, w_up, w_down, 1,
    )
    own_rows, weights, q_pairs, k_pairs, v_pairs, oT, lse = saved
    states_grad, *gathered = backward(
        slots, lengths, predict, correct, att_grad.reshape(-1, CHIP_COLS), q_pairs, k_pairs, v_pairs, oT, lse,
        sums, up_grads, out_grads, ff_early, weights, states, up0, up1, hidden_grad, own_rows, 2,
    )
    dq, dk, dv, do, dg, du, dd, g_one, g_two, predict_grad, correct_grad = lay_out(
        *gathered, gain_one, gain_two
    )
    return (
        new_states[None], states_grad[None], predict_grad, correct_grad[0],
        g_one[0], dq, dk, dv, do, g_two[0], dg, du, dd,
    )


def fits_plane(mesh, states, block_slot, w_query, w_gate):
    ctx, depths = mesh.shape["ctx"], mesh.shape["wsh"]
    return (
        ctx == 2 * CHIPS
        and depths == CHIPS
        and states.shape[0] == depths
        and block_slot.shape[1] * BLK == 2 * PROMPT
        and states.shape[1] == 2 * PROMPT
        and w_query.shape[0] % (32 * depths) == 0
        and w_gate.shape[1] % (32 * CHIPS * depths) == 0
    )


def solution(mesh):
    in_specs = (
        P("wsh", "ctx", None, None),
        P("wsh", None),
        P("wsh", None),
        P("wsh", "ctx"),
        P("wsh", "ctx", None, None),
        P("wsh", "ctx", None, None),
        P(),
        P(),
        P("wsh"),
        P("wsh", None),
        P("wsh", None),
        P("wsh", None),
        P("wsh", None),
        P("wsh"),
        P("wsh", None),
        P("wsh", None),
        P("wsh", None),
    )
    out_specs = (
        P("wsh", "ctx", None, None),
        P("wsh", "ctx", None, None),
        P(),
        P(),
        P("wsh"),
        P("wsh", None),
        P("wsh", None),
        P("wsh", None),
        P("wsh", None),
        P("wsh"),
        P("wsh", None),
        P("wsh", None),
        P("wsh", None),
    )

    def step(*args):
        plane = fits_plane(mesh, args[0], args[1], args[9], args[14])
        body = plane_shards if plane else general_shards
        return jax.shard_map(
            body, mesh=mesh, in_specs=in_specs, out_specs=out_specs, check_vma=False
        )(*args)

    return step
```

```python
import functools
import math

import jax
import jax.numpy as jnp
from jax import lax
from jax.experimental import pallas as pl
from jax.experimental.pallas import tpu as pltpu
from jax.sharding import PartitionSpec as P

HEADS = 12
HD = 64
PROMPT = 1024
BLK = 64


EPSILON = 1e-06
NEGATIVE = -1e30
HIGHEST = lax.Precision.HIGHEST


def rms_forward(tensor, gain_vec):
    factor = lax.rsqrt(jnp.mean(tensor * tensor, axis=-1, keepdims=True) + EPSILON)
    return (tensor * factor * gain_vec, factor)


def rms_backward(tensor, factor, gain_vec, upstream):
    weighted = upstream * gain_vec
    gain_grad = jnp.sum(upstream * tensor * factor, axis=0)
    middle = jnp.mean(weighted * tensor, axis=-1, keepdims=True)
    return (factor * weighted - tensor * factor * factor * factor * middle, gain_grad)


def segment_starts(cont_lengths):
    count = cont_lengths.shape[1]
    index = jnp.arange(count, dtype=jnp.int32)
    before = index[:, None] < index[None, :]
    return PROMPT + jnp.sum(jnp.where(before[None], cont_lengths[:, :, None], 0), axis=1)


def token_places(block_slot, cont_lengths):
    groups, blocks = block_slot.shape
    offsets = jnp.arange(BLK, dtype=jnp.int32)
    places = (block_slot[:, :, None] * BLK + offsets[None, None, :]).reshape(groups, blocks * BLK)
    starts = segment_starts(cont_lengths)
    segments = jnp.sum((places[:, :, None] >= starts[:, None, :]).astype(jnp.int32), axis=2)
    return (places, segments)


def visible(query_place, query_segment, key_place, key_segment):
    earlier = key_place[:, None, :] <= query_place[:, :, None]
    shared = (key_segment[:, None, :] == 0) | (key_segment[:, None, :] == query_segment[:, :, None])
    return earlier & shared


def split_heads(tensor):
    return tensor.reshape(tensor.shape[0], tensor.shape[1], HEADS, HD)


def forward_block(running, query_part, key_part, value_part, allowed):

    def forward_compute(current):
        maximum, denominator, accumulated = current
        scores = jnp.einsum(
            "gqhd,gkhd->ghqk",
            split_heads(query_part),
            split_heads(key_part),
            preferred_element_type=jnp.float32,
        )
        masked = jnp.where(allowed[:, None], scores, NEGATIVE)
        new_max = jnp.maximum(maximum, jnp.max(masked, axis=-1))
        exponent = jnp.where(allowed[:, None], jnp.exp(masked - new_max[..., None]), 0.0)
        factor = jnp.exp(maximum - new_max)
        rescale = jnp.swapaxes(factor, 1, 2)[..., None]
        update = jnp.einsum(
            "ghqk,gkhd->gqhd",
            exponent.astype(jnp.bfloat16),
            split_heads(value_part),
            preferred_element_type=jnp.float32,
        )
        merged = (split_heads(accumulated) * rescale + update).reshape(accumulated.shape)
        return (new_max, denominator * factor + jnp.sum(exponent, axis=-1), merged)

    return lax.cond(jnp.any(allowed), forward_compute, lambda current: current, running)


def backward_block(
    query_part, grad_part, key_part, value_part, allowed, maximum, denominator, delta_sum
):
    scores = jnp.einsum(
        "gqhd,gkhd->ghqk",
        split_heads(query_part),
        split_heads(key_part),
        preferred_element_type=jnp.float32,
    )
    exponent = jnp.where(allowed[:, None], jnp.exp(scores - maximum[..., None]), 0.0)
    probability = exponent / denominator[..., None]
    prob_grad = jnp.einsum(
        "gqhd,gkhd->ghqk",
        split_heads(grad_part),
        split_heads(value_part),
        preferred_element_type=jnp.float32,
    )
    score_grad = (probability * (prob_grad - delta_sum[..., None])).astype(jnp.bfloat16)
    return (probability.astype(jnp.bfloat16), score_grad)


def general_shards(
    states,
    block_slot,
    cont_lengths,
    valid_mask,
    teacher,
    out_grad,
    predict,
    correct,
    norm_attn,
    w_query,
    w_key,
    w_value,
    w_out,
    norm_ffn,
    w_gate,
    w_up,
    w_down,
):
    groups, local_len = valid_mask.shape
    model_width = states.shape[3]
    row_count = groups * local_len
    group_len = block_slot.shape[1] * BLK
    gain_one, query_w, key_w, value_w, out_w, gain_two, gate_w, up_w, down_w = (
        lax.all_gather(norm_attn, "wsh", axis=0, tiled=True),
        lax.all_gather(w_query, "wsh", axis=0, tiled=True),
        lax.all_gather(w_key, "wsh", axis=0, tiled=True),
        lax.all_gather(w_value, "wsh", axis=0, tiled=True),
        lax.all_gather(w_out, "wsh", axis=0, tiled=True),
        lax.all_gather(norm_ffn, "wsh", axis=0, tiled=True),
        lax.all_gather(w_gate, "wsh", axis=0, tiled=True),
        lax.all_gather(w_up, "wsh", axis=0, tiled=True),
        lax.all_gather(w_down, "wsh", axis=0, tiled=True),
    )
    valid_float = valid_mask.astype(jnp.float32)
    valid_total = lax.psum(jnp.sum(valid_float), ("ctx", "wsh"))
    places, segments = token_places(block_slot, cont_lengths)
    offset = lax.axis_index("ctx") * local_len
    own_place = lax.dynamic_slice_in_dim(places, offset, local_len, 1)
    own_segment = lax.dynamic_slice_in_dim(segments, offset, local_len, 1)
    inputs = states.astype(jnp.float32)
    mixed_states = jnp.einsum("ij,gtjd->gtid", predict, inputs, precision=HIGHEST)
    active = mixed_states[:, :, 0].reshape(row_count, model_width)
    gain_first = gain_one.astype(jnp.float32)
    normed, factor_one = rms_forward(active, gain_first)
    normed_low = normed.astype(jnp.bfloat16)
    queries = (
        jnp.dot(normed_low, query_w, preferred_element_type=jnp.float32)
        .astype(jnp.bfloat16)
        .reshape(groups, local_len, model_width)
    )
    key_rows = (
        jnp.dot(normed_low, key_w, preferred_element_type=jnp.float32)
        .astype(jnp.bfloat16)
        .reshape(groups, local_len, model_width)
    )
    values = (
        jnp.dot(normed_low, value_w, preferred_element_type=jnp.float32)
        .astype(jnp.bfloat16)
        .reshape(groups, local_len, model_width)
    )
    initial = (
        jnp.full((groups, HEADS, local_len), NEGATIVE, jnp.float32),
        jnp.zeros((groups, HEADS, local_len), jnp.float32),
        jnp.zeros((groups, local_len, model_width), jnp.float32),
    )
    piece_keys = lax.all_gather(key_rows, "ctx", axis=1, tiled=True)
    piece_values = lax.all_gather(values, "ctx", axis=1, tiled=True)
    piece_len = piece_keys.shape[1]
    block_size = math.gcd(piece_len, local_len)

    def fold_one_block(current, block_index):
        begin = block_index * block_size
        key_part = lax.dynamic_slice_in_dim(piece_keys, begin, block_size, 1)
        value_part = lax.dynamic_slice_in_dim(piece_values, begin, block_size, 1)
        key_place = lax.dynamic_slice_in_dim(places, begin, block_size, 1)
        key_segment = lax.dynamic_slice_in_dim(segments, begin, block_size, 1)
        allowed = visible(own_place, own_segment, key_place, key_segment)
        return (forward_block(current, queries, key_part, value_part, allowed), None)

    finished, unused = lax.scan(
        fold_one_block, initial, jnp.arange(piece_len // block_size, dtype=jnp.int32)
    )
    maximum, denominator, accumulated = finished
    attended = (split_heads(accumulated) / jnp.swapaxes(denominator, 1, 2)[..., None]).reshape(
        row_count, model_width
    )
    attended_low = attended.astype(jnp.bfloat16)
    hidden = active + jnp.dot(attended_low, out_w, preferred_element_type=jnp.float32)
    gain_second = gain_two.astype(jnp.float32)
    normed_two, factor_two = rms_forward(hidden, gain_second)
    normed_two_low = normed_two.astype(jnp.bfloat16)
    gate_proj = jnp.dot(normed_two_low, gate_w, preferred_element_type=jnp.float32)
    up_proj = jnp.dot(normed_two_low, up_w, preferred_element_type=jnp.float32)
    inner_act, inner_pull = jax.vjp(
        lambda gate_in, up_in: jax.nn.gelu(gate_in, approximate=True) * up_in, gate_proj, up_proj
    )
    inner_low = inner_act.astype(jnp.bfloat16)
    result = hidden + jnp.dot(inner_low, down_w, preferred_element_type=jnp.float32)
    difference = (result - active).reshape(groups, local_len, 1, model_width)
    out_states = mixed_states + correct[None, None, :, None] * difference
    new_states = out_states.astype(jnp.bfloat16)
    loss_ratio = lax.axis_size("wsh") * groups * group_len / valid_total
    upstream = out_grad.astype(jnp.float32) + loss_ratio * valid_float[:, :, None, None] * (
        out_states - teacher.astype(jnp.float32)
    )
    correct_local = jnp.sum(upstream * difference, axis=(0, 1, 3))
    result_grad = jnp.einsum("i,gtid->gtd", correct, upstream, precision=HIGHEST).reshape(
        row_count, model_width
    )
    result_low = result_grad.astype(jnp.bfloat16)
    down_grad = jnp.einsum("rf,rd->fd", inner_low, result_low, preferred_element_type=jnp.float32)
    inner_grad = jnp.einsum("rd,fd->rf", result_low, down_w, preferred_element_type=jnp.float32)
    gate_grad, up_grad = inner_pull(inner_grad)
    gate_low = gate_grad.astype(jnp.bfloat16)
    up_low = up_grad.astype(jnp.bfloat16)
    gate_w_grad = jnp.einsum(
        "rd,rf->df", normed_two_low, gate_low, preferred_element_type=jnp.float32
    )
    up_w_grad = jnp.einsum("rd,rf->df", normed_two_low, up_low, preferred_element_type=jnp.float32)
    normed_two_grad = jnp.einsum(
        "rf,df->rd", gate_low, gate_w, preferred_element_type=jnp.float32
    ) + jnp.einsum("rf,df->rd", up_low, up_w, preferred_element_type=jnp.float32)
    hidden_norm_grad, gain_two_grad = rms_backward(hidden, factor_two, gain_second, normed_two_grad)
    hidden_grad = result_grad + hidden_norm_grad
    hidden_low = hidden_grad.astype(jnp.bfloat16)
    out_w_grad = jnp.einsum(
        "rc,rd->cd", attended_low, hidden_low, preferred_element_type=jnp.float32
    )
    attended_grad = jnp.einsum(
        "rd,cd->rc", hidden_low, out_w, preferred_element_type=jnp.float32
    ).astype(jnp.bfloat16)
    delta_sum = jnp.swapaxes(
        jnp.sum(
            split_heads(
                (attended_grad.astype(jnp.float32) * attended).reshape(
                    groups, local_len, model_width
                )
            ),
            axis=-1,
        ),
        1,
        2,
    )
    grad_local = attended_grad.reshape(groups, local_len, model_width)
    zero_grad = jnp.zeros((groups, local_len, model_width), jnp.float32)
    all_keys, all_values = (
        lax.all_gather(key_rows, "ctx", axis=1, tiled=True),
        lax.all_gather(values, "ctx", axis=1, tiled=True),
    )

    def query_step(current, block_index):
        begin = block_index * local_len
        key_part = lax.dynamic_slice_in_dim(all_keys, begin, local_len, 1)
        value_part = lax.dynamic_slice_in_dim(all_values, begin, local_len, 1)
        key_place = lax.dynamic_slice_in_dim(places, begin, local_len, 1)
        key_segment = lax.dynamic_slice_in_dim(segments, begin, local_len, 1)
        allowed = visible(own_place, own_segment, key_place, key_segment)

        def query_compute(query_sum):
            prob_low, score_grad = backward_block(
                queries, grad_local, key_part, value_part, allowed, maximum, denominator, delta_sum
            )
            return query_sum + jnp.einsum(
                "ghqk,gkhd->gqhd",
                score_grad,
                split_heads(key_part),
                preferred_element_type=jnp.float32,
            ).reshape(groups, local_len, model_width)

        return (
            lax.cond(jnp.any(allowed), query_compute, lambda query_sum: query_sum, current),
            None,
        )

    finished, unused = lax.scan(
        query_step, zero_grad, jnp.arange(group_len // local_len, dtype=jnp.int32)
    )
    term_rows = local_len * lax.axis_size("ctx")
    key_block_size = math.gcd(term_rows, local_len)

    def key_one_block(block_index):
        begin = block_index * key_block_size
        key_part = lax.dynamic_slice_in_dim(all_keys, begin, key_block_size, 1)
        value_part = lax.dynamic_slice_in_dim(all_values, begin, key_block_size, 1)
        key_place = lax.dynamic_slice_in_dim(places, begin, key_block_size, 1)
        key_segment = lax.dynamic_slice_in_dim(segments, begin, key_block_size, 1)
        allowed = visible(own_place, own_segment, key_place, key_segment)

        def one_compute(unused_arg):
            prob_low, score_grad = backward_block(
                queries, grad_local, key_part, value_part, allowed, maximum, denominator, delta_sum
            )
            key_add = jnp.einsum(
                "ghqk,gqhd->kghd",
                score_grad,
                split_heads(queries),
                preferred_element_type=jnp.float32,
            ).reshape(key_block_size, groups, model_width)
            value_add = jnp.einsum(
                "ghqk,gqhd->kghd",
                prob_low,
                split_heads(grad_local),
                preferred_element_type=jnp.float32,
            ).reshape(key_block_size, groups, model_width)
            return jnp.stack([key_add, value_add], axis=1)

        return lax.cond(
            jnp.any(allowed),
            one_compute,
            lambda unused_arg: jnp.zeros((key_block_size, 2, groups, model_width), jnp.float32),
            0,
        )

    summed = lax.psum_scatter(
        lax.map(key_one_block, jnp.arange(term_rows // key_block_size, dtype=jnp.int32))
        .reshape(term_rows, 2, groups, model_width)
        .astype(jnp.bfloat16),
        "ctx",
        scatter_dimension=0,
        tiled=True,
    ).astype(jnp.float32)
    key_grad = jnp.swapaxes(summed[:, 0], 0, 1)
    value_grad = jnp.swapaxes(summed[:, 1], 0, 1)
    query_low = finished.reshape(row_count, model_width).astype(jnp.bfloat16)
    key_low = key_grad.reshape(row_count, model_width).astype(jnp.bfloat16)
    value_low = value_grad.reshape(row_count, model_width).astype(jnp.bfloat16)
    query_w_grad = jnp.einsum(
        "rc,rd->cd", normed_low, query_low, preferred_element_type=jnp.float32
    )
    key_w_grad = jnp.einsum("rc,rd->cd", normed_low, key_low, preferred_element_type=jnp.float32)
    value_w_grad = jnp.einsum(
        "rc,rd->cd", normed_low, value_low, preferred_element_type=jnp.float32
    )
    normed_grad = (
        jnp.einsum("rd,cd->rc", query_low, query_w, preferred_element_type=jnp.float32)
        + jnp.einsum("rd,cd->rc", key_low, key_w, preferred_element_type=jnp.float32)
        + jnp.einsum("rd,cd->rc", value_low, value_w, preferred_element_type=jnp.float32)
    )
    active_norm_grad, gain_one_grad = rms_backward(active, factor_one, gain_first, normed_grad)
    active_grad = (hidden_grad + active_norm_grad - result_grad).reshape(
        groups, local_len, 1, model_width
    )
    mixed_grad = jnp.concatenate([upstream[:, :, :1] + active_grad, upstream[:, :, 1:]], axis=2)
    predict_local = jnp.einsum("gtid,gtjd->ij", mixed_grad, inputs, precision=HIGHEST)
    states_grad = jnp.einsum("ij,gtid->gtjd", predict, mixed_grad, precision=HIGHEST).astype(
        jnp.bfloat16
    )
    predict_grad, correct_grad = lax.psum((predict_local, correct_local), ("ctx", "wsh"))
    (
        gain_one_rows,
        query_rows,
        key_grad_rows,
        value_rows,
        out_rows,
        gain_two_rows,
        gate_rows,
        up_rows,
        down_rows,
    ) = (
        lax.psum_scatter(
            gain_one_grad.astype(jnp.bfloat16), "wsh", scatter_dimension=0, tiled=True
        ).astype(jnp.float32),
        lax.psum_scatter(
            query_w_grad.astype(jnp.bfloat16), "wsh", scatter_dimension=0, tiled=True
        ).astype(jnp.float32),
        lax.psum_scatter(
            key_w_grad.astype(jnp.bfloat16), "wsh", scatter_dimension=0, tiled=True
        ).astype(jnp.float32),
        lax.psum_scatter(
            value_w_grad.astype(jnp.bfloat16), "wsh", scatter_dimension=0, tiled=True
        ).astype(jnp.float32),
        lax.psum_scatter(
            out_w_grad.astype(jnp.bfloat16), "wsh", scatter_dimension=0, tiled=True
        ).astype(jnp.float32),
        lax.psum_scatter(
            gain_two_grad.astype(jnp.bfloat16), "wsh", scatter_dimension=0, tiled=True
        ).astype(jnp.float32),
        lax.psum_scatter(
            gate_w_grad.astype(jnp.bfloat16), "wsh", scatter_dimension=0, tiled=True
        ).astype(jnp.float32),
        lax.psum_scatter(
            up_w_grad.astype(jnp.bfloat16), "wsh", scatter_dimension=0, tiled=True
        ).astype(jnp.float32),
        lax.psum_scatter(
            down_grad.astype(jnp.bfloat16), "wsh", scatter_dimension=0, tiled=True
        ).astype(jnp.float32),
    )
    totals = (
        lax.psum(gain_one_rows.astype(jnp.bfloat16), "ctx").astype(jnp.float32),
        lax.psum(query_rows.astype(jnp.bfloat16), "ctx").astype(jnp.float32),
        lax.psum(key_grad_rows.astype(jnp.bfloat16), "ctx").astype(jnp.float32),
        lax.psum(value_rows.astype(jnp.bfloat16), "ctx").astype(jnp.float32),
        lax.psum(out_rows.astype(jnp.bfloat16), "ctx").astype(jnp.float32),
        lax.psum(gain_two_rows.astype(jnp.bfloat16), "ctx").astype(jnp.float32),
        lax.psum(gate_rows.astype(jnp.bfloat16), "ctx").astype(jnp.float32),
        lax.psum(up_rows.astype(jnp.bfloat16), "ctx").astype(jnp.float32),
        lax.psum(down_rows.astype(jnp.bfloat16), "ctx").astype(jnp.float32),
    )
    return (new_states, states_grad, predict_grad, correct_grad) + tuple(totals)


MESH = pl.DeviceIdType.MESH
F32 = jnp.float32
BF16 = jnp.bfloat16
CHIPS = 4
VMEM_LIMIT = 60 * 2**20
DMA = pltpu.SemaphoreType.DMA


def place_on_mesh():
    ctx = lax.axis_index("ctx")
    depth = lax.axis_index("wsh")
    chip = ctx // 2
    core = ctx % 2
    chip_x = chip + 1 - 2 * (chip % 2)
    chip_y = chip + 2 - 4 * (chip // 2)
    return depth, chip, core, chip_x, chip_y, 3 - chip


def signal_all(devices):
    barrier = pltpu.get_barrier_semaphore()
    for device in devices:
        pl.semaphore_signal(barrier, inc=1, device_id=device, device_id_type=MESH)


def wait_all(devices):
    pl.semaphore_wait(pltpu.get_barrier_semaphore(), len(devices))


def remote(src, dst, send, recv, index, device):
    return pltpu.make_async_remote_copy(
        src_ref=src,
        dst_ref=dst,
        send_sem=send.at[index],
        recv_sem=recv.at[index],
        device_id=device,
        device_id_type=MESH,
    )


def comm_params(collective_id):
    return pltpu.CompilerParams(
        collective_id=collective_id, has_side_effects=True, vmem_limit_bytes=VMEM_LIMIT
    )


ANY = pl.BlockSpec(memory_space=pl.ANY)
VM = pl.BlockSpec(memory_space=pltpu.VMEM)
SM = pl.BlockSpec(memory_space=pltpu.SMEM)


def ring_sends(own, out, slot_of, chip, core, depth, chip_x, chip_y, send, recv):
    half = own.shape[0] // 2
    top, low = pl.ds(0, half), pl.ds(half, half)
    dev_x, dev_y = (2 * chip_x + core, depth), (2 * chip_y + core, depth)
    here = slot_of(chip)
    return [
        remote(own.at[top], out.at[here, top], send, recv, 0, dev_x),
        remote(own.at[low], out.at[here, low], send, recv, 1, dev_y),
        remote(own.at[low], out.at[here, low], send, recv, 2, dev_x),
        remote(own.at[top], out.at[here, top], send, recv, 3, dev_y),
        remote(out.at[slot_of(chip_x), top], out.at[slot_of(chip_x), top], send, recv, 4, dev_y),
        remote(out.at[slot_of(chip_y), low], out.at[slot_of(chip_y), low], send, recv, 5, dev_x),
    ]


NT = (((1,), (1,)), ((), ()))
TN = (((0,), (0,)), ((), ()))
TILE = 256
ROWS = 32
LOCAL_HEADS = HEADS // CHIPS
CHIP_COLS = LOCAL_HEADS * HD


def head_mask(rows, head):
    lane = lax.broadcasted_iota(jnp.int32, (rows, CHIP_COLS), 1)
    return (lane >= head * HD) & (lane < (head + 1) * HD)


def aligned(index, size):
    return pl.ds(pl.multiple_of(index * size, size), size)


def norm_factor(rows):
    return lax.rsqrt(jnp.mean(rows * rows, axis=1, keepdims=True) + EPSILON)


def as_column(row):
    return jnp.broadcast_to(row, (8, row.shape[1])).T[:, 0:1]


def mix(states_ref, at, p_ref, i):
    return p_ref[i, 0] * states_ref[at, 0, :].astype(F32) + p_ref[i, 1] * states_ref[at, 1, :].astype(F32)


def plane_sum(parts, near_in, far_in, chip, core, depth, chip_x, chip_y, chip_d, send, recv):
    half = parts.shape[1] // 2
    top, low = pl.ds(0, half), pl.ds(half, half)
    dev_x, dev_y = (2 * chip_x + core, depth), (2 * chip_y + core, depth)
    copies = [
        remote(parts.at[chip_d, top], far_in.at[0], send, recv, 0, dev_x),
        remote(parts.at[chip_d, low], far_in.at[1], send, recv, 1, dev_y),
        remote(parts.at[chip_x, top], near_in.at[0, top], send, recv, 2, dev_x),
        remote(parts.at[chip_y, low], near_in.at[1, low], send, recv, 3, dev_y),
        remote(parts.at[chip_y, top], near_in.at[1, top], send, recv, 4, dev_y),
        remote(parts.at[chip_x, low], near_in.at[0, low], send, recv, 5, dev_x),
    ]

    def give(i):
        for copy in (copies[:2] if i == 2 else copies[2 + i : 3 + i]):
            copy.start()

    def relay():
        for i, (c, rows) in enumerate(((chip_y, slice(0, half)), (chip_x, slice(half, 2 * half)))):
            copies[i].wait_recv()
            parts[c, rows] = (parts[c, rows].astype(F32) + far_in[i].astype(F32)).astype(BF16)
            copies[4 + i].start()

    def receive():
        for copy in copies[2:]:
            copy.wait_recv()

    return give, relay, receive, copies


def plane_peers(chip, core, depth, chip_x, chip_y, chip_d):
    same = [(2 * c + core, depth) for c in (chip_x, chip_y, chip_d)]
    return same + [(2 * c + 1 - core, depth) for c in (chip, chip_x, chip_y, chip_d)]


def total_over_mesh(own_ref, arrived, staged, far, across, peers, bsend, brecv, csend, crecv):
    first = [remote(own_ref, arrived.at[i], bsend, brecv, i, d) for i, d in enumerate(across)]
    second = [remote(staged, far.at[i], csend, crecv, i, d) for i, d in enumerate(peers)]

    def start():
        for copy in first:
            copy.start()

    def turn():
        total = own_ref[...]
        for i, copy in enumerate(first):
            copy.wait_recv()
        for i in range(len(first)):
            total = total + arrived[i]
        staged[...] = total
        for copy in second:
            copy.start()

    def end():
        for copy in second:
            copy.wait_recv()
        total = staged[...]
        for i in range(len(second)):
            total = total + far[i]
        for copy in first + second:
            copy.wait_send()
        return total

    return start, turn, end


def total_scratch(shape, depths):
    return [
        pltpu.VMEM((depths - 1,) + shape, F32),
        pltpu.VMEM(shape, F32),
        pltpu.VMEM((2 * CHIPS - 1,) + shape, F32),
        DMA((depths - 1,)),
        DMA((depths - 1,)),
        DMA((2 * CHIPS - 1,)),
        DMA((2 * CHIPS - 1,)),
    ]


def gelu_parts(v):
    scale = math.sqrt(2 / math.pi)
    square = v * v
    t = jnp.tanh(scale * v * (1.0 + 0.044715 * square))
    rise = 0.5 * (1.0 + t)
    return v * rise, rise + 0.5 * v * (1.0 - t * t) * scale * (1.0 + 0.134145 * square)


def pair_places(slots_ref, pair):
    one, two = slots_ref[2 * pair], slots_ref[2 * pair + 1]
    second = (one >= PROMPT // BLK).astype(jnp.int32)
    return second, jnp.minimum(one, two), jnp.maximum(one, two)


def own_pair(pair, per_device):
    core = lax.axis_index("ctx") % 2
    pairs = per_device // 2
    return (pair // pairs) * per_device + core * pairs + pair % pairs


PER_TILE = TILE // BLK


def fill_bias(bias, kind, tile_step, slots_ref, lengths_ref, per_device, group_pairs):
    lane = lax.broadcasted_iota(jnp.int32, (1, TILE), 1)
    high = jnp.zeros((1, TILE), jnp.int32)
    for i in range(PER_TILE):
        _, prompt, cont = pair_places(slots_ref, own_pair(tile_step * PER_TILE + i, per_device))
        block = prompt if kind == 0 else cont
        high = jnp.where(lane >= i * BLK, (block - i) * BLK + lane, high)
    low = jnp.zeros((1, TILE), jnp.int32)
    if kind == 1:
        start = PROMPT
        for i in range(lengths_ref.shape[0]):
            low = jnp.where(high >= start, start, low)
            start = start + lengths_ref[i]
    offset = lax.broadcasted_iota(jnp.int32, (BLK, TILE), 0)

    def one_block(pair, _):
        _, prompt, cont = pair_places(slots_ref, pair)
        base = (prompt if kind == 0 else cont) * BLK
        seen = offset <= high - base
        if kind == 1:
            seen = seen & (offset >= low - base)
        bias[pair // PER_TILE, aligned(pair % PER_TILE, BLK), 0:TILE] = jnp.where(seen, 0.0, NEGATIVE)
        return 0

    lax.fori_loop(0, group_pairs, one_block, 0)


def either(second, one, two):
    swap = second == 1
    return jnp.where(swap, two, one), jnp.where(swap, one, two)


def to_pair_order(source, target, slots_ref, group_pairs):
    def one_pair(pair, _):
        second, _, _ = pair_places(slots_ref, pair)
        first, last = either(second, source[aligned(2 * pair, BLK), :], source[aligned(2 * pair + 1, BLK), :])
        target[aligned(pair, BLK), :] = first
        target[aligned(group_pairs + pair, BLK), :] = last
        return 0

    lax.fori_loop(0, group_pairs, one_pair, 0)


def own_to_pair_order(source, target, slots_ref, pairs, per_device):
    def one_pair(pair, _):
        second, _, _ = pair_places(slots_ref, own_pair(pair, per_device))
        first, last = either(second, source[aligned(2 * pair, BLK), :], source[aligned(2 * pair + 1, BLK), :])
        target[aligned(pair, BLK), :] = first
        target[aligned(pairs + pair, BLK), :] = last
        return 0

    lax.fori_loop(0, pairs, one_pair, 0)


def own_to_slot_order(source, target, slots_ref, pairs, per_device):
    def one_pair(pair, _):
        second, _, _ = pair_places(slots_ref, own_pair(pair, per_device))
        first, last = either(second, source[aligned(pair, BLK), :], source[aligned(pairs + pair, BLK), :])
        target[aligned(2 * pair, BLK), :] = first
        target[aligned(2 * pair + 1, BLK), :] = last
        return 0

    lax.fori_loop(0, pairs, one_pair, 0)


def line_reduce(pieces, acc, up_in, down_in, up_out, down_out, sems):
    depth, chip, core, _, _, _ = place_on_mesh()
    depths = pieces.shape[0]
    last = depths - 1
    up_send, up_recv, down_send, down_recv = sems
    above = (2 * chip + core, lax.rem(depth + 1, depths))
    below = (2 * chip + core, lax.rem(depth + last, depths))

    def up(source, k):
        return remote(source, up_in.at[k], up_send, up_recv, k, above)

    def down(source, k):
        return remote(source, down_in.at[k], down_send, down_recv, k, below)

    def start():
        @pl.when(depth == 0)
        def _():
            for k in range(last):
                up(pieces.at[last - k], k).start()

        @pl.when(depth == last)
        def _():
            for k in range(last):
                down(pieces.at[k], k).start()

    def hop(k):
        @pl.when((depth >= 1) & (depth <= k))
        def _():
            up(up_in.at[k - 1], k - 1).wait_recv()
            mine = pieces[jnp.clip(depth + last - k, 0, last)]
            up_out[k - 1] = (mine.astype(F32) + up_in[k - 1].astype(F32)).astype(BF16)
            up(up_out.at[k - 1], k).start()

        @pl.when((depth <= last - 1) & (depth >= last - k))
        def _():
            down(down_in.at[k - 1], k - 1).wait_recv()
            mine = pieces[jnp.clip(depth + k - last, 0, last)]
            down_out[k - 1] = (mine.astype(F32) + down_in[k - 1].astype(F32)).astype(BF16)
            down(down_out.at[k - 1], k).start()

    def result():
        acc[...] = pieces[depth].astype(F32)

        @pl.when(depth >= 1)
        def _():
            up(up_in.at[last - 1], last - 1).wait_recv()
            acc[...] += up_in[last - 1].astype(F32)

        @pl.when(depth <= last - 1)
        def _():
            down(down_in.at[last - 1], last - 1).wait_recv()
            acc[...] += down_in[last - 1].astype(F32)

    def finish():
        @pl.when(depth == 0)
        def _():
            for k in range(last):
                up(pieces.at[last - k], k).wait_send()

        @pl.when(depth == last)
        def _():
            for k in range(last):
                down(pieces.at[k], k).wait_send()

        for k in range(1, last):

            @pl.when((depth >= 1) & (depth <= k))
            def _(k=k):
                up(up_out.at[k - 1], k).wait_send()

            @pl.when((depth <= last - 1) & (depth >= last - k))
            def _(k=k):
                down(down_out.at[k - 1], k).wait_send()

    return start, hop, result, finish


def forward(
    slots, lengths, predict, correct, states, out_grad, teacher, valid, gain_one, gain_two,
    w_query, w_key, w_value, w_out, w_gate, w_up, w_down, collective_id,
):
    rows, _, width = states.shape
    shard = w_query.shape[0]
    half = shard // 2
    depths = width // shard
    hidden_cols = w_gate.shape[1]
    columns = hidden_cols // CHIPS
    split = columns // depths
    out_rows = shard // CHIPS
    blocks = rows // ROWS
    col_tiles = columns // TILE
    tokens = 2 * CHIPS * rows
    queries = CHIPS * rows
    tiles = queries // TILE
    per_device = rows // BLK
    group_pairs = tokens // (2 * BLK)
    pairs = queries // (2 * BLK)
    mesh_tokens = tokens * depths
    piece_lanes = 3 * CHIP_COLS

    def kernel(
        slots_ref, lengths_ref, p_ref, c_ref, s_ref, g_ref, t_ref, v_ref, g1_ref, g2_ref,
        wq_ref, wk_ref, wv_ref, wo_ref, wg_ref, wu_ref, wd_ref,
        new_out, up0_out, up1_out, hg_out, da_ref, dwo_ref, ffa_ref, ffb_ref, sums_ref,
        x_out, w_out_ref, q_out, k_out, v_out, oT_out, lse_ref,
        new_ref, up0_ref, up1_ref, hg_ref, all_rows, w_all, q_pairs, k_pairs, v_pairs, oT_ref, dwo, dwo_other,
        w_ff, w_wo, qkv, att_all, packs, packed_in, packed_grad, hidden, own, x_rows, r_rows, xT, innerT, inner, gate, up, gate_low, up_low,
        own_weight, part1, part2, got1, got2, far1, far2, dw, dw_other, a_up, a_down, buf, wide, count, q_slot, k_slot, v_slot, vT,
        lsend, fsend, frecv, fosend, forecv, qsend, qrecv, qosend, qorecv,
        osend, orecv, oosend, oorecv, opsend, oprecv,
        rsend, rrecv, rosend, rorecv, send0, recv0, send1, recv1, send2, recv2, send3, recv3,
        ag1s, ag1r, ag2s, ag2r, dsend, drecv, osems, xsems, *rest,
    ):
        a_sems, total_refs = rest[:4], rest[4:]
        stores = []

        def store(index, source, target):
            copy = pltpu.make_async_copy(source, target, osems.at[index])
            copy.start()
            stores.append(copy)

        depth, chip, core, chip_x, chip_y, chip_d = place_on_mesh()
        near = [(c, (2 * c + core, depth)) for c in (chip_x, chip_y, chip_d)]
        other = (2 * chip + 1 - core, depth)
        across = [
            (2 * chip + core, lax.rem(depth + step, depths)) for step in range(1, depths)
        ]
        peers = plane_peers(chip, core, depth, chip_x, chip_y, chip_d)
        signal_all(peers + across)

        mine = pl.ds(core * half, half)
        loads = [
            pltpu.make_async_copy(w.at[mine], buf.at[i], lsend.at[i])
            for i, w in enumerate((wq_ref, wk_ref, wv_ref))
        ] + [
            pltpu.make_async_copy(wg_ref.at[mine], wide.at[0], lsend.at[3]),
            pltpu.make_async_copy(wu_ref.at[mine], wide.at[1], lsend.at[4]),
            pltpu.make_async_copy(
                wd_ref.at[pl.ds(chip * split + core * half, half)], w_ff.at[2, depth, core], lsend.at[5]
            ),
            pltpu.make_async_copy(
                wo_ref.at[pl.ds(chip * out_rows, out_rows)], w_wo.at[depth, chip], lsend.at[6]
            ),
        ]
        for copy in loads:
            copy.start()
        count[...] = jnp.broadcast_to(
            jnp.sum(v_ref[...].astype(F32), axis=1, keepdims=True), count.shape
        )

        def input_norm(i, _):
            at = aligned(i, ROWS)
            active = mix(s_ref, at, p_ref, 0)
            own[0, at, :] = (active * norm_factor(active)).astype(BF16)
            return 0

        lax.fori_loop(0, blocks, input_norm, 0)

        def gain_column(ref):
            both = jnp.broadcast_to(ref[...].astype(F32).reshape(1, shard), (8, shard)).T
            return jnp.where(core == 0, both[:half, 0:1], both[half:, 0:1])

        one, two = gain_column(g1_ref), gain_column(g2_ref)
        wait_all(peers + across)

        def slot(chip_index):
            return 2 * chip_index + core

        start_count, turn_count, end_count = total_over_mesh(
            count, *total_refs[:3], across, peers, *total_refs[3:]
        )
        start_count()
        ring0 = ring_sends(
            own.at[0], all_rows, slot, chip, core, depth, chip_x, chip_y, rsend, rrecv
        )
        for copy in ring0[:4]:
            copy.start()

        def rows_to_other(index, chip_index):
            ref = all_rows.at[slot(chip_index)]
            return remote(own.at[0] if index == 0 else ref, ref, rosend, rorecv, index, other)

        shared0 = [rows_to_other(i, c) for i, c in enumerate((chip, chip_x, chip_y, chip_d))]
        shared0[0].start()
        all_rows[slot(chip)] = own[0]

        for copy in loads[:3]:
            copy.wait()
        for p in range(CHIPS):

            @pl.when(chip == p)
            def _(p=p):
                cols = jnp.concatenate(
                    [buf[i, :, p * CHIP_COLS : (p + 1) * CHIP_COLS].astype(F32) for i in range(3)], axis=1
                )
                qkv[depth, core] = (cols * one).astype(BF16)

        qkv_mine = qkv.at[depth, core]
        q_copies = [
            remote(qkv_mine, qkv_mine, qsend, qrecv, i, device) for i, device in enumerate(across)
        ]
        q_shared = [remote(qkv_mine, qkv_mine, qosend, qorecv, 0, other)]
        for copy in q_copies + q_shared:
            copy.start()

        loads[6].wait()
        o_copies = [
            remote(w_wo.at[depth, chip], w_wo.at[depth, chip], osend, orecv, i, device)
            for i, device in enumerate(across)
        ]
        o_shared = []
        for i in range(depths - 1):
            came = w_wo.at[lax.rem(depth + depths - 1 - i, depths), chip]
            o_shared.append(remote(came, came, oosend, oorecv, i, other))

        def carried(i, act):
            pl.when(core == (i + 1) % 2)(act)

        def not_carried(i, act):
            pl.when(core != (i + 1) % 2)(act)

        for i in range(depths - 1):
            carried(i, o_copies[i].start)

        for copy in loads[3:6]:
            copy.wait()
        for p in range(CHIPS):

            @pl.when(chip == p)
            def _(p=p):
                for i in range(2):
                    cols = jnp.concatenate(
                        [
                            wide[i, :, (z * CHIPS + p) * split : (z * CHIPS + p + 1) * split].astype(F32)
                            for z in range(depths)
                        ],
                        axis=1,
                    )
                    w_ff[i, depth, core] = (cols * two).astype(BF16)

        line_up = (2 * chip + core, lax.rem(depth + 1, depths))
        line_down = (2 * chip + core, lax.rem(depth + depths - 1, depths))
        hops = []
        for stage in range(1, depths):
            for direction, device, index in ((1, line_up, stage - 1), (-1, line_down, depths + stage - 2)):
                goes = jnp.clip(depth - direction * (stage - 1), 0, depths - 1)
                comes = jnp.clip(depth - direction * stage, 0, depths - 1)
                piece, came = w_ff.at[:, goes, core], w_ff.at[:, comes, core]
                if direction == 1:
                    sends, receives = (depth >= stage - 1) & (depth < depths - 1), depth >= stage
                else:
                    sends, receives = (depth <= depths - stage) & (depth > 0), depth < depths - stage
                hops.append(
                    (
                        stage,
                        sends,
                        receives,
                        remote(piece, piece, fsend, frecv, index, device),
                        remote(came, came, fosend, forecv, index, other),
                    )
                )
        ff_mine = remote(w_ff.at[:, depth, core], w_ff.at[:, depth, core], fosend, forecv, 2 * depths - 2, other)
        ff_mine.start()

        def send_hop(stage):
            for at, sends, _, hop, _ in hops:
                if at == stage:
                    pl.when(sends)(hop.start)

        def take_hop(stage):
            for at, _, receives, hop, share in hops:
                if at == stage:

                    @pl.when(receives)
                    def _(hop=hop, share=share):
                        hop.wait_recv()
                        share.start()

        send_hop(1)
        turn_count()
        ring0[0].wait_recv()
        ring0[4].start()
        ring0[1].wait_recv()
        ring0[5].start()
        for i in range(depths - 1):
            q_copies[i].wait_recv()
            came = qkv.at[lax.rem(depth + depths - 1 - i, depths), core]
            share = remote(came, came, qosend, qorecv, 1 + i, other)
            share.start()
            q_shared.append(share)
        ring0[2].wait_recv()
        shared0[1].start()
        ring0[3].wait_recv()
        shared0[2].start()
        for copy in q_shared:
            copy.wait_recv()
        for i in range(3):
            for z in range(depths):
                for c in range(2):
                    at = (z * 2 + c) * half
                    w_all[i, at : at + half, :] = qkv[z, c, :, i * CHIP_COLS : (i + 1) * CHIP_COLS]

        def project(device_slot, with_queries):
            x = all_rows[device_slot]
            at = aligned(device_slot, rows)
            k_slot[at, :] = jnp.dot(x, w_all[1], preferred_element_type=F32).astype(BF16)
            v_slot[at, :] = jnp.dot(x, w_all[2], preferred_element_type=F32).astype(BF16)
            if with_queries:
                q_slot[aligned(device_slot // 2, rows), :] = jnp.dot(
                    x, w_all[0], preferred_element_type=F32
                ).astype(BF16)

        for c in (chip, chip_x, chip_y):
            project(slot(c), True)
        for i, c in enumerate((chip, chip_x, chip_y)):
            shared0[i].wait_recv()
            project(2 * c + 1 - core, False)
        ring0[4].wait_recv()
        ring0[5].wait_recv()
        shared0[3].start()
        project(slot(chip_d), True)
        for i in range(depths - 1):

            def came_here(i=i):
                o_copies[i].wait_recv()
                o_shared[i].start()

            carried(i, came_here)
        for i in range(depths - 1):
            not_carried(i, o_shared[i].wait_recv)
        carry = pl.ds(core * (depths // 2), depths // 2)
        o_plane = [
            remote(w_wo.at[carry, chip], w_wo.at[carry, chip], opsend, oprecv, i, device)
            for i, (_, device) in enumerate(near)
        ]
        for copy in o_plane:
            copy.start()
        o_across = [
            remote(w_wo.at[carry, c], w_wo.at[carry, c], opsend, oprecv, 3 + i, other)
            for i, (c, _) in enumerate(near)
        ]
        shared0[3].wait_recv()
        project(2 * chip_d + 1 - core, False)

        for i in range(CHIPS):
            x_copy = pltpu.make_async_copy(all_rows.at[2 * i + core], x_out.at[i], xsems.at[i])
            x_copy.start()
            stores.append(x_copy)
        store(0, w_all, w_out_ref)

        to_pair_order(k_slot, k_pairs, slots_ref, group_pairs)
        to_pair_order(v_slot, v_pairs, slots_ref, group_pairs)
        own_to_pair_order(q_slot, q_pairs, slots_ref, pairs, per_device)

        store(1, q_pairs, q_out)
        store(2, k_pairs, k_out)
        store(3, v_pairs, v_out)

        def turn_values(i, _):
            vT[:, aligned(i, TILE)] = v_pairs[aligned(i, TILE), :].T
            return 0

        lax.fori_loop(0, tokens // TILE, turn_values, 0)
        half_keys = group_pairs * BLK
        half_tiles = half_keys // TILE
        scores, bias = gate, up

        def cell(k_tile):
            lanes = (k_tile // CHIPS) * TILE
            return k_tile % CHIPS, slice(lanes, lanes + TILE)

        def attend(kind, step):
            tile = kind * (tiles // 2) + step
            key_tiles = half_tiles * (kind + 1)
            q = q_pairs[aligned(tile, TILE), :]
            fill_bias(bias, kind, step, slots_ref, lengths_ref, per_device, group_pairs)
            for head in range(LOCAL_HEADS):
                heads = slice(head * HD, (head + 1) * HD)
                q_head = jnp.where(head_mask(TILE, head), q, jnp.zeros_like(q))
                top = jnp.full((1, TILE), NEGATIVE, F32)
                for k_tile in range(key_tiles):
                    s = lax.dot_general(
                        k_pairs[k_tile * TILE : (k_tile + 1) * TILE, :], q_head, NT, preferred_element_type=F32
                    )
                    if k_tile >= key_tiles - half_tiles:
                        s = s + bias[k_tile - (key_tiles - half_tiles), :, 0:TILE]
                    index, lanes = cell(k_tile)
                    scores[index, :, lanes] = s
                    top = jnp.maximum(top, jnp.max(s, axis=0, keepdims=True))
                total = jnp.zeros((1, TILE), F32)
                out = jnp.zeros((HD, TILE), F32)
                for k_tile in range(key_tiles):
                    index, lanes = cell(k_tile)
                    e = jnp.exp(scores[index, :, lanes] - top)
                    total = total + jnp.sum(e, axis=0, keepdims=True)
                    out = out + jnp.dot(
                        vT[heads, k_tile * TILE : (k_tile + 1) * TILE], e.astype(BF16), preferred_element_type=F32
                    )
                oT_ref[tile, heads, :] = out / total
                lse_ref[tile, head] = top + jnp.log(total)
            q_slot[aligned(tile, TILE), :] = oT_ref[tile].T.astype(BF16)

        def both_steps(kind):
            def body(step, _):
                attend(kind, step)
                return 0

            lax.fori_loop(0, tiles // 2, body, 0)

        both_steps(1)
        take_hop(1)
        send_hop(2)
        for copy, passed in zip(o_plane, o_across):
            copy.wait_recv()
            passed.start()
        both_steps(0)

        store(4, oT_ref, oT_out)
        own_to_slot_order(q_slot, k_slot, slots_ref, pairs, per_device)
        half_rows = rows // 2

        def pack(value):
            return jnp.concatenate([value[:half_rows].astype(F32), value[half_rows:].astype(F32)], axis=1).astype(BF16)

        def unpack(target, packed):
            target[0:half_rows, :] = packed[:, 0:CHIP_COLS]
            target[half_rows:rows, :] = packed[:, CHIP_COLS : 2 * CHIP_COLS]

        for c in range(CHIPS):
            packs[c] = pack(k_slot[c * rows : (c + 1) * rows, :])
        sends0 = [
            remote(packs.at[c], packed_in.at[i], send0, recv0, i, device)
            for i, (c, device) in enumerate(near)
        ]
        for copy in sends0:
            copy.start()
        unpack(att_all.at[chip], packs[chip])
        take_hop(2)
        send_hop(3)
        for copy in o_across:
            copy.wait_recv()
        for copy in sends0:
            copy.wait()
        for i, (c, _) in enumerate(near):
            unpack(att_all.at[c], packed_in[i])

        def w_out_rows(p):
            return w_wo[p].reshape(CHIP_COLS, width)

        for p in range(CHIPS):
            term = jnp.dot(att_all[p], w_out_rows(p), preferred_element_type=F32)
            hidden[...] = term if p == 0 else hidden[...] + term

        def first_norm(i, _):
            at = aligned(i, ROWS)
            h = hidden[at, :] + mix(s_ref, at, p_ref, 0)
            hidden[at, :] = h
            own[1, at, :] = (h * norm_factor(h)).astype(BF16)
            return 0

        lax.fori_loop(0, blocks, first_norm, 0)

        def ring(source, target, send, recv):
            return ring_sends(
                source, target, lambda c: c, chip, core, depth, chip_x, chip_y, send, recv
            )

        ring1 = ring(own.at[1], x_rows, ag1s, ag1r)
        for copy in ring1[:4]:
            copy.start()
        x_rows[chip] = own[1]
        ring1[0].wait_recv()
        ring1[4].start()
        ring1[1].wait_recv()
        ring1[5].start()
        take_hop(3)
        ff_mine.wait_recv()
        for _, _, receives, _, share in hops:
            pl.when(receives)(share.wait_recv)

        def w_rows(i):
            return w_ff[i].reshape(width, columns)

        def ff_forward(c):
            x = x_rows[c]
            for n in range(col_tiles):
                cols = slice(n * TILE, (n + 1) * TILE)
                g = jnp.dot(x, w_rows(0)[:, cols], preferred_element_type=F32)
                u = jnp.dot(x, w_rows(1)[:, cols], preferred_element_type=F32)
                gate[c, :, cols] = g
                up[c, :, cols] = u
                inner[c, :, cols] = (gelu_parts(g)[0] * u).astype(BF16)
            return jnp.dot(inner[c], w_rows(2), preferred_element_type=F32)

        give1, relay1, receive1, sends1 = plane_sum(
            part1, got1, far1, chip, core, depth, chip_x, chip_y, chip_d, send1, recv1
        )
        up0_ref[...] = ff_forward(chip)
        for i, (c, _) in enumerate(near):
            if i < 2:
                ring1[2 + i].wait_recv()
            else:
                ring1[4].wait_recv()
                ring1[5].wait_recv()
            part1[c] = ff_forward(c).astype(BF16)
            give1(i)
        relay1()

        def turn(i, _):
            xT[:, aligned(i, rows)] = x_rows[i].T
            innerT[:, aligned(i, rows)] = inner[i].T
            return 0

        lax.fori_loop(0, CHIPS, turn, 0)
        valid_count = end_count()
        weight = as_column(v_ref[...].astype(F32)) * (mesh_tokens / valid_count[0:1, 0:1])
        own_weight[...] = jnp.broadcast_to(weight, own_weight.shape)
        receive1()

        def outputs(i, sums):
            at = aligned(i, ROWS)
            a = mix(s_ref, at, p_ref, 0)
            result = hidden[at, :] + up0_ref[at, :]
            for j in range(2):
                result = result + got1[j, at, :].astype(F32)
            difference = result - a
            row_weight = own_weight[at, 0:1]
            c0, c1 = c_ref[0], c_ref[1]
            out0 = a + c0 * difference
            out1 = mix(s_ref, at, p_ref, 1) + c1 * difference
            new_ref[at, 0, :] = out0.astype(BF16)
            new_ref[at, 1, :] = out1.astype(BF16)
            up0 = g_ref[at, 0, :].astype(F32) + row_weight * (out0 - t_ref[at, 0, :].astype(F32))
            up1 = g_ref[at, 1, :].astype(F32) + row_weight * (out1 - t_ref[at, 1, :].astype(F32))
            up0_ref[at, :] = up0
            up1_ref[at, :] = up1
            own[2, at, :] = (c0 * up0 + c1 * up1).astype(BF16)
            return (
                sums[0] + jnp.sum(up0 * difference, axis=0, keepdims=True),
                sums[1] + jnp.sum(up1 * difference, axis=0, keepdims=True),
            )

        zero = jnp.zeros((1, width), F32)
        correct_sums = lax.fori_loop(0, blocks, outputs, (zero, zero))
        sums_ref[...] = jnp.zeros_like(sums_ref)
        sums_ref[2:3, :] = correct_sums[0]
        sums_ref[3:4, :] = correct_sums[1]
        store(5, new_ref, new_out)
        store(6, up0_ref, up0_out)
        store(7, up1_ref, up1_out)

        ring2 = ring(own.at[2], r_rows, ag2s, ag2r)
        for copy in ring2[:4]:
            copy.start()
        r_rows[chip] = own[2]

        def ff_backward(c):
            r = r_rows[c]
            for n in range(col_tiles):
                cols = slice(n * TILE, (n + 1) * TILE)
                inner_grad = lax.dot_general(r, w_rows(2)[cols, :], NT, preferred_element_type=F32)
                value, slope = gelu_parts(gate[c, :, cols])
                gate_low[c, :, cols] = (inner_grad * up[c, :, cols] * slope).astype(BF16)
                up_low[c, :, cols] = (inner_grad * value).astype(BF16)
            return lax.dot_general(
                gate_low[c], w_rows(0), NT, preferred_element_type=F32
            ) + lax.dot_general(up_low[c], w_rows(1), NT, preferred_element_type=F32)

        give2, relay2, receive2, sends2 = plane_sum(
            part2, got2, far2, chip, core, depth, chip_x, chip_y, chip_d, send2, recv2
        )
        hg_ref[...] = ff_backward(chip)
        ring2[0].wait_recv()
        ring2[4].start()
        ring2[1].wait_recv()
        ring2[5].start()
        for i, (c, _) in enumerate(near):
            if i < 2:
                ring2[2 + i].wait_recv()
            else:
                ring2[4].wait_recv()
                ring2[5].wait_recv()
            part2[c] = ff_backward(c).astype(BF16)
            give2(i)

        def weight_grads(terms):
            def body(z, _):
                at = aligned(z, shard)
                for i, left, right in terms:
                    grad = jnp.dot(
                        left[at, :], right[...].reshape(queries, -1), preferred_element_type=F32
                    ).astype(BF16)
                    dw[z, 0, i * half : (i + 1) * half, :] = grad[:half]
                    dw[z, 1, i * half : (i + 1) * half, :] = grad[half:]
                return 0

            lax.fori_loop(0, depths, body, 0)

        early, late = pl.ds(0, half), pl.ds(half, 2 * half)

        def swap_rows(index, part):
            return remote(dw.at[:, 1 - core, part], dw_other.at[:, part], dsend, drecv, index, other)

        def add_cores(part):
            def body(z, _):
                dw_other[z, part, :] = (
                    dw[z, core, part, :].astype(F32) + dw_other[z, part, :].astype(F32)
                ).astype(BF16)
                return 0

            lax.fori_loop(0, depths, body, 0)

        swaps = [swap_rows(0, early), swap_rows(1, late)]
        weight_grads(((0, innerT, r_rows),))
        swaps[0].start()
        for copy in sends1:
            copy.wait_send()
        a_start, a_hop, a_result, a_finish = line_reduce(
            dw_other.at[:, early], gate.at[0, pl.ds(0, half)], a_up, a_down,
            part1.at[pl.ds(0, 2), pl.ds(0, half)], part1.at[pl.ds(2, 2), pl.ds(0, half)], a_sems,
        )
        swaps[0].wait_recv()
        add_cores(early)
        a_start()
        relay2()
        weight_grads(((1, xT, gate_low), (2, xT, up_low)))
        swaps[1].start()
        a_hop(1)
        receive2()

        def second_norm(i, gain_sum):
            at = aligned(i, ROWS)
            h = hidden[at, :]
            weighted = hg_ref[at, :]
            for j in range(2):
                weighted = weighted + got2[j, at, :].astype(F32)
            factor = norm_factor(h)
            mean = jnp.mean(weighted * h, axis=1, keepdims=True)
            result_grad = c_ref[0] * up0_ref[at, :] + c_ref[1] * up1_ref[at, :]
            hidden_grad = result_grad + (factor * weighted - h * (factor * factor * factor * mean))
            hg_ref[at, :] = hidden_grad
            own[3, at, :] = hidden_grad.astype(BF16)
            return gain_sum + jnp.sum(weighted * h * factor, axis=0, keepdims=True)

        sums_ref[1:2, :] = lax.fori_loop(0, blocks, second_norm, zero)
        store(10, hg_ref, hg_out)

        sends3 = [
            remote(packs.at[c], packed_grad.at[i], send3, recv3, i, device)
            for i, (c, device) in enumerate(near)
        ]

        def att_grad(c):
            return lax.dot_general(own[3], w_out_rows(c), NT, preferred_element_type=F32)

        for i in (2, 0, 1):
            packs[near[i][0]] = pack(att_grad(near[i][0]))
            sends3[i].start()
        da_ref[chip] = att_grad(chip).astype(BF16)
        for i, c in enumerate((chip, chip_x, chip_y, chip_d)):
            grad = jnp.dot(att_all[c].T, own[3], preferred_element_type=F32).astype(BF16)
            dwo[i, 0] = grad[:half]
            dwo[i, 1] = grad[half:]
        out_swap = remote(dwo.at[:, 1 - core], dwo_other, dsend, drecv, 2, other)
        out_swap.start()
        swaps[1].wait_recv()
        add_cores(late)
        store(8, dw_other.at[:, late], ffb_ref)
        a_hop(2)
        out_swap.wait_recv()
        for i in range(CHIPS):
            dwo_other[i] = (dwo[i, core].astype(F32) + dwo_other[i].astype(F32)).astype(BF16)
        store(9, dwo_other, dwo_ref)
        a_result()
        ffa_ref[...] = gate[0, 0:half, :].astype(BF16)
        for copy in sends3:
            copy.wait_recv()
        for i, (c, _) in enumerate(near):
            unpack(da_ref.at[c], packed_grad[i])
        sent = ring0 + shared0 + q_copies + q_shared + o_plane + o_across + sends2 + sends3
        for copy in sent + ring1 + ring2 + swaps + [out_swap, ff_mine]:
            copy.wait_send()
        a_finish()
        for i in range(depths - 1):
            carried(i, o_copies[i].wait_send)
            carried(i, o_shared[i].wait_send)
        for _, sends, receives, hop, share in hops:
            pl.when(sends)(hop.wait_send)
            pl.when(receives)(share.wait_send)
        for copy in stores:
            copy.wait()

    block = (rows, width)
    pair = (rows, 2, width)
    wide_rows = (CHIPS, rows, width)
    hid_rows = (CHIPS, rows, columns)

    def out(shape, dtype):
        return jax.ShapeDtypeStruct(shape, dtype)

    vmem = pltpu.VMEM
    outs = [
        out(pair, BF16),
        out(block, F32),
        out(block, F32),
        out(block, F32),
        out((CHIPS, rows, CHIP_COLS), BF16),
        out((CHIPS, half, width), BF16),
        out((half, columns), BF16),
        out((depths, 2 * half, columns), BF16),
        out((8, width), F32),
        out(wide_rows, BF16),
        out((3, width, CHIP_COLS), BF16),
        out((queries, CHIP_COLS), BF16),
        out((tokens, CHIP_COLS), BF16),
        out((tokens, CHIP_COLS), BF16),
        out((tiles, CHIP_COLS, TILE), F32),
        out((tiles, LOCAL_HEADS, 1, TILE), F32),
    ]
    return pl.pallas_call(
        kernel,
        out_shape=outs,
        in_specs=[SM] * 4 + [VM] * 6 + [ANY] * 7,
        out_specs=[ANY] * 4 + [VM, ANY, VM, ANY, VM] + [ANY] * 6 + [VM],
        scratch_shapes=[
            vmem(pair, BF16),
            vmem(block, F32),
            vmem(block, F32),
            vmem(block, F32),
            vmem((2 * CHIPS, rows, width), BF16),
            vmem((3, width, CHIP_COLS), BF16),
            vmem((queries, CHIP_COLS), BF16),
            vmem((tokens, CHIP_COLS), BF16),
            vmem((tokens, CHIP_COLS), BF16),
            vmem((tiles, CHIP_COLS, TILE), F32),
            vmem((CHIPS, 2, half, width), BF16),
            vmem((CHIPS, half, width), BF16),
            vmem((3, depths, 2, half, columns), BF16),
            vmem((depths, CHIPS, out_rows, width), BF16),
            vmem((depths, 2, half, piece_lanes), BF16),
            vmem((CHIPS, rows, CHIP_COLS), BF16),
            vmem((CHIPS, rows // 2, 2 * CHIP_COLS), BF16),
            vmem((3, rows // 2, 2 * CHIP_COLS), BF16),
            vmem((3, rows // 2, 2 * CHIP_COLS), BF16),
            vmem(block, F32),
            vmem((4,) + block, BF16),
            vmem(wide_rows, BF16),
            vmem(wide_rows, BF16),
            vmem((width, queries), BF16),
            vmem((columns, queries), BF16),
            vmem(hid_rows, BF16),
            vmem(hid_rows, F32),
            vmem(hid_rows, F32),
            vmem(hid_rows, BF16),
            vmem(hid_rows, BF16),
            vmem((rows, 128), F32),
            vmem(wide_rows, BF16),
            vmem(wide_rows, BF16),
            vmem((2,) + block, BF16),
            vmem((2,) + block, BF16),
            vmem((2, rows // 2, width), BF16),
            vmem((2, rows // 2, width), BF16),
            vmem((depths, 2, 3 * half, columns), BF16),
            vmem((depths, 3 * half, columns), BF16),
            vmem((depths - 1, half, columns), BF16),
            vmem((depths - 1, half, columns), BF16),
            vmem((3, half, width), BF16),
            vmem((2, half, hidden_cols), BF16),
            vmem((8, 128), F32),
            vmem((queries, CHIP_COLS), BF16),
            vmem((tokens, CHIP_COLS), BF16),
            vmem((tokens, CHIP_COLS), BF16),
            vmem((CHIP_COLS, tokens), BF16),
        ]
        + [DMA((7,))]
        + [DMA((2 * depths - 2,))] * 2
        + [DMA((2 * depths - 1,))] * 2
        + [DMA((depths - 1,))] * 2
        + [DMA((depths,))] * 2
        + [DMA((depths - 1,))] * 4
        + [DMA((6,))] * 2
        + [DMA((6,))] * 2
        + [DMA((4,))] * 2
        + [DMA((3,))] * 2
        + [DMA((6,))] * 4
        + [DMA((3,))] * 2
        + [DMA((6,))] * 4
        + [DMA((3,))] * 2
        + [DMA((11,)), DMA((CHIPS,))]
        + [DMA((depths - 1,))] * 4
        + total_scratch((8, 128), depths),
        compiler_params=comm_params(collective_id),
        name="forward",
    )(
        slots, lengths, predict, correct, states, out_grad, teacher, valid, gain_one, gain_two,
        w_query, w_key, w_value, w_out, w_gate, w_up, w_down,
    )


def backward(
    slots, lengths, predict, correct, att_grad, q_pairs, k_pairs, v_pairs, oT, lse, sums, up_grads,
    out_grads, ff_early, weights, states, up0, up1, hidden_grad, own_rows, collective_id,
):
    rows, _, width = states.shape
    depths, late_rows, ff_columns = up_grads.shape
    half = late_rows // 2
    columns = CHIP_COLS
    lanes_all = 3 * columns
    blocks = rows // ROWS
    tokens = k_pairs.shape[0]
    queries = q_pairs.shape[0]
    tiles = queries // TILE
    per_device = rows // BLK
    group_pairs = tokens // (2 * BLK)
    pairs = queries // (2 * BLK)
    half_tiles = group_pairs * BLK // TILE
    wide_lanes = LOCAL_HEADS * TILE

    def kernel(
        slots_ref, lengths_ref, p_ref, c_ref, g_in, q_in, k_in, v_in, oT_in, lse_ref, sums_ref, u_in,
        og_in, fa_ref, w_in, s_in, up0_in, up1_in, hg_in, x_in,
        grad_ref, fa_all, fb_all, q_all, o_all, total_ref,
        w_all, s_ref, up0_ref, up1_ref, hg_ref, x_own, fa_own, g_ref, q_ref, k_ref, v_ref, oT_ref, u_ref, og_ref,
        g_pairs, kT, doT, dqT, q_stack, do_stack, p_buf, ds_buf, dk_acc, dv_acc, bias, dq_pairs, dq_rows,
        give, kept, came, xT, part, got, far, mine, q_grad, q_other, q_mine, q_far, q_sum,
        o_near, o_mine, o_far, o_sum, u_far, u_sum, all_sums,
        loads, nsend, nrecv, ksend, krecv, send, recv, ssend, srecv, zsend, zrecv, osend, orecv, usend, urecv,
        asend, arecv, fsend, frecv, gsend, grecv, bsend, brecv, psend, precv, *total_refs,
    ):
        depth, chip, core, chip_x, chip_y, chip_d = place_on_mesh()
        near = [(c, (2 * c + core, depth)) for c in (chip_x, chip_y, chip_d)]
        other = (2 * chip + 1 - core, depth)
        across = [
            (2 * chip + core, lax.rem(depth + step, depths)) for step in range(1, depths)
        ]
        peers = plane_peers(chip, core, depth, chip_x, chip_y, chip_d)
        everyone = peers + across
        signal_all(everyone)

        def slot(chip_index):
            return 2 * chip_index + core

        def load(index, source, target):
            copy = pltpu.make_async_copy(source, target, loads.at[index])
            copy.start()
            return copy

        first_loads = [
            load(7 + i, source, target)
            for i, (source, target) in enumerate(
                ((g_in, g_ref), (k_in, k_ref), (q_in, q_ref), (v_in, v_ref), (oT_in, oT_ref))
            )
        ]
        early_load = load(0, fa_ref, fa_own)
        sum_loads = [load(12, u_in, u_ref), load(13, og_in, og_ref)]
        other_loads = [
            load(1 + i, source, target)
            for i, (source, target) in enumerate(
                (
                    (w_in, w_all), (x_in, x_own), (s_in, s_ref), (up0_in, up0_ref), (up1_in, up1_ref), (hg_in, hg_ref)
                )
            )
        ]

        def depth_sum(source_of, inbox, sends, receives):
            return [
                remote(source_of(lax.rem(depth + i + 1, depths)), inbox.at[i], sends, receives, i, device)
                for i, device in enumerate(across)
            ]

        early_load.wait()
        for copy in sum_loads:
            copy.wait()
        wait_all(everyone)
        u_copies = depth_sum(lambda z: u_ref.at[z], u_far, usend, urecv)
        near_grads = [
            remote(og_ref.at[1 + i], o_near.at[i], nsend, nrecv, i, device)
            for i, (_, device) in enumerate(near)
        ]
        a_ring = ring_sends(
            fa_own, fa_all, slot, chip, core, depth, chip_x, chip_y, asend, arecv
        )
        for copy in u_copies + near_grads + a_ring[:4]:
            copy.start()

        def shared(index, ref):
            return remote(ref, ref, psend, precv, index, other)

        in_plane = (chip, chip_x, chip_y, chip_d)
        a_shared = [shared(i, fa_all.at[slot(c)]) for i, c in enumerate(in_plane)]
        b_shared = [shared(4 + i, fb_all.at[slot(c)]) for i, c in enumerate(in_plane)]
        q_shared = [shared(8 + i, q_all.at[slot(c)]) for i, c in enumerate(in_plane)]
        o_shared = shared(12, o_all.at[core])
        fa_all[slot(chip)] = fa_own[...]
        a_shared[0].start()

        for copy in first_loads:
            copy.wait()
        own_to_pair_order(g_ref, g_pairs, slots_ref, pairs, per_device)

        def turn_keys(i, _):
            at = aligned(i, TILE)
            kT[:, at] = k_ref[at, :].T
            return 0

        lax.fori_loop(0, tokens // TILE, turn_keys, 0)

        def attend(kind, step):
            tile = kind * (tiles // 2) + step
            key_tiles = half_tiles * (kind + 1)
            q_tile = q_ref[aligned(tile, TILE), :]
            fill_bias(bias, kind, step, slots_ref, lengths_ref, per_device, group_pairs)
            do_tile = g_pairs[aligned(tile, TILE), :]
            doT[...] = do_tile.astype(F32).T * oT_ref[tile]
            for head in range(LOCAL_HEADS):
                lanes = slice(head * TILE, (head + 1) * TILE)
                heads = slice(head * HD, (head + 1) * HD)
                mask = head_mask(TILE, head)
                q_head = jnp.where(mask, q_tile, jnp.zeros_like(q_tile))
                do_head = jnp.where(mask, do_tile, jnp.zeros_like(do_tile))
                q_stack[lanes, :] = q_head
                do_stack[lanes, :] = do_head
                delta = jnp.sum(doT[heads, :], axis=0, keepdims=True)
                norm = lse_ref[tile, head]
                total = jnp.zeros((HD, TILE), F32)
                for k_tile in range(key_tiles):
                    at = slice(k_tile * TILE, (k_tile + 1) * TILE)
                    s = lax.dot_general(k_ref[at, :], q_head, NT, preferred_element_type=F32)
                    if k_tile >= key_tiles - half_tiles:
                        s = s + bias[k_tile - (key_tiles - half_tiles), :, 0:TILE]
                    dp = lax.dot_general(v_ref[at, :], do_head, NT, preferred_element_type=F32)
                    e = jnp.exp(s - norm)
                    p_buf[at, lanes] = e.astype(BF16)
                    ds = (e * (dp - delta)).astype(BF16)
                    ds_buf[at, lanes] = ds
                    total = total + jnp.dot(kT[heads, at], ds, preferred_element_type=F32)
                dqT[heads, :] = total
            for k_tile in range(key_tiles):
                at = slice(k_tile * TILE, (k_tile + 1) * TILE)
                dv = jnp.dot(p_buf[at, :], do_stack[...], preferred_element_type=F32)
                dk = jnp.dot(ds_buf[at, :], q_stack[...], preferred_element_type=F32)
                if kind == 1:
                    fresh = step == 0
                    dv_acc[at, :] = dv + jnp.where(fresh, 0.0, dv_acc[at, :])
                    dk_acc[at, :] = dk + jnp.where(fresh, 0.0, dk_acc[at, :])
                else:
                    dv_acc[at, :] = dv + dv_acc[at, :]
                    dk_acc[at, :] = dk + dk_acc[at, :]
            dq_pairs[aligned(tile, TILE), :] = dqT[...].T.astype(BF16)

        for kind in (1, 0):

            def body(step, _, kind=kind):
                attend(kind, step)
                return 0

            lax.fori_loop(0, tiles // 2, body, 0)
            if kind == 1:
                a_ring[0].wait_recv()
                a_ring[4].start()
                a_ring[1].wait_recv()
                a_ring[5].start()

        def slot_rows(target, side, chip_index, pair_index):
            pair = chip_index * per_device + side * (per_device // 2) + pair_index
            second, _, _ = pair_places(slots_ref, pair)
            at = 2 * pair_index * BLK
            for i, acc in enumerate((dk_acc, dv_acc)):
                both = either(second, acc[aligned(pair, BLK), :], acc[aligned(group_pairs + pair, BLK), :])
                for j in range(2):
                    target[i, chip_index, at + j * BLK : at + (j + 1) * BLK, :] = both[j].astype(BF16)

        for c in range(CHIPS):
            for i in range(per_device // 2):
                slot_rows(give, 1 - core, c, i)
        swap = remote(give, came, ksend, krecv, 0, other)
        swap.start()
        for c in range(CHIPS):
            for i in range(per_device // 2):
                slot_rows(kept, core, c, i)
        own_to_slot_order(dq_pairs, dq_rows, slots_ref, pairs, per_device)

        for copy in near_grads:
            copy.wait_recv()
        whole = og_ref[0].astype(F32)
        for i in range(3):
            whole = whole + o_near[i].astype(F32)
        o_mine[...] = whole.astype(BF16)
        distance = lax.rem(chip + depths - depth, depths)
        o_copies = [
            remote(o_mine, o_far.at[i], osend, orecv, i, device) for i, device in enumerate(across)
        ]
        for i in range(depths - 1):
            pl.when(distance == i + 1)(o_copies[i].start)
        swap.wait_recv()

        def add_cores(c, _):
            for i in range(2):
                kept[i, c] = (kept[i, c].astype(F32) + came[i, c].astype(F32)).astype(BF16)
            return 0

        lax.fori_loop(0, CHIPS, add_cores, 0)
        for copy in other_loads:
            copy.wait()

        def rows_grad(c):
            return (
                lax.dot_general(
                    dq_rows[aligned(c, rows), :], w_all[0], NT, preferred_element_type=F32
                )
                + lax.dot_general(kept[0, c], w_all[1], NT, preferred_element_type=F32)
                + lax.dot_general(kept[1, c], w_all[2], NT, preferred_element_type=F32)
            )

        give_rows, relay_rows, receive_rows, sends = plane_sum(
            part, got, far, chip, core, depth, chip_x, chip_y, chip_d, send, recv
        )
        for i in (2, 0, 1):
            part[near[i][0]] = rows_grad(near[i][0]).astype(BF16)
            give_rows(i)
        mine[...] = rows_grad(chip)

        def turn(c, _):
            xT[:, aligned(c, rows)] = x_own[c].T
            return 0

        lax.fori_loop(0, CHIPS, turn, 0)

        def weight_grads(z, _):
            at = aligned(z, 2 * half)
            grads = []
            for i in range(3):
                right = dq_rows[...] if i == 0 else kept[i - 1].reshape(queries, columns)
                grads.append(jnp.dot(xT[at, :], right, preferred_element_type=F32))
            grad = jnp.concatenate(grads, axis=1).astype(BF16)
            q_grad[z, 0] = grad[:half]
            q_grad[z, 1] = grad[half:]
            return 0

        lax.fori_loop(0, depths, weight_grads, 0)
        core_swap = remote(q_grad.at[:, 1 - core], q_other, ssend, srecv, 0, other)
        core_swap.start()
        relay_rows()
        core_swap.wait_recv()
        for i in range(depths):
            q_mine[i] = (q_grad[i, core].astype(F32) + q_other[i].astype(F32)).astype(BF16)
        q_copies = depth_sum(lambda z: q_mine.at[z], q_far, zsend, zrecv)
        for copy in q_copies:
            copy.start()

        for copy in u_copies:
            copy.wait_recv()
        whole = u_ref[depth].astype(F32)
        for i in range(depths - 1):
            whole = whole + u_far[i].astype(F32)
        u_sum[...] = whole.astype(BF16)
        b_ring = ring_sends(
            u_sum, fb_all, slot, chip, core, depth, chip_x, chip_y, fsend, frecv
        )
        for copy in b_ring[:4]:
            copy.start()
        fb_all[slot(chip)] = u_sum[...]
        b_shared[0].start()
        a_ring[2].wait_recv()
        a_shared[1].start()
        a_ring[3].wait_recv()
        a_shared[2].start()
        a_ring[4].wait_recv()
        a_ring[5].wait_recv()
        a_shared[3].start()
        receive_rows()

        def state_grads(i, totals):
            at = aligned(i, ROWS)
            s0, s1 = s_ref[at, 0, :].astype(F32), s_ref[at, 1, :].astype(F32)
            a = p_ref[0, 0] * s0 + p_ref[0, 1] * s1
            weighted = mine[at, :]
            for j in range(2):
                weighted = weighted + got[j, at, :].astype(F32)
            factor = norm_factor(a)
            mean = jnp.mean(weighted * a, axis=1, keepdims=True)
            up0, up1 = up0_ref[at, :], up1_ref[at, :]
            result_grad = c_ref[0] * up0 + c_ref[1] * up1
            norm_grad = factor * weighted - a * (factor * factor * factor * mean)
            mixed0 = up0 + (hg_ref[at, :] + norm_grad - result_grad)
            grad_ref[at, 0, :] = (p_ref[0, 0] * mixed0 + p_ref[1, 0] * up1).astype(BF16)
            grad_ref[at, 1, :] = (p_ref[0, 1] * mixed0 + p_ref[1, 1] * up1).astype(BF16)
            terms = (weighted * a * factor, mixed0 * s0, mixed0 * s1, up1 * s0, up1 * s1)
            return tuple(t + jnp.sum(v, axis=0, keepdims=True) for t, v in zip(totals, terms))

        totals = lax.fori_loop(
            0, blocks, state_grads, tuple(jnp.zeros((1, width), F32) for _ in range(5))
        )
        b_ring[0].wait_recv()
        b_ring[4].start()
        b_ring[1].wait_recv()
        b_ring[5].start()
        all_sums[...] = sums_ref[...]
        all_sums[0:1, :] = totals[0]
        for i in range(4):
            all_sums[4 + i : 5 + i, :] = totals[1 + i]
        start, turn_sums, end = total_over_mesh(
            all_sums, *total_refs[:3], across, peers, *total_refs[3:]
        )
        start()
        for copy in q_copies:
            copy.wait_recv()
        whole = q_mine[depth].astype(F32)
        for i in range(depths - 1):
            whole = whole + q_far[i].astype(F32)
        q_sum[...] = whole.astype(BF16)
        q_ring = ring_sends(
            q_sum, q_all, slot, chip, core, depth, chip_x, chip_y, gsend, grecv
        )
        for copy in q_ring[:4]:
            copy.start()
        q_all[slot(chip)] = q_sum[...]
        q_shared[0].start()
        quarter = half // 2
        o_top, o_low = o_all.at[core, pl.ds(0, quarter)], o_all.at[core, pl.ds(quarter, quarter)]
        o_source_top, o_source_low = o_sum.at[pl.ds(0, quarter)], o_sum.at[pl.ds(quarter, quarter)]
        dev_x, dev_y = near[0][1], near[1][1]
        o_ring = [
            remote(o_source_top, o_top, bsend, brecv, 0, dev_x),
            remote(o_source_low, o_low, bsend, brecv, 1, dev_y),
            remote(o_source_low, o_low, bsend, brecv, 2, dev_x),
            remote(o_source_top, o_top, bsend, brecv, 3, dev_y),
            remote(o_top, o_top, bsend, brecv, 4, dev_y),
            remote(o_low, o_low, bsend, brecv, 5, dev_x),
        ]
        source, from_x, from_y = chip == depth, chip_x == depth, chip_y == depth

        @pl.when(source)
        def _():
            for copy in o_copies:
                copy.wait_recv()
            whole = o_mine[...].astype(F32)
            for i in range(depths - 1):
                whole = whole + o_far[i].astype(F32)
            o_sum[...] = whole.astype(BF16)
            for copy in o_ring[:4]:
                copy.start()
            o_all[core] = o_sum[...]

        turn_sums()
        q_ring[0].wait_recv()
        q_ring[4].start()
        q_ring[1].wait_recv()
        q_ring[5].start()

        @pl.when(from_x)
        def _():
            o_ring[0].wait_recv()
            o_ring[4].start()
            o_ring[2].wait_recv()

        @pl.when(from_y)
        def _():
            o_ring[1].wait_recv()
            o_ring[5].start()
            o_ring[3].wait_recv()

        for copies, passed in ((b_ring, b_shared), (q_ring, q_shared)):
            copies[2].wait_recv()
            passed[1].start()
            copies[3].wait_recv()
            passed[2].start()
            copies[4].wait_recv()
            copies[5].wait_recv()
            passed[3].start()

        @pl.when(chip_d == depth)
        def _():
            o_ring[4].wait_recv()
            o_ring[5].wait_recv()

        o_shared.start()
        total_ref[...] = end()
        for copy in a_shared + b_shared + q_shared + [o_shared]:
            copy.wait()
        for copy in u_copies + near_grads + [swap] + sends + [core_swap] + q_copies + a_ring + b_ring + q_ring:
            copy.wait_send()
        for i in range(depths - 1):
            pl.when(distance == i + 1)(o_copies[i].wait_send)

        @pl.when(source)
        def _():
            for copy in o_ring[:4]:
                copy.wait_send()

        pl.when(from_x)(o_ring[4].wait_send)
        pl.when(from_y)(o_ring[5].wait_send)

    vmem = pltpu.VMEM
    block = (rows, width)
    wide_rows = (CHIPS, rows, width)
    q_block, o_block = (half, lanes_all), (half, width)
    kv_half = (2, CHIPS, rows, columns)
    a_block, b_block = ff_early.shape, (late_rows, ff_columns)
    ctx = 2 * CHIPS
    return pl.pallas_call(
        kernel,
        out_shape=[
            jax.ShapeDtypeStruct((rows, 2, width), BF16),
            jax.ShapeDtypeStruct((ctx,) + a_block, BF16),
            jax.ShapeDtypeStruct((ctx,) + b_block, BF16),
            jax.ShapeDtypeStruct((ctx,) + q_block, BF16),
            jax.ShapeDtypeStruct((2,) + o_block, BF16),
            jax.ShapeDtypeStruct((8, width), F32),
        ],
        in_specs=[SM] * 4 + [ANY] * 5 + [VM] * 2 + [ANY] * 9,
        out_specs=[VM] * 6,
        scratch_shapes=[
            vmem((3, width, columns), BF16),
            vmem((rows, 2, width), BF16),
            vmem(block, F32),
            vmem(block, F32),
            vmem(block, F32),
            vmem(wide_rows, BF16),
            vmem(a_block, BF16),
            vmem((queries, columns), BF16),
            vmem((queries, columns), BF16),
            vmem((tokens, columns), BF16),
            vmem((tokens, columns), BF16),
            vmem(oT.shape, F32),
            vmem(up_grads.shape, BF16),
            vmem(out_grads.shape, BF16),
            vmem((queries, columns), BF16),
            vmem((columns, tokens), BF16),
            vmem((columns, TILE), F32),
            vmem((columns, TILE), F32),
            vmem((wide_lanes, columns), BF16),
            vmem((wide_lanes, columns), BF16),
            vmem((tokens, wide_lanes), BF16),
            vmem((tokens, wide_lanes), BF16),
            vmem((tokens, columns), F32),
            vmem((tokens, columns), F32),
            vmem((half_tiles, TILE, TILE), F32),
            vmem((queries, columns), BF16),
            vmem((queries, columns), BF16),
            vmem(kv_half, BF16),
            vmem(kv_half, BF16),
            vmem(kv_half, BF16),
            vmem((width, queries), BF16),
            vmem(wide_rows, BF16),
            vmem((2,) + block, BF16),
            vmem((2, rows // 2, width), BF16),
            vmem(block, F32),
            vmem((depths, 2) + q_block, BF16),
            vmem((depths,) + q_block, BF16),
            vmem((depths,) + q_block, BF16),
            vmem((depths - 1,) + q_block, BF16),
            vmem(q_block, BF16),
            vmem((3,) + o_block, BF16),
            vmem(o_block, BF16),
            vmem((depths - 1,) + o_block, BF16),
            vmem(o_block, BF16),
            vmem((depths - 1,) + b_block, BF16),
            vmem(b_block, BF16),
            vmem((8, width), F32),
            DMA((14,)),
            *[DMA((3,))] * 2,
            *[DMA((1,))] * 2,
            *[DMA((6,))] * 2,
            *[DMA((1,))] * 2,
            *[DMA((depths - 1,))] * 6,
            *[DMA((6,))] * 8,
            *[DMA((13,))] * 2,
            *total_scratch((8, width), depths),
        ],
        compiler_params=comm_params(collective_id),
        name="backward",
    )(
        slots, lengths, predict, correct, att_grad, q_pairs, k_pairs, v_pairs, oT, lse, sums, up_grads,
        out_grads, ff_early, weights, states, up0, up1, hidden_grad, own_rows,
    )


def lay_out(early, late, qkv, out, sums, gain_one, gain_two):
    ctx, half, columns = early.shape
    width = out.shape[2]
    shard = 2 * half
    depths = width // shard
    split = columns // depths
    steps = 1
    strip = half // steps

    def kernel(
        d_ref, g_ref, u_ref, q_ref, o_ref, s_ref, g1_ref, g2_ref,
        dq_ref, dk_ref, dv_ref, do_ref, dg_ref, du_ref, dd_ref, g1_out, g2_out, p_out, c_out, columns_ref,
    ):
        core, step = pl.program_id(0), pl.program_id(1)
        depth = lax.axis_index("wsh")

        @pl.when((core == 0) & (step == 0))
        def _():
            one = g1_ref[...].astype(F32).reshape(1, shard)
            two = g2_ref[...].astype(F32).reshape(1, shard)
            columns_ref[0] = jnp.broadcast_to(as_column(one), (shard, 128))
            columns_ref[1] = jnp.broadcast_to(as_column(two), (shard, 128))
            for z in range(depths):

                @pl.when(depth == z)
                def _(z=z):
                    g1_out[...] = s_ref[0:1, z * shard : (z + 1) * shard] / one
                    g2_out[...] = s_ref[1:2, z * shard : (z + 1) * shard] / two

            scalars = jnp.sum(s_ref[...], axis=1, keepdims=True)
            for i in range(2):
                c_out[:, i : i + 1] = scalars[2 + i : 3 + i]
                for j in range(2):
                    at = 4 + 2 * i + j
                    p_out[i : i + 1, j : j + 1] = scalars[at : at + 1]

        rows = aligned(core * steps + step, strip)
        one, two = columns_ref[0, rows, 0:1], columns_ref[1, rows, 0:1]
        do_ref[...] = o_ref[...].astype(F32)
        for i, ref in enumerate((dq_ref, dk_ref, dv_ref)):
            wide = jnp.concatenate(
                [q_ref[p, :, i * CHIP_COLS : (i + 1) * CHIP_COLS].astype(F32) for p in range(CHIPS)], axis=1
            )
            ref[...] = wide * one
        for source, ref in ((g_ref, dg_ref), (u_ref, du_ref)):
            for z in range(depths):
                wide = jnp.concatenate(
                    [source[p, :, z * split : (z + 1) * split].astype(F32) for p in range(CHIPS)], axis=1
                )
                ref[:, z * CHIPS * split : (z + 1) * CHIPS * split] = wide * two
        dd_ref[...] = d_ref[...].astype(F32)

    early = early.reshape(CHIPS, 2, half, columns)
    late = late.reshape(CHIPS, 2, 2, half, columns)
    qkv = qkv.reshape(CHIPS, 2, half, -1)
    square = jax.ShapeDtypeStruct((shard, width), F32)
    tall = jax.ShapeDtypeStruct((shard, columns * CHIPS), F32)
    row = jax.ShapeDtypeStruct((1, shard), F32)

    def whole(shape):
        return pl.BlockSpec(shape, lambda c, r: (0,) * len(shape))

    def piece(lanes):
        return pl.BlockSpec((CHIPS, None, strip, lanes), lambda c, r: (0, c, r, 0))

    def part(i):
        return pl.BlockSpec((CHIPS, None, None, strip, columns), lambda c, r: (0, c, i, r, 0))

    def strip_of(lanes):
        return pl.BlockSpec((strip, lanes), lambda c, r: (c * steps + r, 0))

    outs = pl.pallas_call(
        kernel,
        grid=(2, steps),
        out_shape=[
            square,
            square,
            square,
            square,
            tall,
            tall,
            jax.ShapeDtypeStruct((CHIPS, 2, half, width), F32),
            row,
            row,
            jax.ShapeDtypeStruct((2, 2), F32),
            jax.ShapeDtypeStruct((1, 2), F32),
        ],
        in_specs=[
            piece(columns),
            part(0),
            part(1),
            piece(3 * CHIP_COLS),
            pl.BlockSpec((None, strip, width), lambda c, r: (c, r, 0)),
            whole((8, width)),
            whole((shard,)),
            whole((shard,)),
        ],
        out_specs=[
            strip_of(width),
            strip_of(width),
            strip_of(width),
            strip_of(width),
            strip_of(columns * CHIPS),
            strip_of(columns * CHIPS),
            piece(width),
            whole((1, shard)),
            whole((1, shard)),
            whole((2, 2)),
            whole((1, 2)),
        ],
        scratch_shapes=[pltpu.VMEM((2, shard, 128), F32)],
        compiler_params=pltpu.CompilerParams(vmem_limit_bytes=VMEM_LIMIT),
        name="lay_out",
    )(early, late, late, qkv, out, sums, gain_one, gain_two)
    return (*outs[:6], outs[6].reshape(ctx * half, width), *outs[7:])


def plane_shards(
    states, block_slot, cont_lengths, valid_mask, teacher, out_grad, predict, correct,
    norm_attn, w_query, w_key, w_value, w_out, norm_ffn, w_gate, w_up, w_down,
):
    slots, lengths = block_slot[0], cont_lengths[0]
    gain_one, gain_two = norm_attn, norm_ffn
    states = states[0]
    new_states, up0, up1, hidden_grad, att_grad, out_grads, ff_early, up_grads, sums, *saved = forward(
        slots, lengths, predict, correct, states, out_grad[0], teacher[0], valid_mask, gain_one, gain_two,
        w_query, w_key, w_value, w_out, w_gate, w_up, w_down, 1,
    )
    own_rows, weights, q_pairs, k_pairs, v_pairs, oT, lse = saved
    states_grad, *gathered = backward(
        slots, lengths, predict, correct, att_grad.reshape(-1, CHIP_COLS), q_pairs, k_pairs, v_pairs, oT, lse,
        sums, up_grads, out_grads, ff_early, weights, states, up0, up1, hidden_grad, own_rows, 2,
    )
    dq, dk, dv, do, dg, du, dd, g_one, g_two, predict_grad, correct_grad = lay_out(
        *gathered, gain_one, gain_two
    )
    return (
        new_states[None], states_grad[None], predict_grad, correct_grad[0],
        g_one[0], dq, dk, dv, do, g_two[0], dg, du, dd,
    )


def fits_plane(mesh, states, block_slot, w_query, w_gate):
    ctx, depths = mesh.shape["ctx"], mesh.shape["wsh"]
    return (
        ctx == 2 * CHIPS
        and depths == CHIPS
        and states.shape[0] == depths
        and block_slot.shape[1] * BLK == 2 * PROMPT
        and states.shape[1] == 2 * PROMPT
        and w_query.shape[0] % (32 * depths) == 0
        and w_gate.shape[1] % (32 * CHIPS * depths) == 0
    )


def solution(mesh):
    in_specs = (
        P("wsh", "ctx", None, None),
        P("wsh", None),
        P("wsh", None),
        P("wsh", "ctx"),
        P("wsh", "ctx", None, None),
        P("wsh", "ctx", None, None),
        P(),
        P(),
        P("wsh"),
        P("wsh", None),
        P("wsh", None),
        P("wsh", None),
        P("wsh", None),
        P("wsh"),
        P("wsh", None),
        P("wsh", None),
        P("wsh", None),
    )
    out_specs = (
        P("wsh", "ctx", None, None),
        P("wsh", "ctx", None, None),
        P(),
        P(),
        P("wsh"),
        P("wsh", None),
        P("wsh", None),
        P("wsh", None),
        P("wsh", None),
        P("wsh"),
        P("wsh", None),
        P("wsh", None),
        P("wsh", None),
    )

    def step(*args):
        plane = fits_plane(mesh, args[0], args[1], args[9], args[14])
        body = plane_shards if plane else general_shards
        return jax.shard_map(
            body, mesh=mesh, in_specs=in_specs, out_specs=out_specs, check_vma=False
        )(*args)

    return step
```

```python
import functools
import math

import jax
import jax.numpy as jnp
from jax import lax
from jax.experimental import pallas as pl
from jax.experimental.pallas import tpu as pltpu
from jax.sharding import PartitionSpec as P

HEADS = 12
HD = 64
PROMPT = 1024
BLK = 64


EPSILON = 1e-06
NEGATIVE = -1e30
HIGHEST = lax.Precision.HIGHEST


def rms_forward(tensor, gain_vec):
    factor = lax.rsqrt(jnp.mean(tensor * tensor, axis=-1, keepdims=True) + EPSILON)
    return (tensor * factor * gain_vec, factor)


def rms_backward(tensor, factor, gain_vec, upstream):
    weighted = upstream * gain_vec
    gain_grad = jnp.sum(upstream * tensor * factor, axis=0)
    middle = jnp.mean(weighted * tensor, axis=-1, keepdims=True)
    return (factor * weighted - tensor * factor * factor * factor * middle, gain_grad)


def segment_starts(cont_lengths):
    count = cont_lengths.shape[1]
    index = jnp.arange(count, dtype=jnp.int32)
    before = index[:, None] < index[None, :]
    return PROMPT + jnp.sum(jnp.where(before[None], cont_lengths[:, :, None], 0), axis=1)


def token_places(block_slot, cont_lengths):
    groups, blocks = block_slot.shape
    offsets = jnp.arange(BLK, dtype=jnp.int32)
    places = (block_slot[:, :, None] * BLK + offsets[None, None, :]).reshape(groups, blocks * BLK)
    starts = segment_starts(cont_lengths)
    segments = jnp.sum((places[:, :, None] >= starts[:, None, :]).astype(jnp.int32), axis=2)
    return (places, segments)


def visible(query_place, query_segment, key_place, key_segment):
    earlier = key_place[:, None, :] <= query_place[:, :, None]
    shared = (key_segment[:, None, :] == 0) | (key_segment[:, None, :] == query_segment[:, :, None])
    return earlier & shared


def split_heads(tensor):
    return tensor.reshape(tensor.shape[0], tensor.shape[1], HEADS, HD)


def forward_block(running, query_part, key_part, value_part, allowed):

    def forward_compute(current):
        maximum, denominator, accumulated = current
        scores = jnp.einsum(
            "gqhd,gkhd->ghqk",
            split_heads(query_part),
            split_heads(key_part),
            preferred_element_type=jnp.float32,
        )
        masked = jnp.where(allowed[:, None], scores, NEGATIVE)
        new_max = jnp.maximum(maximum, jnp.max(masked, axis=-1))
        exponent = jnp.where(allowed[:, None], jnp.exp(masked - new_max[..., None]), 0.0)
        factor = jnp.exp(maximum - new_max)
        rescale = jnp.swapaxes(factor, 1, 2)[..., None]
        update = jnp.einsum(
            "ghqk,gkhd->gqhd",
            exponent.astype(jnp.bfloat16),
            split_heads(value_part),
            preferred_element_type=jnp.float32,
        )
        merged = (split_heads(accumulated) * rescale + update).reshape(accumulated.shape)
        return (new_max, denominator * factor + jnp.sum(exponent, axis=-1), merged)

    return lax.cond(jnp.any(allowed), forward_compute, lambda current: current, running)


def backward_block(
    query_part, grad_part, key_part, value_part, allowed, maximum, denominator, delta_sum
):
    scores = jnp.einsum(
        "gqhd,gkhd->ghqk",
        split_heads(query_part),
        split_heads(key_part),
        preferred_element_type=jnp.float32,
    )
    exponent = jnp.where(allowed[:, None], jnp.exp(scores - maximum[..., None]), 0.0)
    probability = exponent / denominator[..., None]
    prob_grad = jnp.einsum(
        "gqhd,gkhd->ghqk",
        split_heads(grad_part),
        split_heads(value_part),
        preferred_element_type=jnp.float32,
    )
    score_grad = (probability * (prob_grad - delta_sum[..., None])).astype(jnp.bfloat16)
    return (probability.astype(jnp.bfloat16), score_grad)


def general_shards(
    states,
    block_slot,
    cont_lengths,
    valid_mask,
    teacher,
    out_grad,
    predict,
    correct,
    norm_attn,
    w_query,
    w_key,
    w_value,
    w_out,
    norm_ffn,
    w_gate,
    w_up,
    w_down,
):
    groups, local_len = valid_mask.shape
    model_width = states.shape[3]
    row_count = groups * local_len
    group_len = block_slot.shape[1] * BLK
    gain_one, query_w, key_w, value_w, out_w, gain_two, gate_w, up_w, down_w = (
        lax.all_gather(norm_attn, "wsh", axis=0, tiled=True),
        lax.all_gather(w_query, "wsh", axis=0, tiled=True),
        lax.all_gather(w_key, "wsh", axis=0, tiled=True),
        lax.all_gather(w_value, "wsh", axis=0, tiled=True),
        lax.all_gather(w_out, "wsh", axis=0, tiled=True),
        lax.all_gather(norm_ffn, "wsh", axis=0, tiled=True),
        lax.all_gather(w_gate, "wsh", axis=0, tiled=True),
        lax.all_gather(w_up, "wsh", axis=0, tiled=True),
        lax.all_gather(w_down, "wsh", axis=0, tiled=True),
    )
    valid_float = valid_mask.astype(jnp.float32)
    valid_total = lax.psum(jnp.sum(valid_float), ("ctx", "wsh"))
    places, segments = token_places(block_slot, cont_lengths)
    offset = lax.axis_index("ctx") * local_len
    own_place = lax.dynamic_slice_in_dim(places, offset, local_len, 1)
    own_segment = lax.dynamic_slice_in_dim(segments, offset, local_len, 1)
    inputs = states.astype(jnp.float32)
    mixed_states = jnp.einsum("ij,gtjd->gtid", predict, inputs, precision=HIGHEST)
    active = mixed_states[:, :, 0].reshape(row_count, model_width)
    gain_first = gain_one.astype(jnp.float32)
    normed, factor_one = rms_forward(active, gain_first)
    normed_low = normed.astype(jnp.bfloat16)
    queries = (
        jnp.dot(normed_low, query_w, preferred_element_type=jnp.float32)
        .astype(jnp.bfloat16)
        .reshape(groups, local_len, model_width)
    )
    key_rows = (
        jnp.dot(normed_low, key_w, preferred_element_type=jnp.float32)
        .astype(jnp.bfloat16)
        .reshape(groups, local_len, model_width)
    )
    values = (
        jnp.dot(normed_low, value_w, preferred_element_type=jnp.float32)
        .astype(jnp.bfloat16)
        .reshape(groups, local_len, model_width)
    )
    initial = (
        jnp.full((groups, HEADS, local_len), NEGATIVE, jnp.float32),
        jnp.zeros((groups, HEADS, local_len), jnp.float32),
        jnp.zeros((groups, local_len, model_width), jnp.float32),
    )
    piece_keys = lax.all_gather(key_rows, "ctx", axis=1, tiled=True)
    piece_values = lax.all_gather(values, "ctx", axis=1, tiled=True)
    piece_len = piece_keys.shape[1]
    block_size = math.gcd(piece_len, local_len)

    def fold_one_block(current, block_index):
        begin = block_index * block_size
        key_part = lax.dynamic_slice_in_dim(piece_keys, begin, block_size, 1)
        value_part = lax.dynamic_slice_in_dim(piece_values, begin, block_size, 1)
        key_place = lax.dynamic_slice_in_dim(places, begin, block_size, 1)
        key_segment = lax.dynamic_slice_in_dim(segments, begin, block_size, 1)
        allowed = visible(own_place, own_segment, key_place, key_segment)
        return (forward_block(current, queries, key_part, value_part, allowed), None)

    finished, unused = lax.scan(
        fold_one_block, initial, jnp.arange(piece_len // block_size, dtype=jnp.int32)
    )
    maximum, denominator, accumulated = finished
    attended = (split_heads(accumulated) / jnp.swapaxes(denominator, 1, 2)[..., None]).reshape(
        row_count, model_width
    )
    attended_low = attended.astype(jnp.bfloat16)
    hidden = active + jnp.dot(attended_low, out_w, preferred_element_type=jnp.float32)
    gain_second = gain_two.astype(jnp.float32)
    normed_two, factor_two = rms_forward(hidden, gain_second)
    normed_two_low = normed_two.astype(jnp.bfloat16)
    gate_proj = jnp.dot(normed_two_low, gate_w, preferred_element_type=jnp.float32)
    up_proj = jnp.dot(normed_two_low, up_w, preferred_element_type=jnp.float32)
    inner_act, inner_pull = jax.vjp(
        lambda gate_in, up_in: jax.nn.gelu(gate_in, approximate=True) * up_in, gate_proj, up_proj
    )
    inner_low = inner_act.astype(jnp.bfloat16)
    result = hidden + jnp.dot(inner_low, down_w, preferred_element_type=jnp.float32)
    difference = (result - active).reshape(groups, local_len, 1, model_width)
    out_states = mixed_states + correct[None, None, :, None] * difference
    new_states = out_states.astype(jnp.bfloat16)
    loss_ratio = lax.axis_size("wsh") * groups * group_len / valid_total
    upstream = out_grad.astype(jnp.float32) + loss_ratio * valid_float[:, :, None, None] * (
        out_states - teacher.astype(jnp.float32)
    )
    correct_local = jnp.sum(upstream * difference, axis=(0, 1, 3))
    result_grad = jnp.einsum("i,gtid->gtd", correct, upstream, precision=HIGHEST).reshape(
        row_count, model_width
    )
    result_low = result_grad.astype(jnp.bfloat16)
    down_grad = jnp.einsum("rf,rd->fd", inner_low, result_low, preferred_element_type=jnp.float32)
    inner_grad = jnp.einsum("rd,fd->rf", result_low, down_w, preferred_element_type=jnp.float32)
    gate_grad, up_grad = inner_pull(inner_grad)
    gate_low = gate_grad.astype(jnp.bfloat16)
    up_low = up_grad.astype(jnp.bfloat16)
    gate_w_grad = jnp.einsum(
        "rd,rf->df", normed_two_low, gate_low, preferred_element_type=jnp.float32
    )
    up_w_grad = jnp.einsum("rd,rf->df", normed_two_low, up_low, preferred_element_type=jnp.float32)
    normed_two_grad = jnp.einsum(
        "rf,df->rd", gate_low, gate_w, preferred_element_type=jnp.float32
    ) + jnp.einsum("rf,df->rd", up_low, up_w, preferred_element_type=jnp.float32)
    hidden_norm_grad, gain_two_grad = rms_backward(hidden, factor_two, gain_second, normed_two_grad)
    hidden_grad = result_grad + hidden_norm_grad
    hidden_low = hidden_grad.astype(jnp.bfloat16)
    out_w_grad = jnp.einsum(
        "rc,rd->cd", attended_low, hidden_low, preferred_element_type=jnp.float32
    )
    attended_grad = jnp.einsum(
        "rd,cd->rc", hidden_low, out_w, preferred_element_type=jnp.float32
    ).astype(jnp.bfloat16)
    delta_sum = jnp.swapaxes(
        jnp.sum(
            split_heads(
                (attended_grad.astype(jnp.float32) * attended).reshape(
                    groups, local_len, model_width
                )
            ),
            axis=-1,
        ),
        1,
        2,
    )
    grad_local = attended_grad.reshape(groups, local_len, model_width)
    zero_grad = jnp.zeros((groups, local_len, model_width), jnp.float32)
    all_keys, all_values = (
        lax.all_gather(key_rows, "ctx", axis=1, tiled=True),
        lax.all_gather(values, "ctx", axis=1, tiled=True),
    )

    def query_step(current, block_index):
        begin = block_index * local_len
        key_part = lax.dynamic_slice_in_dim(all_keys, begin, local_len, 1)
        value_part = lax.dynamic_slice_in_dim(all_values, begin, local_len, 1)
        key_place = lax.dynamic_slice_in_dim(places, begin, local_len, 1)
        key_segment = lax.dynamic_slice_in_dim(segments, begin, local_len, 1)
        allowed = visible(own_place, own_segment, key_place, key_segment)

        def query_compute(query_sum):
            prob_low, score_grad = backward_block(
                queries, grad_local, key_part, value_part, allowed, maximum, denominator, delta_sum
            )
            return query_sum + jnp.einsum(
                "ghqk,gkhd->gqhd",
                score_grad,
                split_heads(key_part),
                preferred_element_type=jnp.float32,
            ).reshape(groups, local_len, model_width)

        return (
            lax.cond(jnp.any(allowed), query_compute, lambda query_sum: query_sum, current),
            None,
        )

    finished, unused = lax.scan(
        query_step, zero_grad, jnp.arange(group_len // local_len, dtype=jnp.int32)
    )
    term_rows = local_len * lax.axis_size("ctx")
    key_block_size = math.gcd(term_rows, local_len)

    def key_one_block(block_index):
        begin = block_index * key_block_size
        key_part = lax.dynamic_slice_in_dim(all_keys, begin, key_block_size, 1)
        value_part = lax.dynamic_slice_in_dim(all_values, begin, key_block_size, 1)
        key_place = lax.dynamic_slice_in_dim(places, begin, key_block_size, 1)
        key_segment = lax.dynamic_slice_in_dim(segments, begin, key_block_size, 1)
        allowed = visible(own_place, own_segment, key_place, key_segment)

        def one_compute(unused_arg):
            prob_low, score_grad = backward_block(
                queries, grad_local, key_part, value_part, allowed, maximum, denominator, delta_sum
            )
            key_add = jnp.einsum(
                "ghqk,gqhd->kghd",
                score_grad,
                split_heads(queries),
                preferred_element_type=jnp.float32,
            ).reshape(key_block_size, groups, model_width)
            value_add = jnp.einsum(
                "ghqk,gqhd->kghd",
                prob_low,
                split_heads(grad_local),
                preferred_element_type=jnp.float32,
            ).reshape(key_block_size, groups, model_width)
            return jnp.stack([key_add, value_add], axis=1)

        return lax.cond(
            jnp.any(allowed),
            one_compute,
            lambda unused_arg: jnp.zeros((key_block_size, 2, groups, model_width), jnp.float32),
            0,
        )

    summed = lax.psum_scatter(
        lax.map(key_one_block, jnp.arange(term_rows // key_block_size, dtype=jnp.int32))
        .reshape(term_rows, 2, groups, model_width)
        .astype(jnp.bfloat16),
        "ctx",
        scatter_dimension=0,
        tiled=True,
    ).astype(jnp.float32)
    key_grad = jnp.swapaxes(summed[:, 0], 0, 1)
    value_grad = jnp.swapaxes(summed[:, 1], 0, 1)
    query_low = finished.reshape(row_count, model_width).astype(jnp.bfloat16)
    key_low = key_grad.reshape(row_count, model_width).astype(jnp.bfloat16)
    value_low = value_grad.reshape(row_count, model_width).astype(jnp.bfloat16)
    query_w_grad = jnp.einsum(
        "rc,rd->cd", normed_low, query_low, preferred_element_type=jnp.float32
    )
    key_w_grad = jnp.einsum("rc,rd->cd", normed_low, key_low, preferred_element_type=jnp.float32)
    value_w_grad = jnp.einsum(
        "rc,rd->cd", normed_low, value_low, preferred_element_type=jnp.float32
    )
    normed_grad = (
        jnp.einsum("rd,cd->rc", query_low, query_w, preferred_element_type=jnp.float32)
        + jnp.einsum("rd,cd->rc", key_low, key_w, preferred_element_type=jnp.float32)
        + jnp.einsum("rd,cd->rc", value_low, value_w, preferred_element_type=jnp.float32)
    )
    active_norm_grad, gain_one_grad = rms_backward(active, factor_one, gain_first, normed_grad)
    active_grad = (hidden_grad + active_norm_grad - result_grad).reshape(
        groups, local_len, 1, model_width
    )
    mixed_grad = jnp.concatenate([upstream[:, :, :1] + active_grad, upstream[:, :, 1:]], axis=2)
    predict_local = jnp.einsum("gtid,gtjd->ij", mixed_grad, inputs, precision=HIGHEST)
    states_grad = jnp.einsum("ij,gtid->gtjd", predict, mixed_grad, precision=HIGHEST).astype(
        jnp.bfloat16
    )
    predict_grad, correct_grad = lax.psum((predict_local, correct_local), ("ctx", "wsh"))
    (
        gain_one_rows,
        query_rows,
        key_grad_rows,
        value_rows,
        out_rows,
        gain_two_rows,
        gate_rows,
        up_rows,
        down_rows,
    ) = (
        lax.psum_scatter(
            gain_one_grad.astype(jnp.bfloat16), "wsh", scatter_dimension=0, tiled=True
        ).astype(jnp.float32),
        lax.psum_scatter(
            query_w_grad.astype(jnp.bfloat16), "wsh", scatter_dimension=0, tiled=True
        ).astype(jnp.float32),
        lax.psum_scatter(
            key_w_grad.astype(jnp.bfloat16), "wsh", scatter_dimension=0, tiled=True
        ).astype(jnp.float32),
        lax.psum_scatter(
            value_w_grad.astype(jnp.bfloat16), "wsh", scatter_dimension=0, tiled=True
        ).astype(jnp.float32),
        lax.psum_scatter(
            out_w_grad.astype(jnp.bfloat16), "wsh", scatter_dimension=0, tiled=True
        ).astype(jnp.float32),
        lax.psum_scatter(
            gain_two_grad.astype(jnp.bfloat16), "wsh", scatter_dimension=0, tiled=True
        ).astype(jnp.float32),
        lax.psum_scatter(
            gate_w_grad.astype(jnp.bfloat16), "wsh", scatter_dimension=0, tiled=True
        ).astype(jnp.float32),
        lax.psum_scatter(
            up_w_grad.astype(jnp.bfloat16), "wsh", scatter_dimension=0, tiled=True
        ).astype(jnp.float32),
        lax.psum_scatter(
            down_grad.astype(jnp.bfloat16), "wsh", scatter_dimension=0, tiled=True
        ).astype(jnp.float32),
    )
    totals = (
        lax.psum(gain_one_rows.astype(jnp.bfloat16), "ctx").astype(jnp.float32),
        lax.psum(query_rows.astype(jnp.bfloat16), "ctx").astype(jnp.float32),
        lax.psum(key_grad_rows.astype(jnp.bfloat16), "ctx").astype(jnp.float32),
        lax.psum(value_rows.astype(jnp.bfloat16), "ctx").astype(jnp.float32),
        lax.psum(out_rows.astype(jnp.bfloat16), "ctx").astype(jnp.float32),
        lax.psum(gain_two_rows.astype(jnp.bfloat16), "ctx").astype(jnp.float32),
        lax.psum(gate_rows.astype(jnp.bfloat16), "ctx").astype(jnp.float32),
        lax.psum(up_rows.astype(jnp.bfloat16), "ctx").astype(jnp.float32),
        lax.psum(down_rows.astype(jnp.bfloat16), "ctx").astype(jnp.float32),
    )
    return (new_states, states_grad, predict_grad, correct_grad) + tuple(totals)


MESH = pl.DeviceIdType.MESH
F32 = jnp.float32
BF16 = jnp.bfloat16
CHIPS = 4
VMEM_LIMIT = 60 * 2**20
DMA = pltpu.SemaphoreType.DMA


def place_on_mesh():
    ctx = lax.axis_index("ctx")
    depth = lax.axis_index("wsh")
    chip = ctx // 2
    core = ctx % 2
    chip_x = chip + 1 - 2 * (chip % 2)
    chip_y = chip + 2 - 4 * (chip // 2)
    return depth, chip, core, chip_x, chip_y, 3 - chip


def signal_all(devices):
    barrier = pltpu.get_barrier_semaphore()
    for device in devices:
        pl.semaphore_signal(barrier, inc=1, device_id=device, device_id_type=MESH)


def wait_all(devices):
    pl.semaphore_wait(pltpu.get_barrier_semaphore(), len(devices))


def remote(src, dst, send, recv, index, device):
    return pltpu.make_async_remote_copy(
        src_ref=src,
        dst_ref=dst,
        send_sem=send.at[index],
        recv_sem=recv.at[index],
        device_id=device,
        device_id_type=MESH,
    )


def comm_params(collective_id):
    return pltpu.CompilerParams(
        collective_id=collective_id, has_side_effects=True, vmem_limit_bytes=VMEM_LIMIT
    )


ANY = pl.BlockSpec(memory_space=pl.ANY)
VM = pl.BlockSpec(memory_space=pltpu.VMEM)
SM = pl.BlockSpec(memory_space=pltpu.SMEM)


def ring_sends(own, out, slot_of, chip, core, depth, chip_x, chip_y, send, recv):
    half = own.shape[0] // 2
    top, low = pl.ds(0, half), pl.ds(half, half)
    dev_x, dev_y = (2 * chip_x + core, depth), (2 * chip_y + core, depth)
    here = slot_of(chip)
    return [
        remote(own.at[top], out.at[here, top], send, recv, 0, dev_x),
        remote(own.at[low], out.at[here, low], send, recv, 1, dev_y),
        remote(own.at[low], out.at[here, low], send, recv, 2, dev_x),
        remote(own.at[top], out.at[here, top], send, recv, 3, dev_y),
        remote(out.at[slot_of(chip_x), top], out.at[slot_of(chip_x), top], send, recv, 4, dev_y),
        remote(out.at[slot_of(chip_y), low], out.at[slot_of(chip_y), low], send, recv, 5, dev_x),
    ]


NT = (((1,), (1,)), ((), ()))
TN = (((0,), (0,)), ((), ()))
TILE = 256
ROWS = 32
LOCAL_HEADS = HEADS // CHIPS
CHIP_COLS = LOCAL_HEADS * HD


def head_mask(rows, head):
    lane = lax.broadcasted_iota(jnp.int32, (rows, CHIP_COLS), 1)
    return (lane >= head * HD) & (lane < (head + 1) * HD)


def aligned(index, size):
    return pl.ds(pl.multiple_of(index * size, size), size)


def norm_factor(rows):
    return lax.rsqrt(jnp.mean(rows * rows, axis=1, keepdims=True) + EPSILON)


def as_column(row):
    return jnp.broadcast_to(row, (8, row.shape[1])).T[:, 0:1]


def mix(states_ref, at, p_ref, i):
    return p_ref[i, 0] * states_ref[at, 0, :].astype(F32) + p_ref[i, 1] * states_ref[at, 1, :].astype(F32)


def plane_sum(parts, near_in, far_in, chip, core, depth, chip_x, chip_y, chip_d, send, recv):
    half = parts.shape[1] // 2
    top, low = pl.ds(0, half), pl.ds(half, half)
    dev_x, dev_y = (2 * chip_x + core, depth), (2 * chip_y + core, depth)
    copies = [
        remote(parts.at[chip_d, top], far_in.at[0], send, recv, 0, dev_x),
        remote(parts.at[chip_d, low], far_in.at[1], send, recv, 1, dev_y),
        remote(parts.at[chip_x, top], near_in.at[0, top], send, recv, 2, dev_x),
        remote(parts.at[chip_y, low], near_in.at[1, low], send, recv, 3, dev_y),
        remote(parts.at[chip_y, top], near_in.at[1, top], send, recv, 4, dev_y),
        remote(parts.at[chip_x, low], near_in.at[0, low], send, recv, 5, dev_x),
    ]

    def give(i):
        for copy in (copies[:2] if i == 2 else copies[2 + i : 3 + i]):
            copy.start()

    def relay():
        for i, (c, rows) in enumerate(((chip_y, slice(0, half)), (chip_x, slice(half, 2 * half)))):
            copies[i].wait_recv()
            parts[c, rows] = (parts[c, rows].astype(F32) + far_in[i].astype(F32)).astype(BF16)
            copies[4 + i].start()

    def receive():
        for copy in copies[2:]:
            copy.wait_recv()

    return give, relay, receive, copies


def plane_peers(chip, core, depth, chip_x, chip_y, chip_d):
    same = [(2 * c + core, depth) for c in (chip_x, chip_y, chip_d)]
    return same + [(2 * c + 1 - core, depth) for c in (chip, chip_x, chip_y, chip_d)]


def total_over_mesh(own_ref, arrived, staged, far, across, peers, bsend, brecv, csend, crecv):
    first = [remote(own_ref, arrived.at[i], bsend, brecv, i, d) for i, d in enumerate(across)]
    second = [remote(staged, far.at[i], csend, crecv, i, d) for i, d in enumerate(peers)]

    def start():
        for copy in first:
            copy.start()

    def turn():
        total = own_ref[...]
        for i, copy in enumerate(first):
            copy.wait_recv()
        for i in range(len(first)):
            total = total + arrived[i]
        staged[...] = total
        for copy in second:
            copy.start()

    def end():
        for copy in second:
            copy.wait_recv()
        total = staged[...]
        for i in range(len(second)):
            total = total + far[i]
        for copy in first + second:
            copy.wait_send()
        return total

    return start, turn, end


def total_scratch(shape, depths):
    return [
        pltpu.VMEM((depths - 1,) + shape, F32),
        pltpu.VMEM(shape, F32),
        pltpu.VMEM((2 * CHIPS - 1,) + shape, F32),
        DMA((depths - 1,)),
        DMA((depths - 1,)),
        DMA((2 * CHIPS - 1,)),
        DMA((2 * CHIPS - 1,)),
    ]


def gelu_parts(v):
    scale = math.sqrt(2 / math.pi)
    square = v * v
    t = jnp.tanh(scale * v * (1.0 + 0.044715 * square))
    rise = 0.5 * (1.0 + t)
    return v * rise, rise + 0.5 * v * (1.0 - t * t) * scale * (1.0 + 0.134145 * square)


def pair_places(slots_ref, pair):
    one, two = slots_ref[2 * pair], slots_ref[2 * pair + 1]
    second = (one >= PROMPT // BLK).astype(jnp.int32)
    return second, jnp.minimum(one, two), jnp.maximum(one, two)


def own_pair(pair, per_device):
    core = lax.axis_index("ctx") % 2
    pairs = per_device // 2
    return (pair // pairs) * per_device + core * pairs + pair % pairs


PER_TILE = TILE // BLK


def fill_bias(bias, kind, tile_step, slots_ref, lengths_ref, per_device, group_pairs):
    lane = lax.broadcasted_iota(jnp.int32, (1, TILE), 1)
    high = jnp.zeros((1, TILE), jnp.int32)
    for i in range(PER_TILE):
        _, prompt, cont = pair_places(slots_ref, own_pair(tile_step * PER_TILE + i, per_device))
        block = prompt if kind == 0 else cont
        high = jnp.where(lane >= i * BLK, (block - i) * BLK + lane, high)
    low = jnp.zeros((1, TILE), jnp.int32)
    if kind == 1:
        start = PROMPT
        for i in range(lengths_ref.shape[0]):
            low = jnp.where(high >= start, start, low)
            start = start + lengths_ref[i]
    offset = lax.broadcasted_iota(jnp.int32, (BLK, TILE), 0)

    def one_block(pair, _):
        _, prompt, cont = pair_places(slots_ref, pair)
        base = (prompt if kind == 0 else cont) * BLK
        seen = offset <= high - base
        if kind == 1:
            seen = seen & (offset >= low - base)
        bias[pair // PER_TILE, aligned(pair % PER_TILE, BLK), 0:TILE] = jnp.where(seen, 0.0, NEGATIVE)
        return 0

    lax.fori_loop(0, group_pairs, one_block, 0)


def either(second, one, two):
    swap = second == 1
    return jnp.where(swap, two, one), jnp.where(swap, one, two)


def to_pair_order(source, target, slots_ref, group_pairs):
    def one_pair(pair, _):
        second, _, _ = pair_places(slots_ref, pair)
        first, last = either(second, source[aligned(2 * pair, BLK), :], source[aligned(2 * pair + 1, BLK), :])
        target[aligned(pair, BLK), :] = first
        target[aligned(group_pairs + pair, BLK), :] = last
        return 0

    lax.fori_loop(0, group_pairs, one_pair, 0)


def own_to_pair_order(source, target, slots_ref, pairs, per_device):
    def one_pair(pair, _):
        second, _, _ = pair_places(slots_ref, own_pair(pair, per_device))
        first, last = either(second, source[aligned(2 * pair, BLK), :], source[aligned(2 * pair + 1, BLK), :])
        target[aligned(pair, BLK), :] = first
        target[aligned(pairs + pair, BLK), :] = last
        return 0

    lax.fori_loop(0, pairs, one_pair, 0)


def own_to_slot_order(source, target, slots_ref, pairs, per_device):
    def one_pair(pair, _):
        second, _, _ = pair_places(slots_ref, own_pair(pair, per_device))
        first, last = either(second, source[aligned(pair, BLK), :], source[aligned(pairs + pair, BLK), :])
        target[aligned(2 * pair, BLK), :] = first
        target[aligned(2 * pair + 1, BLK), :] = last
        return 0

    lax.fori_loop(0, pairs, one_pair, 0)


def line_reduce(pieces, acc, up_in, down_in, up_out, down_out, sems):
    depth, chip, core, _, _, _ = place_on_mesh()
    depths = pieces.shape[0]
    last = depths - 1
    up_send, up_recv, down_send, down_recv = sems
    above = (2 * chip + core, lax.rem(depth + 1, depths))
    below = (2 * chip + core, lax.rem(depth + last, depths))

    def up(source, k):
        return remote(source, up_in.at[k], up_send, up_recv, k, above)

    def down(source, k):
        return remote(source, down_in.at[k], down_send, down_recv, k, below)

    def start():
        @pl.when(depth == 0)
        def _():
            for k in range(last):
                up(pieces.at[last - k], k).start()

        @pl.when(depth == last)
        def _():
            for k in range(last):
                down(pieces.at[k], k).start()

    def hop(k):
        @pl.when((depth >= 1) & (depth <= k))
        def _():
            up(up_in.at[k - 1], k - 1).wait_recv()
            mine = pieces[jnp.clip(depth + last - k, 0, last)]
            up_out[k - 1] = (mine.astype(F32) + up_in[k - 1].astype(F32)).astype(BF16)
            up(up_out.at[k - 1], k).start()

        @pl.when((depth <= last - 1) & (depth >= last - k))
        def _():
            down(down_in.at[k - 1], k - 1).wait_recv()
            mine = pieces[jnp.clip(depth + k - last, 0, last)]
            down_out[k - 1] = (mine.astype(F32) + down_in[k - 1].astype(F32)).astype(BF16)
            down(down_out.at[k - 1], k).start()

    def result():
        acc[...] = pieces[depth].astype(F32)

        @pl.when(depth >= 1)
        def _():
            up(up_in.at[last - 1], last - 1).wait_recv()
            acc[...] += up_in[last - 1].astype(F32)

        @pl.when(depth <= last - 1)
        def _():
            down(down_in.at[last - 1], last - 1).wait_recv()
            acc[...] += down_in[last - 1].astype(F32)

    def finish():
        @pl.when(depth == 0)
        def _():
            for k in range(last):
                up(pieces.at[last - k], k).wait_send()

        @pl.when(depth == last)
        def _():
            for k in range(last):
                down(pieces.at[k], k).wait_send()

        for k in range(1, last):

            @pl.when((depth >= 1) & (depth <= k))
            def _(k=k):
                up(up_out.at[k - 1], k).wait_send()

            @pl.when((depth <= last - 1) & (depth >= last - k))
            def _(k=k):
                down(down_out.at[k - 1], k).wait_send()

    return start, hop, result, finish


def forward(
    slots, lengths, predict, correct, states, out_grad, teacher, valid, gain_one, gain_two,
    w_query, w_key, w_value, w_out, w_gate, w_up, w_down, collective_id,
):
    rows, _, width = states.shape
    shard = w_query.shape[0]
    half = shard // 2
    depths = width // shard
    hidden_cols = w_gate.shape[1]
    columns = hidden_cols // CHIPS
    split = columns // depths
    out_rows = shard // CHIPS
    blocks = rows // ROWS
    col_tiles = columns // TILE
    tokens = 2 * CHIPS * rows
    queries = CHIPS * rows
    tiles = queries // TILE
    per_device = rows // BLK
    group_pairs = tokens // (2 * BLK)
    pairs = queries // (2 * BLK)
    mesh_tokens = tokens * depths
    piece_lanes = 3 * CHIP_COLS

    def kernel(
        slots_ref, lengths_ref, p_ref, c_ref, s_ref, g_in, t_in, v_ref, g1_ref, g2_ref,
        wq_ref, wk_ref, wv_ref, wo_ref, wg_ref, wu_ref, wd_ref,
        new_out, up0_out, up1_out, hg_out, da_ref, dwo_ref, ffa_ref, ffb_ref, sums_ref,
        x_out, w_out_ref, q_out, k_out, v_out, oT_out, lse_ref,
        new_ref, up0_ref, up1_ref, hg_ref, all_rows, w_all, q_pairs, k_pairs, v_pairs, oT_ref, dwo, dwo_other,
        g_ref, t_ref, w_ff, w_wo, qkv, att_all, packs, packed_in, packed_grad, hidden, own, x_rows, r_rows, xT, innerT, inner, gate, up, gate_low, up_low,
        own_weight, part1, part2, got1, got2, far1, far2, dw, dw_other, a_up, a_down, buf, wide, count, q_slot, k_slot, v_slot, vT,
        lsend, fsend, frecv, fosend, forecv, qsend, qrecv, qosend, qorecv,
        osend, orecv, oosend, oorecv, opsend, oprecv,
        rsend, rrecv, rosend, rorecv, send0, recv0, send1, recv1, send2, recv2, send3, recv3,
        ag1s, ag1r, ag2s, ag2r, dsend, drecv, osems, xsems, *rest,
    ):
        a_sems, total_refs = rest[:4], rest[4:]
        stores = []

        def store(index, source, target):
            copy = pltpu.make_async_copy(source, target, osems.at[index])
            copy.start()
            stores.append(copy)

        depth, chip, core, chip_x, chip_y, chip_d = place_on_mesh()
        near = [(c, (2 * c + core, depth)) for c in (chip_x, chip_y, chip_d)]
        other = (2 * chip + 1 - core, depth)
        across = [
            (2 * chip + core, lax.rem(depth + step, depths)) for step in range(1, depths)
        ]
        peers = plane_peers(chip, core, depth, chip_x, chip_y, chip_d)
        signal_all(peers + across)

        mine = pl.ds(core * half, half)
        loads = [
            pltpu.make_async_copy(w.at[mine], buf.at[i], lsend.at[i])
            for i, w in enumerate((wq_ref, wk_ref, wv_ref))
        ] + [
            pltpu.make_async_copy(wg_ref.at[mine], wide.at[0], lsend.at[3]),
            pltpu.make_async_copy(wu_ref.at[mine], wide.at[1], lsend.at[4]),
            pltpu.make_async_copy(
                wd_ref.at[pl.ds(chip * split + core * half, half)], w_ff.at[2, depth, core], lsend.at[5]
            ),
            pltpu.make_async_copy(
                wo_ref.at[pl.ds(chip * out_rows, out_rows)], w_wo.at[depth, chip], lsend.at[6]
            ),
            pltpu.make_async_copy(g_in, g_ref, lsend.at[7]),
            pltpu.make_async_copy(t_in, t_ref, lsend.at[8]),
        ]
        for copy in loads:
            copy.start()
        count[...] = jnp.broadcast_to(
            jnp.sum(v_ref[...].astype(F32), axis=1, keepdims=True), count.shape
        )

        def input_norm(i, _):
            at = aligned(i, ROWS)
            active = mix(s_ref, at, p_ref, 0)
            own[0, at, :] = (active * norm_factor(active)).astype(BF16)
            return 0

        lax.fori_loop(0, blocks, input_norm, 0)

        def gain_column(ref):
            both = jnp.broadcast_to(ref[...].astype(F32).reshape(1, shard), (8, shard)).T
            return jnp.where(core == 0, both[:half, 0:1], both[half:, 0:1])

        one, two = gain_column(g1_ref), gain_column(g2_ref)
        wait_all(peers + across)

        def slot(chip_index):
            return 2 * chip_index + core

        start_count, turn_count, end_count = total_over_mesh(
            count, *total_refs[:3], across, peers, *total_refs[3:]
        )
        start_count()
        ring0 = ring_sends(
            own.at[0], all_rows, slot, chip, core, depth, chip_x, chip_y, rsend, rrecv
        )
        for copy in ring0[:4]:
            copy.start()

        def rows_to_other(index, chip_index):
            ref = all_rows.at[slot(chip_index)]
            return remote(own.at[0] if index == 0 else ref, ref, rosend, rorecv, index, other)

        shared0 = [rows_to_other(i, c) for i, c in enumerate((chip, chip_x, chip_y, chip_d))]
        shared0[0].start()
        all_rows[slot(chip)] = own[0]

        for copy in loads[:3]:
            copy.wait()
        for p in range(CHIPS):

            @pl.when(chip == p)
            def _(p=p):
                cols = jnp.concatenate(
                    [buf[i, :, p * CHIP_COLS : (p + 1) * CHIP_COLS].astype(F32) for i in range(3)], axis=1
                )
                qkv[depth, core] = (cols * one).astype(BF16)

        qkv_mine = qkv.at[depth, core]
        q_copies = [
            remote(qkv_mine, qkv_mine, qsend, qrecv, i, device) for i, device in enumerate(across)
        ]
        q_shared = [remote(qkv_mine, qkv_mine, qosend, qorecv, 0, other)]
        for copy in q_copies + q_shared:
            copy.start()

        loads[6].wait()
        o_copies = [
            remote(w_wo.at[depth, chip], w_wo.at[depth, chip], osend, orecv, i, device)
            for i, device in enumerate(across)
        ]
        o_shared = []
        for i in range(depths - 1):
            came = w_wo.at[lax.rem(depth + depths - 1 - i, depths), chip]
            o_shared.append(remote(came, came, oosend, oorecv, i, other))

        def carried(i, act):
            pl.when(core == (i + 1) % 2)(act)

        def not_carried(i, act):
            pl.when(core != (i + 1) % 2)(act)

        for i in range(depths - 1):
            carried(i, o_copies[i].start)

        for copy in loads[3:6]:
            copy.wait()
        for p in range(CHIPS):

            @pl.when(chip == p)
            def _(p=p):
                for i in range(2):
                    cols = jnp.concatenate(
                        [
                            wide[i, :, (z * CHIPS + p) * split : (z * CHIPS + p + 1) * split].astype(F32)
                            for z in range(depths)
                        ],
                        axis=1,
                    )
                    w_ff[i, depth, core] = (cols * two).astype(BF16)

        line_up = (2 * chip + core, lax.rem(depth + 1, depths))
        line_down = (2 * chip + core, lax.rem(depth + depths - 1, depths))
        hops = []
        for stage in range(1, depths):
            for direction, device, index in ((1, line_up, stage - 1), (-1, line_down, depths + stage - 2)):
                goes = jnp.clip(depth - direction * (stage - 1), 0, depths - 1)
                comes = jnp.clip(depth - direction * stage, 0, depths - 1)
                piece, came = w_ff.at[:, goes, core], w_ff.at[:, comes, core]
                if direction == 1:
                    sends, receives = (depth >= stage - 1) & (depth < depths - 1), depth >= stage
                else:
                    sends, receives = (depth <= depths - stage) & (depth > 0), depth < depths - stage
                hops.append(
                    (
                        stage,
                        sends,
                        receives,
                        remote(piece, piece, fsend, frecv, index, device),
                        remote(came, came, fosend, forecv, index, other),
                    )
                )
        ff_mine = remote(w_ff.at[:, depth, core], w_ff.at[:, depth, core], fosend, forecv, 2 * depths - 2, other)
        ff_mine.start()

        def send_hop(stage):
            for at, sends, _, hop, _ in hops:
                if at == stage:
                    pl.when(sends)(hop.start)

        def take_hop(stage):
            for at, _, receives, hop, share in hops:
                if at == stage:

                    @pl.when(receives)
                    def _(hop=hop, share=share):
                        hop.wait_recv()
                        share.start()

        send_hop(1)
        turn_count()
        ring0[0].wait_recv()
        ring0[4].start()
        ring0[1].wait_recv()
        ring0[5].start()
        for i in range(depths - 1):
            q_copies[i].wait_recv()
            came = qkv.at[lax.rem(depth + depths - 1 - i, depths), core]
            share = remote(came, came, qosend, qorecv, 1 + i, other)
            share.start()
            q_shared.append(share)
        ring0[2].wait_recv()
        shared0[1].start()
        ring0[3].wait_recv()
        shared0[2].start()
        for copy in q_shared:
            copy.wait_recv()
        for i in range(3):
            for z in range(depths):
                for c in range(2):
                    at = (z * 2 + c) * half
                    w_all[i, at : at + half, :] = qkv[z, c, :, i * CHIP_COLS : (i + 1) * CHIP_COLS]

        def project(device_slot, with_queries):
            x = all_rows[device_slot]
            at = aligned(device_slot, rows)
            k_slot[at, :] = jnp.dot(x, w_all[1], preferred_element_type=F32).astype(BF16)
            v_slot[at, :] = jnp.dot(x, w_all[2], preferred_element_type=F32).astype(BF16)
            if with_queries:
                q_slot[aligned(device_slot // 2, rows), :] = jnp.dot(
                    x, w_all[0], preferred_element_type=F32
                ).astype(BF16)

        for c in (chip, chip_x, chip_y):
            project(slot(c), True)
        for i, c in enumerate((chip, chip_x, chip_y)):
            shared0[i].wait_recv()
            project(2 * c + 1 - core, False)
        ring0[4].wait_recv()
        ring0[5].wait_recv()
        shared0[3].start()
        project(slot(chip_d), True)
        for i in range(depths - 1):

            def came_here(i=i):
                o_copies[i].wait_recv()
                o_shared[i].start()

            carried(i, came_here)
        for i in range(depths - 1):
            not_carried(i, o_shared[i].wait_recv)
        carry = pl.ds(core * (depths // 2), depths // 2)
        o_plane = [
            remote(w_wo.at[carry, chip], w_wo.at[carry, chip], opsend, oprecv, i, device)
            for i, (_, device) in enumerate(near)
        ]
        for copy in o_plane:
            copy.start()
        o_across = [
            remote(w_wo.at[carry, c], w_wo.at[carry, c], opsend, oprecv, 3 + i, other)
            for i, (c, _) in enumerate(near)
        ]
        shared0[3].wait_recv()
        project(2 * chip_d + 1 - core, False)

        for i in range(CHIPS):
            x_copy = pltpu.make_async_copy(all_rows.at[2 * i + core], x_out.at[i], xsems.at[i])
            x_copy.start()
            stores.append(x_copy)
        store(0, w_all, w_out_ref)

        to_pair_order(k_slot, k_pairs, slots_ref, group_pairs)
        to_pair_order(v_slot, v_pairs, slots_ref, group_pairs)
        own_to_pair_order(q_slot, q_pairs, slots_ref, pairs, per_device)

        store(1, q_pairs, q_out)
        store(2, k_pairs, k_out)
        store(3, v_pairs, v_out)

        def turn_values(i, _):
            vT[:, aligned(i, TILE)] = v_pairs[aligned(i, TILE), :].T
            return 0

        lax.fori_loop(0, tokens // TILE, turn_values, 0)
        half_keys = group_pairs * BLK
        half_tiles = half_keys // TILE
        scores, bias = gate, up

        def cell(k_tile):
            lanes = (k_tile // CHIPS) * TILE
            return k_tile % CHIPS, slice(lanes, lanes + TILE)

        def attend(kind, step):
            tile = kind * (tiles // 2) + step
            key_tiles = half_tiles * (kind + 1)
            q = q_pairs[aligned(tile, TILE), :]
            fill_bias(bias, kind, step, slots_ref, lengths_ref, per_device, group_pairs)
            for head in range(LOCAL_HEADS):
                heads = slice(head * HD, (head + 1) * HD)
                q_head = jnp.where(head_mask(TILE, head), q, jnp.zeros_like(q))
                top = jnp.full((1, TILE), NEGATIVE, F32)
                for k_tile in range(key_tiles):
                    s = lax.dot_general(
                        k_pairs[k_tile * TILE : (k_tile + 1) * TILE, :], q_head, NT, preferred_element_type=F32
                    )
                    if k_tile >= key_tiles - half_tiles:
                        s = s + bias[k_tile - (key_tiles - half_tiles), :, 0:TILE]
                    index, lanes = cell(k_tile)
                    scores[index, :, lanes] = s
                    top = jnp.maximum(top, jnp.max(s, axis=0, keepdims=True))
                total = jnp.zeros((1, TILE), F32)
                out = jnp.zeros((HD, TILE), F32)
                for k_tile in range(key_tiles):
                    index, lanes = cell(k_tile)
                    e = jnp.exp(scores[index, :, lanes] - top)
                    total = total + jnp.sum(e, axis=0, keepdims=True)
                    out = out + jnp.dot(
                        vT[heads, k_tile * TILE : (k_tile + 1) * TILE], e.astype(BF16), preferred_element_type=F32
                    )
                oT_ref[tile, heads, :] = out / total
                lse_ref[tile, head] = top + jnp.log(total)
            q_slot[aligned(tile, TILE), :] = oT_ref[tile].T.astype(BF16)

        def both_steps(kind):
            def body(step, _):
                attend(kind, step)
                return 0

            lax.fori_loop(0, tiles // 2, body, 0)

        both_steps(1)
        take_hop(1)
        send_hop(2)
        for copy, passed in zip(o_plane, o_across):
            copy.wait_recv()
            passed.start()
        both_steps(0)

        store(4, oT_ref, oT_out)
        own_to_slot_order(q_slot, k_slot, slots_ref, pairs, per_device)
        half_rows = rows // 2

        def pack(value):
            return jnp.concatenate([value[:half_rows].astype(F32), value[half_rows:].astype(F32)], axis=1).astype(BF16)

        def unpack(target, packed):
            target[0:half_rows, :] = packed[:, 0:CHIP_COLS]
            target[half_rows:rows, :] = packed[:, CHIP_COLS : 2 * CHIP_COLS]

        for c in range(CHIPS):
            packs[c] = pack(k_slot[c * rows : (c + 1) * rows, :])
        sends0 = [
            remote(packs.at[c], packed_in.at[i], send0, recv0, i, device)
            for i, (c, device) in enumerate(near)
        ]
        for copy in sends0:
            copy.start()
        unpack(att_all.at[chip], packs[chip])
        take_hop(2)
        send_hop(3)
        for copy in o_across:
            copy.wait_recv()
        for copy in sends0:
            copy.wait()
        for i, (c, _) in enumerate(near):
            unpack(att_all.at[c], packed_in[i])

        def w_out_rows(p):
            return w_wo[p].reshape(CHIP_COLS, width)

        for p in range(CHIPS):
            term = jnp.dot(att_all[p], w_out_rows(p), preferred_element_type=F32)
            hidden[...] = term if p == 0 else hidden[...] + term

        def first_norm(i, _):
            at = aligned(i, ROWS)
            h = hidden[at, :] + mix(s_ref, at, p_ref, 0)
            hidden[at, :] = h
            own[1, at, :] = (h * norm_factor(h)).astype(BF16)
            return 0

        lax.fori_loop(0, blocks, first_norm, 0)

        def ring(source, target, send, recv):
            return ring_sends(
                source, target, lambda c: c, chip, core, depth, chip_x, chip_y, send, recv
            )

        ring1 = ring(own.at[1], x_rows, ag1s, ag1r)
        for copy in ring1[:4]:
            copy.start()
        x_rows[chip] = own[1]
        ring1[0].wait_recv()
        ring1[4].start()
        ring1[1].wait_recv()
        ring1[5].start()
        take_hop(3)
        ff_mine.wait_recv()
        for _, _, receives, _, share in hops:
            pl.when(receives)(share.wait_recv)

        def w_rows(i):
            return w_ff[i].reshape(width, columns)

        def ff_forward(c):
            x = x_rows[c]
            for n in range(col_tiles):
                cols = slice(n * TILE, (n + 1) * TILE)
                g = jnp.dot(x, w_rows(0)[:, cols], preferred_element_type=F32)
                u = jnp.dot(x, w_rows(1)[:, cols], preferred_element_type=F32)
                gate[c, :, cols] = g
                up[c, :, cols] = u
                inner[c, :, cols] = (gelu_parts(g)[0] * u).astype(BF16)
            return jnp.dot(inner[c], w_rows(2), preferred_element_type=F32)

        give1, relay1, receive1, sends1 = plane_sum(
            part1, got1, far1, chip, core, depth, chip_x, chip_y, chip_d, send1, recv1
        )
        up0_ref[...] = ff_forward(chip)
        for i, (c, _) in enumerate(near):
            if i < 2:
                ring1[2 + i].wait_recv()
            else:
                ring1[4].wait_recv()
                ring1[5].wait_recv()
            part1[c] = ff_forward(c).astype(BF16)
            give1(i)
        relay1()

        def turn(i, _):
            xT[:, aligned(i, rows)] = x_rows[i].T
            innerT[:, aligned(i, rows)] = inner[i].T
            return 0

        lax.fori_loop(0, CHIPS, turn, 0)
        for copy in loads[7:]:
            copy.wait()
        valid_count = end_count()
        weight = as_column(v_ref[...].astype(F32)) * (mesh_tokens / valid_count[0:1, 0:1])
        own_weight[...] = jnp.broadcast_to(weight, own_weight.shape)
        receive1()

        def outputs(i, sums):
            at = aligned(i, ROWS)
            a = mix(s_ref, at, p_ref, 0)
            result = hidden[at, :] + up0_ref[at, :]
            for j in range(2):
                result = result + got1[j, at, :].astype(F32)
            difference = result - a
            row_weight = own_weight[at, 0:1]
            c0, c1 = c_ref[0], c_ref[1]
            out0 = a + c0 * difference
            out1 = mix(s_ref, at, p_ref, 1) + c1 * difference
            new_ref[at, 0, :] = out0.astype(BF16)
            new_ref[at, 1, :] = out1.astype(BF16)
            up0 = g_ref[at, 0, :].astype(F32) + row_weight * (out0 - t_ref[at, 0, :].astype(F32))
            up1 = g_ref[at, 1, :].astype(F32) + row_weight * (out1 - t_ref[at, 1, :].astype(F32))
            up0_ref[at, :] = up0
            up1_ref[at, :] = up1
            own[2, at, :] = (c0 * up0 + c1 * up1).astype(BF16)
            return (
                sums[0] + jnp.sum(up0 * difference, axis=0, keepdims=True),
                sums[1] + jnp.sum(up1 * difference, axis=0, keepdims=True),
            )

        zero = jnp.zeros((1, width), F32)
        correct_sums = lax.fori_loop(0, blocks, outputs, (zero, zero))
        sums_ref[...] = jnp.zeros_like(sums_ref)
        sums_ref[2:3, :] = correct_sums[0]
        sums_ref[3:4, :] = correct_sums[1]
        store(5, new_ref, new_out)
        store(6, up0_ref, up0_out)
        store(7, up1_ref, up1_out)

        ring2 = ring(own.at[2], r_rows, ag2s, ag2r)
        for copy in ring2[:4]:
            copy.start()
        r_rows[chip] = own[2]

        def ff_backward(c):
            r = r_rows[c]
            for n in range(col_tiles):
                cols = slice(n * TILE, (n + 1) * TILE)
                inner_grad = lax.dot_general(r, w_rows(2)[cols, :], NT, preferred_element_type=F32)
                value, slope = gelu_parts(gate[c, :, cols])
                gate_low[c, :, cols] = (inner_grad * up[c, :, cols] * slope).astype(BF16)
                up_low[c, :, cols] = (inner_grad * value).astype(BF16)
            return lax.dot_general(
                gate_low[c], w_rows(0), NT, preferred_element_type=F32
            ) + lax.dot_general(up_low[c], w_rows(1), NT, preferred_element_type=F32)

        give2, relay2, receive2, sends2 = plane_sum(
            part2, got2, far2, chip, core, depth, chip_x, chip_y, chip_d, send2, recv2
        )
        hg_ref[...] = ff_backward(chip)
        ring2[0].wait_recv()
        ring2[4].start()
        ring2[1].wait_recv()
        ring2[5].start()
        for i, (c, _) in enumerate(near):
            if i < 2:
                ring2[2 + i].wait_recv()
            else:
                ring2[4].wait_recv()
                ring2[5].wait_recv()
            part2[c] = ff_backward(c).astype(BF16)
            give2(i)

        def weight_grads(terms):
            def body(z, _):
                at = aligned(z, shard)
                for i, left, right in terms:
                    grad = jnp.dot(
                        left[at, :], right[...].reshape(queries, -1), preferred_element_type=F32
                    ).astype(BF16)
                    dw[z, 0, i * half : (i + 1) * half, :] = grad[:half]
                    dw[z, 1, i * half : (i + 1) * half, :] = grad[half:]
                return 0

            lax.fori_loop(0, depths, body, 0)

        early, late = pl.ds(0, half), pl.ds(half, 2 * half)

        def swap_rows(index, part):
            return remote(dw.at[:, 1 - core, part], dw_other.at[:, part], dsend, drecv, index, other)

        def add_cores(part):
            def body(z, _):
                dw_other[z, part, :] = (
                    dw[z, core, part, :].astype(F32) + dw_other[z, part, :].astype(F32)
                ).astype(BF16)
                return 0

            lax.fori_loop(0, depths, body, 0)

        swaps = [swap_rows(0, early), swap_rows(1, late)]
        weight_grads(((0, innerT, r_rows),))
        swaps[0].start()
        for copy in sends1:
            copy.wait_send()
        a_start, a_hop, a_result, a_finish = line_reduce(
            dw_other.at[:, early], gate.at[0, pl.ds(0, half)], a_up, a_down,
            part1.at[pl.ds(0, 2), pl.ds(0, half)], part1.at[pl.ds(2, 2), pl.ds(0, half)], a_sems,
        )
        swaps[0].wait_recv()
        add_cores(early)
        a_start()
        relay2()
        weight_grads(((1, xT, gate_low), (2, xT, up_low)))
        swaps[1].start()
        a_hop(1)
        receive2()

        def second_norm(i, gain_sum):
            at = aligned(i, ROWS)
            h = hidden[at, :]
            weighted = hg_ref[at, :]
            for j in range(2):
                weighted = weighted + got2[j, at, :].astype(F32)
            factor = norm_factor(h)
            mean = jnp.mean(weighted * h, axis=1, keepdims=True)
            result_grad = c_ref[0] * up0_ref[at, :] + c_ref[1] * up1_ref[at, :]
            hidden_grad = result_grad + (factor * weighted - h * (factor * factor * factor * mean))
            hg_ref[at, :] = hidden_grad
            own[3, at, :] = hidden_grad.astype(BF16)
            return gain_sum + jnp.sum(weighted * h * factor, axis=0, keepdims=True)

        sums_ref[1:2, :] = lax.fori_loop(0, blocks, second_norm, zero)
        store(10, hg_ref, hg_out)

        sends3 = [
            remote(packs.at[c], packed_grad.at[i], send3, recv3, i, device)
            for i, (c, device) in enumerate(near)
        ]

        def att_grad(c):
            return lax.dot_general(own[3], w_out_rows(c), NT, preferred_element_type=F32)

        for i in (2, 0, 1):
            packs[near[i][0]] = pack(att_grad(near[i][0]))
            sends3[i].start()
        da_ref[chip] = att_grad(chip).astype(BF16)
        for i, c in enumerate((chip, chip_x, chip_y, chip_d)):
            grad = jnp.dot(att_all[c].T, own[3], preferred_element_type=F32).astype(BF16)
            dwo[i, 0] = grad[:half]
            dwo[i, 1] = grad[half:]
        out_swap = remote(dwo.at[:, 1 - core], dwo_other, dsend, drecv, 2, other)
        out_swap.start()
        swaps[1].wait_recv()
        add_cores(late)
        store(8, dw_other.at[:, late], ffb_ref)
        a_hop(2)
        out_swap.wait_recv()
        for i in range(CHIPS):
            dwo_other[i] = (dwo[i, core].astype(F32) + dwo_other[i].astype(F32)).astype(BF16)
        store(9, dwo_other, dwo_ref)
        a_result()
        ffa_ref[...] = gate[0, 0:half, :].astype(BF16)
        for copy in sends3:
            copy.wait_recv()
        for i, (c, _) in enumerate(near):
            unpack(da_ref.at[c], packed_grad[i])
        sent = ring0 + shared0 + q_copies + q_shared + o_plane + o_across + sends2 + sends3
        for copy in sent + ring1 + ring2 + swaps + [out_swap, ff_mine]:
            copy.wait_send()
        a_finish()
        for i in range(depths - 1):
            carried(i, o_copies[i].wait_send)
            carried(i, o_shared[i].wait_send)
        for _, sends, receives, hop, share in hops:
            pl.when(sends)(hop.wait_send)
            pl.when(receives)(share.wait_send)
        for copy in stores:
            copy.wait()

    block = (rows, width)
    pair = (rows, 2, width)
    wide_rows = (CHIPS, rows, width)
    hid_rows = (CHIPS, rows, columns)

    def out(shape, dtype):
        return jax.ShapeDtypeStruct(shape, dtype)

    vmem = pltpu.VMEM
    outs = [
        out(pair, BF16),
        out(block, F32),
        out(block, F32),
        out(block, F32),
        out((CHIPS, rows, CHIP_COLS), BF16),
        out((CHIPS, half, width), BF16),
        out((half, columns), BF16),
        out((depths, 2 * half, columns), BF16),
        out((8, width), F32),
        out(wide_rows, BF16),
        out((3, width, CHIP_COLS), BF16),
        out((queries, CHIP_COLS), BF16),
        out((tokens, CHIP_COLS), BF16),
        out((tokens, CHIP_COLS), BF16),
        out((tiles, CHIP_COLS, TILE), F32),
        out((tiles, LOCAL_HEADS, 1, TILE), F32),
    ]
    return pl.pallas_call(
        kernel,
        out_shape=outs,
        in_specs=[SM] * 4 + [VM, ANY, ANY] + [VM] * 3 + [ANY] * 7,
        out_specs=[ANY] * 4 + [VM, ANY, VM, ANY, VM] + [ANY] * 6 + [VM],
        scratch_shapes=[
            vmem(pair, BF16),
            vmem(block, F32),
            vmem(block, F32),
            vmem(block, F32),
            vmem((2 * CHIPS, rows, width), BF16),
            vmem((3, width, CHIP_COLS), BF16),
            vmem((queries, CHIP_COLS), BF16),
            vmem((tokens, CHIP_COLS), BF16),
            vmem((tokens, CHIP_COLS), BF16),
            vmem((tiles, CHIP_COLS, TILE), F32),
            vmem((CHIPS, 2, half, width), BF16),
            vmem((CHIPS, half, width), BF16),
            vmem(pair, BF16),
            vmem(pair, BF16),
            vmem((3, depths, 2, half, columns), BF16),
            vmem((depths, CHIPS, out_rows, width), BF16),
            vmem((depths, 2, half, piece_lanes), BF16),
            vmem((CHIPS, rows, CHIP_COLS), BF16),
            vmem((CHIPS, rows // 2, 2 * CHIP_COLS), BF16),
            vmem((3, rows // 2, 2 * CHIP_COLS), BF16),
            vmem((3, rows // 2, 2 * CHIP_COLS), BF16),
            vmem(block, F32),
            vmem((4,) + block, BF16),
            vmem(wide_rows, BF16),
            vmem(wide_rows, BF16),
            vmem((width, queries), BF16),
            vmem((columns, queries), BF16),
            vmem(hid_rows, BF16),
            vmem(hid_rows, F32),
            vmem(hid_rows, F32),
            vmem(hid_rows, BF16),
            vmem(hid_rows, BF16),
            vmem((rows, 128), F32),
            vmem(wide_rows, BF16),
            vmem(wide_rows, BF16),
            vmem((2,) + block, BF16),
            vmem((2,) + block, BF16),
            vmem((2, rows // 2, width), BF16),
            vmem((2, rows // 2, width), BF16),
            vmem((depths, 2, 3 * half, columns), BF16),
            vmem((depths, 3 * half, columns), BF16),
            vmem((depths - 1, half, columns), BF16),
            vmem((depths - 1, half, columns), BF16),
            vmem((3, half, width), BF16),
            vmem((2, half, hidden_cols), BF16),
            vmem((8, 128), F32),
            vmem((queries, CHIP_COLS), BF16),
            vmem((tokens, CHIP_COLS), BF16),
            vmem((tokens, CHIP_COLS), BF16),
            vmem((CHIP_COLS, tokens), BF16),
        ]
        + [DMA((9,))]
        + [DMA((2 * depths - 2,))] * 2
        + [DMA((2 * depths - 1,))] * 2
        + [DMA((depths - 1,))] * 2
        + [DMA((depths,))] * 2
        + [DMA((depths - 1,))] * 4
        + [DMA((6,))] * 2
        + [DMA((6,))] * 2
        + [DMA((4,))] * 2
        + [DMA((3,))] * 2
        + [DMA((6,))] * 4
        + [DMA((3,))] * 2
        + [DMA((6,))] * 4
        + [DMA((3,))] * 2
        + [DMA((11,)), DMA((CHIPS,))]
        + [DMA((depths - 1,))] * 4
        + total_scratch((8, 128), depths),
        compiler_params=comm_params(collective_id),
        name="forward",
    )(
        slots, lengths, predict, correct, states, out_grad, teacher, valid, gain_one, gain_two,
        w_query, w_key, w_value, w_out, w_gate, w_up, w_down,
    )


def backward(
    slots, lengths, predict, correct, att_grad, q_pairs, k_pairs, v_pairs, oT, lse, sums, up_grads,
    out_grads, ff_early, weights, states, up0, up1, hidden_grad, own_rows, collective_id,
):
    rows, _, width = states.shape
    depths, late_rows, ff_columns = up_grads.shape
    half = late_rows // 2
    columns = CHIP_COLS
    lanes_all = 3 * columns
    blocks = rows // ROWS
    tokens = k_pairs.shape[0]
    queries = q_pairs.shape[0]
    tiles = queries // TILE
    per_device = rows // BLK
    group_pairs = tokens // (2 * BLK)
    pairs = queries // (2 * BLK)
    half_tiles = group_pairs * BLK // TILE
    wide_lanes = LOCAL_HEADS * TILE

    def kernel(
        slots_ref, lengths_ref, p_ref, c_ref, g_in, q_in, k_in, v_in, oT_in, lse_ref, sums_ref, u_in,
        og_in, fa_ref, w_in, s_in, up0_in, up1_in, hg_in, x_in,
        grad_out, fa_out, fb_out, q_all, o_all, total_ref,
        grad_ref, fa_all, fb_all, w_all, s_ref, up0_ref, up1_ref, hg_ref, x_own, fa_own, g_ref, q_ref, k_ref, v_ref, oT_ref, u_ref, og_ref,
        g_pairs, kT, doT, dqT, q_stack, do_stack, p_buf, ds_buf, dk_acc, dv_acc, bias, dq_pairs, dq_rows,
        give, kept, came, xT, part, got, far, mine, q_grad, q_other, q_mine, q_far, q_sum,
        o_near, o_mine, o_far, o_sum, u_far, u_sum, all_sums,
        loads, nsend, nrecv, ksend, krecv, send, recv, ssend, srecv, zsend, zrecv, osend, orecv, usend, urecv,
        asend, arecv, fsend, frecv, gsend, grecv, bsend, brecv, psend, precv, *total_refs,
    ):
        depth, chip, core, chip_x, chip_y, chip_d = place_on_mesh()
        near = [(c, (2 * c + core, depth)) for c in (chip_x, chip_y, chip_d)]
        other = (2 * chip + 1 - core, depth)
        across = [
            (2 * chip + core, lax.rem(depth + step, depths)) for step in range(1, depths)
        ]
        peers = plane_peers(chip, core, depth, chip_x, chip_y, chip_d)
        everyone = peers + across
        signal_all(everyone)

        def slot(chip_index):
            return 2 * chip_index + core

        def load(index, source, target):
            copy = pltpu.make_async_copy(source, target, loads.at[index])
            copy.start()
            return copy

        first_loads = [
            load(7 + i, source, target)
            for i, (source, target) in enumerate(
                ((g_in, g_ref), (k_in, k_ref), (q_in, q_ref), (v_in, v_ref), (oT_in, oT_ref))
            )
        ]
        early_load = load(0, fa_ref, fa_own)
        sum_loads = [load(12, u_in, u_ref), load(13, og_in, og_ref)]
        other_loads = [
            load(1 + i, source, target)
            for i, (source, target) in enumerate(
                (
                    (w_in, w_all), (x_in, x_own), (s_in, s_ref), (up0_in, up0_ref), (up1_in, up1_ref), (hg_in, hg_ref)
                )
            )
        ]

        def depth_sum(source_of, inbox, sends, receives):
            return [
                remote(source_of(lax.rem(depth + i + 1, depths)), inbox.at[i], sends, receives, i, device)
                for i, device in enumerate(across)
            ]

        early_load.wait()
        for copy in sum_loads:
            copy.wait()
        wait_all(everyone)
        u_copies = depth_sum(lambda z: u_ref.at[z], u_far, usend, urecv)
        near_grads = [
            remote(og_ref.at[1 + i], o_near.at[i], nsend, nrecv, i, device)
            for i, (_, device) in enumerate(near)
        ]
        a_ring = ring_sends(
            fa_own, fa_all, slot, chip, core, depth, chip_x, chip_y, asend, arecv
        )
        for copy in u_copies + near_grads + a_ring[:4]:
            copy.start()

        def shared(index, ref):
            return remote(ref, ref, psend, precv, index, other)

        in_plane = (chip, chip_x, chip_y, chip_d)
        a_shared = [shared(i, fa_all.at[slot(c)]) for i, c in enumerate(in_plane)]
        b_shared = [shared(4 + i, fb_all.at[slot(c)]) for i, c in enumerate(in_plane)]
        q_shared = [shared(8 + i, q_all.at[slot(c)]) for i, c in enumerate(in_plane)]
        o_shared = shared(12, o_all.at[core])
        fa_all[slot(chip)] = fa_own[...]
        a_shared[0].start()

        for copy in first_loads:
            copy.wait()
        own_to_pair_order(g_ref, g_pairs, slots_ref, pairs, per_device)

        def turn_keys(i, _):
            at = aligned(i, TILE)
            kT[:, at] = k_ref[at, :].T
            return 0

        lax.fori_loop(0, tokens // TILE, turn_keys, 0)

        def attend(kind, step):
            tile = kind * (tiles // 2) + step
            key_tiles = half_tiles * (kind + 1)
            q_tile = q_ref[aligned(tile, TILE), :]
            fill_bias(bias, kind, step, slots_ref, lengths_ref, per_device, group_pairs)
            do_tile = g_pairs[aligned(tile, TILE), :]
            doT[...] = do_tile.astype(F32).T * oT_ref[tile]
            for head in range(LOCAL_HEADS):
                lanes = slice(head * TILE, (head + 1) * TILE)
                heads = slice(head * HD, (head + 1) * HD)
                mask = head_mask(TILE, head)
                q_head = jnp.where(mask, q_tile, jnp.zeros_like(q_tile))
                do_head = jnp.where(mask, do_tile, jnp.zeros_like(do_tile))
                q_stack[lanes, :] = q_head
                do_stack[lanes, :] = do_head
                delta = jnp.sum(doT[heads, :], axis=0, keepdims=True)
                norm = lse_ref[tile, head]
                total = jnp.zeros((HD, TILE), F32)
                for k_tile in range(key_tiles):
                    at = slice(k_tile * TILE, (k_tile + 1) * TILE)
                    s = lax.dot_general(k_ref[at, :], q_head, NT, preferred_element_type=F32)
                    if k_tile >= key_tiles - half_tiles:
                        s = s + bias[k_tile - (key_tiles - half_tiles), :, 0:TILE]
                    dp = lax.dot_general(v_ref[at, :], do_head, NT, preferred_element_type=F32)
                    e = jnp.exp(s - norm)
                    p_buf[at, lanes] = e.astype(BF16)
                    ds = (e * (dp - delta)).astype(BF16)
                    ds_buf[at, lanes] = ds
                    total = total + jnp.dot(kT[heads, at], ds, preferred_element_type=F32)
                dqT[heads, :] = total
            for k_tile in range(key_tiles):
                at = slice(k_tile * TILE, (k_tile + 1) * TILE)
                dv = jnp.dot(p_buf[at, :], do_stack[...], preferred_element_type=F32)
                dk = jnp.dot(ds_buf[at, :], q_stack[...], preferred_element_type=F32)
                if kind == 1:
                    fresh = step == 0
                    dv_acc[at, :] = dv + jnp.where(fresh, 0.0, dv_acc[at, :])
                    dk_acc[at, :] = dk + jnp.where(fresh, 0.0, dk_acc[at, :])
                else:
                    dv_acc[at, :] = dv + dv_acc[at, :]
                    dk_acc[at, :] = dk + dk_acc[at, :]
            dq_pairs[aligned(tile, TILE), :] = dqT[...].T.astype(BF16)

        for kind in (1, 0):

            def body(step, _, kind=kind):
                attend(kind, step)
                return 0

            lax.fori_loop(0, tiles // 2, body, 0)
            if kind == 1:
                a_ring[0].wait_recv()
                a_ring[4].start()
                a_ring[1].wait_recv()
                a_ring[5].start()

        def slot_rows(target, side, chip_index, pair_index):
            pair = chip_index * per_device + side * (per_device // 2) + pair_index
            second, _, _ = pair_places(slots_ref, pair)
            at = 2 * pair_index * BLK
            for i, acc in enumerate((dk_acc, dv_acc)):
                both = either(second, acc[aligned(pair, BLK), :], acc[aligned(group_pairs + pair, BLK), :])
                for j in range(2):
                    target[i, chip_index, at + j * BLK : at + (j + 1) * BLK, :] = both[j].astype(BF16)

        for c in range(CHIPS):
            for i in range(per_device // 2):
                slot_rows(give, 1 - core, c, i)
        swap = remote(give, came, ksend, krecv, 0, other)
        swap.start()
        for c in range(CHIPS):
            for i in range(per_device // 2):
                slot_rows(kept, core, c, i)
        own_to_slot_order(dq_pairs, dq_rows, slots_ref, pairs, per_device)

        for copy in near_grads:
            copy.wait_recv()
        whole = og_ref[0].astype(F32)
        for i in range(3):
            whole = whole + o_near[i].astype(F32)
        o_mine[...] = whole.astype(BF16)
        distance = lax.rem(chip + depths - depth, depths)
        o_copies = [
            remote(o_mine, o_far.at[i], osend, orecv, i, device) for i, device in enumerate(across)
        ]
        for i in range(depths - 1):
            pl.when(distance == i + 1)(o_copies[i].start)
        swap.wait_recv()

        def add_cores(c, _):
            for i in range(2):
                kept[i, c] = (kept[i, c].astype(F32) + came[i, c].astype(F32)).astype(BF16)
            return 0

        lax.fori_loop(0, CHIPS, add_cores, 0)
        for copy in other_loads:
            copy.wait()

        def rows_grad(c):
            return (
                lax.dot_general(
                    dq_rows[aligned(c, rows), :], w_all[0], NT, preferred_element_type=F32
                )
                + lax.dot_general(kept[0, c], w_all[1], NT, preferred_element_type=F32)
                + lax.dot_general(kept[1, c], w_all[2], NT, preferred_element_type=F32)
            )

        give_rows, relay_rows, receive_rows, sends = plane_sum(
            part, got, far, chip, core, depth, chip_x, chip_y, chip_d, send, recv
        )
        for i in (2, 0, 1):
            part[near[i][0]] = rows_grad(near[i][0]).astype(BF16)
            give_rows(i)
        mine[...] = rows_grad(chip)

        def turn(c, _):
            xT[:, aligned(c, rows)] = x_own[c].T
            return 0

        lax.fori_loop(0, CHIPS, turn, 0)

        def weight_grads(z, _):
            at = aligned(z, 2 * half)
            grads = []
            for i in range(3):
                right = dq_rows[...] if i == 0 else kept[i - 1].reshape(queries, columns)
                grads.append(jnp.dot(xT[at, :], right, preferred_element_type=F32))
            grad = jnp.concatenate(grads, axis=1).astype(BF16)
            q_grad[z, 0] = grad[:half]
            q_grad[z, 1] = grad[half:]
            return 0

        lax.fori_loop(0, depths, weight_grads, 0)
        core_swap = remote(q_grad.at[:, 1 - core], q_other, ssend, srecv, 0, other)
        core_swap.start()
        relay_rows()
        core_swap.wait_recv()
        for i in range(depths):
            q_mine[i] = (q_grad[i, core].astype(F32) + q_other[i].astype(F32)).astype(BF16)
        q_copies = depth_sum(lambda z: q_mine.at[z], q_far, zsend, zrecv)
        for copy in q_copies:
            copy.start()

        for copy in u_copies:
            copy.wait_recv()
        whole = u_ref[depth].astype(F32)
        for i in range(depths - 1):
            whole = whole + u_far[i].astype(F32)
        u_sum[...] = whole.astype(BF16)
        b_ring = ring_sends(
            u_sum, fb_all, slot, chip, core, depth, chip_x, chip_y, fsend, frecv
        )
        for copy in b_ring[:4]:
            copy.start()
        fb_all[slot(chip)] = u_sum[...]
        b_shared[0].start()
        a_ring[2].wait_recv()
        a_shared[1].start()
        a_ring[3].wait_recv()
        a_shared[2].start()
        a_ring[4].wait_recv()
        a_ring[5].wait_recv()
        a_shared[3].start()
        receive_rows()

        def state_grads(i, totals):
            at = aligned(i, ROWS)
            s0, s1 = s_ref[at, 0, :].astype(F32), s_ref[at, 1, :].astype(F32)
            a = p_ref[0, 0] * s0 + p_ref[0, 1] * s1
            weighted = mine[at, :]
            for j in range(2):
                weighted = weighted + got[j, at, :].astype(F32)
            factor = norm_factor(a)
            mean = jnp.mean(weighted * a, axis=1, keepdims=True)
            up0, up1 = up0_ref[at, :], up1_ref[at, :]
            result_grad = c_ref[0] * up0 + c_ref[1] * up1
            norm_grad = factor * weighted - a * (factor * factor * factor * mean)
            mixed0 = up0 + (hg_ref[at, :] + norm_grad - result_grad)
            grad_ref[at, 0, :] = (p_ref[0, 0] * mixed0 + p_ref[1, 0] * up1).astype(BF16)
            grad_ref[at, 1, :] = (p_ref[0, 1] * mixed0 + p_ref[1, 1] * up1).astype(BF16)
            terms = (weighted * a * factor, mixed0 * s0, mixed0 * s1, up1 * s0, up1 * s1)
            return tuple(t + jnp.sum(v, axis=0, keepdims=True) for t, v in zip(totals, terms))

        totals = lax.fori_loop(
            0, blocks, state_grads, tuple(jnp.zeros((1, width), F32) for _ in range(5))
        )
        b_ring[0].wait_recv()
        b_ring[4].start()
        b_ring[1].wait_recv()
        b_ring[5].start()
        stores = [load(14, grad_ref, grad_out)]
        all_sums[...] = sums_ref[...]
        all_sums[0:1, :] = totals[0]
        for i in range(4):
            all_sums[4 + i : 5 + i, :] = totals[1 + i]
        start, turn_sums, end = total_over_mesh(
            all_sums, *total_refs[:3], across, peers, *total_refs[3:]
        )
        start()
        for copy in q_copies:
            copy.wait_recv()
        whole = q_mine[depth].astype(F32)
        for i in range(depths - 1):
            whole = whole + q_far[i].astype(F32)
        q_sum[...] = whole.astype(BF16)
        q_ring = ring_sends(
            q_sum, q_all, slot, chip, core, depth, chip_x, chip_y, gsend, grecv
        )
        for copy in q_ring[:4]:
            copy.start()
        q_all[slot(chip)] = q_sum[...]
        q_shared[0].start()
        quarter = half // 2
        o_top, o_low = o_all.at[core, pl.ds(0, quarter)], o_all.at[core, pl.ds(quarter, quarter)]
        o_source_top, o_source_low = o_sum.at[pl.ds(0, quarter)], o_sum.at[pl.ds(quarter, quarter)]
        dev_x, dev_y = near[0][1], near[1][1]
        o_ring = [
            remote(o_source_top, o_top, bsend, brecv, 0, dev_x),
            remote(o_source_low, o_low, bsend, brecv, 1, dev_y),
            remote(o_source_low, o_low, bsend, brecv, 2, dev_x),
            remote(o_source_top, o_top, bsend, brecv, 3, dev_y),
            remote(o_top, o_top, bsend, brecv, 4, dev_y),
            remote(o_low, o_low, bsend, brecv, 5, dev_x),
        ]
        source, from_x, from_y = chip == depth, chip_x == depth, chip_y == depth

        @pl.when(source)
        def _():
            for copy in o_copies:
                copy.wait_recv()
            whole = o_mine[...].astype(F32)
            for i in range(depths - 1):
                whole = whole + o_far[i].astype(F32)
            o_sum[...] = whole.astype(BF16)
            for copy in o_ring[:4]:
                copy.start()
            o_all[core] = o_sum[...]

        turn_sums()
        q_ring[0].wait_recv()
        q_ring[4].start()
        q_ring[1].wait_recv()
        q_ring[5].start()

        @pl.when(from_x)
        def _():
            o_ring[0].wait_recv()
            o_ring[4].start()
            o_ring[2].wait_recv()

        @pl.when(from_y)
        def _():
            o_ring[1].wait_recv()
            o_ring[5].start()
            o_ring[3].wait_recv()

        for copy in a_shared:
            copy.wait_recv()
        stores.append(load(15, fa_all, fa_out))
        for copies, passed in ((b_ring, b_shared), (q_ring, q_shared)):
            copies[2].wait_recv()
            passed[1].start()
            copies[3].wait_recv()
            passed[2].start()
            copies[4].wait_recv()
            copies[5].wait_recv()
            passed[3].start()
        for copy in b_shared:
            copy.wait_recv()
        stores.append(load(16, fb_all, fb_out))

        @pl.when(chip_d == depth)
        def _():
            o_ring[4].wait_recv()
            o_ring[5].wait_recv()

        o_shared.start()
        total_ref[...] = end()
        for copy in q_shared + [o_shared]:
            copy.wait()
        for copy in a_shared + b_shared:
            copy.wait_send()
        for copy in stores:
            copy.wait()
        for copy in u_copies + near_grads + [swap] + sends + [core_swap] + q_copies + a_ring + b_ring + q_ring:
            copy.wait_send()
        for i in range(depths - 1):
            pl.when(distance == i + 1)(o_copies[i].wait_send)

        @pl.when(source)
        def _():
            for copy in o_ring[:4]:
                copy.wait_send()

        pl.when(from_x)(o_ring[4].wait_send)
        pl.when(from_y)(o_ring[5].wait_send)

    vmem = pltpu.VMEM
    block = (rows, width)
    wide_rows = (CHIPS, rows, width)
    q_block, o_block = (half, lanes_all), (half, width)
    kv_half = (2, CHIPS, rows, columns)
    a_block, b_block = ff_early.shape, (late_rows, ff_columns)
    ctx = 2 * CHIPS
    return pl.pallas_call(
        kernel,
        out_shape=[
            jax.ShapeDtypeStruct((rows, 2, width), BF16),
            jax.ShapeDtypeStruct((ctx,) + a_block, BF16),
            jax.ShapeDtypeStruct((ctx,) + b_block, BF16),
            jax.ShapeDtypeStruct((ctx,) + q_block, BF16),
            jax.ShapeDtypeStruct((2,) + o_block, BF16),
            jax.ShapeDtypeStruct((8, width), F32),
        ],
        in_specs=[SM] * 4 + [ANY] * 5 + [VM] * 2 + [ANY] * 9,
        out_specs=[ANY] * 3 + [VM] * 3,
        scratch_shapes=[
            vmem((rows, 2, width), BF16),
            vmem((ctx,) + a_block, BF16),
            vmem((ctx,) + b_block, BF16),
            vmem((3, width, columns), BF16),
            vmem((rows, 2, width), BF16),
            vmem(block, F32),
            vmem(block, F32),
            vmem(block, F32),
            vmem(wide_rows, BF16),
            vmem(a_block, BF16),
            vmem((queries, columns), BF16),
            vmem((queries, columns), BF16),
            vmem((tokens, columns), BF16),
            vmem((tokens, columns), BF16),
            vmem(oT.shape, F32),
            vmem(up_grads.shape, BF16),
            vmem(out_grads.shape, BF16),
            vmem((queries, columns), BF16),
            vmem((columns, tokens), BF16),
            vmem((columns, TILE), F32),
            vmem((columns, TILE), F32),
            vmem((wide_lanes, columns), BF16),
            vmem((wide_lanes, columns), BF16),
            vmem((tokens, wide_lanes), BF16),
            vmem((tokens, wide_lanes), BF16),
            vmem((tokens, columns), F32),
            vmem((tokens, columns), F32),
            vmem((half_tiles, TILE, TILE), F32),
            vmem((queries, columns), BF16),
            vmem((queries, columns), BF16),
            vmem(kv_half, BF16),
            vmem(kv_half, BF16),
            vmem(kv_half, BF16),
            vmem((width, queries), BF16),
            vmem(wide_rows, BF16),
            vmem((2,) + block, BF16),
            vmem((2, rows // 2, width), BF16),
            vmem(block, F32),
            vmem((depths, 2) + q_block, BF16),
            vmem((depths,) + q_block, BF16),
            vmem((depths,) + q_block, BF16),
            vmem((depths - 1,) + q_block, BF16),
            vmem(q_block, BF16),
            vmem((3,) + o_block, BF16),
            vmem(o_block, BF16),
            vmem((depths - 1,) + o_block, BF16),
            vmem(o_block, BF16),
            vmem((depths - 1,) + b_block, BF16),
            vmem(b_block, BF16),
            vmem((8, width), F32),
            DMA((17,)),
            *[DMA((3,))] * 2,
            *[DMA((1,))] * 2,
            *[DMA((6,))] * 2,
            *[DMA((1,))] * 2,
            *[DMA((depths - 1,))] * 6,
            *[DMA((6,))] * 8,
            *[DMA((13,))] * 2,
            *total_scratch((8, width), depths),
        ],
        compiler_params=comm_params(collective_id),
        name="backward",
    )(
        slots, lengths, predict, correct, att_grad, q_pairs, k_pairs, v_pairs, oT, lse, sums, up_grads,
        out_grads, ff_early, weights, states, up0, up1, hidden_grad, own_rows,
    )


def lay_out(new_states, states_grad, early, late, qkv, out, sums, gain_one, gain_two):
    ctx, half, columns = early.shape
    width = out.shape[2]
    shard = 2 * half
    depths = width // shard
    split = columns // depths
    steps = 1
    strip = half // steps

    def kernel(
        new_in, grad_in, d_ref, g_ref, u_ref, q_ref, o_ref, s_ref, g1_ref, g2_ref,
        new_ref, grad_ref, dq_ref, dk_ref, dv_ref, do_ref, dg_ref, du_ref, dd_ref, g1_out, g2_out, p_out, c_out, columns_ref,
    ):
        core, step = pl.program_id(0), pl.program_id(1)
        depth = lax.axis_index("wsh")

        @pl.when((core == 0) & (step == 0))
        def _():
            one = g1_ref[...].astype(F32).reshape(1, shard)
            two = g2_ref[...].astype(F32).reshape(1, shard)
            columns_ref[0] = jnp.broadcast_to(as_column(one), (shard, 128))
            columns_ref[1] = jnp.broadcast_to(as_column(two), (shard, 128))
            for z in range(depths):

                @pl.when(depth == z)
                def _(z=z):
                    g1_out[...] = s_ref[0:1, z * shard : (z + 1) * shard] / one
                    g2_out[...] = s_ref[1:2, z * shard : (z + 1) * shard] / two

            scalars = jnp.sum(s_ref[...], axis=1, keepdims=True)
            for i in range(2):
                c_out[:, i : i + 1] = scalars[2 + i : 3 + i]
                for j in range(2):
                    at = 4 + 2 * i + j
                    p_out[i : i + 1, j : j + 1] = scalars[at : at + 1]

        rows = aligned(core * steps + step, strip)
        one, two = columns_ref[0, rows, 0:1], columns_ref[1, rows, 0:1]
        new_ref[...] = new_in[...]
        grad_ref[...] = grad_in[...]
        do_ref[...] = o_ref[...].astype(F32)
        for i, ref in enumerate((dq_ref, dk_ref, dv_ref)):
            wide = jnp.concatenate(
                [q_ref[p, :, i * CHIP_COLS : (i + 1) * CHIP_COLS].astype(F32) for p in range(CHIPS)], axis=1
            )
            ref[...] = wide * one
        for source, ref in ((g_ref, dg_ref), (u_ref, du_ref)):
            for z in range(depths):
                wide = jnp.concatenate(
                    [source[p, :, z * split : (z + 1) * split].astype(F32) for p in range(CHIPS)], axis=1
                )
                ref[:, z * CHIPS * split : (z + 1) * CHIPS * split] = wide * two
        dd_ref[...] = d_ref[...].astype(F32)

    early = early.reshape(CHIPS, 2, half, columns)
    late = late.reshape(CHIPS, 2, 2, half, columns)
    qkv = qkv.reshape(CHIPS, 2, half, -1)
    square = jax.ShapeDtypeStruct((shard, width), F32)
    tall = jax.ShapeDtypeStruct((shard, columns * CHIPS), F32)
    row = jax.ShapeDtypeStruct((1, shard), F32)

    def whole(shape):
        return pl.BlockSpec(shape, lambda c, r: (0,) * len(shape))

    def piece(lanes):
        return pl.BlockSpec((CHIPS, None, strip, lanes), lambda c, r: (0, c, r, 0))

    def part(i):
        return pl.BlockSpec((CHIPS, None, None, strip, columns), lambda c, r: (0, c, i, r, 0))

    def strip_of(lanes):
        return pl.BlockSpec((strip, lanes), lambda c, r: (c * steps + r, 0))

    rows = new_states.shape[0] // (2 * steps)
    state_rows = pl.BlockSpec((rows,) + new_states.shape[1:], lambda c, r: (c * steps + r, 0, 0))
    outs = pl.pallas_call(
        kernel,
        grid=(2, steps),
        out_shape=[
            jax.ShapeDtypeStruct(new_states.shape, BF16),
            jax.ShapeDtypeStruct(states_grad.shape, BF16),
            square,
            square,
            square,
            square,
            tall,
            tall,
            jax.ShapeDtypeStruct((CHIPS, 2, half, width), F32),
            row,
            row,
            jax.ShapeDtypeStruct((2, 2), F32),
            jax.ShapeDtypeStruct((1, 2), F32),
        ],
        in_specs=[
            state_rows,
            state_rows,
            piece(columns),
            part(0),
            part(1),
            piece(3 * CHIP_COLS),
            pl.BlockSpec((None, strip, width), lambda c, r: (c, r, 0)),
            whole((8, width)),
            whole((shard,)),
            whole((shard,)),
        ],
        out_specs=[
            state_rows,
            state_rows,
            strip_of(width),
            strip_of(width),
            strip_of(width),
            strip_of(width),
            strip_of(columns * CHIPS),
            strip_of(columns * CHIPS),
            piece(width),
            whole((1, shard)),
            whole((1, shard)),
            whole((2, 2)),
            whole((1, 2)),
        ],
        scratch_shapes=[pltpu.VMEM((2, shard, 128), F32)],
        compiler_params=pltpu.CompilerParams(vmem_limit_bytes=VMEM_LIMIT),
        name="lay_out",
    )(new_states, states_grad, early, late, late, qkv, out, sums, gain_one, gain_two)
    return (*outs[:8], outs[8].reshape(ctx * half, width), *outs[9:])


def plane_shards(
    states, block_slot, cont_lengths, valid_mask, teacher, out_grad, predict, correct,
    norm_attn, w_query, w_key, w_value, w_out, norm_ffn, w_gate, w_up, w_down,
):
    slots, lengths = block_slot[0], cont_lengths[0]
    gain_one, gain_two = norm_attn, norm_ffn
    states = states[0]
    new_states, up0, up1, hidden_grad, att_grad, out_grads, ff_early, up_grads, sums, *saved = forward(
        slots, lengths, predict, correct, states, out_grad[0], teacher[0], valid_mask, gain_one, gain_two,
        w_query, w_key, w_value, w_out, w_gate, w_up, w_down, 1,
    )
    own_rows, weights, q_pairs, k_pairs, v_pairs, oT, lse = saved
    states_grad, *gathered = backward(
        slots, lengths, predict, correct, att_grad.reshape(-1, CHIP_COLS), q_pairs, k_pairs, v_pairs, oT, lse,
        sums, up_grads, out_grads, ff_early, weights, states, up0, up1, hidden_grad, own_rows, 2,
    )
    new_states, states_grad, dq, dk, dv, do, dg, du, dd, g_one, g_two, predict_grad, correct_grad = lay_out(
        new_states, states_grad, *gathered, gain_one, gain_two
    )
    return (
        new_states[None], states_grad[None], predict_grad, correct_grad[0],
        g_one[0], dq, dk, dv, do, g_two[0], dg, du, dd,
    )


def fits_plane(mesh, states, block_slot, w_query, w_gate):
    ctx, depths = mesh.shape["ctx"], mesh.shape["wsh"]
    return (
        ctx == 2 * CHIPS
        and depths == CHIPS
        and states.shape[0] == depths
        and block_slot.shape[1] * BLK == 2 * PROMPT
        and states.shape[1] == 2 * PROMPT
        and w_query.shape[0] % (32 * depths) == 0
        and w_gate.shape[1] % (32 * CHIPS * depths) == 0
    )


def solution(mesh):
    in_specs = (
        P("wsh", "ctx", None, None),
        P("wsh", None),
        P("wsh", None),
        P("wsh", "ctx"),
        P("wsh", "ctx", None, None),
        P("wsh", "ctx", None, None),
        P(),
        P(),
        P("wsh"),
        P("wsh", None),
        P("wsh", None),
        P("wsh", None),
        P("wsh", None),
        P("wsh"),
        P("wsh", None),
        P("wsh", None),
        P("wsh", None),
    )
    out_specs = (
        P("wsh", "ctx", None, None),
        P("wsh", "ctx", None, None),
        P(),
        P(),
        P("wsh"),
        P("wsh", None),
        P("wsh", None),
        P("wsh", None),
        P("wsh", None),
        P("wsh"),
        P("wsh", None),
        P("wsh", None),
        P("wsh", None),
    )

    def step(*args):
        plane = fits_plane(mesh, args[0], args[1], args[9], args[14])
        body = plane_shards if plane else general_shards
        return jax.shard_map(
            body, mesh=mesh, in_specs=in_specs, out_specs=out_specs, check_vma=False
        )(*args)

    return step
```

```python
import functools
import math

import jax
import jax.numpy as jnp
from jax import lax
from jax.experimental import pallas as pl
from jax.experimental.pallas import tpu as pltpu
from jax.sharding import PartitionSpec as P

HEADS = 12
HD = 64
PROMPT = 1024
BLK = 64


EPSILON = 1e-06
NEGATIVE = -1e30
HIGHEST = lax.Precision.HIGHEST


def rms_forward(tensor, gain_vec):
    factor = lax.rsqrt(jnp.mean(tensor * tensor, axis=-1, keepdims=True) + EPSILON)
    return (tensor * factor * gain_vec, factor)


def rms_backward(tensor, factor, gain_vec, upstream):
    weighted = upstream * gain_vec
    gain_grad = jnp.sum(upstream * tensor * factor, axis=0)
    middle = jnp.mean(weighted * tensor, axis=-1, keepdims=True)
    return (factor * weighted - tensor * factor * factor * factor * middle, gain_grad)


def segment_starts(cont_lengths):
    count = cont_lengths.shape[1]
    index = jnp.arange(count, dtype=jnp.int32)
    before = index[:, None] < index[None, :]
    return PROMPT + jnp.sum(jnp.where(before[None], cont_lengths[:, :, None], 0), axis=1)


def token_places(block_slot, cont_lengths):
    groups, blocks = block_slot.shape
    offsets = jnp.arange(BLK, dtype=jnp.int32)
    places = (block_slot[:, :, None] * BLK + offsets[None, None, :]).reshape(groups, blocks * BLK)
    starts = segment_starts(cont_lengths)
    segments = jnp.sum((places[:, :, None] >= starts[:, None, :]).astype(jnp.int32), axis=2)
    return (places, segments)


def visible(query_place, query_segment, key_place, key_segment):
    earlier = key_place[:, None, :] <= query_place[:, :, None]
    shared = (key_segment[:, None, :] == 0) | (key_segment[:, None, :] == query_segment[:, :, None])
    return earlier & shared


def split_heads(tensor):
    return tensor.reshape(tensor.shape[0], tensor.shape[1], HEADS, HD)


def forward_block(running, query_part, key_part, value_part, allowed):

    def forward_compute(current):
        maximum, denominator, accumulated = current
        scores = jnp.einsum(
            "gqhd,gkhd->ghqk",
            split_heads(query_part),
            split_heads(key_part),
            preferred_element_type=jnp.float32,
        )
        masked = jnp.where(allowed[:, None], scores, NEGATIVE)
        new_max = jnp.maximum(maximum, jnp.max(masked, axis=-1))
        exponent = jnp.where(allowed[:, None], jnp.exp(masked - new_max[..., None]), 0.0)
        factor = jnp.exp(maximum - new_max)
        rescale = jnp.swapaxes(factor, 1, 2)[..., None]
        update = jnp.einsum(
            "ghqk,gkhd->gqhd",
            exponent.astype(jnp.bfloat16),
            split_heads(value_part),
            preferred_element_type=jnp.float32,
        )
        merged = (split_heads(accumulated) * rescale + update).reshape(accumulated.shape)
        return (new_max, denominator * factor + jnp.sum(exponent, axis=-1), merged)

    return lax.cond(jnp.any(allowed), forward_compute, lambda current: current, running)


def backward_block(
    query_part, grad_part, key_part, value_part, allowed, maximum, denominator, delta_sum
):
    scores = jnp.einsum(
        "gqhd,gkhd->ghqk",
        split_heads(query_part),
        split_heads(key_part),
        preferred_element_type=jnp.float32,
    )
    exponent = jnp.where(allowed[:, None], jnp.exp(scores - maximum[..., None]), 0.0)
    probability = exponent / denominator[..., None]
    prob_grad = jnp.einsum(
        "gqhd,gkhd->ghqk",
        split_heads(grad_part),
        split_heads(value_part),
        preferred_element_type=jnp.float32,
    )
    score_grad = (probability * (prob_grad - delta_sum[..., None])).astype(jnp.bfloat16)
    return (probability.astype(jnp.bfloat16), score_grad)


def general_shards(
    states,
    block_slot,
    cont_lengths,
    valid_mask,
    teacher,
    out_grad,
    predict,
    correct,
    norm_attn,
    w_query,
    w_key,
    w_value,
    w_out,
    norm_ffn,
    w_gate,
    w_up,
    w_down,
):
    groups, local_len = valid_mask.shape
    model_width = states.shape[3]
    row_count = groups * local_len
    group_len = block_slot.shape[1] * BLK
    gain_one, query_w, key_w, value_w, out_w, gain_two, gate_w, up_w, down_w = (
        lax.all_gather(norm_attn, "wsh", axis=0, tiled=True),
        lax.all_gather(w_query, "wsh", axis=0, tiled=True),
        lax.all_gather(w_key, "wsh", axis=0, tiled=True),
        lax.all_gather(w_value, "wsh", axis=0, tiled=True),
        lax.all_gather(w_out, "wsh", axis=0, tiled=True),
        lax.all_gather(norm_ffn, "wsh", axis=0, tiled=True),
        lax.all_gather(w_gate, "wsh", axis=0, tiled=True),
        lax.all_gather(w_up, "wsh", axis=0, tiled=True),
        lax.all_gather(w_down, "wsh", axis=0, tiled=True),
    )
    valid_float = valid_mask.astype(jnp.float32)
    valid_total = lax.psum(jnp.sum(valid_float), ("ctx", "wsh"))
    places, segments = token_places(block_slot, cont_lengths)
    offset = lax.axis_index("ctx") * local_len
    own_place = lax.dynamic_slice_in_dim(places, offset, local_len, 1)
    own_segment = lax.dynamic_slice_in_dim(segments, offset, local_len, 1)
    inputs = states.astype(jnp.float32)
    mixed_states = jnp.einsum("ij,gtjd->gtid", predict, inputs, precision=HIGHEST)
    active = mixed_states[:, :, 0].reshape(row_count, model_width)
    gain_first = gain_one.astype(jnp.float32)
    normed, factor_one = rms_forward(active, gain_first)
    normed_low = normed.astype(jnp.bfloat16)
    queries = (
        jnp.dot(normed_low, query_w, preferred_element_type=jnp.float32)
        .astype(jnp.bfloat16)
        .reshape(groups, local_len, model_width)
    )
    key_rows = (
        jnp.dot(normed_low, key_w, preferred_element_type=jnp.float32)
        .astype(jnp.bfloat16)
        .reshape(groups, local_len, model_width)
    )
    values = (
        jnp.dot(normed_low, value_w, preferred_element_type=jnp.float32)
        .astype(jnp.bfloat16)
        .reshape(groups, local_len, model_width)
    )
    initial = (
        jnp.full((groups, HEADS, local_len), NEGATIVE, jnp.float32),
        jnp.zeros((groups, HEADS, local_len), jnp.float32),
        jnp.zeros((groups, local_len, model_width), jnp.float32),
    )
    piece_keys = lax.all_gather(key_rows, "ctx", axis=1, tiled=True)
    piece_values = lax.all_gather(values, "ctx", axis=1, tiled=True)
    piece_len = piece_keys.shape[1]
    block_size = math.gcd(piece_len, local_len)

    def fold_one_block(current, block_index):
        begin = block_index * block_size
        key_part = lax.dynamic_slice_in_dim(piece_keys, begin, block_size, 1)
        value_part = lax.dynamic_slice_in_dim(piece_values, begin, block_size, 1)
        key_place = lax.dynamic_slice_in_dim(places, begin, block_size, 1)
        key_segment = lax.dynamic_slice_in_dim(segments, begin, block_size, 1)
        allowed = visible(own_place, own_segment, key_place, key_segment)
        return (forward_block(current, queries, key_part, value_part, allowed), None)

    finished, unused = lax.scan(
        fold_one_block, initial, jnp.arange(piece_len // block_size, dtype=jnp.int32)
    )
    maximum, denominator, accumulated = finished
    attended = (split_heads(accumulated) / jnp.swapaxes(denominator, 1, 2)[..., None]).reshape(
        row_count, model_width
    )
    attended_low = attended.astype(jnp.bfloat16)
    hidden = active + jnp.dot(attended_low, out_w, preferred_element_type=jnp.float32)
    gain_second = gain_two.astype(jnp.float32)
    normed_two, factor_two = rms_forward(hidden, gain_second)
    normed_two_low = normed_two.astype(jnp.bfloat16)
    gate_proj = jnp.dot(normed_two_low, gate_w, preferred_element_type=jnp.float32)
    up_proj = jnp.dot(normed_two_low, up_w, preferred_element_type=jnp.float32)
    inner_act, inner_pull = jax.vjp(
        lambda gate_in, up_in: jax.nn.gelu(gate_in, approximate=True) * up_in, gate_proj, up_proj
    )
    inner_low = inner_act.astype(jnp.bfloat16)
    result = hidden + jnp.dot(inner_low, down_w, preferred_element_type=jnp.float32)
    difference = (result - active).reshape(groups, local_len, 1, model_width)
    out_states = mixed_states + correct[None, None, :, None] * difference
    new_states = out_states.astype(jnp.bfloat16)
    loss_ratio = lax.axis_size("wsh") * groups * group_len / valid_total
    upstream = out_grad.astype(jnp.float32) + loss_ratio * valid_float[:, :, None, None] * (
        out_states - teacher.astype(jnp.float32)
    )
    correct_local = jnp.sum(upstream * difference, axis=(0, 1, 3))
    result_grad = jnp.einsum("i,gtid->gtd", correct, upstream, precision=HIGHEST).reshape(
        row_count, model_width
    )
    result_low = result_grad.astype(jnp.bfloat16)
    down_grad = jnp.einsum("rf,rd->fd", inner_low, result_low, preferred_element_type=jnp.float32)
    inner_grad = jnp.einsum("rd,fd->rf", result_low, down_w, preferred_element_type=jnp.float32)
    gate_grad, up_grad = inner_pull(inner_grad)
    gate_low = gate_grad.astype(jnp.bfloat16)
    up_low = up_grad.astype(jnp.bfloat16)
    gate_w_grad = jnp.einsum(
        "rd,rf->df", normed_two_low, gate_low, preferred_element_type=jnp.float32
    )
    up_w_grad = jnp.einsum("rd,rf->df", normed_two_low, up_low, preferred_element_type=jnp.float32)
    normed_two_grad = jnp.einsum(
        "rf,df->rd", gate_low, gate_w, preferred_element_type=jnp.float32
    ) + jnp.einsum("rf,df->rd", up_low, up_w, preferred_element_type=jnp.float32)
    hidden_norm_grad, gain_two_grad = rms_backward(hidden, factor_two, gain_second, normed_two_grad)
    hidden_grad = result_grad + hidden_norm_grad
    hidden_low = hidden_grad.astype(jnp.bfloat16)
    out_w_grad = jnp.einsum(
        "rc,rd->cd", attended_low, hidden_low, preferred_element_type=jnp.float32
    )
    attended_grad = jnp.einsum(
        "rd,cd->rc", hidden_low, out_w, preferred_element_type=jnp.float32
    ).astype(jnp.bfloat16)
    delta_sum = jnp.swapaxes(
        jnp.sum(
            split_heads(
                (attended_grad.astype(jnp.float32) * attended).reshape(
                    groups, local_len, model_width
                )
            ),
            axis=-1,
        ),
        1,
        2,
    )
    grad_local = attended_grad.reshape(groups, local_len, model_width)
    zero_grad = jnp.zeros((groups, local_len, model_width), jnp.float32)
    all_keys, all_values = (
        lax.all_gather(key_rows, "ctx", axis=1, tiled=True),
        lax.all_gather(values, "ctx", axis=1, tiled=True),
    )

    def query_step(current, block_index):
        begin = block_index * local_len
        key_part = lax.dynamic_slice_in_dim(all_keys, begin, local_len, 1)
        value_part = lax.dynamic_slice_in_dim(all_values, begin, local_len, 1)
        key_place = lax.dynamic_slice_in_dim(places, begin, local_len, 1)
        key_segment = lax.dynamic_slice_in_dim(segments, begin, local_len, 1)
        allowed = visible(own_place, own_segment, key_place, key_segment)

        def query_compute(query_sum):
            prob_low, score_grad = backward_block(
                queries, grad_local, key_part, value_part, allowed, maximum, denominator, delta_sum
            )
            return query_sum + jnp.einsum(
                "ghqk,gkhd->gqhd",
                score_grad,
                split_heads(key_part),
                preferred_element_type=jnp.float32,
            ).reshape(groups, local_len, model_width)

        return (
            lax.cond(jnp.any(allowed), query_compute, lambda query_sum: query_sum, current),
            None,
        )

    finished, unused = lax.scan(
        query_step, zero_grad, jnp.arange(group_len // local_len, dtype=jnp.int32)
    )
    term_rows = local_len * lax.axis_size("ctx")
    key_block_size = math.gcd(term_rows, local_len)

    def key_one_block(block_index):
        begin = block_index * key_block_size
        key_part = lax.dynamic_slice_in_dim(all_keys, begin, key_block_size, 1)
        value_part = lax.dynamic_slice_in_dim(all_values, begin, key_block_size, 1)
        key_place = lax.dynamic_slice_in_dim(places, begin, key_block_size, 1)
        key_segment = lax.dynamic_slice_in_dim(segments, begin, key_block_size, 1)
        allowed = visible(own_place, own_segment, key_place, key_segment)

        def one_compute(unused_arg):
            prob_low, score_grad = backward_block(
                queries, grad_local, key_part, value_part, allowed, maximum, denominator, delta_sum
            )
            key_add = jnp.einsum(
                "ghqk,gqhd->kghd",
                score_grad,
                split_heads(queries),
                preferred_element_type=jnp.float32,
            ).reshape(key_block_size, groups, model_width)
            value_add = jnp.einsum(
                "ghqk,gqhd->kghd",
                prob_low,
                split_heads(grad_local),
                preferred_element_type=jnp.float32,
            ).reshape(key_block_size, groups, model_width)
            return jnp.stack([key_add, value_add], axis=1)

        return lax.cond(
            jnp.any(allowed),
            one_compute,
            lambda unused_arg: jnp.zeros((key_block_size, 2, groups, model_width), jnp.float32),
            0,
        )

    summed = lax.psum_scatter(
        lax.map(key_one_block, jnp.arange(term_rows // key_block_size, dtype=jnp.int32))
        .reshape(term_rows, 2, groups, model_width)
        .astype(jnp.bfloat16),
        "ctx",
        scatter_dimension=0,
        tiled=True,
    ).astype(jnp.float32)
    key_grad = jnp.swapaxes(summed[:, 0], 0, 1)
    value_grad = jnp.swapaxes(summed[:, 1], 0, 1)
    query_low = finished.reshape(row_count, model_width).astype(jnp.bfloat16)
    key_low = key_grad.reshape(row_count, model_width).astype(jnp.bfloat16)
    value_low = value_grad.reshape(row_count, model_width).astype(jnp.bfloat16)
    query_w_grad = jnp.einsum(
        "rc,rd->cd", normed_low, query_low, preferred_element_type=jnp.float32
    )
    key_w_grad = jnp.einsum("rc,rd->cd", normed_low, key_low, preferred_element_type=jnp.float32)
    value_w_grad = jnp.einsum(
        "rc,rd->cd", normed_low, value_low, preferred_element_type=jnp.float32
    )
    normed_grad = (
        jnp.einsum("rd,cd->rc", query_low, query_w, preferred_element_type=jnp.float32)
        + jnp.einsum("rd,cd->rc", key_low, key_w, preferred_element_type=jnp.float32)
        + jnp.einsum("rd,cd->rc", value_low, value_w, preferred_element_type=jnp.float32)
    )
    active_norm_grad, gain_one_grad = rms_backward(active, factor_one, gain_first, normed_grad)
    active_grad = (hidden_grad + active_norm_grad - result_grad).reshape(
        groups, local_len, 1, model_width
    )
    mixed_grad = jnp.concatenate([upstream[:, :, :1] + active_grad, upstream[:, :, 1:]], axis=2)
    predict_local = jnp.einsum("gtid,gtjd->ij", mixed_grad, inputs, precision=HIGHEST)
    states_grad = jnp.einsum("ij,gtid->gtjd", predict, mixed_grad, precision=HIGHEST).astype(
        jnp.bfloat16
    )
    predict_grad, correct_grad = lax.psum((predict_local, correct_local), ("ctx", "wsh"))
    (
        gain_one_rows,
        query_rows,
        key_grad_rows,
        value_rows,
        out_rows,
        gain_two_rows,
        gate_rows,
        up_rows,
        down_rows,
    ) = (
        lax.psum_scatter(
            gain_one_grad.astype(jnp.bfloat16), "wsh", scatter_dimension=0, tiled=True
        ).astype(jnp.float32),
        lax.psum_scatter(
            query_w_grad.astype(jnp.bfloat16), "wsh", scatter_dimension=0, tiled=True
        ).astype(jnp.float32),
        lax.psum_scatter(
            key_w_grad.astype(jnp.bfloat16), "wsh", scatter_dimension=0, tiled=True
        ).astype(jnp.float32),
        lax.psum_scatter(
            value_w_grad.astype(jnp.bfloat16), "wsh", scatter_dimension=0, tiled=True
        ).astype(jnp.float32),
        lax.psum_scatter(
            out_w_grad.astype(jnp.bfloat16), "wsh", scatter_dimension=0, tiled=True
        ).astype(jnp.float32),
        lax.psum_scatter(
            gain_two_grad.astype(jnp.bfloat16), "wsh", scatter_dimension=0, tiled=True
        ).astype(jnp.float32),
        lax.psum_scatter(
            gate_w_grad.astype(jnp.bfloat16), "wsh", scatter_dimension=0, tiled=True
        ).astype(jnp.float32),
        lax.psum_scatter(
            up_w_grad.astype(jnp.bfloat16), "wsh", scatter_dimension=0, tiled=True
        ).astype(jnp.float32),
        lax.psum_scatter(
            down_grad.astype(jnp.bfloat16), "wsh", scatter_dimension=0, tiled=True
        ).astype(jnp.float32),
    )
    totals = (
        lax.psum(gain_one_rows.astype(jnp.bfloat16), "ctx").astype(jnp.float32),
        lax.psum(query_rows.astype(jnp.bfloat16), "ctx").astype(jnp.float32),
        lax.psum(key_grad_rows.astype(jnp.bfloat16), "ctx").astype(jnp.float32),
        lax.psum(value_rows.astype(jnp.bfloat16), "ctx").astype(jnp.float32),
        lax.psum(out_rows.astype(jnp.bfloat16), "ctx").astype(jnp.float32),
        lax.psum(gain_two_rows.astype(jnp.bfloat16), "ctx").astype(jnp.float32),
        lax.psum(gate_rows.astype(jnp.bfloat16), "ctx").astype(jnp.float32),
        lax.psum(up_rows.astype(jnp.bfloat16), "ctx").astype(jnp.float32),
        lax.psum(down_rows.astype(jnp.bfloat16), "ctx").astype(jnp.float32),
    )
    return (new_states, states_grad, predict_grad, correct_grad) + tuple(totals)


MESH = pl.DeviceIdType.MESH
F32 = jnp.float32
BF16 = jnp.bfloat16
CHIPS = 4
VMEM_LIMIT = 60 * 2**20
DMA = pltpu.SemaphoreType.DMA


def place_on_mesh():
    ctx = lax.axis_index("ctx")
    depth = lax.axis_index("wsh")
    chip = ctx // 2
    core = ctx % 2
    chip_x = chip + 1 - 2 * (chip % 2)
    chip_y = chip + 2 - 4 * (chip // 2)
    return depth, chip, core, chip_x, chip_y, 3 - chip


def signal_all(devices):
    barrier = pltpu.get_barrier_semaphore()
    for device in devices:
        pl.semaphore_signal(barrier, inc=1, device_id=device, device_id_type=MESH)


def wait_all(devices):
    pl.semaphore_wait(pltpu.get_barrier_semaphore(), len(devices))


def remote(src, dst, send, recv, index, device):
    return pltpu.make_async_remote_copy(
        src_ref=src,
        dst_ref=dst,
        send_sem=send.at[index],
        recv_sem=recv.at[index],
        device_id=device,
        device_id_type=MESH,
    )


def comm_params(collective_id):
    return pltpu.CompilerParams(
        collective_id=collective_id, has_side_effects=True, vmem_limit_bytes=VMEM_LIMIT
    )


ANY = pl.BlockSpec(memory_space=pl.ANY)
VM = pl.BlockSpec(memory_space=pltpu.VMEM)
SM = pl.BlockSpec(memory_space=pltpu.SMEM)


def ring_sends(own, out, slot_of, chip, core, depth, chip_x, chip_y, send, recv):
    half = own.shape[0] // 2
    top, low = pl.ds(0, half), pl.ds(half, half)
    dev_x, dev_y = (2 * chip_x + core, depth), (2 * chip_y + core, depth)
    here = slot_of(chip)
    return [
        remote(own.at[top], out.at[here, top], send, recv, 0, dev_x),
        remote(own.at[low], out.at[here, low], send, recv, 1, dev_y),
        remote(own.at[low], out.at[here, low], send, recv, 2, dev_x),
        remote(own.at[top], out.at[here, top], send, recv, 3, dev_y),
        remote(out.at[slot_of(chip_x), top], out.at[slot_of(chip_x), top], send, recv, 4, dev_y),
        remote(out.at[slot_of(chip_y), low], out.at[slot_of(chip_y), low], send, recv, 5, dev_x),
    ]


NT = (((1,), (1,)), ((), ()))
TN = (((0,), (0,)), ((), ()))
TILE = 256
ROWS = 32
LOCAL_HEADS = HEADS // CHIPS
CHIP_COLS = LOCAL_HEADS * HD


def head_mask(rows, head):
    lane = lax.broadcasted_iota(jnp.int32, (rows, CHIP_COLS), 1)
    return (lane >= head * HD) & (lane < (head + 1) * HD)


def aligned(index, size):
    return pl.ds(pl.multiple_of(index * size, size), size)


def norm_factor(rows):
    return lax.rsqrt(jnp.mean(rows * rows, axis=1, keepdims=True) + EPSILON)


def as_column(row):
    return jnp.broadcast_to(row, (8, row.shape[1])).T[:, 0:1]


def mix(states_ref, at, p_ref, i):
    return p_ref[i, 0] * states_ref[at, 0, :].astype(F32) + p_ref[i, 1] * states_ref[at, 1, :].astype(F32)


def plane_sum(parts, near_in, far_in, chip, core, depth, chip_x, chip_y, chip_d, send, recv):
    half = parts.shape[1] // 2
    top, low = pl.ds(0, half), pl.ds(half, half)
    dev_x, dev_y = (2 * chip_x + core, depth), (2 * chip_y + core, depth)
    copies = [
        remote(parts.at[chip_d, top], far_in.at[0], send, recv, 0, dev_x),
        remote(parts.at[chip_d, low], far_in.at[1], send, recv, 1, dev_y),
        remote(parts.at[chip_x, top], near_in.at[0, top], send, recv, 2, dev_x),
        remote(parts.at[chip_y, low], near_in.at[1, low], send, recv, 3, dev_y),
        remote(parts.at[chip_y, top], near_in.at[1, top], send, recv, 4, dev_y),
        remote(parts.at[chip_x, low], near_in.at[0, low], send, recv, 5, dev_x),
    ]

    def give(i):
        for copy in (copies[:2] if i == 2 else copies[2 + i : 3 + i]):
            copy.start()

    def relay():
        for i, (c, rows) in enumerate(((chip_y, slice(0, half)), (chip_x, slice(half, 2 * half)))):
            copies[i].wait_recv()
            parts[c, rows] = (parts[c, rows].astype(F32) + far_in[i].astype(F32)).astype(BF16)
            copies[4 + i].start()

    def receive():
        for copy in copies[2:]:
            copy.wait_recv()

    return give, relay, receive, copies


def plane_peers(chip, core, depth, chip_x, chip_y, chip_d):
    same = [(2 * c + core, depth) for c in (chip_x, chip_y, chip_d)]
    return same + [(2 * c + 1 - core, depth) for c in (chip, chip_x, chip_y, chip_d)]


def total_over_mesh(own_ref, arrived, staged, far, across, peers, bsend, brecv, csend, crecv):
    first = [remote(own_ref, arrived.at[i], bsend, brecv, i, d) for i, d in enumerate(across)]
    second = [remote(staged, far.at[i], csend, crecv, i, d) for i, d in enumerate(peers)]

    def start():
        for copy in first:
            copy.start()

    def turn():
        total = own_ref[...]
        for i, copy in enumerate(first):
            copy.wait_recv()
        for i in range(len(first)):
            total = total + arrived[i]
        staged[...] = total
        for copy in second:
            copy.start()

    def end():
        for copy in second:
            copy.wait_recv()
        total = staged[...]
        for i in range(len(second)):
            total = total + far[i]
        for copy in first + second:
            copy.wait_send()
        return total

    return start, turn, end


def total_scratch(shape, depths):
    return [
        pltpu.VMEM((depths - 1,) + shape, F32),
        pltpu.VMEM(shape, F32),
        pltpu.VMEM((2 * CHIPS - 1,) + shape, F32),
        DMA((depths - 1,)),
        DMA((depths - 1,)),
        DMA((2 * CHIPS - 1,)),
        DMA((2 * CHIPS - 1,)),
    ]


def gelu_parts(v):
    scale = math.sqrt(2 / math.pi)
    square = v * v
    t = jnp.tanh(scale * v * (1.0 + 0.044715 * square))
    rise = 0.5 * (1.0 + t)
    return v * rise, rise + 0.5 * v * (1.0 - t * t) * scale * (1.0 + 0.134145 * square)


def pair_places(slots_ref, pair):
    one, two = slots_ref[2 * pair], slots_ref[2 * pair + 1]
    second = (one >= PROMPT // BLK).astype(jnp.int32)
    return second, jnp.minimum(one, two), jnp.maximum(one, two)


def own_pair(pair, per_device):
    core = lax.axis_index("ctx") % 2
    pairs = per_device // 2
    return (pair // pairs) * per_device + core * pairs + pair % pairs


PER_TILE = TILE // BLK


def fill_bias(bias, kind, tile_step, slots_ref, lengths_ref, per_device, group_pairs):
    lane = lax.broadcasted_iota(jnp.int32, (1, TILE), 1)
    high = jnp.zeros((1, TILE), jnp.int32)
    for i in range(PER_TILE):
        _, prompt, cont = pair_places(slots_ref, own_pair(tile_step * PER_TILE + i, per_device))
        block = prompt if kind == 0 else cont
        high = jnp.where(lane >= i * BLK, (block - i) * BLK + lane, high)
    low = jnp.zeros((1, TILE), jnp.int32)
    if kind == 1:
        start = PROMPT
        for i in range(lengths_ref.shape[0]):
            low = jnp.where(high >= start, start, low)
            start = start + lengths_ref[i]
    offset = lax.broadcasted_iota(jnp.int32, (BLK, TILE), 0)

    def one_block(pair, _):
        _, prompt, cont = pair_places(slots_ref, pair)
        base = (prompt if kind == 0 else cont) * BLK
        seen = offset <= high - base
        if kind == 1:
            seen = seen & (offset >= low - base)
        bias[pair // PER_TILE, aligned(pair % PER_TILE, BLK), 0:TILE] = jnp.where(seen, 0.0, NEGATIVE)
        return 0

    lax.fori_loop(0, group_pairs, one_block, 0)


def either(second, one, two):
    swap = second == 1
    return jnp.where(swap, two, one), jnp.where(swap, one, two)


def to_pair_order(source, target, slots_ref, group_pairs):
    def one_pair(pair, _):
        second, _, _ = pair_places(slots_ref, pair)
        first, last = either(second, source[aligned(2 * pair, BLK), :], source[aligned(2 * pair + 1, BLK), :])
        target[aligned(pair, BLK), :] = first
        target[aligned(group_pairs + pair, BLK), :] = last
        return 0

    lax.fori_loop(0, group_pairs, one_pair, 0)


def own_to_pair_order(source, target, slots_ref, pairs, per_device):
    def one_pair(pair, _):
        second, _, _ = pair_places(slots_ref, own_pair(pair, per_device))
        first, last = either(second, source[aligned(2 * pair, BLK), :], source[aligned(2 * pair + 1, BLK), :])
        target[aligned(pair, BLK), :] = first
        target[aligned(pairs + pair, BLK), :] = last
        return 0

    lax.fori_loop(0, pairs, one_pair, 0)


def own_to_slot_order(source, target, slots_ref, pairs, per_device):
    def one_pair(pair, _):
        second, _, _ = pair_places(slots_ref, own_pair(pair, per_device))
        first, last = either(second, source[aligned(pair, BLK), :], source[aligned(pairs + pair, BLK), :])
        target[aligned(2 * pair, BLK), :] = first
        target[aligned(2 * pair + 1, BLK), :] = last
        return 0

    lax.fori_loop(0, pairs, one_pair, 0)


def line_reduce(pieces, acc, up_in, down_in, up_out, down_out, sems):
    depth, chip, core, _, _, _ = place_on_mesh()
    depths = pieces.shape[0]
    last = depths - 1
    up_send, up_recv, down_send, down_recv = sems
    above = (2 * chip + core, lax.rem(depth + 1, depths))
    below = (2 * chip + core, lax.rem(depth + last, depths))

    def up(source, k):
        return remote(source, up_in.at[k], up_send, up_recv, k, above)

    def down(source, k):
        return remote(source, down_in.at[k], down_send, down_recv, k, below)

    def start():
        @pl.when(depth == 0)
        def _():
            for k in range(last):
                up(pieces.at[last - k], k).start()

        @pl.when(depth == last)
        def _():
            for k in range(last):
                down(pieces.at[k], k).start()

    def hop(k):
        @pl.when((depth >= 1) & (depth <= k))
        def _():
            up(up_in.at[k - 1], k - 1).wait_recv()
            mine = pieces[jnp.clip(depth + last - k, 0, last)]
            up_out[k - 1] = (mine.astype(F32) + up_in[k - 1].astype(F32)).astype(BF16)
            up(up_out.at[k - 1], k).start()

        @pl.when((depth <= last - 1) & (depth >= last - k))
        def _():
            down(down_in.at[k - 1], k - 1).wait_recv()
            mine = pieces[jnp.clip(depth + k - last, 0, last)]
            down_out[k - 1] = (mine.astype(F32) + down_in[k - 1].astype(F32)).astype(BF16)
            down(down_out.at[k - 1], k).start()

    def result():
        acc[...] = pieces[depth].astype(F32)

        @pl.when(depth >= 1)
        def _():
            up(up_in.at[last - 1], last - 1).wait_recv()
            acc[...] += up_in[last - 1].astype(F32)

        @pl.when(depth <= last - 1)
        def _():
            down(down_in.at[last - 1], last - 1).wait_recv()
            acc[...] += down_in[last - 1].astype(F32)

    def finish():
        @pl.when(depth == 0)
        def _():
            for k in range(last):
                up(pieces.at[last - k], k).wait_send()

        @pl.when(depth == last)
        def _():
            for k in range(last):
                down(pieces.at[k], k).wait_send()

        for k in range(1, last):

            @pl.when((depth >= 1) & (depth <= k))
            def _(k=k):
                up(up_out.at[k - 1], k).wait_send()

            @pl.when((depth <= last - 1) & (depth >= last - k))
            def _(k=k):
                down(down_out.at[k - 1], k).wait_send()

    return start, hop, result, finish


def forward(
    slots, lengths, predict, correct, states, out_grad, teacher, valid, gain_one, gain_two,
    w_query, w_key, w_value, w_out, w_gate, w_up, w_down, collective_id,
):
    rows, _, width = states.shape
    shard = w_query.shape[0]
    half = shard // 2
    depths = width // shard
    hidden_cols = w_gate.shape[1]
    columns = hidden_cols // CHIPS
    split = columns // depths
    out_rows = shard // CHIPS
    blocks = rows // ROWS
    col_tiles = columns // TILE
    tokens = 2 * CHIPS * rows
    queries = CHIPS * rows
    tiles = queries // TILE
    per_device = rows // BLK
    group_pairs = tokens // (2 * BLK)
    pairs = queries // (2 * BLK)
    mesh_tokens = tokens * depths
    piece_lanes = 3 * CHIP_COLS

    def kernel(
        slots_ref, lengths_ref, p_ref, c_ref, s_ref, g_in, t_in, v_ref, g1_ref, g2_ref,
        wq_ref, wk_ref, wv_ref, wo_ref, wg_ref, wu_ref, wd_ref,
        new_out, up0_out, up1_out, hg_out, da_ref, dwo_ref, ffa_ref, ffb_ref, sums_ref,
        x_out, w_out_ref, q_out, k_out, v_out, oT_out, lse_ref,
        new_ref, up0_ref, up1_ref, hg_ref, all_rows, w_all, q_pairs, k_pairs, v_pairs, oT_ref, dwo, dwo_other,
        g_ref, t_ref, w_ff, w_wo, qkv, att_all, packs, packed_in, packed_grad, hidden, own, x_rows, r_rows, xT, innerT, inner, gate, up, gate_low, up_low,
        own_weight, part1, part2, got1, got2, far1, far2, dw, dw_other, a_up, a_down, buf, wide, count, q_slot, k_slot, v_slot, vT,
        lsend, fsend, frecv, fosend, forecv, qsend, qrecv, qosend, qorecv,
        osend, orecv, oosend, oorecv, opsend, oprecv,
        rsend, rrecv, rosend, rorecv, send0, recv0, send1, recv1, send2, recv2, send3, recv3,
        ag1s, ag1r, ag2s, ag2r, dsend, drecv, osems, xsems, *rest,
    ):
        a_sems, total_refs = rest[:4], rest[4:]
        stores = []

        def store(index, source, target):
            copy = pltpu.make_async_copy(source, target, osems.at[index])
            copy.start()
            stores.append(copy)

        depth, chip, core, chip_x, chip_y, chip_d = place_on_mesh()
        near = [(c, (2 * c + core, depth)) for c in (chip_x, chip_y, chip_d)]
        other = (2 * chip + 1 - core, depth)
        across = [
            (2 * chip + core, lax.rem(depth + step, depths)) for step in range(1, depths)
        ]
        peers = plane_peers(chip, core, depth, chip_x, chip_y, chip_d)
        signal_all(peers + across)

        mine = pl.ds(core * half, half)
        loads = [
            pltpu.make_async_copy(w.at[mine], buf.at[i], lsend.at[i])
            for i, w in enumerate((wq_ref, wk_ref, wv_ref))
        ] + [
            pltpu.make_async_copy(wg_ref.at[mine], wide.at[0], lsend.at[3]),
            pltpu.make_async_copy(wu_ref.at[mine], wide.at[1], lsend.at[4]),
            pltpu.make_async_copy(
                wd_ref.at[pl.ds(chip * split + core * half, half)], w_ff.at[2, depth, core], lsend.at[5]
            ),
            pltpu.make_async_copy(
                wo_ref.at[pl.ds(chip * out_rows, out_rows)], w_wo.at[depth, chip], lsend.at[6]
            ),
            pltpu.make_async_copy(g_in, g_ref, lsend.at[7]),
            pltpu.make_async_copy(t_in, t_ref, lsend.at[8]),
        ]
        for copy in loads:
            copy.start()
        count[...] = jnp.broadcast_to(
            jnp.sum(v_ref[...].astype(F32), axis=1, keepdims=True), count.shape
        )

        def input_norm(i, _):
            at = aligned(i, ROWS)
            active = mix(s_ref, at, p_ref, 0)
            own[0, at, :] = (active * norm_factor(active)).astype(BF16)
            return 0

        lax.fori_loop(0, blocks, input_norm, 0)

        def gain_column(ref):
            both = jnp.broadcast_to(ref[...].astype(F32).reshape(1, shard), (8, shard)).T
            return jnp.where(core == 0, both[:half, 0:1], both[half:, 0:1])

        one, two = gain_column(g1_ref), gain_column(g2_ref)
        wait_all(peers + across)

        def slot(chip_index):
            return 2 * chip_index + core

        start_count, turn_count, end_count = total_over_mesh(
            count, *total_refs[:3], across, peers, *total_refs[3:]
        )
        start_count()
        ring0 = ring_sends(
            own.at[0], all_rows, slot, chip, core, depth, chip_x, chip_y, rsend, rrecv
        )
        for copy in ring0[:4]:
            copy.start()

        def rows_to_other(index, chip_index):
            ref = all_rows.at[slot(chip_index)]
            return remote(own.at[0] if index == 0 else ref, ref, rosend, rorecv, index, other)

        shared0 = [rows_to_other(i, c) for i, c in enumerate((chip, chip_x, chip_y, chip_d))]
        shared0[0].start()
        all_rows[slot(chip)] = own[0]

        for copy in loads[:3]:
            copy.wait()
        for p in range(CHIPS):

            @pl.when(chip == p)
            def _(p=p):
                cols = jnp.concatenate(
                    [buf[i, :, p * CHIP_COLS : (p + 1) * CHIP_COLS].astype(F32) for i in range(3)], axis=1
                )
                qkv[depth, core] = (cols * one).astype(BF16)

        qkv_mine = qkv.at[depth, core]
        q_copies = [
            remote(qkv_mine, qkv_mine, qsend, qrecv, i, device) for i, device in enumerate(across)
        ]
        q_shared = [remote(qkv_mine, qkv_mine, qosend, qorecv, 0, other)]
        for copy in q_copies + q_shared:
            copy.start()

        loads[6].wait()
        o_copies = [
            remote(w_wo.at[depth, chip], w_wo.at[depth, chip], osend, orecv, i, device)
            for i, device in enumerate(across)
        ]
        o_shared = []
        for i in range(depths - 1):
            came = w_wo.at[lax.rem(depth + depths - 1 - i, depths), chip]
            o_shared.append(remote(came, came, oosend, oorecv, i, other))

        def carried(i, act):
            pl.when(core == (i + 1) % 2)(act)

        def not_carried(i, act):
            pl.when(core != (i + 1) % 2)(act)

        for i in range(depths - 1):
            carried(i, o_copies[i].start)

        for copy in loads[3:6]:
            copy.wait()
        for p in range(CHIPS):

            @pl.when(chip == p)
            def _(p=p):
                for i in range(2):
                    cols = jnp.concatenate(
                        [
                            wide[i, :, (z * CHIPS + p) * split : (z * CHIPS + p + 1) * split].astype(F32)
                            for z in range(depths)
                        ],
                        axis=1,
                    )
                    w_ff[i, depth, core] = (cols * two).astype(BF16)

        line_up = (2 * chip + core, lax.rem(depth + 1, depths))
        line_down = (2 * chip + core, lax.rem(depth + depths - 1, depths))
        hops = []
        for stage in range(1, depths):
            for direction, device, index in ((1, line_up, stage - 1), (-1, line_down, depths + stage - 2)):
                goes = jnp.clip(depth - direction * (stage - 1), 0, depths - 1)
                comes = jnp.clip(depth - direction * stage, 0, depths - 1)
                piece, came = w_ff.at[:, goes, core], w_ff.at[:, comes, core]
                if direction == 1:
                    sends, receives = (depth >= stage - 1) & (depth < depths - 1), depth >= stage
                else:
                    sends, receives = (depth <= depths - stage) & (depth > 0), depth < depths - stage
                hops.append(
                    (
                        stage,
                        sends,
                        receives,
                        remote(piece, piece, fsend, frecv, index, device),
                        remote(came, came, fosend, forecv, index, other),
                    )
                )
        ff_mine = remote(w_ff.at[:, depth, core], w_ff.at[:, depth, core], fosend, forecv, 2 * depths - 2, other)
        ff_mine.start()

        def send_hop(stage):
            for at, sends, _, hop, _ in hops:
                if at == stage:
                    pl.when(sends)(hop.start)

        def take_hop(stage):
            for at, _, receives, hop, share in hops:
                if at == stage:

                    @pl.when(receives)
                    def _(hop=hop, share=share):
                        hop.wait_recv()
                        share.start()

        send_hop(1)
        turn_count()
        ring0[0].wait_recv()
        ring0[4].start()
        ring0[1].wait_recv()
        ring0[5].start()
        for i in range(depths - 1):
            q_copies[i].wait_recv()
            came = qkv.at[lax.rem(depth + depths - 1 - i, depths), core]
            share = remote(came, came, qosend, qorecv, 1 + i, other)
            share.start()
            q_shared.append(share)
        ring0[2].wait_recv()
        shared0[1].start()
        ring0[3].wait_recv()
        shared0[2].start()
        for copy in q_shared:
            copy.wait_recv()
        for i in range(3):
            for z in range(depths):
                for c in range(2):
                    at = (z * 2 + c) * half
                    w_all[i, at : at + half, :] = qkv[z, c, :, i * CHIP_COLS : (i + 1) * CHIP_COLS]

        def project(device_slot, with_queries):
            x = all_rows[device_slot]
            at = aligned(device_slot, rows)
            k_slot[at, :] = jnp.dot(x, w_all[1], preferred_element_type=F32).astype(BF16)
            v_slot[at, :] = jnp.dot(x, w_all[2], preferred_element_type=F32).astype(BF16)
            if with_queries:
                q_slot[aligned(device_slot // 2, rows), :] = jnp.dot(
                    x, w_all[0], preferred_element_type=F32
                ).astype(BF16)

        for c in (chip, chip_x, chip_y):
            project(slot(c), True)
        for i, c in enumerate((chip, chip_x, chip_y)):
            shared0[i].wait_recv()
            project(2 * c + 1 - core, False)
        ring0[4].wait_recv()
        ring0[5].wait_recv()
        shared0[3].start()
        project(slot(chip_d), True)
        for i in range(depths - 1):

            def came_here(i=i):
                o_copies[i].wait_recv()
                o_shared[i].start()

            carried(i, came_here)
        for i in range(depths - 1):
            not_carried(i, o_shared[i].wait_recv)
        carry = pl.ds(core * (depths // 2), depths // 2)
        o_plane = [
            remote(w_wo.at[carry, chip], w_wo.at[carry, chip], opsend, oprecv, i, device)
            for i, (_, device) in enumerate(near)
        ]
        for copy in o_plane:
            copy.start()
        o_across = [
            remote(w_wo.at[carry, c], w_wo.at[carry, c], opsend, oprecv, 3 + i, other)
            for i, (c, _) in enumerate(near)
        ]
        shared0[3].wait_recv()
        project(2 * chip_d + 1 - core, False)

        for i in range(CHIPS):
            x_copy = pltpu.make_async_copy(all_rows.at[2 * i + core], x_out.at[i], xsems.at[i])
            x_copy.start()
            stores.append(x_copy)
        store(0, w_all, w_out_ref)

        to_pair_order(k_slot, k_pairs, slots_ref, group_pairs)
        to_pair_order(v_slot, v_pairs, slots_ref, group_pairs)
        own_to_pair_order(q_slot, q_pairs, slots_ref, pairs, per_device)

        store(1, q_pairs, q_out)
        store(2, k_pairs, k_out)
        store(3, v_pairs, v_out)

        def turn_values(i, _):
            vT[:, aligned(i, TILE)] = v_pairs[aligned(i, TILE), :].T
            return 0

        lax.fori_loop(0, tokens // TILE, turn_values, 0)
        half_keys = group_pairs * BLK
        half_tiles = half_keys // TILE
        scores, bias = gate, up

        def cell(k_tile):
            lanes = (k_tile // CHIPS) * TILE
            return k_tile % CHIPS, slice(lanes, lanes + TILE)

        def attend(kind, step):
            tile = kind * (tiles // 2) + step
            key_tiles = half_tiles * (kind + 1)
            q = q_pairs[aligned(tile, TILE), :]
            fill_bias(bias, kind, step, slots_ref, lengths_ref, per_device, group_pairs)
            for head in range(LOCAL_HEADS):
                heads = slice(head * HD, (head + 1) * HD)
                q_head = jnp.where(head_mask(TILE, head), q, jnp.zeros_like(q))
                top = jnp.full((1, TILE), NEGATIVE, F32)
                for k_tile in range(key_tiles):
                    s = lax.dot_general(
                        k_pairs[k_tile * TILE : (k_tile + 1) * TILE, :], q_head, NT, preferred_element_type=F32
                    )
                    if k_tile >= key_tiles - half_tiles:
                        s = s + bias[k_tile - (key_tiles - half_tiles), :, 0:TILE]
                    index, lanes = cell(k_tile)
                    scores[index, :, lanes] = s
                    top = jnp.maximum(top, jnp.max(s, axis=0, keepdims=True))
                total = jnp.zeros((1, TILE), F32)
                out = jnp.zeros((HD, TILE), F32)
                for k_tile in range(key_tiles):
                    index, lanes = cell(k_tile)
                    e = jnp.exp(scores[index, :, lanes] - top)
                    total = total + jnp.sum(e, axis=0, keepdims=True)
                    out = out + jnp.dot(
                        vT[heads, k_tile * TILE : (k_tile + 1) * TILE], e.astype(BF16), preferred_element_type=F32
                    )
                oT_ref[tile, heads, :] = out / total
                lse_ref[tile, head] = top + jnp.log(total)
            q_slot[aligned(tile, TILE), :] = oT_ref[tile].T.astype(BF16)

        def both_steps(kind):
            def body(step, _):
                attend(kind, step)
                return 0

            lax.fori_loop(0, tiles // 2, body, 0)

        both_steps(1)
        take_hop(1)
        send_hop(2)
        for copy, passed in zip(o_plane, o_across):
            copy.wait_recv()
            passed.start()
        both_steps(0)

        store(4, oT_ref, oT_out)
        own_to_slot_order(q_slot, k_slot, slots_ref, pairs, per_device)
        half_rows = rows // 2

        def pack(value):
            return jnp.concatenate([value[:half_rows].astype(F32), value[half_rows:].astype(F32)], axis=1).astype(BF16)

        def unpack(target, packed):
            target[0:half_rows, :] = packed[:, 0:CHIP_COLS]
            target[half_rows:rows, :] = packed[:, CHIP_COLS : 2 * CHIP_COLS]

        for c in range(CHIPS):
            packs[c] = pack(k_slot[c * rows : (c + 1) * rows, :])
        sends0 = [
            remote(packs.at[c], packed_in.at[i], send0, recv0, i, device)
            for i, (c, device) in enumerate(near)
        ]
        for copy in sends0:
            copy.start()
        unpack(att_all.at[chip], packs[chip])
        for copy in o_across:
            copy.wait_recv()
        for copy in sends0:
            copy.wait()
        for i, (c, _) in enumerate(near):
            unpack(att_all.at[c], packed_in[i])

        def w_out_rows(p):
            return w_wo[p].reshape(CHIP_COLS, width)

        for p in range(CHIPS):
            term = jnp.dot(att_all[p], w_out_rows(p), preferred_element_type=F32)
            hidden[...] = term if p == 0 else hidden[...] + term

        take_hop(2)
        send_hop(3)

        def first_norm(i, _):
            at = aligned(i, ROWS)
            h = hidden[at, :] + mix(s_ref, at, p_ref, 0)
            hidden[at, :] = h
            own[1, at, :] = (h * norm_factor(h)).astype(BF16)
            return 0

        lax.fori_loop(0, blocks, first_norm, 0)

        def ring(source, target, send, recv):
            return ring_sends(
                source, target, lambda c: c, chip, core, depth, chip_x, chip_y, send, recv
            )

        ring1 = ring(own.at[1], x_rows, ag1s, ag1r)
        for copy in ring1[:4]:
            copy.start()
        x_rows[chip] = own[1]
        ring1[0].wait_recv()
        ring1[4].start()
        ring1[1].wait_recv()
        ring1[5].start()
        take_hop(3)
        ff_mine.wait_recv()
        for _, _, receives, _, share in hops:
            pl.when(receives)(share.wait_recv)

        def w_rows(i):
            return w_ff[i].reshape(width, columns)

        def ff_forward(c):
            x = x_rows[c]
            for n in range(col_tiles):
                cols = slice(n * TILE, (n + 1) * TILE)
                g = jnp.dot(x, w_rows(0)[:, cols], preferred_element_type=F32)
                u = jnp.dot(x, w_rows(1)[:, cols], preferred_element_type=F32)
                gate[c, :, cols] = g
                up[c, :, cols] = u
                inner[c, :, cols] = (gelu_parts(g)[0] * u).astype(BF16)
            return jnp.dot(inner[c], w_rows(2), preferred_element_type=F32)

        give1, relay1, receive1, sends1 = plane_sum(
            part1, got1, far1, chip, core, depth, chip_x, chip_y, chip_d, send1, recv1
        )
        up0_ref[...] = ff_forward(chip)
        for i, (c, _) in enumerate(near):
            if i < 2:
                ring1[2 + i].wait_recv()
            else:
                ring1[4].wait_recv()
                ring1[5].wait_recv()
            part1[c] = ff_forward(c).astype(BF16)
            give1(i)
        relay1()

        def turn(i, _):
            xT[:, aligned(i, rows)] = x_rows[i].T
            innerT[:, aligned(i, rows)] = inner[i].T
            return 0

        lax.fori_loop(0, CHIPS, turn, 0)
        for copy in loads[7:]:
            copy.wait()
        valid_count = end_count()
        weight = as_column(v_ref[...].astype(F32)) * (mesh_tokens / valid_count[0:1, 0:1])
        own_weight[...] = jnp.broadcast_to(weight, own_weight.shape)
        receive1()

        def outputs(i, sums):
            at = aligned(i, ROWS)
            a = mix(s_ref, at, p_ref, 0)
            result = hidden[at, :] + up0_ref[at, :]
            for j in range(2):
                result = result + got1[j, at, :].astype(F32)
            difference = result - a
            row_weight = own_weight[at, 0:1]
            c0, c1 = c_ref[0], c_ref[1]
            out0 = a + c0 * difference
            out1 = mix(s_ref, at, p_ref, 1) + c1 * difference
            new_ref[at, 0, :] = out0.astype(BF16)
            new_ref[at, 1, :] = out1.astype(BF16)
            up0 = g_ref[at, 0, :].astype(F32) + row_weight * (out0 - t_ref[at, 0, :].astype(F32))
            up1 = g_ref[at, 1, :].astype(F32) + row_weight * (out1 - t_ref[at, 1, :].astype(F32))
            up0_ref[at, :] = up0
            up1_ref[at, :] = up1
            own[2, at, :] = (c0 * up0 + c1 * up1).astype(BF16)
            return (
                sums[0] + jnp.sum(up0 * difference, axis=0, keepdims=True),
                sums[1] + jnp.sum(up1 * difference, axis=0, keepdims=True),
            )

        zero = jnp.zeros((1, width), F32)
        correct_sums = lax.fori_loop(0, blocks, outputs, (zero, zero))
        sums_ref[...] = jnp.zeros_like(sums_ref)
        sums_ref[2:3, :] = correct_sums[0]
        sums_ref[3:4, :] = correct_sums[1]
        store(5, new_ref, new_out)
        store(6, up0_ref, up0_out)
        store(7, up1_ref, up1_out)

        ring2 = ring(own.at[2], r_rows, ag2s, ag2r)
        for copy in ring2[:4]:
            copy.start()
        r_rows[chip] = own[2]

        def ff_backward(c):
            r = r_rows[c]
            for n in range(col_tiles):
                cols = slice(n * TILE, (n + 1) * TILE)
                inner_grad = lax.dot_general(r, w_rows(2)[cols, :], NT, preferred_element_type=F32)
                value, slope = gelu_parts(gate[c, :, cols])
                gate_low[c, :, cols] = (inner_grad * up[c, :, cols] * slope).astype(BF16)
                up_low[c, :, cols] = (inner_grad * value).astype(BF16)
            return lax.dot_general(
                gate_low[c], w_rows(0), NT, preferred_element_type=F32
            ) + lax.dot_general(up_low[c], w_rows(1), NT, preferred_element_type=F32)

        give2, relay2, receive2, sends2 = plane_sum(
            part2, got2, far2, chip, core, depth, chip_x, chip_y, chip_d, send2, recv2
        )
        hg_ref[...] = ff_backward(chip)
        ring2[0].wait_recv()
        ring2[4].start()
        ring2[1].wait_recv()
        ring2[5].start()
        for i, (c, _) in enumerate(near):
            if i < 2:
                ring2[2 + i].wait_recv()
            else:
                ring2[4].wait_recv()
                ring2[5].wait_recv()
            part2[c] = ff_backward(c).astype(BF16)
            give2(i)

        def weight_grads(terms):
            def body(z, _):
                at = aligned(z, shard)
                for i, left, right in terms:
                    grad = jnp.dot(
                        left[at, :], right[...].reshape(queries, -1), preferred_element_type=F32
                    ).astype(BF16)
                    dw[z, 0, i * half : (i + 1) * half, :] = grad[:half]
                    dw[z, 1, i * half : (i + 1) * half, :] = grad[half:]
                return 0

            lax.fori_loop(0, depths, body, 0)

        early, late = pl.ds(0, half), pl.ds(half, 2 * half)

        def swap_rows(index, part):
            return remote(dw.at[:, 1 - core, part], dw_other.at[:, part], dsend, drecv, index, other)

        def add_cores(part):
            def body(z, _):
                dw_other[z, part, :] = (
                    dw[z, core, part, :].astype(F32) + dw_other[z, part, :].astype(F32)
                ).astype(BF16)
                return 0

            lax.fori_loop(0, depths, body, 0)

        swaps = [swap_rows(0, early), swap_rows(1, late)]
        weight_grads(((0, innerT, r_rows),))
        swaps[0].start()
        for copy in sends1:
            copy.wait_send()
        a_start, a_hop, a_result, a_finish = line_reduce(
            dw_other.at[:, early], gate.at[0, pl.ds(0, half)], a_up, a_down,
            part1.at[pl.ds(0, 2), pl.ds(0, half)], part1.at[pl.ds(2, 2), pl.ds(0, half)], a_sems,
        )
        swaps[0].wait_recv()
        add_cores(early)
        a_start()
        relay2()
        weight_grads(((1, xT, gate_low), (2, xT, up_low)))
        swaps[1].start()
        a_hop(1)
        receive2()

        def second_norm(i, gain_sum):
            at = aligned(i, ROWS)
            h = hidden[at, :]
            weighted = hg_ref[at, :]
            for j in range(2):
                weighted = weighted + got2[j, at, :].astype(F32)
            factor = norm_factor(h)
            mean = jnp.mean(weighted * h, axis=1, keepdims=True)
            result_grad = c_ref[0] * up0_ref[at, :] + c_ref[1] * up1_ref[at, :]
            hidden_grad = result_grad + (factor * weighted - h * (factor * factor * factor * mean))
            hg_ref[at, :] = hidden_grad
            own[3, at, :] = hidden_grad.astype(BF16)
            return gain_sum + jnp.sum(weighted * h * factor, axis=0, keepdims=True)

        sums_ref[1:2, :] = lax.fori_loop(0, blocks, second_norm, zero)
        store(10, hg_ref, hg_out)

        sends3 = [
            remote(packs.at[c], packed_grad.at[i], send3, recv3, i, device)
            for i, (c, device) in enumerate(near)
        ]

        def att_grad(c):
            return lax.dot_general(own[3], w_out_rows(c), NT, preferred_element_type=F32)

        for i in (2, 0, 1):
            packs[near[i][0]] = pack(att_grad(near[i][0]))
            sends3[i].start()
        da_ref[chip] = att_grad(chip).astype(BF16)
        for i, c in enumerate((chip, chip_x, chip_y, chip_d)):
            grad = jnp.dot(att_all[c].T, own[3], preferred_element_type=F32).astype(BF16)
            dwo[i, 0] = grad[:half]
            dwo[i, 1] = grad[half:]
        out_swap = remote(dwo.at[:, 1 - core], dwo_other, dsend, drecv, 2, other)
        out_swap.start()
        swaps[1].wait_recv()
        add_cores(late)
        store(8, dw_other.at[:, late], ffb_ref)
        a_hop(2)
        out_swap.wait_recv()
        for i in range(CHIPS):
            dwo_other[i] = (dwo[i, core].astype(F32) + dwo_other[i].astype(F32)).astype(BF16)
        store(9, dwo_other, dwo_ref)
        a_result()
        ffa_ref[...] = gate[0, 0:half, :].astype(BF16)
        for copy in sends3:
            copy.wait_recv()
        for i, (c, _) in enumerate(near):
            unpack(da_ref.at[c], packed_grad[i])
        sent = ring0 + shared0 + q_copies + q_shared + o_plane + o_across + sends2 + sends3
        for copy in sent + ring1 + ring2 + swaps + [out_swap, ff_mine]:
            copy.wait_send()
        a_finish()
        for i in range(depths - 1):
            carried(i, o_copies[i].wait_send)
            carried(i, o_shared[i].wait_send)
        for _, sends, receives, hop, share in hops:
            pl.when(sends)(hop.wait_send)
            pl.when(receives)(share.wait_send)
        for copy in stores:
            copy.wait()

    block = (rows, width)
    pair = (rows, 2, width)
    wide_rows = (CHIPS, rows, width)
    hid_rows = (CHIPS, rows, columns)

    def out(shape, dtype):
        return jax.ShapeDtypeStruct(shape, dtype)

    vmem = pltpu.VMEM
    outs = [
        out(pair, BF16),
        out(block, F32),
        out(block, F32),
        out(block, F32),
        out((CHIPS, rows, CHIP_COLS), BF16),
        out((CHIPS, half, width), BF16),
        out((half, columns), BF16),
        out((depths, 2 * half, columns), BF16),
        out((8, width), F32),
        out(wide_rows, BF16),
        out((3, width, CHIP_COLS), BF16),
        out((queries, CHIP_COLS), BF16),
        out((tokens, CHIP_COLS), BF16),
        out((tokens, CHIP_COLS), BF16),
        out((tiles, CHIP_COLS, TILE), F32),
        out((tiles, LOCAL_HEADS, 1, TILE), F32),
    ]
    return pl.pallas_call(
        kernel,
        out_shape=outs,
        in_specs=[SM] * 4 + [VM, ANY, ANY] + [VM] * 3 + [ANY] * 7,
        out_specs=[ANY] * 4 + [VM, ANY, VM, ANY, VM] + [ANY] * 6 + [VM],
        scratch_shapes=[
            vmem(pair, BF16),
            vmem(block, F32),
            vmem(block, F32),
            vmem(block, F32),
            vmem((2 * CHIPS, rows, width), BF16),
            vmem((3, width, CHIP_COLS), BF16),
            vmem((queries, CHIP_COLS), BF16),
            vmem((tokens, CHIP_COLS), BF16),
            vmem((tokens, CHIP_COLS), BF16),
            vmem((tiles, CHIP_COLS, TILE), F32),
            vmem((CHIPS, 2, half, width), BF16),
            vmem((CHIPS, half, width), BF16),
            vmem(pair, BF16),
            vmem(pair, BF16),
            vmem((3, depths, 2, half, columns), BF16),
            vmem((depths, CHIPS, out_rows, width), BF16),
            vmem((depths, 2, half, piece_lanes), BF16),
            vmem((CHIPS, rows, CHIP_COLS), BF16),
            vmem((CHIPS, rows // 2, 2 * CHIP_COLS), BF16),
            vmem((3, rows // 2, 2 * CHIP_COLS), BF16),
            vmem((3, rows // 2, 2 * CHIP_COLS), BF16),
            vmem(block, F32),
            vmem((4,) + block, BF16),
            vmem(wide_rows, BF16),
            vmem(wide_rows, BF16),
            vmem((width, queries), BF16),
            vmem((columns, queries), BF16),
            vmem(hid_rows, BF16),
            vmem(hid_rows, F32),
            vmem(hid_rows, F32),
            vmem(hid_rows, BF16),
            vmem(hid_rows, BF16),
            vmem((rows, 128), F32),
            vmem(wide_rows, BF16),
            vmem(wide_rows, BF16),
            vmem((2,) + block, BF16),
            vmem((2,) + block, BF16),
            vmem((2, rows // 2, width), BF16),
            vmem((2, rows // 2, width), BF16),
            vmem((depths, 2, 3 * half, columns), BF16),
            vmem((depths, 3 * half, columns), BF16),
            vmem((depths - 1, half, columns), BF16),
            vmem((depths - 1, half, columns), BF16),
            vmem((3, half, width), BF16),
            vmem((2, half, hidden_cols), BF16),
            vmem((8, 128), F32),
            vmem((queries, CHIP_COLS), BF16),
            vmem((tokens, CHIP_COLS), BF16),
            vmem((tokens, CHIP_COLS), BF16),
            vmem((CHIP_COLS, tokens), BF16),
        ]
        + [DMA((9,))]
        + [DMA((2 * depths - 2,))] * 2
        + [DMA((2 * depths - 1,))] * 2
        + [DMA((depths - 1,))] * 2
        + [DMA((depths,))] * 2
        + [DMA((depths - 1,))] * 4
        + [DMA((6,))] * 2
        + [DMA((6,))] * 2
        + [DMA((4,))] * 2
        + [DMA((3,))] * 2
        + [DMA((6,))] * 4
        + [DMA((3,))] * 2
        + [DMA((6,))] * 4
        + [DMA((3,))] * 2
        + [DMA((11,)), DMA((CHIPS,))]
        + [DMA((depths - 1,))] * 4
        + total_scratch((8, 128), depths),
        compiler_params=comm_params(collective_id),
        name="forward",
    )(
        slots, lengths, predict, correct, states, out_grad, teacher, valid, gain_one, gain_two,
        w_query, w_key, w_value, w_out, w_gate, w_up, w_down,
    )


def backward(
    slots, lengths, predict, correct, att_grad, q_pairs, k_pairs, v_pairs, oT, lse, sums, up_grads,
    out_grads, ff_early, weights, states, up0, up1, hidden_grad, own_rows, collective_id,
):
    rows, _, width = states.shape
    depths, late_rows, ff_columns = up_grads.shape
    half = late_rows // 2
    columns = CHIP_COLS
    lanes_all = 3 * columns
    blocks = rows // ROWS
    tokens = k_pairs.shape[0]
    queries = q_pairs.shape[0]
    tiles = queries // TILE
    per_device = rows // BLK
    group_pairs = tokens // (2 * BLK)
    pairs = queries // (2 * BLK)
    half_tiles = group_pairs * BLK // TILE
    wide_lanes = LOCAL_HEADS * TILE

    def kernel(
        slots_ref, lengths_ref, p_ref, c_ref, g_in, q_in, k_in, v_in, oT_in, lse_ref, sums_ref, u_in,
        og_in, fa_ref, w_in, s_in, up0_in, up1_in, hg_in, x_in,
        grad_out, fa_out, fb_out, q_all, o_all, total_ref,
        grad_ref, fa_all, fb_all, w_all, s_ref, up0_ref, up1_ref, hg_ref, x_own, fa_own, g_ref, q_ref, k_ref, v_ref, oT_ref, u_ref, og_ref,
        g_pairs, kT, doT, dqT, q_stack, do_stack, p_buf, ds_buf, dk_acc, dv_acc, bias, dq_pairs, dq_rows,
        give, kept, came, xT, part, got, far, mine, q_grad, q_other, q_mine, q_far, q_sum,
        o_near, o_mine, o_far, o_sum, u_far, u_sum, all_sums,
        loads, nsend, nrecv, ksend, krecv, send, recv, ssend, srecv, zsend, zrecv, osend, orecv, usend, urecv,
        asend, arecv, fsend, frecv, gsend, grecv, bsend, brecv, psend, precv, *total_refs,
    ):
        depth, chip, core, chip_x, chip_y, chip_d = place_on_mesh()
        near = [(c, (2 * c + core, depth)) for c in (chip_x, chip_y, chip_d)]
        other = (2 * chip + 1 - core, depth)
        across = [
            (2 * chip + core, lax.rem(depth + step, depths)) for step in range(1, depths)
        ]
        peers = plane_peers(chip, core, depth, chip_x, chip_y, chip_d)
        everyone = peers + across
        signal_all(everyone)

        def slot(chip_index):
            return 2 * chip_index + core

        def load(index, source, target):
            copy = pltpu.make_async_copy(source, target, loads.at[index])
            copy.start()
            return copy

        first_loads = [
            load(7 + i, source, target)
            for i, (source, target) in enumerate(
                ((g_in, g_ref), (k_in, k_ref), (q_in, q_ref), (v_in, v_ref), (oT_in, oT_ref))
            )
        ]
        early_load = load(0, fa_ref, fa_own)
        sum_loads = [load(12, u_in, u_ref), load(13, og_in, og_ref)]
        other_loads = [
            load(1 + i, source, target)
            for i, (source, target) in enumerate(
                (
                    (w_in, w_all), (x_in, x_own), (s_in, s_ref), (up0_in, up0_ref), (up1_in, up1_ref), (hg_in, hg_ref)
                )
            )
        ]

        def depth_sum(source_of, inbox, sends, receives):
            return [
                remote(source_of(lax.rem(depth + i + 1, depths)), inbox.at[i], sends, receives, i, device)
                for i, device in enumerate(across)
            ]

        early_load.wait()
        for copy in sum_loads:
            copy.wait()
        wait_all(everyone)
        u_copies = depth_sum(lambda z: u_ref.at[z], u_far, usend, urecv)
        near_grads = [
            remote(og_ref.at[1 + i], o_near.at[i], nsend, nrecv, i, device)
            for i, (_, device) in enumerate(near)
        ]
        a_ring = ring_sends(
            fa_own, fa_all, slot, chip, core, depth, chip_x, chip_y, asend, arecv
        )
        for copy in u_copies + near_grads + a_ring[:4]:
            copy.start()

        def shared(index, ref):
            return remote(ref, ref, psend, precv, index, other)

        in_plane = (chip, chip_x, chip_y, chip_d)
        a_shared = [shared(i, fa_all.at[slot(c)]) for i, c in enumerate(in_plane)]
        b_shared = [shared(4 + i, fb_all.at[slot(c)]) for i, c in enumerate(in_plane)]
        q_shared = [shared(8 + i, q_all.at[slot(c)]) for i, c in enumerate(in_plane)]
        o_shared = shared(12, o_all.at[core])
        fa_all[slot(chip)] = fa_own[...]
        a_shared[0].start()

        for copy in first_loads:
            copy.wait()
        own_to_pair_order(g_ref, g_pairs, slots_ref, pairs, per_device)

        def turn_keys(i, _):
            at = aligned(i, TILE)
            kT[:, at] = k_ref[at, :].T
            return 0

        lax.fori_loop(0, tokens // TILE, turn_keys, 0)

        def attend(kind, step):
            tile = kind * (tiles // 2) + step
            key_tiles = half_tiles * (kind + 1)
            q_tile = q_ref[aligned(tile, TILE), :]
            fill_bias(bias, kind, step, slots_ref, lengths_ref, per_device, group_pairs)
            do_tile = g_pairs[aligned(tile, TILE), :]
            doT[...] = do_tile.astype(F32).T * oT_ref[tile]
            for head in range(LOCAL_HEADS):
                lanes = slice(head * TILE, (head + 1) * TILE)
                heads = slice(head * HD, (head + 1) * HD)
                mask = head_mask(TILE, head)
                q_head = jnp.where(mask, q_tile, jnp.zeros_like(q_tile))
                do_head = jnp.where(mask, do_tile, jnp.zeros_like(do_tile))
                q_stack[lanes, :] = q_head
                do_stack[lanes, :] = do_head
                delta = jnp.sum(doT[heads, :], axis=0, keepdims=True)
                norm = lse_ref[tile, head]
                total = jnp.zeros((HD, TILE), F32)
                for k_tile in range(key_tiles):
                    at = slice(k_tile * TILE, (k_tile + 1) * TILE)
                    s = lax.dot_general(k_ref[at, :], q_head, NT, preferred_element_type=F32)
                    if k_tile >= key_tiles - half_tiles:
                        s = s + bias[k_tile - (key_tiles - half_tiles), :, 0:TILE]
                    dp = lax.dot_general(v_ref[at, :], do_head, NT, preferred_element_type=F32)
                    e = jnp.exp(s - norm)
                    p_buf[at, lanes] = e.astype(BF16)
                    ds = (e * (dp - delta)).astype(BF16)
                    ds_buf[at, lanes] = ds
                    total = total + jnp.dot(kT[heads, at], ds, preferred_element_type=F32)
                dqT[heads, :] = total
            for k_tile in range(key_tiles):
                at = slice(k_tile * TILE, (k_tile + 1) * TILE)
                dv = jnp.dot(p_buf[at, :], do_stack[...], preferred_element_type=F32)
                dk = jnp.dot(ds_buf[at, :], q_stack[...], preferred_element_type=F32)
                if kind == 1:
                    fresh = step == 0
                    dv_acc[at, :] = dv + jnp.where(fresh, 0.0, dv_acc[at, :])
                    dk_acc[at, :] = dk + jnp.where(fresh, 0.0, dk_acc[at, :])
                else:
                    dv_acc[at, :] = dv + dv_acc[at, :]
                    dk_acc[at, :] = dk + dk_acc[at, :]
            dq_pairs[aligned(tile, TILE), :] = dqT[...].T.astype(BF16)

        for kind in (1, 0):

            def body(step, _, kind=kind):
                attend(kind, step)
                return 0

            lax.fori_loop(0, tiles // 2, body, 0)
            if kind == 1:
                a_ring[0].wait_recv()
                a_ring[4].start()
                a_ring[1].wait_recv()
                a_ring[5].start()

        def slot_rows(target, side, chip_index, pair_index):
            pair = chip_index * per_device + side * (per_device // 2) + pair_index
            second, _, _ = pair_places(slots_ref, pair)
            at = 2 * pair_index * BLK
            for i, acc in enumerate((dk_acc, dv_acc)):
                both = either(second, acc[aligned(pair, BLK), :], acc[aligned(group_pairs + pair, BLK), :])
                for j in range(2):
                    target[i, chip_index, at + j * BLK : at + (j + 1) * BLK, :] = both[j].astype(BF16)

        for c in range(CHIPS):
            for i in range(per_device // 2):
                slot_rows(give, 1 - core, c, i)
        swap = remote(give, came, ksend, krecv, 0, other)
        swap.start()
        for c in range(CHIPS):
            for i in range(per_device // 2):
                slot_rows(kept, core, c, i)
        own_to_slot_order(dq_pairs, dq_rows, slots_ref, pairs, per_device)

        for copy in near_grads:
            copy.wait_recv()
        whole = og_ref[0].astype(F32)
        for i in range(3):
            whole = whole + o_near[i].astype(F32)
        o_mine[...] = whole.astype(BF16)
        distance = lax.rem(chip + depths - depth, depths)
        o_copies = [
            remote(o_mine, o_far.at[i], osend, orecv, i, device) for i, device in enumerate(across)
        ]
        for i in range(depths - 1):
            pl.when(distance == i + 1)(o_copies[i].start)
        swap.wait_recv()

        def add_cores(c, _):
            for i in range(2):
                kept[i, c] = (kept[i, c].astype(F32) + came[i, c].astype(F32)).astype(BF16)
            return 0

        lax.fori_loop(0, CHIPS, add_cores, 0)
        for copy in other_loads:
            copy.wait()

        def rows_grad(c):
            return (
                lax.dot_general(
                    dq_rows[aligned(c, rows), :], w_all[0], NT, preferred_element_type=F32
                )
                + lax.dot_general(kept[0, c], w_all[1], NT, preferred_element_type=F32)
                + lax.dot_general(kept[1, c], w_all[2], NT, preferred_element_type=F32)
            )

        give_rows, relay_rows, receive_rows, sends = plane_sum(
            part, got, far, chip, core, depth, chip_x, chip_y, chip_d, send, recv
        )
        for i in (2, 0, 1):
            part[near[i][0]] = rows_grad(near[i][0]).astype(BF16)
            give_rows(i)
        mine[...] = rows_grad(chip)

        def turn(c, _):
            xT[:, aligned(c, rows)] = x_own[c].T
            return 0

        lax.fori_loop(0, CHIPS, turn, 0)

        def weight_grads(z, _):
            at = aligned(z, 2 * half)
            grads = []
            for i in range(3):
                right = dq_rows[...] if i == 0 else kept[i - 1].reshape(queries, columns)
                grads.append(jnp.dot(xT[at, :], right, preferred_element_type=F32))
            grad = jnp.concatenate(grads, axis=1).astype(BF16)
            q_grad[z, 0] = grad[:half]
            q_grad[z, 1] = grad[half:]
            return 0

        lax.fori_loop(0, depths, weight_grads, 0)
        core_swap = remote(q_grad.at[:, 1 - core], q_other, ssend, srecv, 0, other)
        core_swap.start()
        relay_rows()
        core_swap.wait_recv()
        for i in range(depths):
            q_mine[i] = (q_grad[i, core].astype(F32) + q_other[i].astype(F32)).astype(BF16)
        q_copies = depth_sum(lambda z: q_mine.at[z], q_far, zsend, zrecv)
        for copy in q_copies:
            copy.start()

        for copy in u_copies:
            copy.wait_recv()
        whole = u_ref[depth].astype(F32)
        for i in range(depths - 1):
            whole = whole + u_far[i].astype(F32)
        u_sum[...] = whole.astype(BF16)
        b_ring = ring_sends(
            u_sum, fb_all, slot, chip, core, depth, chip_x, chip_y, fsend, frecv
        )
        for copy in b_ring[:4]:
            copy.start()
        fb_all[slot(chip)] = u_sum[...]
        b_shared[0].start()
        a_ring[2].wait_recv()
        a_shared[1].start()
        a_ring[3].wait_recv()
        a_shared[2].start()
        a_ring[4].wait_recv()
        a_ring[5].wait_recv()
        a_shared[3].start()
        receive_rows()

        def state_grads(i, totals):
            at = aligned(i, ROWS)
            s0, s1 = s_ref[at, 0, :].astype(F32), s_ref[at, 1, :].astype(F32)
            a = p_ref[0, 0] * s0 + p_ref[0, 1] * s1
            weighted = mine[at, :]
            for j in range(2):
                weighted = weighted + got[j, at, :].astype(F32)
            factor = norm_factor(a)
            mean = jnp.mean(weighted * a, axis=1, keepdims=True)
            up0, up1 = up0_ref[at, :], up1_ref[at, :]
            result_grad = c_ref[0] * up0 + c_ref[1] * up1
            norm_grad = factor * weighted - a * (factor * factor * factor * mean)
            mixed0 = up0 + (hg_ref[at, :] + norm_grad - result_grad)
            grad_ref[at, 0, :] = (p_ref[0, 0] * mixed0 + p_ref[1, 0] * up1).astype(BF16)
            grad_ref[at, 1, :] = (p_ref[0, 1] * mixed0 + p_ref[1, 1] * up1).astype(BF16)
            terms = (weighted * a * factor, mixed0 * s0, mixed0 * s1, up1 * s0, up1 * s1)
            return tuple(t + jnp.sum(v, axis=0, keepdims=True) for t, v in zip(totals, terms))

        totals = lax.fori_loop(
            0, blocks, state_grads, tuple(jnp.zeros((1, width), F32) for _ in range(5))
        )
        b_ring[0].wait_recv()
        b_ring[4].start()
        b_ring[1].wait_recv()
        b_ring[5].start()
        stores = [load(14, grad_ref, grad_out)]
        all_sums[...] = sums_ref[...]
        all_sums[0:1, :] = totals[0]
        for i in range(4):
            all_sums[4 + i : 5 + i, :] = totals[1 + i]
        start, turn_sums, end = total_over_mesh(
            all_sums, *total_refs[:3], across, peers, *total_refs[3:]
        )
        start()
        for copy in q_copies:
            copy.wait_recv()
        turn_sums()
        whole = q_mine[depth].astype(F32)
        for i in range(depths - 1):
            whole = whole + q_far[i].astype(F32)
        q_sum[...] = whole.astype(BF16)
        q_ring = ring_sends(
            q_sum, q_all, slot, chip, core, depth, chip_x, chip_y, gsend, grecv
        )
        for copy in q_ring[:4]:
            copy.start()
        q_all[slot(chip)] = q_sum[...]
        q_shared[0].start()
        quarter = half // 2
        o_top, o_low = o_all.at[core, pl.ds(0, quarter)], o_all.at[core, pl.ds(quarter, quarter)]
        o_source_top, o_source_low = o_sum.at[pl.ds(0, quarter)], o_sum.at[pl.ds(quarter, quarter)]
        dev_x, dev_y = near[0][1], near[1][1]
        o_ring = [
            remote(o_source_top, o_top, bsend, brecv, 0, dev_x),
            remote(o_source_low, o_low, bsend, brecv, 1, dev_y),
            remote(o_source_low, o_low, bsend, brecv, 2, dev_x),
            remote(o_source_top, o_top, bsend, brecv, 3, dev_y),
            remote(o_top, o_top, bsend, brecv, 4, dev_y),
            remote(o_low, o_low, bsend, brecv, 5, dev_x),
        ]
        source, from_x, from_y = chip == depth, chip_x == depth, chip_y == depth

        @pl.when(source)
        def _():
            for copy in o_copies:
                copy.wait_recv()
            whole = o_mine[...].astype(F32)
            for i in range(depths - 1):
                whole = whole + o_far[i].astype(F32)
            o_sum[...] = whole.astype(BF16)
            for copy in o_ring[:4]:
                copy.start()
            o_all[core] = o_sum[...]

        q_ring[0].wait_recv()
        q_ring[4].start()
        q_ring[1].wait_recv()
        q_ring[5].start()

        @pl.when(from_x)
        def _():
            o_ring[0].wait_recv()
            o_ring[4].start()
            o_ring[2].wait_recv()

        @pl.when(from_y)
        def _():
            o_ring[1].wait_recv()
            o_ring[5].start()
            o_ring[3].wait_recv()

        for copy in a_shared:
            copy.wait_recv()
        stores.append(load(15, fa_all, fa_out))
        for copies, passed in ((b_ring, b_shared), (q_ring, q_shared)):
            copies[2].wait_recv()
            passed[1].start()
            copies[3].wait_recv()
            passed[2].start()
            copies[4].wait_recv()
            copies[5].wait_recv()
            passed[3].start()
        for copy in b_shared:
            copy.wait_recv()
        stores.append(load(16, fb_all, fb_out))

        @pl.when(chip_d == depth)
        def _():
            o_ring[4].wait_recv()
            o_ring[5].wait_recv()

        o_shared.start()
        total_ref[...] = end()
        for copy in q_shared + [o_shared]:
            copy.wait()
        for copy in a_shared + b_shared:
            copy.wait_send()
        for copy in stores:
            copy.wait()
        for copy in u_copies + near_grads + [swap] + sends + [core_swap] + q_copies + a_ring + b_ring + q_ring:
            copy.wait_send()
        for i in range(depths - 1):
            pl.when(distance == i + 1)(o_copies[i].wait_send)

        @pl.when(source)
        def _():
            for copy in o_ring[:4]:
                copy.wait_send()

        pl.when(from_x)(o_ring[4].wait_send)
        pl.when(from_y)(o_ring[5].wait_send)

    vmem = pltpu.VMEM
    block = (rows, width)
    wide_rows = (CHIPS, rows, width)
    q_block, o_block = (half, lanes_all), (half, width)
    kv_half = (2, CHIPS, rows, columns)
    a_block, b_block = ff_early.shape, (late_rows, ff_columns)
    ctx = 2 * CHIPS
    return pl.pallas_call(
        kernel,
        out_shape=[
            jax.ShapeDtypeStruct((rows, 2, width), BF16),
            jax.ShapeDtypeStruct((ctx,) + a_block, BF16),
            jax.ShapeDtypeStruct((ctx,) + b_block, BF16),
            jax.ShapeDtypeStruct((ctx,) + q_block, BF16),
            jax.ShapeDtypeStruct((2,) + o_block, BF16),
            jax.ShapeDtypeStruct((8, width), F32),
        ],
        in_specs=[SM] * 4 + [ANY] * 5 + [VM] * 2 + [ANY] * 9,
        out_specs=[ANY] * 3 + [VM] * 3,
        scratch_shapes=[
            vmem((rows, 2, width), BF16),
            vmem((ctx,) + a_block, BF16),
            vmem((ctx,) + b_block, BF16),
            vmem((3, width, columns), BF16),
            vmem((rows, 2, width), BF16),
            vmem(block, F32),
            vmem(block, F32),
            vmem(block, F32),
            vmem(wide_rows, BF16),
            vmem(a_block, BF16),
            vmem((queries, columns), BF16),
            vmem((queries, columns), BF16),
            vmem((tokens, columns), BF16),
            vmem((tokens, columns), BF16),
            vmem(oT.shape, F32),
            vmem(up_grads.shape, BF16),
            vmem(out_grads.shape, BF16),
            vmem((queries, columns), BF16),
            vmem((columns, tokens), BF16),
            vmem((columns, TILE), F32),
            vmem((columns, TILE), F32),
            vmem((wide_lanes, columns), BF16),
            vmem((wide_lanes, columns), BF16),
            vmem((tokens, wide_lanes), BF16),
            vmem((tokens, wide_lanes), BF16),
            vmem((tokens, columns), F32),
            vmem((tokens, columns), F32),
            vmem((half_tiles, TILE, TILE), F32),
            vmem((queries, columns), BF16),
            vmem((queries, columns), BF16),
            vmem(kv_half, BF16),
            vmem(kv_half, BF16),
            vmem(kv_half, BF16),
            vmem((width, queries), BF16),
            vmem(wide_rows, BF16),
            vmem((2,) + block, BF16),
            vmem((2, rows // 2, width), BF16),
            vmem(block, F32),
            vmem((depths, 2) + q_block, BF16),
            vmem((depths,) + q_block, BF16),
            vmem((depths,) + q_block, BF16),
            vmem((depths - 1,) + q_block, BF16),
            vmem(q_block, BF16),
            vmem((3,) + o_block, BF16),
            vmem(o_block, BF16),
            vmem((depths - 1,) + o_block, BF16),
            vmem(o_block, BF16),
            vmem((depths - 1,) + b_block, BF16),
            vmem(b_block, BF16),
            vmem((8, width), F32),
            DMA((17,)),
            *[DMA((3,))] * 2,
            *[DMA((1,))] * 2,
            *[DMA((6,))] * 2,
            *[DMA((1,))] * 2,
            *[DMA((depths - 1,))] * 6,
            *[DMA((6,))] * 8,
            *[DMA((13,))] * 2,
            *total_scratch((8, width), depths),
        ],
        compiler_params=comm_params(collective_id),
        name="backward",
    )(
        slots, lengths, predict, correct, att_grad, q_pairs, k_pairs, v_pairs, oT, lse, sums, up_grads,
        out_grads, ff_early, weights, states, up0, up1, hidden_grad, own_rows,
    )


def lay_out(new_states, states_grad, early, late, qkv, out, sums, gain_one, gain_two):
    ctx, half, columns = early.shape
    width = out.shape[2]
    shard = 2 * half
    depths = width // shard
    split = columns // depths
    steps = 1
    strip = half // steps

    def kernel(
        new_in, grad_in, d_ref, g_ref, u_ref, q_ref, o_ref, s_ref, g1_ref, g2_ref,
        new_ref, grad_ref, dq_ref, dk_ref, dv_ref, do_ref, dg_ref, du_ref, dd_ref, g1_out, g2_out, p_out, c_out, columns_ref,
    ):
        core, step = pl.program_id(0), pl.program_id(1)
        depth = lax.axis_index("wsh")

        @pl.when((core == 0) & (step == 0))
        def _():
            one = g1_ref[...].astype(F32).reshape(1, shard)
            two = g2_ref[...].astype(F32).reshape(1, shard)
            columns_ref[0] = jnp.broadcast_to(as_column(one), (shard, 128))
            columns_ref[1] = jnp.broadcast_to(as_column(two), (shard, 128))
            for z in range(depths):

                @pl.when(depth == z)
                def _(z=z):
                    g1_out[...] = s_ref[0:1, z * shard : (z + 1) * shard] / one
                    g2_out[...] = s_ref[1:2, z * shard : (z + 1) * shard] / two

            scalars = jnp.sum(s_ref[...], axis=1, keepdims=True)
            for i in range(2):
                c_out[:, i : i + 1] = scalars[2 + i : 3 + i]
                for j in range(2):
                    at = 4 + 2 * i + j
                    p_out[i : i + 1, j : j + 1] = scalars[at : at + 1]

        rows = aligned(core * steps + step, strip)
        one, two = columns_ref[0, rows, 0:1], columns_ref[1, rows, 0:1]
        new_ref[...] = new_in[...]
        grad_ref[...] = grad_in[...]
        do_ref[...] = o_ref[...].astype(F32)
        for i, ref in enumerate((dq_ref, dk_ref, dv_ref)):
            wide = jnp.concatenate(
                [q_ref[p, :, i * CHIP_COLS : (i + 1) * CHIP_COLS].astype(F32) for p in range(CHIPS)], axis=1
            )
            ref[...] = wide * one
        for source, ref in ((g_ref, dg_ref), (u_ref, du_ref)):
            for z in range(depths):
                wide = jnp.concatenate(
                    [source[p, :, z * split : (z + 1) * split].astype(F32) for p in range(CHIPS)], axis=1
                )
                ref[:, z * CHIPS * split : (z + 1) * CHIPS * split] = wide * two
        dd_ref[...] = d_ref[...].astype(F32)

    early = early.reshape(CHIPS, 2, half, columns)
    late = late.reshape(CHIPS, 2, 2, half, columns)
    qkv = qkv.reshape(CHIPS, 2, half, -1)
    square = jax.ShapeDtypeStruct((shard, width), F32)
    tall = jax.ShapeDtypeStruct((shard, columns * CHIPS), F32)
    row = jax.ShapeDtypeStruct((1, shard), F32)

    def whole(shape):
        return pl.BlockSpec(shape, lambda c, r: (0,) * len(shape))

    def piece(lanes):
        return pl.BlockSpec((CHIPS, None, strip, lanes), lambda c, r: (0, c, r, 0))

    def part(i):
        return pl.BlockSpec((CHIPS, None, None, strip, columns), lambda c, r: (0, c, i, r, 0))

    def strip_of(lanes):
        return pl.BlockSpec((strip, lanes), lambda c, r: (c * steps + r, 0))

    rows = new_states.shape[0] // (2 * steps)
    state_rows = pl.BlockSpec((rows,) + new_states.shape[1:], lambda c, r: (c * steps + r, 0, 0))
    outs = pl.pallas_call(
        kernel,
        grid=(2, steps),
        out_shape=[
            jax.ShapeDtypeStruct(new_states.shape, BF16),
            jax.ShapeDtypeStruct(states_grad.shape, BF16),
            square,
            square,
            square,
            square,
            tall,
            tall,
            jax.ShapeDtypeStruct((CHIPS, 2, half, width), F32),
            row,
            row,
            jax.ShapeDtypeStruct((2, 2), F32),
            jax.ShapeDtypeStruct((1, 2), F32),
        ],
        in_specs=[
            state_rows,
            state_rows,
            piece(columns),
            part(0),
            part(1),
            piece(3 * CHIP_COLS),
            pl.BlockSpec((None, strip, width), lambda c, r: (c, r, 0)),
            whole((8, width)),
            whole((shard,)),
            whole((shard,)),
        ],
        out_specs=[
            state_rows,
            state_rows,
            strip_of(width),
            strip_of(width),
            strip_of(width),
            strip_of(width),
            strip_of(columns * CHIPS),
            strip_of(columns * CHIPS),
            piece(width),
            whole((1, shard)),
            whole((1, shard)),
            whole((2, 2)),
            whole((1, 2)),
        ],
        scratch_shapes=[pltpu.VMEM((2, shard, 128), F32)],
        compiler_params=pltpu.CompilerParams(vmem_limit_bytes=VMEM_LIMIT),
        name="lay_out",
    )(new_states, states_grad, early, late, late, qkv, out, sums, gain_one, gain_two)
    return (*outs[:8], outs[8].reshape(ctx * half, width), *outs[9:])


def plane_shards(
    states, block_slot, cont_lengths, valid_mask, teacher, out_grad, predict, correct,
    norm_attn, w_query, w_key, w_value, w_out, norm_ffn, w_gate, w_up, w_down,
):
    slots, lengths = block_slot[0], cont_lengths[0]
    gain_one, gain_two = norm_attn, norm_ffn
    states = states[0]
    new_states, up0, up1, hidden_grad, att_grad, out_grads, ff_early, up_grads, sums, *saved = forward(
        slots, lengths, predict, correct, states, out_grad[0], teacher[0], valid_mask, gain_one, gain_two,
        w_query, w_key, w_value, w_out, w_gate, w_up, w_down, 1,
    )
    own_rows, weights, q_pairs, k_pairs, v_pairs, oT, lse = saved
    states_grad, *gathered = backward(
        slots, lengths, predict, correct, att_grad.reshape(-1, CHIP_COLS), q_pairs, k_pairs, v_pairs, oT, lse,
        sums, up_grads, out_grads, ff_early, weights, states, up0, up1, hidden_grad, own_rows, 2,
    )
    new_states, states_grad, dq, dk, dv, do, dg, du, dd, g_one, g_two, predict_grad, correct_grad = lay_out(
        new_states, states_grad, *gathered, gain_one, gain_two
    )
    return (
        new_states[None], states_grad[None], predict_grad, correct_grad[0],
        g_one[0], dq, dk, dv, do, g_two[0], dg, du, dd,
    )


def fits_plane(mesh, states, block_slot, w_query, w_gate):
    ctx, depths = mesh.shape["ctx"], mesh.shape["wsh"]
    return (
        ctx == 2 * CHIPS
        and depths == CHIPS
        and states.shape[0] == depths
        and block_slot.shape[1] * BLK == 2 * PROMPT
        and states.shape[1] == 2 * PROMPT
        and w_query.shape[0] % (32 * depths) == 0
        and w_gate.shape[1] % (32 * CHIPS * depths) == 0
    )


def solution(mesh):
    in_specs = (
        P("wsh", "ctx", None, None),
        P("wsh", None),
        P("wsh", None),
        P("wsh", "ctx"),
        P("wsh", "ctx", None, None),
        P("wsh", "ctx", None, None),
        P(),
        P(),
        P("wsh"),
        P("wsh", None),
        P("wsh", None),
        P("wsh", None),
        P("wsh", None),
        P("wsh"),
        P("wsh", None),
        P("wsh", None),
        P("wsh", None),
    )
    out_specs = (
        P("wsh", "ctx", None, None),
        P("wsh", "ctx", None, None),
        P(),
        P(),
        P("wsh"),
        P("wsh", None),
        P("wsh", None),
        P("wsh", None),
        P("wsh", None),
        P("wsh"),
        P("wsh", None),
        P("wsh", None),
        P("wsh", None),
    )

    def step(*args):
        plane = fits_plane(mesh, args[0], args[1], args[9], args[14])
        body = plane_shards if plane else general_shards
        return jax.shard_map(
            body, mesh=mesh, in_specs=in_specs, out_specs=out_specs, check_vma=False
        )(*args)

    return step
```
